256 devices in a mesh: lat: 8 (over z), lon: 32 (over x, y, core).
Axes of the slice: x: 4, y: 4, z: 8, core: 2. Of those that a mesh axis runs over, the one named last changes fastest.
Arguments:
- surface_forcing: float32 [4320, 2048], P('lon', 'lat'), may hold values from -40 to 40
- ocean_mask: int32 [4320, 2048], P('lon', 'lat'), may hold values 0 or 1
- self_coupling: float32 [4320, 2048], P('lon', 'lat'), may hold values from 0.2 to 2
- east_coupling: float32 [4320, 2048], P('lon', 'lat'), may hold values from 0.3 to 3
- north_coupling: float32 [4320, 2048], P('lon', 'lat'), may hold values from 0.3 to 3
- zonal_weight: float32 [2048], P('lat'), may hold values from 0.5 to 50
- aligned_inverse: float32 [16, 128, 128], P('lat'), may hold values from -1 to 4, as said below
- staggered_inverse: float32 [16, 128, 128], P('lat'), may hold values from -1 to 4, as said below
Outputs:
- solution: float32 [4320, 2048], P('lon', 'lat')
- residual: float32 [4320, 2048], P('lon', 'lat')
- direction: float32 [4320, 2048], P('lon', 'lat')
The draws below stay inside these ranges and needn't reach their ends.
Inputs may be any that keep to these rules, and one draw needn't show every extreme that they name: `aligned_inverse`: each block is symmetric and positive definite. `staggered_inverse`: each block is symmetric and positive definite.
All inputs are finite; a program needn't handle non-finite values. No bound on the sum of `ocean_mask` on one device may be relied on, other than what follows from the above.
Results may differ from the reference program's by a relative error of at most 0.00023.
Values sent between devices are 32-bit elements; how exact they have to be, the bound alone decides.
No kernel may reach another device: no remote copies, remote signals or barrier semaphores. Data moves between devices by JAX's collectives and lax.ppermute only.
A program may use at most 64 MiB of HBM per device.

```python
import math
import jax
import jax.numpy as jnp
from jax import lax

NLON = 4320
BL = 128
NLAT = 2048
NBLK = 16


def draw_surface_forcing(key, part):
    first = jax.random.fold_in(jax.random.fold_in(key, 7), 0)
    lon_pos = jnp.arange(NLON).astype(jnp.float32) / NLON
    lat_pos = jnp.arange(NLAT).astype(jnp.float32) / NLAT
    ramp = (1.0 + 2.0 * lon_pos)[:, None] * (1.0 + 2.0 * lat_pos)[None, :]
    values = ramp * jnp.clip(jax.random.normal(first, (NLON, NLAT), jnp.float32), -4.4, 4.4)
    return values


def inverse_blocks(key, ratio, lowest, highest):
    first, second = jax.random.split(key, 2)
    index = jnp.arange(BL)
    distance = jnp.abs(index[:, None] - index[None, :]).astype(jnp.float32)
    decaying = jnp.power(jnp.float32(ratio), distance)
    mixing = jax.random.uniform(first, (NBLK, BL, BL), jnp.float32, -1.0, 1.0)
    gram = jnp.einsum('bij,bkj->bik', mixing, mixing) / (2.0 * BL)
    core = 0.5 * jnp.eye(BL, dtype=jnp.float32)[None] + decaying[None] + gram
    scales = jnp.exp(jax.random.uniform(second, (NBLK, BL), jnp.float32, jnp.log(lowest), jnp.log(highest)))
    return 0.3 * scales[:, :, None] * core * scales[:, None, :]


def draw_aligned_inverse(key, part):
    return inverse_blocks(jax.random.fold_in(key, 11), 0.6, 0.5, 2.0)


def draw_staggered_inverse(key, part):
    return inverse_blocks(jax.random.fold_in(key, 23), 0.6, 0.5, 2.0)


def place_ends(array, stream_key, smallest, high):
    extent = array.shape
    spot = [jax.random.randint(jax.random.fold_in(stream_key, axis), (), 0, extent[axis]) for axis in range(len(extent))]
    array = array.at[tuple(spot)].set(smallest)
    longest = extent.index(max(extent))
    spot[longest] = (spot[longest] + 1) % extent[longest]
    return array.at[tuple(spot)].set(high)


def shard_levels(key, extent, cuts, smallest, top_value):
    factor_of = 1.0
    for dim, shards_of in cuts:
        steps = jax.random.uniform(jax.random.fold_in(jax.random.fold_in(key, 6), dim), (shards_of,), jnp.float32, smallest / len(cuts), top_value / len(cuts))
        factor_of = factor_of * jnp.repeat(jnp.exp(steps), extent[dim] // shards_of).reshape((-1,) + (1,) * (len(extent) - 1 - dim))
    return factor_of


def setup_inputs(seed: int = 0) -> dict:
    keys = jax.random.split(jax.random.key(seed), 9)
    return {
        "surface_forcing": draw_surface_forcing(jax.random.fold_in(keys[8], 71), 0),
        "ocean_mask": place_ends((jax.random.randint(keys[1], (NLON, NLAT), 0, 5) < 4).astype(jnp.int32), jax.random.fold_in(keys[1], 1), 0, 1),
        "self_coupling": jnp.clip(jnp.exp(math.log(2.0) - 2.3025851 * jax.random.uniform(keys[2], (NLON, NLAT), jnp.float32) ** shard_levels(keys[2], (NLON, NLAT), ((0, 32), (1, 8)), -0.2, 0.2)), 0.2, 2.0),
        "east_coupling": jnp.clip(jnp.exp(math.log(3.0) - 2.3025851 * jax.random.uniform(keys[3], (NLON, NLAT), jnp.float32) ** shard_levels(keys[3], (NLON, NLAT), ((0, 32), (1, 8)), -0.2, 0.2)), 0.3, 3.0),
        "north_coupling": jnp.clip(jnp.exp(math.log(3.0) - 2.3025851 * jax.random.uniform(keys[4], (NLON, NLAT), jnp.float32) ** shard_levels(keys[4], (NLON, NLAT), ((0, 32), (1, 8)), -0.2, 0.2)), 0.3, 3.0),
        "zonal_weight": jnp.clip(jnp.exp(math.log(50.0) - 4.6051702 * jax.random.uniform(keys[5], (NLAT,), jnp.float32) ** shard_levels(keys[5], (NLAT,), ((0, 8),), -0.2, 0.2)), 0.5, 50.0),
        "aligned_inverse": draw_aligned_inverse(jax.random.fold_in(keys[8], 71), 0),
        "staggered_inverse": draw_staggered_inverse(jax.random.fold_in(keys[8], 71), 0),
    }


FULL_TURN = 6.283185307179586

def blockwise(parts, inverse):
    shaped = parts.reshape(2, NLON, NBLK, BL)
    result = jnp.einsum('bij,smbj->smbi', inverse, shaped, precision=lax.Precision.HIGHEST)
    return result.reshape(2, NLON, NLAT)

def staggered(parts, inverse):
    half = BL // 2
    zeros = jnp.zeros((2, NLON, half), parts.dtype)
    moved = jnp.concatenate([parts[:, :, half:], zeros], axis=2)
    result = blockwise(moved, inverse)
    return jnp.concatenate([zeros, result[:, :, :NLAT - half]], axis=2)

def precondition(field, wet, zonal_weight, aligned_inverse, staggered_inverse):
    spectrum = jnp.fft.fft(field, axis=0)
    modes = jnp.arange(NLON).astype(jnp.float32)
    wave = 2.0 - 2.0 * jnp.cos(FULL_TURN * modes / NLON)
    scale = lax.rsqrt(1.0 + zonal_weight[None, :] * wave[:, None])
    parts = jnp.stack([spectrum.real, spectrum.imag]) * scale
    combined = (blockwise(parts, aligned_inverse) + staggered(parts, staggered_inverse)) * scale
    back = jnp.fft.ifft(combined[0] + 1j * combined[1], axis=0).real
    return wet * back

def reference(surface_forcing, ocean_mask, self_coupling, east_coupling, north_coupling, zonal_weight, aligned_inverse, staggered_inverse):
    wet = ocean_mask.astype(jnp.float32)
    row_index = jnp.arange(NLAT)
    top_flag = jnp.where(row_index < NLAT - 1, 1.0, 0.0).astype(jnp.float32)
    east = east_coupling * wet * jnp.roll(wet, -1, axis=0)
    north = north_coupling * wet * jnp.roll(wet, -1, axis=1) * top_flag[None, :]
    west = jnp.roll(east, 1, axis=0)
    south = jnp.roll(north, 1, axis=1)

    def operate(field):
        result = (1.0 - wet) * field + wet * self_coupling * field
        result = result + east * (field - jnp.roll(field, -1, axis=0))
        result = result + west * (field - jnp.roll(field, 1, axis=0))
        result = result + north * (field - jnp.roll(field, -1, axis=1))
        result = result + south * (field - jnp.roll(field, 1, axis=1))
        return result
    rhs_wet = wet * surface_forcing
    first = precondition(rhs_wet, wet, zonal_weight, aligned_inverse, staggered_inverse)
    rz_now = jnp.sum(rhs_wet * first)
    image = operate(first)
    curvature = jnp.sum(first * image)
    alpha = rz_now / curvature
    solution = alpha * first
    residual = rhs_wet - alpha * image
    second = precondition(residual, wet, zonal_weight, aligned_inverse, staggered_inverse)
    rz_next = jnp.sum(residual * second)
    direction = second + rz_next / rz_now * first
    return (solution, residual, direction)
```

```python
import jax
import jax.numpy as jnp
import numpy as np
from jax import lax
from jax.experimental import pallas as pl
from jax.experimental.pallas import tpu as pltpu
from jax.sharding import Mesh
from jax.sharding import PartitionSpec as P

LON = ("lon_0", "lon_1", "lon_2")
LAT_LON = ("lat", "lon_0", "lon_1", "lon_2")
HIGHEST = lax.Precision.HIGHEST
TURN = 2.0 * np.pi
ROWS = 8
WIDE = 256
HALO = 136
FOLD = 68
SCALARS = 208


def tables(groups, length):
    period = groups * length
    index = np.arange(length)
    inner = TURN * (np.outer(index, index) % length) / length
    wave_of = np.zeros(groups, np.int64)
    wave_of[1] = groups // 2
    for m in range(1, groups // 2):
        wave_of[2 * m] = wave_of[2 * m + 1] = m
    turn = TURN * (np.outer(wave_of, index) % period) / period
    matrices = np.zeros((2, WIDE, WIDE))
    matrices[0, :length, :length] = np.cos(inner)
    matrices[1, :length, :length] = np.sin(inner)
    twiddle = np.zeros((2, groups, WIDE))
    twiddle[0, :, :length] = np.cos(turn)
    twiddle[1, :, :length] = np.sin(turn)
    chunk = np.arange(groups)
    outer = np.zeros((2, groups, groups))
    for c in range(groups):
        phase = TURN * (chunk * wave_of[c] % groups) / groups
        if c < 2:
            outer[0, :, c] = outer[1, :, c] = np.cos(phase)
        elif c % 2 == 0:
            outer[0, :, c], outer[1, :, c] = 2 * np.cos(phase), -2 * np.sin(phase)
        else:
            outer[0, :, c], outer[1, :, c] = -2 * np.sin(phase), -2 * np.cos(phase)
    modes = wave_of[:, None] + groups * index[None, :]
    wave = np.zeros((groups, WIDE))
    wave[:, :length] = 4.0 * np.sin(np.pi * modes / period) ** 2
    return (
        matrices.astype(np.float32),
        (matrices / period).astype(np.float32),
        twiddle.astype(np.float32),
        outer.astype(np.float32),
        wave.astype(np.float32),
    )


def real_fft(values):
    count = len(values)
    if count == 2:
        return [(values[0] + values[1], None), (values[0] - values[1], None)]
    even, odd = real_fft(values[0::2]), real_fft(values[1::2])
    out = [None] * (count // 2 + 1)
    for k in range(count // 4 + 1):
        (er, ei), (re, im) = even[k], odd[k]
        if k == 0:
            out[0], out[count // 2] = (er + re, None), (er - re, None)
        elif k == count // 4:
            out[k] = (er, -re)
        else:
            c, s = float(np.cos(TURN * k / count)), float(-np.sin(TURN * k / count))
            tr, ti = re * c - im * s, im * c + re * s
            out[k], out[count // 2 - k] = (er + tr, ei + ti), (er - tr, ti - ei)
    return out


def real_ifft(spectrum):
    count = 2 * (len(spectrum) - 1)
    if count == 2:
        return [spectrum[0][0] + spectrum[1][0], spectrum[0][0] - spectrum[1][0]]
    even, odd = [], []
    for k in range(count // 4 + 1):
        (ar, ai), (br, bi) = spectrum[k], spectrum[count // 2 - k]
        if k == 0:
            even.append((ar + br, None))
            odd.append((ar - br, None))
        elif k == count // 4:
            even.append((2.0 * ar, None))
            odd.append((-2.0 * ai, None))
        else:
            c, s = float(np.cos(TURN * k / count)), float(np.sin(TURN * k / count))
            dr, di = ar - br, ai + bi
            even.append((ar + br, ai - bi))
            odd.append((dr * c - di * s, dr * s + di * c))
    first, second = real_ifft(even), real_ifft(odd)
    out = []
    for a, b in zip(first, second, strict=True):
        out += [a, b]
    return out


def dot(a, b):
    return jnp.dot(a, b, precision=HIGHEST, preferred_element_type=jnp.float32)


def rows_of(p):
    return slice(ROWS * p, ROWS * (p + 1))


def lanes(shape):
    return lax.broadcasted_iota(jnp.int32, shape, len(shape) - 1)


def transform(chunks, matrix_ref, twiddle_ref, left, right):
    groups = len(chunks)
    mixed = real_fft(chunks)
    for m in range(groups // 2 + 1):
        re, im = mixed[m]
        if m == 0:
            left[rows_of(0), :] = re
            right[rows_of(0), :] = re
            continue
        c = 1 if m == groups // 2 else 2 * m
        cos, sin = twiddle_ref[0, c : c + 1, :], twiddle_ref[1, c : c + 1, :]
        if m == groups // 2:
            left[rows_of(1), :] = re * (cos + sin)
            right[rows_of(1), :] = re * (cos - sin)
        else:
            tr, ti = re * cos + im * sin, im * cos - re * sin
            left[rows_of(c), :] = tr
            right[rows_of(c), :] = ti
            left[rows_of(c + 1), :] = ti
            right[rows_of(c + 1), :] = -tr
    return dot(left[...], matrix_ref[0]) + dot(right[...], matrix_ref[1])


def transform_back(spectrum, groups, scaled_ref, twiddle_ref):
    pc, ps = dot(spectrum, scaled_ref[0]), dot(spectrum, scaled_ref[1])
    mixed = []
    for m in range(groups // 2 + 1):
        if m == 0:
            mixed.append((pc[rows_of(0)] + ps[rows_of(0)], None))
            continue
        c = 1 if m == groups // 2 else 2 * m
        cos, sin = twiddle_ref[0, c : c + 1, :], twiddle_ref[1, c : c + 1, :]
        if m == groups // 2:
            mixed.append((pc[rows_of(1)] * (cos + sin) + ps[rows_of(1)] * (cos - sin), None))
        else:
            hr = pc[rows_of(c)] - ps[rows_of(c + 1)]
            hi = ps[rows_of(c)] + pc[rows_of(c + 1)]
            mixed.append((hr * cos - hi * sin, hi * cos + hr * sin))
    return real_ifft(mixed)


def row_back(spectrum, scaled_ref, twiddle_ref, outer_ref):
    pc, ps = dot(spectrum, scaled_ref[0]), dot(spectrum, scaled_ref[1])
    cos, sin = twiddle_ref[0], twiddle_ref[1]
    return dot(outer_ref[0], pc * cos - ps * sin) + dot(outer_ref[1], ps * cos + pc * sin)


def forward_kernel(groups, field_ref, matrix_ref, twiddle_ref, out_ref, left, right):
    chunks = [field_ref[rows_of(p), :WIDE] for p in range(groups)]
    out_ref[...] = transform(chunks, matrix_ref, twiddle_ref, left, right)


def blocks_kernel(spec_ref, scale_ref, aligned_ref, scaled_ref, part_ref, down_ref, up_ref):
    count, block = aligned_ref.shape[0], aligned_ref.shape[1]
    half, rows = block // 2, count * block
    scaled = spec_ref[...] * scale_ref[...]
    scaled_ref[...] = scaled
    for b in range(count):
        part_ref[b * block : (b + 1) * block, :] = dot(
            aligned_ref[b], scaled[b * block : (b + 1) * block]
        )
    down_ref[:half, :] = scaled[:half]
    down_ref[half : half + 8, :] = part_ref[:8, :]
    down_ref[half + 8 :, :] = scale_ref[:8, :]
    up_ref[:half, :] = scaled[rows - half :]
    up_ref[half : half + 8, :] = part_ref[rows - 8 :, :]
    up_ref[half + 8 :, :] = scale_ref[rows - 8 :, :]


def combine(scaled_ref, part_ref, scale_ref, above_ref, below_ref, stag_ref, stag_below_ref):
    count, block = stag_ref.shape[0], stag_ref.shape[1]
    half, rows = block // 2, count * block
    before = dot(
        stag_below_ref[...],
        jnp.concatenate([below_ref[:half, :], scaled_ref[:half, :]], axis=0),
    )
    pieces = [before[half:]]
    for b in range(count - 1):
        pieces.append(dot(stag_ref[b], scaled_ref[half + b * block : half + (b + 1) * block, :]))
    after = dot(
        stag_ref[count - 1],
        jnp.concatenate([scaled_ref[rows - half :, :], above_ref[:half, :]], axis=0),
    )
    pieces.append(after[:half])
    full = (part_ref[...] + jnp.concatenate(pieces, axis=0)) * scale_ref[...]
    return full, before, after


def halo_kernel(
    scaled_ref, part_ref, scale_ref, above_ref, below_ref, stag_ref, stag_below_ref, out_ref, low, high
):
    half = stag_ref.shape[1] // 2
    full, before, after = combine(
        scaled_ref, part_ref, scale_ref, above_ref, below_ref, stag_ref, stag_below_ref
    )
    row_below = (before[half - 1 : half] + below_ref[half + 7 : half + 8, :]) * below_ref[
        half + 15 : half + 16, :
    ]
    row_above = (after[half : half + 1] + above_ref[half : half + 1, :]) * above_ref[
        half + 8 : half + 9, :
    ]
    out_ref[:, :128] = full[:, :128]
    low[...] = full[:, :128]
    high[...] = full[:, 128:]
    groups = full.shape[0] // ROWS

    def strided(start):
        at = pl.ds(start, groups, stride=ROWS)
        return jnp.concatenate([low[at, :], high[at, :]], axis=1)

    row = lax.broadcasted_iota(jnp.int32, (groups, WIDE), 0)
    up = jnp.where(row == 0, row_below, pltpu.roll(strided(ROWS - 1), 1, 0))
    down = jnp.where(row == groups - 1, row_above, pltpu.roll(strided(0), groups - 1, 0))
    lane = lanes((groups, 128)) + 128
    for s, part in enumerate(
        (
            pltpu.roll(up, HALO, 1),
            pltpu.roll(up, HALO - FOLD, 1),
            pltpu.roll(down, HALO, 1),
            pltpu.roll(down, HALO - FOLD, 1),
        )
    ):
        at = pl.ds(s, groups, stride=ROWS)
        high[at, :] = jnp.where(lane >= HALO, part[:, 128:], high[at, :])
    out_ref[:, 128:] = high[...]


def sums_kernel(
    weight,
    length,
    scaled_ref,
    part_ref,
    scale_ref,
    above_ref,
    below_ref,
    stag_ref,
    stag_below_ref,
    image_ref,
    rhs_ref,
    weight_ref,
    sums_ref,
    out_ref,
):
    full, _, _ = combine(
        scaled_ref, part_ref, scale_ref, above_ref, below_ref, stag_ref, stag_below_ref
    )
    lane = lanes(full.shape)
    held = lane < length
    norm = weight_ref[0, 0]
    own = jnp.sum(jnp.where(held, full * image_ref[...], 0.0)) * norm
    cross = jnp.sum(jnp.where(held, full * rhs_ref[...], 0.0)) * norm
    out = jnp.where(lane == SCALARS, sums_ref[0, 0], full)
    out = jnp.where(lane == SCALARS + 1, sums_ref[0, 1], out)
    out = jnp.where(lane == SCALARS + 2, own, out)
    out_ref[...] = jnp.where(lane == SCALARS + 3, cross, out)


def step_kernel(
    groups,
    length,
    spec_ref,
    rhs_ref,
    diagonal_ref,
    wet_ref,
    east_ref,
    west_ref,
    north_ref,
    south_ref,
    matrix_ref,
    inverse_ref,
    twiddle_ref,
    outer_ref,
    out_ref,
    first_ref,
    image_ref,
    sums_ref,
    left,
    right,
    low,
    high,
    tail,
):
    lane_row = lanes((groups, WIDE))
    stride = 3 * ROWS
    tail[...] = spec_ref[:, 128:]

    def halo_row(s):
        blank = jnp.zeros((groups, 128), jnp.float32)
        parts = [
            jnp.concatenate([tail[pl.ds(s + n, groups, stride=ROWS), :], blank], axis=1)
            for n in range(2)
        ]
        row = jnp.where(
            lane_row < FOLD,
            pltpu.roll(parts[0], WIDE - (HALO - 128), 1),
            pltpu.roll(parts[1], FOLD - (HALO - 128), 1),
        )
        return row_back(row, inverse_ref, twiddle_ref, outer_ref)

    for start, s in ((ROWS - 1, 0), (2 * ROWS, 2)):
        row = halo_row(s)
        low[pl.ds(start, groups, stride=stride), :] = row[:, :128]
        high[pl.ds(start, groups, stride=stride), :] = row[:, 128:]

    def neighbour(start):
        at = slice(start, start + ROWS)
        return jnp.concatenate([low[at, :], high[at, :]], axis=1)

    cells = transform_back(spec_ref[...], groups, inverse_ref, twiddle_ref)
    for p in range(groups):
        v = cells[p] * wet_ref[rows_of(p), :]
        first_ref[rows_of(p), :] = v
        low[stride * p + ROWS : stride * p + 2 * ROWS, :] = v[:, :128]
        high[stride * p + ROWS : stride * p + 2 * ROWS, :] = v[:, 128:]
    lane = lanes((ROWS, WIDE))
    rz = jnp.zeros((ROWS, WIDE), jnp.float32)
    curvature = jnp.zeros((ROWS, WIDE), jnp.float32)
    images = []
    for p in range(groups):
        at = rows_of(p)
        v = first_ref[at, :]
        after = first_ref[rows_of((p + 1) % groups), 0:1]
        before = first_ref[rows_of((p - 1) % groups), length - 1 : length]
        ring = jnp.where(lane == length, after, jnp.where(lane == WIDE - 1, before, v))
        base = stride * p + ROWS
        image = diagonal_ref[at, :] * v
        image = image + east_ref[at, :] * (v - pltpu.roll(ring, WIDE - 1, 1))
        image = image + west_ref[at, :] * (v - pltpu.roll(ring, 1, 1))
        image = image + north_ref[at, :] * (v - neighbour(base + 1))
        image = image + south_ref[at, :] * (v - neighbour(base - 1))
        image_ref[at, :] = image
        images.append(image)
        rz = rz + rhs_ref[at, :WIDE] * v
        curvature = curvature + v * image
    small = lanes((8, 128))
    sums_ref[...] = jnp.where(
        small == 0, jnp.sum(rz), jnp.where(small == 1, jnp.sum(curvature), 0.0)
    )
    out_ref[...] = transform(images, matrix_ref, twiddle_ref, left, right)


def last_kernel(
    groups,
    length,
    spec_ref,
    wet_ref,
    first_ref,
    image_ref,
    inverse_ref,
    twiddle_ref,
    out_ref,
    sums_ref,
):
    riders = jnp.sum(spec_ref[:, 128:], axis=0, keepdims=True) * (1.0 / ROWS)
    sums_ref[...] = jnp.broadcast_to(riders, (8, 128))
    cells = transform_back(spec_ref[...], groups, inverse_ref, twiddle_ref)
    blank = jnp.zeros((ROWS, WIDE), jnp.float32)
    for p in range(groups):
        at = rows_of(p)
        parts = [first_ref[at, :], image_ref[at, :], cells[p] * wet_ref[at, :]]
        packed = jnp.concatenate([parts[0], blank], axis=1)
        for n in (1, 2):
            shifted = pltpu.roll(jnp.concatenate([parts[n], blank], axis=1), n * length, 1)
            packed = packed + shifted
        out_ref[at, :] = packed


def call(kernel, out_shapes, scratch=(), name=None):
    single = not isinstance(out_shapes, (list, tuple)) or isinstance(out_shapes[0], int)
    shapes = [out_shapes] if single else out_shapes
    outs = [jax.ShapeDtypeStruct(s, jnp.float32) for s in shapes]
    return pl.pallas_call(
        kernel,
        out_shape=outs[0] if single else outs,
        scratch_shapes=[pltpu.VMEM(s, jnp.float32) for s in scratch],
        compiler_params=pltpu.CompilerParams(vmem_limit_bytes=48 * 2**20),
        name=name,
    )


def exchanged(value):
    groups = lax.axis_size(LON)
    parts = value.reshape(groups, ROWS, value.shape[1])
    return lax.all_to_all(parts, LON, split_axis=0, concat_axis=0, tiled=True).reshape(value.shape)


def from_lat(value, steps, ring):
    count = lax.axis_size("lat")
    pairs = [(d + steps, d) for d in range(count)]
    if ring:
        pairs = [(s % count, d) for s, d in pairs]
    return lax.ppermute(value, "lat", [(s, d) for s, d in pairs if 0 <= s < count])


def from_slab(value, steps):
    count = lax.axis_size("lat") * lax.axis_size(LON)
    pairs = [(d + steps, d) for d in range(count)]
    return lax.ppermute(value, LAT_LON, [(s, d) for s, d in pairs if 0 <= s < count])


def widened(value):
    return jnp.pad(value, [(0, 0)] * (value.ndim - 1) + [(0, WIDE - value.shape[-1])])


def local(
    surface_forcing,
    ocean_mask,
    self_coupling,
    east_coupling,
    north_coupling,
    zonal_weight,
    aligned_inverse,
    staggered_inverse,
):
    groups = lax.axis_size(LON)
    length, rows = surface_forcing.shape
    matrices, inverse, twiddle, outer, wave = tables(groups, length)
    channel = lax.axis_index(LON)
    count, block = aligned_inverse.shape[0], aligned_inverse.shape[1]
    half = block // 2

    wet_cells = ocean_mask.astype(jnp.float32)
    rhs_cells = wet_cells * surface_forcing
    fields = [
        rhs_cells,
        wet_cells * self_coupling,
        wet_cells * east_coupling,
        wet_cells * north_coupling,
    ]
    stacked = jnp.concatenate(fields, axis=0)
    stacked = jnp.pad(stacked, ((0, -stacked.shape[0] % 128), (0, 0)))
    slab = exchanged(stacked.T)

    def field(n):
        return slab[:, n * length : (n + 1) * length].reshape(groups, ROWS, length)

    own, east, north = field(1), field(2), field(3)
    ocean = own > 0.0
    wet = ocean.astype(jnp.float32)
    wet_next = jnp.concatenate([wet[:, :, 1:], jnp.roll(wet[:, :, :1], -1, axis=0)], axis=2)
    east = east * wet_next
    west = jnp.concatenate([jnp.roll(east[:, :, -1:], 1, axis=0), east[:, :, :-1]], axis=2)
    wet_above = from_slab(wet[:, 0, :], 1)
    north_below = from_slab(north[:, -1, :], -1)
    south = jnp.concatenate([north_below[:, None, :], north[:, :-1, :]], axis=1) * wet
    north = north * jnp.concatenate([wet[:, 1:, :], wet_above[:, None, :]], axis=1)
    diagonal = jnp.where(ocean, own, 1.0)
    flat = [widened(v).reshape(rows, WIDE) for v in (diagonal, wet, east, west, north, south)]
    wet_slab = flat[1]

    scale = lax.rsqrt(1.0 + zonal_weight[:, None] * lax.dynamic_slice_in_dim(wave, channel, 1, 0))
    stag_below = from_lat(staggered_inverse[count - 1], -1, False)
    weight = jnp.where(channel < 2, 1.0, 2.0).astype(jnp.float32) / (groups * length)

    wide = (rows, WIDE)
    edge = (half + 16, WIDE)
    transforms = [wide, wide]

    def blocks(spectrum):
        scaled, part, down, up = call(blocks_kernel, [wide, wide, edge, edge], name="blocks")(
            spectrum, scale, aligned_inverse
        )
        above, below = from_lat(down, 1, False), from_lat(up, -1, False)
        return scaled, part, scale, above, below, staggered_inverse, stag_below

    spec_rhs = exchanged(
        call(lambda *r: forward_kernel(groups, *r), wide, transforms, name="forward")(
            slab, matrices, twiddle
        )
    )
    filtered = exchanged(call(halo_kernel, wide, [(rows, 128)] * 2, name="halo")(*blocks(spec_rhs)))
    spec, first, image, sums = call(
        lambda *r: step_kernel(groups, length, *r),
        [wide, wide, wide, (8, 128)],
        transforms + [(3 * rows, 128)] * 2 + [(rows, 128)],
        name="step",
    )(filtered, slab, *flat, matrices, inverse, twiddle, outer)
    spec_image = exchanged(spec)
    smem = pl.BlockSpec(memory_space=pltpu.SMEM)
    vmem = pl.BlockSpec(memory_space=pltpu.VMEM)
    filtered = pl.pallas_call(
        lambda *r: sums_kernel(None, length, *r),
        out_shape=jax.ShapeDtypeStruct(wide, jnp.float32),
        in_specs=[vmem] * 9 + [smem, smem],
        out_specs=vmem,
        compiler_params=pltpu.CompilerParams(vmem_limit_bytes=48 * 2**20),
        name="sums",
    )(*blocks(spec_image), spec_image, spec_rhs, weight.reshape(1, 1), sums)
    packed, lon_sums = call(
        lambda *r: last_kernel(groups, length, *r), [(rows, 2 * WIDE), (8, 128)], name="last"
    )(exchanged(filtered), wet_slab, first, image, inverse, twiddle)

    behind = from_lat(lon_sums, -1, True)
    pair = lon_sums + behind
    three = pair + from_lat(lon_sums, 1, True)
    totals = three + from_lat(three, 3, True) + from_lat(pair, -2, True)
    at = SCALARS - 128
    rz, curvature, own_sum, cross = [totals[0, at + n] for n in range(4)]
    alpha = rz / curvature
    rz_next = rz - alpha * curvature - alpha * cross + alpha * alpha * own_sum

    back = exchanged(packed).T
    first, image, image_back = [back[n * length : (n + 1) * length] for n in range(3)]
    solution = alpha * first
    residual = rhs_cells - alpha * image
    direction = (first - alpha * image_back) + rz_next / rz * first
    return (solution, residual, direction)


def solution(mesh):
    torus = Mesh(
        mesh.devices.reshape(mesh.shape["lat"], 4, 4, 2), ("lat", "lon_0", "lon_1", "lon_2")
    )
    return jax.shard_map(
        local,
        mesh=torus,
        in_specs=(
            P(LON, "lat"),
            P(LON, "lat"),
            P(LON, "lat"),
            P(LON, "lat"),
            P(LON, "lat"),
            P("lat"),
            P("lat", None, None),
            P("lat", None, None),
        ),
        out_specs=(P(LON, "lat"), P(LON, "lat"), P(LON, "lat")),
        check_vma=False,
    )
```

```python
import jax
import jax.numpy as jnp
import numpy as np
from jax import lax
from jax.experimental import pallas as pl
from jax.experimental.pallas import tpu as pltpu
from jax.sharding import Mesh
from jax.sharding import PartitionSpec as P

LON = ("lon_0", "lon_1", "lon_2")
LAT_LON = ("lat", "lon_0", "lon_1", "lon_2")
TURN = 2.0 * np.pi
ROWS = 8
WIDE = 256
HALO = 136
FOLD = 68
LATE = HALO + FOLD
SCALARS = WIDE - 4


def tables(groups, length):
    period = groups * length
    index = np.arange(length)
    inner = TURN * (np.outer(index, index) % length) / length
    wave_of = np.zeros(groups, np.int64)
    wave_of[1] = groups // 2
    for m in range(1, groups // 2):
        wave_of[2 * m] = wave_of[2 * m + 1] = m
    turn = TURN * (np.outer(wave_of, index) % period) / period
    matrices = np.zeros((2, WIDE, WIDE), np.float32)
    matrices[0, :length, :length] = np.cos(inner)
    matrices[1, :length, :length] = np.sin(inner)
    coarse = matrices.astype(jnp.bfloat16)
    rest = (matrices - coarse.astype(np.float32)).astype(jnp.bfloat16)
    twiddle = np.zeros((2, groups, WIDE))
    twiddle[0, :, :length] = np.cos(turn)
    twiddle[1, :, :length] = np.sin(turn)
    chunk = np.arange(groups)
    outer = np.zeros((2, groups, groups))
    for c in range(groups):
        phase = TURN * (chunk * wave_of[c] % groups) / groups
        if c < 2:
            outer[0, :, c] = outer[1, :, c] = np.cos(phase)
        elif c % 2 == 0:
            outer[0, :, c], outer[1, :, c] = 2 * np.cos(phase), -2 * np.sin(phase)
        else:
            outer[0, :, c], outer[1, :, c] = -2 * np.sin(phase), -2 * np.cos(phase)
    modes = wave_of[:, None] + groups * index[None, :]
    wave = np.zeros((groups, WIDE))
    wave[:, :length] = 4.0 * np.sin(np.pi * modes / period) ** 2
    return (
        np.stack([coarse, rest]),
        twiddle.astype(np.float32),
        outer.astype(np.float32),
        wave.astype(np.float32),
    )


def real_fft(values):
    count = len(values)
    if count == 2:
        return [(values[0] + values[1], None), (values[0] - values[1], None)]
    even, odd = real_fft(values[0::2]), real_fft(values[1::2])
    out = [None] * (count // 2 + 1)
    for k in range(count // 4 + 1):
        (er, ei), (re, im) = even[k], odd[k]
        if k == 0:
            out[0], out[count // 2] = (er + re, None), (er - re, None)
        elif k == count // 4:
            out[k] = (er, -re)
        else:
            c, s = float(np.cos(TURN * k / count)), float(-np.sin(TURN * k / count))
            tr, ti = re * c - im * s, im * c + re * s
            out[k], out[count // 2 - k] = (er + tr, ei + ti), (er - tr, ti - ei)
    return out


def real_ifft(spectrum):
    count = 2 * (len(spectrum) - 1)
    if count == 2:
        return [spectrum[0][0] + spectrum[1][0], spectrum[0][0] - spectrum[1][0]]
    even, odd = [], []
    for k in range(count // 4 + 1):
        (ar, ai), (br, bi) = spectrum[k], spectrum[count // 2 - k]
        if k == 0:
            even.append((ar + br, None))
            odd.append((ar - br, None))
        elif k == count // 4:
            even.append((2.0 * ar, None))
            odd.append((-2.0 * ai, None))
        else:
            c, s = float(np.cos(TURN * k / count)), float(np.sin(TURN * k / count))
            dr, di = ar - br, ai + bi
            even.append((ar + br, ai - bi))
            odd.append((dr * c - di * s, dr * s + di * c))
    first, second = real_ifft(even), real_ifft(odd)
    out = []
    for a, b in zip(first, second, strict=True):
        out += [a, b]
    return out


def split(a):
    coarse = a.astype(jnp.bfloat16)
    return coarse, (a - coarse.astype(jnp.float32)).astype(jnp.bfloat16)


def product(a, b):
    (ac, ar), (bc, br) = a, b

    def one(x, y):
        return jnp.dot(x, y, preferred_element_type=jnp.float32)

    return one(ac, bc) + (one(ac, br) + one(ar, bc))


def dot(a, b):
    return product(split(a), split(b))


def table(matrix_ref, n):
    return matrix_ref[0, n], matrix_ref[1, n]


def rows_of(p):
    return slice(ROWS * p, ROWS * (p + 1))


def lanes(shape):
    return lax.broadcasted_iota(jnp.int32, shape, len(shape) - 1)


def sublanes(shape):
    return lax.broadcasted_iota(jnp.int32, shape, len(shape) - 2)


def shifted(value, lanes_right):
    return pltpu.roll(value, lanes_right % value.shape[1], 1)


def pack_kernel(forcing_ref, mask_ref, self_ref, out_ref, tall):
    length = forcing_ref.shape[0]
    wet = mask_ref[...].astype(jnp.float32)
    tall[:length, :] = wet * forcing_ref[...]
    tall[length:, :] = (wet * self_ref[...])[: WIDE - length]
    out_ref[...] = tall[...].T


def pack_rest_kernel(mask_ref, self_ref, east_ref, north_ref, out_ref, late_ref, tall, short):
    length, rows = mask_ref.shape
    cut = WIDE - length
    n_at = 2 * length - cut
    e_at = n_at + length
    count = WIDE + 128 - e_at
    wet = mask_ref[...].astype(jnp.float32)
    east = wet * east_ref[...]
    tall[:length, :] = jnp.zeros((length, rows), jnp.float32)
    tall[length:n_at, :] = (wet * self_ref[...])[cut:]
    tall[n_at:e_at, :] = wet * north_ref[...]
    tall[e_at:, :] = east[:count]
    out_ref[...] = tall[...].T
    short[...] = jnp.zeros((128, rows), jnp.float32)
    short[LATE - 128 : LATE - 128 + length - count, :] = east[count:]
    late_ref[...] = short[...].T


def coefficients_kernel(
    groups,
    length,
    slab_ref,
    second_ref,
    diagonal_ref,
    wet_ref,
    next_ref,
    east_ref,
    north_ref,
    south_ref,
    low_row_ref,
    top_row_ref,
):
    cut = WIDE - length
    n_at = 2 * length - cut
    e_at = n_at + length
    count = WIDE + 128 - e_at
    lane, row = lanes((ROWS, WIDE)), sublanes((ROWS, WIDE))
    held = lane < length

    def one(p):
        at = rows_of(p)
        late = second_ref[at, :]
        own = jnp.where(
            lane < cut,
            shifted(slab_ref[at, :], -length),
            jnp.where(held, shifted(late, cut - length)[:, :WIDE], 0.0),
        )
        return late, own, (own > 0.0).astype(jnp.float32)

    for p in range(groups):
        wet_ref[rows_of(p), :] = one(p)[2]
    for p in range(groups):
        at = rows_of(p)
        late, own, wet = one(p)
        after = wet_ref[rows_of((p + 1) % groups), 0:1]
        north = jnp.where(held, shifted(late, -n_at)[:, :WIDE], 0.0)
        diagonal_ref[at, :] = jnp.where(wet > 0.0, own, 1.0)
        next_ref[at, :] = shifted(jnp.where(lane == length, after, wet), -1)
        east_ref[at, :] = jnp.where(lane < count, shifted(late, -e_at)[:, :WIDE], 0.0)
        north_ref[at, :] = north * jnp.where(row == ROWS - 1, 1.0, pltpu.roll(wet, ROWS - 1, 0))
        south_ref[at, :] = wet * jnp.where(row == 0, 1.0, pltpu.roll(north, 1, 0))
        low_row_ref[p : p + 1, :] = wet[:1]
        top_row_ref[p : p + 1, :] = north[ROWS - 1 :]


def transform(chunks, matrix_ref, twiddle_ref, left, right):
    groups = len(chunks)
    mixed = real_fft(chunks)
    for m in range(groups // 2 + 1):
        re, im = mixed[m]
        if m == 0:
            left[rows_of(0), :] = re
            right[rows_of(0), :] = re
            continue
        c = 1 if m == groups // 2 else 2 * m
        cos, sin = twiddle_ref[0, c : c + 1, :], twiddle_ref[1, c : c + 1, :]
        if m == groups // 2:
            left[rows_of(1), :] = re * (cos + sin)
            right[rows_of(1), :] = re * (cos - sin)
        else:
            tr, ti = re * cos + im * sin, im * cos - re * sin
            left[rows_of(c), :] = tr
            right[rows_of(c), :] = ti
            left[rows_of(c + 1), :] = ti
            right[rows_of(c + 1), :] = -tr
    return product(split(left[...]), table(matrix_ref, 0)) + product(
        split(right[...]), table(matrix_ref, 1)
    )


def transform_back(spectrum, groups, matrix_ref, twiddle_ref):
    parts = split(spectrum)
    pc, ps = product(parts, table(matrix_ref, 0)), product(parts, table(matrix_ref, 1))
    mixed = []
    for m in range(groups // 2 + 1):
        if m == 0:
            mixed.append((pc[rows_of(0)] + ps[rows_of(0)], None))
            continue
        c = 1 if m == groups // 2 else 2 * m
        cos, sin = twiddle_ref[0, c : c + 1, :], twiddle_ref[1, c : c + 1, :]
        if m == groups // 2:
            mixed.append((pc[rows_of(1)] * (cos + sin) + ps[rows_of(1)] * (cos - sin), None))
        else:
            hr = pc[rows_of(c)] - ps[rows_of(c + 1)]
            hi = ps[rows_of(c)] + pc[rows_of(c + 1)]
            mixed.append((hr * cos - hi * sin, hi * cos + hr * sin))
    return real_ifft(mixed)


def row_back(spectrum, matrix_ref, twiddle_ref, outer_ref):
    parts = split(spectrum)
    pc, ps = product(parts, table(matrix_ref, 0)), product(parts, table(matrix_ref, 1))
    cos, sin = twiddle_ref[0], twiddle_ref[1]
    return dot(outer_ref[0], pc * cos - ps * sin) + dot(outer_ref[1], ps * cos + pc * sin)


def forward_kernel(groups, field_ref, rest_ref, matrix_ref, twiddle_ref, out_ref, left, right):
    chunks = [field_ref[rows_of(p), :] for p in range(groups)]
    spectrum = transform(chunks, matrix_ref, twiddle_ref, left, right)
    out_ref[:, :WIDE] = spectrum + rest_ref[:, :WIDE]
    out_ref[:, WIDE:] = rest_ref[:, WIDE:]


def blocks_kernel(spec_ref, scale_ref, aligned_ref, scaled_ref, part_ref, down_ref, up_ref):
    count, block = aligned_ref.shape[0], aligned_ref.shape[1]
    half, rows = block // 2, count * block
    scaled = spec_ref[:, :WIDE] * scale_ref[...]
    scaled_ref[...] = scaled
    for b in range(count):
        part_ref[b * block : (b + 1) * block, :] = dot(
            aligned_ref[b], scaled[b * block : (b + 1) * block]
        )
    down_ref[:half, :] = scaled[:half]
    down_ref[half : half + 8, :] = part_ref[:8, :]
    down_ref[half + 8 :, :] = scale_ref[:8, :]
    up_ref[:half, :] = scaled[rows - half :]
    up_ref[half : half + 8, :] = part_ref[rows - 8 :, :]
    up_ref[half + 8 :, :] = scale_ref[rows - 8 :, :]


def combine(norm, scaled_ref, part_ref, scale_ref, above_ref, below_ref, stag_ref, stag_below_ref):
    count, block = stag_ref.shape[0], stag_ref.shape[1]
    half, rows = block // 2, count * block
    before = dot(
        stag_below_ref[...],
        jnp.concatenate([below_ref[:half, :], scaled_ref[:half, :]], axis=0),
    )
    pieces = [before[half:]]
    for b in range(count - 1):
        pieces.append(dot(stag_ref[b], scaled_ref[half + b * block : half + (b + 1) * block, :]))
    after = dot(
        stag_ref[count - 1],
        jnp.concatenate([scaled_ref[rows - half :, :], above_ref[:half, :]], axis=0),
    )
    pieces.append(after[:half])
    full = (part_ref[...] + jnp.concatenate(pieces, axis=0)) * (scale_ref[...] * norm)
    return full, before, after


def halo_kernel(
    norm,
    scaled_ref,
    part_ref,
    scale_ref,
    above_ref,
    below_ref,
    stag_ref,
    stag_below_ref,
    late_ref,
    out_ref,
    low,
    high,
):
    half = stag_ref.shape[1] // 2
    full, before, after = combine(
        norm, scaled_ref, part_ref, scale_ref, above_ref, below_ref, stag_ref, stag_below_ref
    )
    row_below = (before[half - 1 : half] + below_ref[half + 7 : half + 8, :]) * (
        below_ref[half + 15 : half + 16, :] * norm
    )
    row_above = (after[half : half + 1] + above_ref[half : half + 1, :]) * (
        above_ref[half + 8 : half + 9, :] * norm
    )
    out_ref[:, :128] = full[:, :128]
    low[...] = full[:, :128]
    high[...] = full[:, 128:]
    groups = full.shape[0] // ROWS

    def strided(start):
        at = pl.ds(start, groups, stride=ROWS)
        return jnp.concatenate([low[at, :], high[at, :]], axis=1)

    row = lax.broadcasted_iota(jnp.int32, (groups, WIDE), 0)
    up = jnp.where(row == 0, row_below, pltpu.roll(strided(ROWS - 1), 1, 0))
    down = jnp.where(row == groups - 1, row_above, pltpu.roll(strided(0), groups - 1, 0))
    lane = lanes((groups, 128)) + 128
    for s, part in enumerate(
        (
            pltpu.roll(up, HALO, 1),
            pltpu.roll(up, HALO - FOLD, 1),
            pltpu.roll(down, HALO, 1),
            pltpu.roll(down, HALO - FOLD, 1),
        )
    ):
        at = pl.ds(s, groups, stride=ROWS)
        high[at, :] = jnp.where(lane >= HALO, part[:, 128:], high[at, :])
    out_ref[:, 128:] = jnp.where(
        lanes(high.shape) < LATE - 128, high[...], late_ref[...]
    )


def sums_kernel(
    norm,
    length,
    scaled_ref,
    part_ref,
    scale_ref,
    above_ref,
    below_ref,
    stag_ref,
    stag_below_ref,
    spec_ref,
    rhs_ref,
    image_ref,
    weight_ref,
    sums_ref,
    out_ref,
):
    full, _, _ = combine(
        norm, scaled_ref, part_ref, scale_ref, above_ref, below_ref, stag_ref, stag_below_ref
    )
    lane = lanes(full.shape)
    held = jnp.where(lane < length, full, 0.0)
    weight = weight_ref[0, 0]
    own = jnp.sum(held * spec_ref[...]) * weight
    cross = jnp.sum(held * rhs_ref[:, :WIDE]) * weight
    out = jnp.where(lane < length, full, shifted(image_ref[...], length))
    for n, value in enumerate((sums_ref[0, 0], sums_ref[0, 1], own, cross)):
        out = jnp.where(lane == SCALARS + n, value, out)
    out_ref[...] = out


def step_kernel(
    groups,
    length,
    spec_ref,
    rhs_ref,
    diagonal_ref,
    wet_ref,
    next_ref,
    east_ref,
    north_ref,
    south_ref,
    wet_above_ref,
    north_below_ref,
    matrix_ref,
    twiddle_ref,
    outer_ref,
    out_ref,
    first_ref,
    image_ref,
    sums_ref,
    left,
    right,
    low,
    high,
    tail,
):
    lane_row = lanes((groups, WIDE))
    stride = 3 * ROWS
    tail[...] = spec_ref[:, 128:]

    def halo_row(s):
        blank = jnp.zeros((groups, 128), jnp.float32)
        parts = [
            jnp.concatenate([tail[pl.ds(s + n, groups, stride=ROWS), :], blank], axis=1)
            for n in range(2)
        ]
        row = jnp.where(
            lane_row < FOLD, shifted(parts[0], 128 - HALO), shifted(parts[1], FOLD + 128 - HALO)
        )
        return row_back(row, matrix_ref, twiddle_ref, outer_ref)

    for start, s in ((ROWS - 1, 0), (2 * ROWS, 2)):
        row = halo_row(s)
        low[pl.ds(start, groups, stride=stride), :] = row[:, :128]
        high[pl.ds(start, groups, stride=stride), :] = row[:, 128:]

    def neighbour(start):
        at = slice(start, start + ROWS)
        return jnp.concatenate([low[at, :], high[at, :]], axis=1)

    cells = transform_back(spec_ref[...], groups, matrix_ref, twiddle_ref)
    for p in range(groups):
        v = cells[p] * wet_ref[rows_of(p), :]
        first_ref[rows_of(p), :] = v
        low[stride * p + ROWS : stride * p + 2 * ROWS, :] = v[:, :128]
        high[stride * p + ROWS : stride * p + 2 * ROWS, :] = v[:, 128:]
    lane, row = lanes((ROWS, WIDE)), sublanes((ROWS, WIDE))
    count = WIDE + 128 - (2 * length - (WIDE - length)) - length
    rz = jnp.zeros((ROWS, WIDE), jnp.float32)
    curvature = jnp.zeros((ROWS, WIDE), jnp.float32)
    images, fluxes = [], []
    for p in range(groups):
        at = rows_of(p)
        v = first_ref[at, :]
        after = first_ref[rows_of((p + 1) % groups), 0:1]
        east = jnp.where(lane < count, east_ref[at, :], shifted(spec_ref[at, :], count - LATE))
        flux = v - shifted(jnp.where(lane == length, after, v), -1)
        fluxes.append(jnp.where(lane < length, east * next_ref[at, :] * flux, 0.0))
    for p in range(groups):
        at = rows_of(p)
        v = first_ref[at, :]
        before = fluxes[(p - 1) % groups][:, length - 1 : length]
        flux = fluxes[p]
        north, south = north_ref[at, :], south_ref[at, :]
        north = jnp.where(row == ROWS - 1, north * wet_above_ref[p : p + 1, :], north)
        south = jnp.where(row == 0, south * north_below_ref[p : p + 1, :], south)
        base = stride * p + ROWS
        image = diagonal_ref[at, :] * v
        image = image + (flux - shifted(jnp.where(lane == WIDE - 1, before, flux), 1))
        image = image + north * (v - neighbour(base + 1))
        image = image + south * (v - neighbour(base - 1))
        image = jnp.where(lane < length, image, 0.0)
        image_ref[at, :] = image
        images.append(image)
        rz = rz + rhs_ref[at, :] * v
        curvature = curvature + v * image
    small = lanes((8, 128))
    sums_ref[...] = jnp.where(
        small == 0, jnp.sum(rz), jnp.where(small == 1, jnp.sum(curvature), 0.0)
    )
    spectrum = transform(images, matrix_ref, twiddle_ref, left, right)
    out_ref[...] = jnp.where(
        lanes(out_ref.shape) < length, spectrum, shifted(first_ref[...], length)
    )


def gather_kernel(spec_ref, sums_ref):
    riders = jnp.sum(spec_ref[:, 128:], axis=0, keepdims=True) * (1.0 / ROWS)
    sums_ref[...] = jnp.broadcast_to(riders, (8, 128))


def last_kernel(
    groups, length, spec_ref, wet_ref, first_ref, image_ref, matrix_ref, twiddle_ref, out_ref
):
    cells = transform_back(spec_ref[...], groups, matrix_ref, twiddle_ref)
    lane = lanes((ROWS, WIDE))
    cut = WIDE - length
    image_cut = SCALARS - length
    image_at = 2 * length - cut
    for p in range(groups):
        at = rows_of(p)
        out = jnp.where(
            lane < length, cells[p] * wet_ref[at, :], shifted(first_ref[at, :], length - cut)
        )
        out_ref[at, :] = jnp.where(
            lane < image_at, out, shifted(image_ref[at, :], image_at - image_cut)
        )


def unpack_kernel(length, count, slab_ref, out_ref):
    turned = slab_ref[:, 128:].T
    out_ref[:count, :] = turned[length - 128 : length - 128 + count]


def finish_kernel(
    length,
    back_ref,
    first_ref,
    image_ref,
    forcing_ref,
    mask_ref,
    three_ref,
    others_ref,
    pair_ref,
    solution_ref,
    residual_ref,
    direction_ref,
):
    at = SCALARS - 128
    totals = three_ref[:1, :] + others_ref[:1, :] + pair_ref[:1, :]
    rz, curvature, own, cross = [totals[:, at + n : at + n + 1] for n in range(4)]
    alpha = rz / curvature
    rz_next = rz - alpha * curvature - alpha * cross + alpha * alpha * own
    beta = rz_next / rz
    back = back_ref[...].T
    cut = WIDE - length
    image_cut = SCALARS - length
    image_at = 2 * length - cut
    rhs = mask_ref[...].astype(jnp.float32) * forcing_ref[...]

    def store(where, rows_back, first):
        solution_ref[where, :] = alpha * first
        direction_ref[where, :] = (first - alpha * rows_back) + beta * first

    store(slice(0, cut), back[:cut], first_ref[:cut, :])
    store(slice(cut, length), back[cut:length], back[length:image_at])
    residual_ref[:image_cut, :] = rhs[:image_cut] - alpha * image_ref[:image_cut, :]
    residual_ref[image_cut:, :] = (
        rhs[image_cut:] - alpha * back[image_at : image_at + length - image_cut]
    )


def call(kernel, out_shapes, scratch=(), name=None):
    single = not isinstance(out_shapes, (list, tuple)) or isinstance(out_shapes[0], int)
    shapes = [out_shapes] if single else out_shapes
    outs = [jax.ShapeDtypeStruct(s, jnp.float32) for s in shapes]
    return pl.pallas_call(
        kernel,
        out_shape=outs[0] if single else outs,
        scratch_shapes=[pltpu.VMEM(s, jnp.float32) for s in scratch],
        compiler_params=pltpu.CompilerParams(vmem_limit_bytes=16 * 2**20),
        name=name,
    )


def exchanged(value):
    groups = lax.axis_size(LON)
    parts = value.reshape(groups, ROWS, value.shape[-1])
    return lax.all_to_all(parts, LON, split_axis=0, concat_axis=0, tiled=True).reshape(value.shape)


def from_lat(value, steps, ring):
    count = lax.axis_size("lat")
    pairs = [(d + steps, d) for d in range(count)]
    if ring:
        pairs = [(s % count, d) for s, d in pairs]
    return lax.ppermute(value, "lat", [(s, d) for s, d in pairs if 0 <= s < count])


def from_slab(value, steps):
    count = lax.axis_size("lat") * lax.axis_size(LON)
    pairs = [(d + steps, d) for d in range(count)]
    return lax.ppermute(value, LAT_LON, [(s, d) for s, d in pairs if 0 <= s < count])


def after(value, *others):
    return lax.optimization_barrier((value, *others))[0]


def local(
    surface_forcing,
    ocean_mask,
    self_coupling,
    east_coupling,
    north_coupling,
    zonal_weight,
    aligned_inverse,
    staggered_inverse,
):
    groups = lax.axis_size(LON)
    length, rows = surface_forcing.shape
    norm = 1.0 / (groups * length)
    matrices, twiddle, outer, wave = tables(groups, length)
    channel = lax.axis_index(LON)
    count, block = aligned_inverse.shape[0], aligned_inverse.shape[1]
    half = block // 2
    wide = (rows, WIDE)
    transforms = [wide, wide]

    packed = call(pack_kernel, wide, [wide], name="pack")(
        surface_forcing, ocean_mask, self_coupling
    )
    slab = exchanged(packed)
    rest, late = call(
        pack_rest_kernel,
        [(rows, WIDE + 128), (rows, 128)],
        [(WIDE + 128, rows), (128, rows)],
        name="pack_rest",
    )(after(ocean_mask, packed), self_coupling, east_coupling, north_coupling)
    scale = lax.rsqrt(1.0 + zonal_weight[:, None] * lax.dynamic_slice_in_dim(wave, channel, 1, 0))
    stag_below = from_lat(after(staggered_inverse[count - 1], packed), -1, False)
    weight = jnp.where(channel < 2, 1.0, 2.0).astype(jnp.float32)

    edge = (half + 16, WIDE)

    def blocks(spectrum):
        scaled, part, down, up = call(blocks_kernel, [wide, wide, edge, edge], name="blocks")(
            spectrum, scale, aligned_inverse
        )
        above, below = from_lat(down, 1, False), from_lat(up, -1, False)
        return scaled, part, scale, above, below, staggered_inverse, stag_below

    spec_rhs = exchanged(
        call(lambda *r: forward_kernel(groups, *r), (rows, WIDE + 128), transforms, name="forward")(
            slab, rest, matrices, twiddle
        )
    )
    pieces = blocks(spec_rhs)
    *flat, low_row, top_row = call(
        lambda *r: coefficients_kernel(groups, length, *r),
        [wide] * 6 + [(groups, WIDE)] * 2,
        name="coefficients",
    )(slab, after(spec_rhs, pieces[0]))
    wet_slab = flat[1]
    wet_above, north_below = from_slab(low_row, 1), from_slab(top_row, -1)
    filtered = exchanged(
        call(lambda *r: halo_kernel(norm, *r), wide, [(rows, 128)] * 2, name="halo")(*pieces, late)
    )
    spec, first, image, sums = call(
        lambda *r: step_kernel(groups, length, *r),
        [wide, wide, wide, (8, 128)],
        transforms + [(3 * rows, 128)] * 2 + [(rows, 128)],
        name="step",
    )(filtered, slab, *flat, wet_above, north_below, matrices, twiddle, outer)
    spec_image = exchanged(spec)
    smem = pl.BlockSpec(memory_space=pltpu.SMEM)
    vmem = pl.BlockSpec(memory_space=pltpu.VMEM)
    summed = pl.pallas_call(
        lambda *r: sums_kernel(norm, length, *r),
        out_shape=jax.ShapeDtypeStruct(wide, jnp.float32),
        in_specs=[vmem] * 10 + [smem, smem],
        out_specs=vmem,
        compiler_params=pltpu.CompilerParams(vmem_limit_bytes=16 * 2**20),
        name="sums",
    )(*blocks(spec_image), spec_image, spec_rhs, image, weight.reshape(1, 1), sums)
    cut, image_cut = WIDE - length, SCALARS - length
    first_cells = call(
        lambda *r: unpack_kernel(length, cut, *r), (length, rows), name="unpack_first"
    )(after(spec_image, summed))
    filtered = exchanged(summed)
    lon_sums = call(gather_kernel, (8, 128), name="gather")(filtered)
    behind, ahead = from_lat(lon_sums, -1, True), from_lat(lon_sums, 1, True)
    packed = call(lambda *r: last_kernel(groups, length, *r), wide, name="last")(
        filtered, wet_slab, first, image, matrices, twiddle
    )
    image_cells = call(
        lambda *r: unpack_kernel(length, image_cut, *r), (length, rows), name="unpack_image"
    )(after(filtered, packed))

    pair = lon_sums + behind
    three = pair + ahead
    others, last_pair = from_lat(three, 3, True), from_lat(pair, -2, True)
    cells = (length, rows)
    return tuple(
        call(lambda *r: finish_kernel(length, *r), [cells] * 3, name="finish")(
            exchanged(packed),
            first_cells,
            image_cells,
            surface_forcing,
            ocean_mask,
            three,
            others,
            last_pair,
        )
    )


def solution(mesh):
    torus = Mesh(
        mesh.devices.reshape(mesh.shape["lat"], 4, 4, 2), ("lat", "lon_0", "lon_1", "lon_2")
    )
    return jax.shard_map(
        local,
        mesh=torus,
        in_specs=(
            P(LON, "lat"),
            P(LON, "lat"),
            P(LON, "lat"),
            P(LON, "lat"),
            P(LON, "lat"),
            P("lat"),
            P("lat", None, None),
            P("lat", None, None),
        ),
        out_specs=(P(LON, "lat"), P(LON, "lat"), P(LON, "lat")),
        check_vma=False,
    )
```

```python
import jax
import jax.numpy as jnp
import numpy as np
from jax import lax
from jax.experimental import pallas as pl
from jax.experimental.pallas import tpu as pltpu
from jax.sharding import Mesh
from jax.sharding import PartitionSpec as P

LON = ("lon_0", "lon_1", "lon_2")
LAT_LON = ("lat", "lon_0", "lon_1", "lon_2")
TURN = 2.0 * np.pi
ROWS = 8
WIDE = 256
HALO = 136
FOLD = 68
LATE = HALO + FOLD
SCALARS = WIDE - 4


def tables(groups, length):
    period = groups * length
    index = np.arange(length)
    inner = TURN * (np.outer(index, index) % length) / length
    wave_of = np.zeros(groups, np.int64)
    wave_of[1] = groups // 2
    for m in range(1, groups // 2):
        wave_of[2 * m] = wave_of[2 * m + 1] = m
    turn = TURN * (np.outer(wave_of, index) % period) / period
    matrices = np.zeros((2, WIDE, WIDE), np.float32)
    matrices[0, :length, :length] = np.cos(inner)
    matrices[1, :length, :length] = np.sin(inner)
    coarse = matrices.astype(jnp.bfloat16)
    rest = (matrices - coarse.astype(np.float32)).astype(jnp.bfloat16)
    twiddle = np.zeros((2, groups, WIDE))
    twiddle[0, :, :length] = np.cos(turn)
    twiddle[1, :, :length] = np.sin(turn)
    chunk = np.arange(groups)
    outer = np.zeros((2, groups, groups))
    for c in range(groups):
        phase = TURN * (chunk * wave_of[c] % groups) / groups
        if c < 2:
            outer[0, :, c] = outer[1, :, c] = np.cos(phase)
        elif c % 2 == 0:
            outer[0, :, c], outer[1, :, c] = 2 * np.cos(phase), -2 * np.sin(phase)
        else:
            outer[0, :, c], outer[1, :, c] = -2 * np.sin(phase), -2 * np.cos(phase)
    modes = wave_of[:, None] + groups * index[None, :]
    wave = np.zeros((groups, WIDE))
    wave[:, :length] = 4.0 * np.sin(np.pi * modes / period) ** 2
    return (
        np.stack([coarse, rest]),
        twiddle.astype(np.float32),
        outer.astype(np.float32),
        wave.astype(np.float32),
    )


def real_fft(values):
    count = len(values)
    if count == 2:
        return [(values[0] + values[1], None), (values[0] - values[1], None)]
    even, odd = real_fft(values[0::2]), real_fft(values[1::2])
    out = [None] * (count // 2 + 1)
    for k in range(count // 4 + 1):
        (er, ei), (re, im) = even[k], odd[k]
        if k == 0:
            out[0], out[count // 2] = (er + re, None), (er - re, None)
        elif k == count // 4:
            out[k] = (er, -re)
        else:
            c, s = float(np.cos(TURN * k / count)), float(-np.sin(TURN * k / count))
            tr, ti = re * c - im * s, im * c + re * s
            out[k], out[count // 2 - k] = (er + tr, ei + ti), (er - tr, ti - ei)
    return out


def real_ifft(spectrum):
    count = 2 * (len(spectrum) - 1)
    if count == 2:
        return [spectrum[0][0] + spectrum[1][0], spectrum[0][0] - spectrum[1][0]]
    even, odd = [], []
    for k in range(count // 4 + 1):
        (ar, ai), (br, bi) = spectrum[k], spectrum[count // 2 - k]
        if k == 0:
            even.append((ar + br, None))
            odd.append((ar - br, None))
        elif k == count // 4:
            even.append((2.0 * ar, None))
            odd.append((-2.0 * ai, None))
        else:
            c, s = float(np.cos(TURN * k / count)), float(np.sin(TURN * k / count))
            dr, di = ar - br, ai + bi
            even.append((ar + br, ai - bi))
            odd.append((dr * c - di * s, dr * s + di * c))
    first, second = real_ifft(even), real_ifft(odd)
    out = []
    for a, b in zip(first, second, strict=True):
        out += [a, b]
    return out


def split(a):
    coarse = a.astype(jnp.bfloat16)
    return coarse, (a - coarse.astype(jnp.float32)).astype(jnp.bfloat16)


def product(a, b):
    (ac, ar), (bc, br) = a, b

    def one(x, y):
        return jnp.dot(x, y, preferred_element_type=jnp.float32)

    return one(ac, bc) + (one(ac, br) + one(ar, bc))


def dot(a, b):
    return product(split(a), split(b))


def table(matrix_ref, n):
    return matrix_ref[0, n], matrix_ref[1, n]


def rows_of(p):
    return slice(ROWS * p, ROWS * (p + 1))


def lanes(shape):
    return lax.broadcasted_iota(jnp.int32, shape, len(shape) - 1)


def sublanes(shape):
    return lax.broadcasted_iota(jnp.int32, shape, len(shape) - 2)


def shifted(value, lanes_right):
    return pltpu.roll(value, lanes_right % value.shape[1], 1)


def pack_kernel(
    forcing_ref, mask_ref, self_ref, out_ref, forcing, mask, coupling, tall, arrived
):
    copies = [
        pltpu.make_async_copy(source, target, arrived.at[n])
        for n, (source, target) in enumerate(
            ((forcing_ref, forcing), (mask_ref, mask), (self_ref, coupling))
        )
    ]
    for copy in copies:
        copy.start()
    for copy in copies:
        copy.wait()
    length = forcing.shape[0]
    wet = mask[...].astype(jnp.float32)
    tall[:length, :] = wet * forcing[...]
    tall[length:, :] = (wet * coupling[...])[: WIDE - length]
    out_ref[...] = tall[...].T


def edges_kernel(mask_ref, north_ref, wet_ref, top_ref, tall):
    length, rows = mask_ref.shape
    tall[length:, :] = jnp.zeros((WIDE - length, 128), jnp.float32)
    tall[:length, :] = mask_ref[:, :128].astype(jnp.float32)
    wet_ref[...] = tall[...].T[:ROWS]
    tall[:length, :] = mask_ref[:, rows - 128 :].astype(jnp.float32) * north_ref[:, rows - 128 :]
    top_ref[...] = tall[...].T[128 - ROWS :]


def lane_plan(length):
    cut = WIDE - length
    north = 2 * length - cut
    south = north + length
    east = south + length
    return cut, north, south, east, 2 * WIDE - east


def pack_rest_kernel(
    mask_ref,
    self_ref,
    east_ref,
    north_ref,
    wet_above_ref,
    top_below_ref,
    out_ref,
    late_ref,
    tall,
    short,
):
    length, rows = mask_ref.shape
    cut, n_at, s_at, e_at, count = lane_plan(length)
    lane = lanes((length, rows))
    wet = mask_ref[...].astype(jnp.float32)
    north = wet * north_ref[...]
    east = wet * east_ref[...]
    wet_above = wet_above_ref[...].T[:length, :1]
    top_below = top_below_ref[...].T[:length, ROWS - 1 :]
    tall[:length, :] = jnp.zeros((length, rows), jnp.float32)
    tall[length:n_at, :] = (wet * self_ref[...])[cut:]
    tall[n_at:s_at, :] = north * jnp.where(lane == rows - 1, wet_above, shifted(wet, -1))
    tall[s_at:e_at, :] = wet * jnp.where(lane == 0, top_below, shifted(north, 1))
    tall[e_at:, :] = east[:count]
    out_ref[...] = tall[...].T
    short[...] = jnp.zeros((128, rows), jnp.float32)
    short[LATE - 128 : LATE - 128 + length - count, :] = east[count:]
    late_ref[...] = short[...].T


def coefficients_kernel(
    groups, length, slab_ref, second_ref, own_ref, next_ref, east_ref, north_ref, south_ref
):
    cut, n_at, s_at, e_at, count = lane_plan(length)
    lane = lanes((ROWS, WIDE))
    held = lane < length
    for p in range(groups):
        at = rows_of(p)
        late = second_ref[at, :]
        own_ref[at, :] = jnp.where(
            lane < cut,
            shifted(slab_ref[at, :], -length),
            jnp.where(held, shifted(late[:, :WIDE], cut - length), 0.0),
        )
        north_ref[at, :] = jnp.where(held, shifted(late, -n_at)[:, :WIDE], 0.0)
        south_ref[at, :] = jnp.where(held, shifted(late[:, WIDE:], WIDE - s_at), 0.0)
        east_ref[at, :] = jnp.where(lane < count, shifted(late[:, WIDE:], WIDE - e_at), 0.0)
    for p in range(groups):
        own = own_ref[rows_of(p), :]
        after = own_ref[rows_of((p + 1) % groups), 0:1]
        ocean = jnp.where(lane == length, after, own) > 0.0
        next_ref[rows_of(p), :] = shifted(ocean.astype(jnp.float32), -1)


def transform(chunks, matrix_ref, twiddle_ref, left, right):
    groups = len(chunks)
    mixed = real_fft(chunks)
    for m in range(groups // 2 + 1):
        re, im = mixed[m]
        if m == 0:
            left[rows_of(0), :] = re
            right[rows_of(0), :] = re
            continue
        c = 1 if m == groups // 2 else 2 * m
        cos, sin = twiddle_ref[0, c : c + 1, :], twiddle_ref[1, c : c + 1, :]
        if m == groups // 2:
            left[rows_of(1), :] = re * (cos + sin)
            right[rows_of(1), :] = re * (cos - sin)
        else:
            tr, ti = re * cos + im * sin, im * cos - re * sin
            left[rows_of(c), :] = tr
            right[rows_of(c), :] = ti
            left[rows_of(c + 1), :] = ti
            right[rows_of(c + 1), :] = -tr
    return product(split(left[...]), table(matrix_ref, 0)) + product(
        split(right[...]), table(matrix_ref, 1)
    )


def transform_back(spectrum, groups, matrix_ref, twiddle_ref):
    parts = split(spectrum)
    pc, ps = product(parts, table(matrix_ref, 0)), product(parts, table(matrix_ref, 1))
    mixed = []
    for m in range(groups // 2 + 1):
        if m == 0:
            mixed.append((pc[rows_of(0)] + ps[rows_of(0)], None))
            continue
        c = 1 if m == groups // 2 else 2 * m
        cos, sin = twiddle_ref[0, c : c + 1, :], twiddle_ref[1, c : c + 1, :]
        if m == groups // 2:
            mixed.append((pc[rows_of(1)] * (cos + sin) + ps[rows_of(1)] * (cos - sin), None))
        else:
            hr = pc[rows_of(c)] - ps[rows_of(c + 1)]
            hi = ps[rows_of(c)] + pc[rows_of(c + 1)]
            mixed.append((hr * cos - hi * sin, hi * cos + hr * sin))
    return real_ifft(mixed)


def row_back(spectrum, matrix_ref, twiddle_ref, outer_ref):
    parts = split(spectrum)
    pc, ps = product(parts, table(matrix_ref, 0)), product(parts, table(matrix_ref, 1))
    cos, sin = twiddle_ref[0], twiddle_ref[1]
    return dot(outer_ref[0], pc * cos - ps * sin) + dot(outer_ref[1], ps * cos + pc * sin)


def forward_kernel(groups, field_ref, rest_ref, matrix_ref, twiddle_ref, out_ref, left, right):
    chunks = [field_ref[rows_of(p), :] for p in range(groups)]
    spectrum = transform(chunks, matrix_ref, twiddle_ref, left, right)
    out_ref[:, :WIDE] = spectrum + rest_ref[:, :WIDE]
    out_ref[:, WIDE:] = rest_ref[:, WIDE:]


def blocks_kernel(spec_ref, scale_ref, aligned_ref, scaled_ref, part_ref, down_ref, up_ref):
    count, block = aligned_ref.shape[0], aligned_ref.shape[1]
    half, rows = block // 2, count * block
    scaled = spec_ref[:, :WIDE] * scale_ref[...]
    scaled_ref[...] = scaled
    for b in range(count):
        part_ref[b * block : (b + 1) * block, :] = dot(
            aligned_ref[b], scaled[b * block : (b + 1) * block]
        )
    down_ref[:half, :] = scaled[:half]
    down_ref[half : half + 8, :] = part_ref[:8, :]
    down_ref[half + 8 :, :] = scale_ref[:8, :]
    up_ref[:half, :] = scaled[rows - half :]
    up_ref[half : half + 8, :] = part_ref[rows - 8 :, :]
    up_ref[half + 8 :, :] = scale_ref[rows - 8 :, :]


def combine(norm, scaled_ref, part_ref, scale_ref, above_ref, below_ref, stag_ref, stag_below_ref):
    count, block = stag_ref.shape[0], stag_ref.shape[1]
    half, rows = block // 2, count * block
    before = dot(
        stag_below_ref[...],
        jnp.concatenate([below_ref[:half, :], scaled_ref[:half, :]], axis=0),
    )
    pieces = [before[half:]]
    for b in range(count - 1):
        pieces.append(dot(stag_ref[b], scaled_ref[half + b * block : half + (b + 1) * block, :]))
    after = dot(
        stag_ref[count - 1],
        jnp.concatenate([scaled_ref[rows - half :, :], above_ref[:half, :]], axis=0),
    )
    pieces.append(after[:half])
    full = (part_ref[...] + jnp.concatenate(pieces, axis=0)) * (scale_ref[...] * norm)
    return full, before, after


def halo_kernel(
    norm,
    scaled_ref,
    part_ref,
    scale_ref,
    above_ref,
    below_ref,
    stag_ref,
    stag_below_ref,
    late_ref,
    out_ref,
    low,
    high,
):
    half = stag_ref.shape[1] // 2
    full, before, after = combine(
        norm, scaled_ref, part_ref, scale_ref, above_ref, below_ref, stag_ref, stag_below_ref
    )
    row_below = (before[half - 1 : half] + below_ref[half + 7 : half + 8, :]) * (
        below_ref[half + 15 : half + 16, :] * norm
    )
    row_above = (after[half : half + 1] + above_ref[half : half + 1, :]) * (
        above_ref[half + 8 : half + 9, :] * norm
    )
    out_ref[:, :128] = full[:, :128]
    low[...] = full[:, :128]
    high[...] = full[:, 128:]
    groups = full.shape[0] // ROWS

    def strided(start):
        at = pl.ds(start, groups, stride=ROWS)
        return jnp.concatenate([low[at, :], high[at, :]], axis=1)

    row = lax.broadcasted_iota(jnp.int32, (groups, WIDE), 0)
    up = jnp.where(row == 0, row_below, pltpu.roll(strided(ROWS - 1), 1, 0))
    down = jnp.where(row == groups - 1, row_above, pltpu.roll(strided(0), groups - 1, 0))
    lane = lanes((groups, 128)) + 128
    for s, part in enumerate(
        (
            pltpu.roll(up, HALO, 1),
            pltpu.roll(up, HALO - FOLD, 1),
            pltpu.roll(down, HALO, 1),
            pltpu.roll(down, HALO - FOLD, 1),
        )
    ):
        at = pl.ds(s, groups, stride=ROWS)
        high[at, :] = jnp.where(lane >= HALO, part[:, 128:], high[at, :])
    out_ref[:, 128:] = jnp.where(
        lanes(high.shape) < LATE - 128, high[...], late_ref[...]
    )


def sums_kernel(
    norm,
    length,
    scaled_ref,
    part_ref,
    scale_ref,
    above_ref,
    below_ref,
    stag_ref,
    stag_below_ref,
    spec_ref,
    image_ref,
    weight_ref,
    sums_ref,
    out_ref,
):
    full, _, _ = combine(
        norm, scaled_ref, part_ref, scale_ref, above_ref, below_ref, stag_ref, stag_below_ref
    )
    lane = lanes(full.shape)
    held = jnp.where(lane < length, full, 0.0)
    weight = weight_ref[0, 0]
    own = jnp.sum(held * spec_ref[...]) * weight
    out = jnp.where(lane < length, full, shifted(image_ref[...], length))
    for n, value in enumerate((sums_ref[0, 0], sums_ref[0, 1], own)):
        out = jnp.where(lane == SCALARS + n, value, out)
    out_ref[...] = out


def step_kernel(
    groups,
    length,
    spec_ref,
    rhs_ref,
    own_ref,
    next_ref,
    east_ref,
    north_ref,
    south_ref,
    matrix_ref,
    twiddle_ref,
    outer_ref,
    out_ref,
    first_ref,
    image_ref,
    sums_ref,
    left,
    right,
    low,
    high,
    tail,
):
    lane_row = lanes((groups, WIDE))
    stride = 3 * ROWS
    tail[...] = spec_ref[:, 128:]

    def halo_row(s):
        blank = jnp.zeros((groups, 128), jnp.float32)
        parts = [
            jnp.concatenate([tail[pl.ds(s + n, groups, stride=ROWS), :], blank], axis=1)
            for n in range(2)
        ]
        row = jnp.where(
            lane_row < FOLD, shifted(parts[0], 128 - HALO), shifted(parts[1], FOLD + 128 - HALO)
        )
        return row_back(row, matrix_ref, twiddle_ref, outer_ref)

    for start, s in ((ROWS - 1, 0), (2 * ROWS, 2)):
        row = halo_row(s)
        low[pl.ds(start, groups, stride=stride), :] = row[:, :128]
        high[pl.ds(start, groups, stride=stride), :] = row[:, 128:]

    def neighbour(start):
        at = slice(start, start + ROWS)
        return jnp.concatenate([low[at, :], high[at, :]], axis=1)

    cells = transform_back(spec_ref[...], groups, matrix_ref, twiddle_ref)
    for p in range(groups):
        v = jnp.where(own_ref[rows_of(p), :] > 0.0, cells[p], 0.0)
        first_ref[rows_of(p), :] = v
        low[stride * p + ROWS : stride * p + 2 * ROWS, :] = v[:, :128]
        high[stride * p + ROWS : stride * p + 2 * ROWS, :] = v[:, 128:]
    lane = lanes((ROWS, WIDE))
    count = lane_plan(length)[-1]
    rz = jnp.zeros((ROWS, WIDE), jnp.float32)
    curvature = jnp.zeros((ROWS, WIDE), jnp.float32)
    images, fluxes = [], []
    for p in range(groups):
        at = rows_of(p)
        v = first_ref[at, :]
        after = first_ref[rows_of((p + 1) % groups), 0:1]
        east = jnp.where(lane < count, east_ref[at, :], shifted(spec_ref[at, :], count - LATE))
        flux = v - shifted(jnp.where(lane == length, after, v), -1)
        fluxes.append(jnp.where(lane < length, east * next_ref[at, :] * flux, 0.0))
    for p in range(groups):
        at = rows_of(p)
        v = first_ref[at, :]
        before = fluxes[(p - 1) % groups][:, length - 1 : length]
        flux = fluxes[p]
        own = own_ref[at, :]
        base = stride * p + ROWS
        image = jnp.where(own > 0.0, own, 1.0) * v
        image = image + (flux - shifted(jnp.where(lane == WIDE - 1, before, flux), 1))
        image = image + north_ref[at, :] * (v - neighbour(base + 1))
        image = image + south_ref[at, :] * (v - neighbour(base - 1))
        image = jnp.where(lane < length, image, 0.0)
        image_ref[at, :] = image
        images.append(image)
        rz = rz + rhs_ref[at, :] * v
        curvature = curvature + v * image
    small = lanes((8, 128))
    sums_ref[...] = jnp.where(
        small == 0, jnp.sum(rz), jnp.where(small == 1, jnp.sum(curvature), 0.0)
    )
    spectrum = transform(images, matrix_ref, twiddle_ref, left, right)
    out_ref[...] = jnp.where(
        lanes(out_ref.shape) < length, spectrum, shifted(first_ref[...], length)
    )


def gather_kernel(spec_ref, sums_ref):
    riders = jnp.sum(spec_ref[:, 128:], axis=0, keepdims=True) * (1.0 / ROWS)
    sums_ref[...] = jnp.broadcast_to(riders, (8, 128))


def last_kernel(
    groups, length, spec_ref, own_ref, first_ref, image_ref, matrix_ref, twiddle_ref, out_ref
):
    cells = transform_back(spec_ref[...], groups, matrix_ref, twiddle_ref)
    lane = lanes((ROWS, WIDE))
    cut = WIDE - length
    image_cut = SCALARS - length
    image_at = 2 * length - cut
    for p in range(groups):
        at = rows_of(p)
        cell = jnp.where(own_ref[at, :] > 0.0, cells[p], 0.0)
        out = jnp.where(lane < length, cell, shifted(first_ref[at, :], length - cut))
        out_ref[at, :] = jnp.where(
            lane < image_at, out, shifted(image_ref[at, :], image_at - image_cut)
        )


def insert_kernel(packed_ref, riders_ref, out_ref):
    out_ref[:, :128] = packed_ref[:, :128]
    lane = lanes((packed_ref.shape[0], 128))
    out_ref[:, 128:] = jnp.where(lane < SCALARS - 128, packed_ref[:, 128:], riders_ref[:1, :])


def unpack_kernel(length, count, slab_ref, out_ref):
    turned = slab_ref[:, 128:].T
    out_ref[:count, :] = turned[length - 128 : length - 128 + count]


def finish_kernel(
    length,
    copies,
    back_ref,
    first_ref,
    image_ref,
    forcing_ref,
    mask_ref,
    solution_ref,
    residual_ref,
    direction_ref,
):
    at = SCALARS - 128
    totals = jnp.sum(back_ref[:, 128:], axis=0, keepdims=True) * (1.0 / copies)
    rz, curvature, own = [totals[:, at + n : at + n + 1] for n in range(3)]
    alpha = rz / curvature
    rz_next = rz - 2.0 * alpha * curvature + alpha * alpha * own
    beta = rz_next / rz
    back = back_ref[...].T
    cut = WIDE - length
    image_cut = SCALARS - length
    image_at = 2 * length - cut
    rhs = mask_ref[...].astype(jnp.float32) * forcing_ref[...]

    def store(where, rows_back, first):
        solution_ref[where, :] = alpha * first
        direction_ref[where, :] = (first - alpha * rows_back) + beta * first

    store(slice(0, cut), back[:cut], first_ref[:cut, :])
    store(slice(cut, length), back[cut:length], back[length:image_at])
    residual_ref[:image_cut, :] = rhs[:image_cut] - alpha * image_ref[:image_cut, :]
    residual_ref[image_cut:, :] = (
        rhs[image_cut:] - alpha * back[image_at : image_at + length - image_cut]
    )


def call(kernel, out_shapes, scratch=(), name=None):
    single = not isinstance(out_shapes, (list, tuple)) or isinstance(out_shapes[0], int)
    shapes = [out_shapes] if single else out_shapes
    outs = [jax.ShapeDtypeStruct(s, jnp.float32) for s in shapes]
    return pl.pallas_call(
        kernel,
        out_shape=outs[0] if single else outs,
        scratch_shapes=[pltpu.VMEM(s, jnp.float32) for s in scratch],
        compiler_params=pltpu.CompilerParams(vmem_limit_bytes=16 * 2**20),
        name=name,
    )


def exchanged(value):
    groups = lax.axis_size(LON)
    parts = value.reshape(groups, ROWS, value.shape[-1])
    return lax.all_to_all(parts, LON, split_axis=0, concat_axis=0, tiled=True).reshape(value.shape)


def from_lat(value, steps, ring):
    count = lax.axis_size("lat")
    pairs = [(d + steps, d) for d in range(count)]
    if ring:
        pairs = [(s % count, d) for s, d in pairs]
    return lax.ppermute(value, "lat", [(s, d) for s, d in pairs if 0 <= s < count])


def around_lat(value):
    lats, lons = lax.axis_size("lat"), lax.axis_size(LON)
    pairs = [
        (g * lons + q, (g + q) % lats * lons + q) for g in range(lats) for q in range(lons)
    ]
    return lax.ppermute(value, LAT_LON, pairs)


def after(value, *others):
    return lax.optimization_barrier((value, *others))[0]


def local(
    surface_forcing,
    ocean_mask,
    self_coupling,
    east_coupling,
    north_coupling,
    zonal_weight,
    aligned_inverse,
    staggered_inverse,
):
    groups = lax.axis_size(LON)
    length, rows = surface_forcing.shape
    norm = 1.0 / (groups * length)
    matrices, twiddle, outer, wave = tables(groups, length)
    channel = lax.axis_index(LON)
    count, block = aligned_inverse.shape[0], aligned_inverse.shape[1]
    half = block // 2
    wide = (rows, WIDE)
    transforms = [wide, wide]

    cells = (length, rows)
    anywhere = pl.BlockSpec(memory_space=pltpu.HBM)
    packed = pl.pallas_call(
        pack_kernel,
        out_shape=jax.ShapeDtypeStruct(wide, jnp.float32),
        in_specs=[anywhere] * 3,
        scratch_shapes=[
            pltpu.VMEM(cells, jnp.float32),
            pltpu.VMEM(cells, jnp.int32),
            pltpu.VMEM(cells, jnp.float32),
            pltpu.VMEM(wide, jnp.float32),
            pltpu.SemaphoreType.DMA((3,)),
        ],
        compiler_params=pltpu.CompilerParams(vmem_limit_bytes=8 * 2**20),
        name="pack",
    )(surface_forcing, ocean_mask, self_coupling)
    slab = exchanged(packed)

    mask, north_cells = lax.optimization_barrier((ocean_mask, north_coupling, packed))[:2]
    wet_first, top_last = call(
        edges_kernel, [(ROWS, WIDE)] * 2, [(WIDE, 128)], name="edges"
    )(mask, north_cells)
    rest, late = call(
        pack_rest_kernel,
        [(rows, 2 * WIDE), (rows, 128)],
        [(2 * WIDE, rows), (128, rows)],
        name="pack_rest",
    )(
        mask,
        self_coupling,
        east_coupling,
        north_cells,
        from_lat(wet_first, 1, False),
        from_lat(top_last, -1, False),
    )
    spectrum = call(
        lambda *r: forward_kernel(groups, *r), (rows, 2 * WIDE), transforms, name="forward"
    )(slab, rest, matrices, twiddle)
    spec_rhs = exchanged(spectrum)

    stag_below = from_lat(after(staggered_inverse[count - 1], spectrum), -1, False)
    weights = after(zonal_weight, spectrum)
    scale = lax.rsqrt(1.0 + weights[:, None] * lax.dynamic_slice_in_dim(wave, channel, 1, 0))
    weight = jnp.where(channel < 2, 1.0, 2.0).astype(jnp.float32)
    spec_rhs = after(spec_rhs, stag_below, scale)

    edge = (half + 16, WIDE)

    def blocks(spectrum):
        scaled, part, down, up = call(blocks_kernel, [wide, wide, edge, edge], name="blocks")(
            spectrum, scale, aligned_inverse
        )
        above, below = from_lat(down, 1, False), from_lat(up, -1, False)
        return scaled, part, scale, above, below, staggered_inverse, stag_below

    pieces = blocks(spec_rhs)
    flat = call(
        lambda *r: coefficients_kernel(groups, length, *r), [wide] * 5, name="coefficients"
    )(slab, after(spec_rhs, pieces[0]))
    late = after(late, *flat)
    filtered = exchanged(
        call(lambda *r: halo_kernel(norm, *r), wide, [(rows, 128)] * 2, name="halo")(*pieces, late)
    )
    spec, first, image, sums = call(
        lambda *r: step_kernel(groups, length, *r),
        [wide, wide, wide, (8, 128)],
        transforms + [(3 * rows, 128)] * 2 + [(rows, 128)],
        name="step",
    )(filtered, slab, *flat, matrices, twiddle, outer)
    spec_image = exchanged(spec)
    smem = pl.BlockSpec(memory_space=pltpu.SMEM)
    vmem = pl.BlockSpec(memory_space=pltpu.VMEM)
    pieces = blocks(spec_image)
    cut, image_cut = WIDE - length, SCALARS - length
    first_cells = call(lambda *r: unpack_kernel(length, cut, *r), cells, name="unpack_first")(
        after(spec_image, pieces[0])
    )
    summed = pl.pallas_call(
        lambda *r: sums_kernel(norm, length, *r),
        out_shape=jax.ShapeDtypeStruct(wide, jnp.float32),
        in_specs=[vmem] * 9 + [smem, smem],
        out_specs=vmem,
        compiler_params=pltpu.CompilerParams(vmem_limit_bytes=16 * 2**20),
        name="sums",
    )(*pieces, spec_image, after(image, first_cells), weight.reshape(1, 1), sums)
    filtered = exchanged(summed)
    riders = around_lat(call(gather_kernel, (8, 128), name="gather")(filtered))
    packed = call(lambda *r: last_kernel(groups, length, *r), wide, name="last")(
        filtered, flat[0], first, image, matrices, twiddle
    )
    image_cells = call(
        lambda *r: unpack_kernel(length, image_cut, *r), cells, name="unpack_image"
    )(after(filtered, packed))
    packed = call(insert_kernel, wide, name="insert")(after(packed, image_cells), riders)
    copies = ROWS * groups // lax.axis_size("lat")
    return tuple(
        call(lambda *r: finish_kernel(length, copies, *r), [cells] * 3, name="finish")(
            exchanged(packed), first_cells, image_cells, surface_forcing, ocean_mask
        )
    )


def solution(mesh):
    torus = Mesh(
        mesh.devices.reshape(mesh.shape["lat"], 4, 4, 2), ("lat", "lon_0", "lon_1", "lon_2")
    )
    return jax.shard_map(
        local,
        mesh=torus,
        in_specs=(
            P(LON, "lat"),
            P(LON, "lat"),
            P(LON, "lat"),
            P(LON, "lat"),
            P(LON, "lat"),
            P("lat"),
            P("lat", None, None),
            P("lat", None, None),
        ),
        out_specs=(P(LON, "lat"), P(LON, "lat"), P(LON, "lat")),
        check_vma=False,
    )
```

```python
import jax
import jax.numpy as jnp
import numpy as np
from jax import lax
from jax.experimental import pallas as pl
from jax.experimental.pallas import tpu as pltpu
from jax.sharding import Mesh
from jax.sharding import PartitionSpec as P

LON = ("lon_0", "lon_1", "lon_2")
TURN = 2.0 * np.pi
ROWS = 8
WIDE = 256
HALO = 136
FOLD = 68
LATE = HALO + FOLD
SCALARS = WIDE - 4


def tables(groups, length):
    period = groups * length
    index = np.arange(length)
    inner = TURN * (np.outer(index, index) % length) / length
    wave_of = np.zeros(groups, np.int64)
    wave_of[1] = groups // 2
    for m in range(1, groups // 2):
        wave_of[2 * m] = wave_of[2 * m + 1] = m
    turn = TURN * (np.outer(wave_of, index) % period) / period
    matrices = np.zeros((2, WIDE, WIDE), np.float32)
    matrices[0, :length, :length] = np.cos(inner)
    matrices[1, :length, :length] = np.sin(inner)
    coarse = matrices.astype(jnp.bfloat16)
    rest = (matrices - coarse.astype(np.float32)).astype(jnp.bfloat16)
    twiddle = np.zeros((2, groups, WIDE))
    twiddle[0, :, :length] = np.cos(turn)
    twiddle[1, :, :length] = np.sin(turn)
    chunk = np.arange(groups)
    outer = np.zeros((2, groups, groups))
    for c in range(groups):
        phase = TURN * (chunk * wave_of[c] % groups) / groups
        if c < 2:
            outer[0, :, c] = outer[1, :, c] = np.cos(phase)
        elif c % 2 == 0:
            outer[0, :, c], outer[1, :, c] = 2 * np.cos(phase), -2 * np.sin(phase)
        else:
            outer[0, :, c], outer[1, :, c] = -2 * np.sin(phase), -2 * np.cos(phase)
    modes = wave_of[:, None] + groups * index[None, :]
    wave = np.zeros((groups, WIDE))
    wave[:, :length] = 4.0 * np.sin(np.pi * modes / period) ** 2
    return (
        np.stack([coarse, rest]),
        twiddle.astype(np.float32),
        outer.astype(np.float32),
        wave.astype(np.float32),
    )


def real_fft(values):
    count = len(values)
    if count == 2:
        return [(values[0] + values[1], None), (values[0] - values[1], None)]
    even, odd = real_fft(values[0::2]), real_fft(values[1::2])
    out = [None] * (count // 2 + 1)
    for k in range(count // 4 + 1):
        (er, ei), (re, im) = even[k], odd[k]
        if k == 0:
            out[0], out[count // 2] = (er + re, None), (er - re, None)
        elif k == count // 4:
            out[k] = (er, -re)
        else:
            c, s = float(np.cos(TURN * k / count)), float(-np.sin(TURN * k / count))
            tr, ti = re * c - im * s, im * c + re * s
            out[k], out[count // 2 - k] = (er + tr, ei + ti), (er - tr, ti - ei)
    return out


def real_ifft(spectrum):
    count = 2 * (len(spectrum) - 1)
    if count == 2:
        return [spectrum[0][0] + spectrum[1][0], spectrum[0][0] - spectrum[1][0]]
    even, odd = [], []
    for k in range(count // 4 + 1):
        (ar, ai), (br, bi) = spectrum[k], spectrum[count // 2 - k]
        if k == 0:
            even.append((ar + br, None))
            odd.append((ar - br, None))
        elif k == count // 4:
            even.append((2.0 * ar, None))
            odd.append((-2.0 * ai, None))
        else:
            c, s = float(np.cos(TURN * k / count)), float(np.sin(TURN * k / count))
            dr, di = ar - br, ai + bi
            even.append((ar + br, ai - bi))
            odd.append((dr * c - di * s, dr * s + di * c))
    first, second = real_ifft(even), real_ifft(odd)
    out = []
    for a, b in zip(first, second, strict=True):
        out += [a, b]
    return out


def split(a):
    coarse = a.astype(jnp.bfloat16)
    return coarse, (a - coarse.astype(jnp.float32)).astype(jnp.bfloat16)


def product(a, b):
    (ac, ar), (bc, br) = a, b

    def one(x, y):
        return jnp.dot(x, y, preferred_element_type=jnp.float32)

    return one(ac, bc) + (one(ac, br) + one(ar, bc))


def dot(a, b):
    return product(split(a), split(b))


def table(matrix_ref, n):
    return matrix_ref[0, n], matrix_ref[1, n]


def rows_of(p):
    return slice(ROWS * p, ROWS * (p + 1))


def lanes(shape):
    return lax.broadcasted_iota(jnp.int32, shape, len(shape) - 1)


def sublanes(shape):
    return lax.broadcasted_iota(jnp.int32, shape, len(shape) - 2)


def shifted(value, lanes_right):
    return pltpu.roll(value, lanes_right % value.shape[1], 1)


def pack_kernel(rhs_ref, own_ref, out_ref, tall):
    length = rhs_ref.shape[0]
    tall[:length, :] = rhs_ref[...]
    tall[length:, :] = own_ref[: WIDE - length, :]
    out_ref[...] = tall[...].T


def edges_kernel(mask_ref, north_ref, wet_ref, top_ref, tall):
    length, rows = mask_ref.shape
    tall[length:, :] = jnp.zeros((WIDE - length, 128), jnp.float32)
    tall[:length, :] = mask_ref[:, :128].astype(jnp.float32)
    wet_ref[...] = tall[...].T[:ROWS]
    tall[:length, :] = mask_ref[:, rows - 128 :].astype(jnp.float32) * north_ref[:, rows - 128 :]
    top_ref[...] = tall[...].T[128 - ROWS :]


def lane_plan(length):
    cut = WIDE - length
    north = 2 * length - cut
    south = north + length
    east = south + length
    return cut, north, south, east, 2 * WIDE - east


def pack_rest_kernel(
    mask_ref,
    self_ref,
    east_ref,
    north_ref,
    flags_ref,
    wet_above_ref,
    top_below_ref,
    out_ref,
    late_ref,
    tall,
    short,
):
    length, rows = mask_ref.shape
    cut, n_at, s_at, e_at, count = lane_plan(length)
    lane = lanes((length, rows))
    wet = mask_ref[...].astype(jnp.float32)
    north = wet * north_ref[...]
    east = wet * east_ref[...]
    wet_above = wet_above_ref[...].T[:length, :1] * flags_ref[:1, :1]
    top_below = top_below_ref[...].T[:length, ROWS - 1 :] * flags_ref[1:2, :1]
    tall[:length, :] = jnp.zeros((length, rows), jnp.float32)
    tall[length:n_at, :] = (wet * self_ref[...])[cut:]
    tall[n_at:s_at, :] = north * jnp.where(lane == rows - 1, wet_above, shifted(wet, -1))
    tall[s_at:e_at, :] = wet * jnp.where(lane == 0, top_below, shifted(north, 1))
    tall[e_at:, :] = east[:count]
    out_ref[...] = tall[...].T
    short[...] = jnp.zeros((128, rows), jnp.float32)
    short[LATE - 128 : LATE - 128 + length - count, :] = east[count:]
    late_ref[...] = short[...].T


def coefficients_kernel(
    groups, length, slab_ref, second_ref, own_ref, next_ref, east_ref, north_ref, south_ref
):
    cut, n_at, s_at, e_at, count = lane_plan(length)
    lane = lanes((ROWS, WIDE))
    held = lane < length
    for p in range(groups):
        at = rows_of(p)
        late = second_ref[at, :]
        own_ref[at, :] = jnp.where(
            lane < cut,
            shifted(slab_ref[at, :], -length),
            jnp.where(held, shifted(late[:, :WIDE], cut - length), 0.0),
        )
        north_ref[at, :] = jnp.where(held, shifted(late, -n_at)[:, :WIDE], 0.0)
        south_ref[at, :] = jnp.where(held, shifted(late[:, WIDE:], WIDE - s_at), 0.0)
        east_ref[at, :] = jnp.where(lane < count, shifted(late[:, WIDE:], WIDE - e_at), 0.0)
    for p in range(groups):
        own = own_ref[rows_of(p), :]
        after = own_ref[rows_of((p + 1) % groups), 0:1]
        ocean = jnp.where(lane == length, after, own) > 0.0
        next_ref[rows_of(p), :] = shifted(ocean.astype(jnp.float32), -1)


def transform(chunks, matrix_ref, twiddle_ref, left, right):
    groups = len(chunks)
    mixed = real_fft(chunks)
    for m in range(groups // 2 + 1):
        re, im = mixed[m]
        if m == 0:
            left[rows_of(0), :] = re
            right[rows_of(0), :] = re
            continue
        c = 1 if m == groups // 2 else 2 * m
        cos, sin = twiddle_ref[0, c : c + 1, :], twiddle_ref[1, c : c + 1, :]
        if m == groups // 2:
            left[rows_of(1), :] = re * (cos + sin)
            right[rows_of(1), :] = re * (cos - sin)
        else:
            tr, ti = re * cos + im * sin, im * cos - re * sin
            left[rows_of(c), :] = tr
            right[rows_of(c), :] = ti
            left[rows_of(c + 1), :] = ti
            right[rows_of(c + 1), :] = -tr
    return product(split(left[...]), table(matrix_ref, 0)) + product(
        split(right[...]), table(matrix_ref, 1)
    )


def transform_back(spectrum, groups, matrix_ref, twiddle_ref):
    parts = split(spectrum)
    pc, ps = product(parts, table(matrix_ref, 0)), product(parts, table(matrix_ref, 1))
    mixed = []
    for m in range(groups // 2 + 1):
        if m == 0:
            mixed.append((pc[rows_of(0)] + ps[rows_of(0)], None))
            continue
        c = 1 if m == groups // 2 else 2 * m
        cos, sin = twiddle_ref[0, c : c + 1, :], twiddle_ref[1, c : c + 1, :]
        if m == groups // 2:
            mixed.append((pc[rows_of(1)] * (cos + sin) + ps[rows_of(1)] * (cos - sin), None))
        else:
            hr = pc[rows_of(c)] - ps[rows_of(c + 1)]
            hi = ps[rows_of(c)] + pc[rows_of(c + 1)]
            mixed.append((hr * cos - hi * sin, hi * cos + hr * sin))
    return real_ifft(mixed)


def row_back(spectrum, matrix_ref, twiddle_ref, outer_ref):
    parts = split(spectrum)
    pc, ps = product(parts, table(matrix_ref, 0)), product(parts, table(matrix_ref, 1))
    cos, sin = twiddle_ref[0], twiddle_ref[1]
    return dot(outer_ref[0], pc * cos - ps * sin) + dot(outer_ref[1], ps * cos + pc * sin)


def forward_kernel(groups, field_ref, rest_ref, matrix_ref, twiddle_ref, out_ref, left, right):
    chunks = [field_ref[rows_of(p), :] for p in range(groups)]
    spectrum = transform(chunks, matrix_ref, twiddle_ref, left, right)
    out_ref[:, :WIDE] = spectrum + rest_ref[:, :WIDE]
    out_ref[:, WIDE:] = rest_ref[:, WIDE:]


def blocks_kernel(spec_ref, scale_ref, aligned_ref, scaled_ref, part_ref, down_ref, up_ref):
    count, block = aligned_ref.shape[0], aligned_ref.shape[1]
    half, rows = block // 2, count * block
    scaled = spec_ref[:, :WIDE] * scale_ref[...]
    scaled_ref[...] = scaled
    for b in range(count):
        part_ref[b * block : (b + 1) * block, :] = dot(
            aligned_ref[b], scaled[b * block : (b + 1) * block]
        )
    down_ref[:half, :] = scaled[:half]
    down_ref[half : half + 8, :] = part_ref[:8, :]
    down_ref[half + 8 :, :] = scale_ref[:8, :]
    up_ref[:half, :] = scaled[rows - half :]
    up_ref[half : half + 8, :] = part_ref[rows - 8 :, :]
    up_ref[half + 8 :, :] = scale_ref[rows - 8 :, :]


def combine(
    norm, scaled_ref, part_ref, scale_ref, above_ref, below_ref, stag_ref, stag_below_ref, flags_ref
):
    count, block = stag_ref.shape[0], stag_ref.shape[1]
    half, rows = block // 2, count * block
    before = flags_ref[1:2, :] * dot(
        stag_below_ref[...],
        jnp.concatenate([below_ref[:half, :], scaled_ref[:half, :]], axis=0),
    )
    upper = above_ref[:half, :] * flags_ref[:1, :]
    pieces = [before[half:]]
    for b in range(count - 1):
        pieces.append(dot(stag_ref[b], scaled_ref[half + b * block : half + (b + 1) * block, :]))
    after = dot(
        stag_ref[count - 1],
        jnp.concatenate([scaled_ref[rows - half :, :], upper], axis=0),
    )
    pieces.append(after[:half])
    full = (part_ref[...] + jnp.concatenate(pieces, axis=0)) * (scale_ref[...] * norm)
    return full, before, after


def halo_kernel(
    norm,
    scaled_ref,
    part_ref,
    scale_ref,
    above_ref,
    below_ref,
    stag_ref,
    stag_below_ref,
    flags_ref,
    late_ref,
    out_ref,
    low,
    high,
):
    half = stag_ref.shape[1] // 2
    full, before, after = combine(
        norm,
        scaled_ref,
        part_ref,
        scale_ref,
        above_ref,
        below_ref,
        stag_ref,
        stag_below_ref,
        flags_ref,
    )
    row_below = (before[half - 1 : half] + below_ref[half + 7 : half + 8, :]) * (
        below_ref[half + 15 : half + 16, :] * norm
    )
    row_above = (after[half : half + 1] + above_ref[half : half + 1, :]) * (
        above_ref[half + 8 : half + 9, :] * norm
    )
    out_ref[:, :128] = full[:, :128]
    low[...] = full[:, :128]
    high[...] = full[:, 128:]
    groups = full.shape[0] // ROWS

    def strided(start):
        at = pl.ds(start, groups, stride=ROWS)
        return jnp.concatenate([low[at, :], high[at, :]], axis=1)

    row = lax.broadcasted_iota(jnp.int32, (groups, WIDE), 0)
    up = jnp.where(row == 0, row_below, pltpu.roll(strided(ROWS - 1), 1, 0))
    down = jnp.where(row == groups - 1, row_above, pltpu.roll(strided(0), groups - 1, 0))
    lane = lanes((groups, 128)) + 128
    for s, part in enumerate(
        (
            pltpu.roll(up, HALO, 1),
            pltpu.roll(up, HALO - FOLD, 1),
            pltpu.roll(down, HALO, 1),
            pltpu.roll(down, HALO - FOLD, 1),
        )
    ):
        at = pl.ds(s, groups, stride=ROWS)
        high[at, :] = jnp.where(lane >= HALO, part[:, 128:], high[at, :])
    out_ref[:, 128:] = jnp.where(
        lanes(high.shape) < LATE - 128, high[...], late_ref[...]
    )


def sums_kernel(
    norm,
    length,
    scaled_ref,
    part_ref,
    scale_ref,
    above_ref,
    below_ref,
    stag_ref,
    stag_below_ref,
    flags_ref,
    spec_ref,
    aside_ref,
    sums_ref,
    out_ref,
    sums_out_ref,
):
    full, _, _ = combine(
        norm,
        scaled_ref,
        part_ref,
        scale_ref,
        above_ref,
        below_ref,
        stag_ref,
        stag_below_ref,
        flags_ref,
    )
    lane = lanes(full.shape)
    held = jnp.where(lane < length, full, 0.0)
    own = jnp.sum(held * spec_ref[...], axis=0, keepdims=True)
    own = jnp.sum(own[:, :128] + own[:, 128:], axis=1, keepdims=True) * flags_ref[2:3, :1]
    small = lanes((8, 128))
    sums_out_ref[...] = jnp.where(small == SCALARS - 128 + 2, own, sums_ref[...])
    out_ref[...] = held + aside_ref[...]


def step_kernel(
    groups,
    length,
    spec_ref,
    rhs_ref,
    own_ref,
    next_ref,
    east_ref,
    north_ref,
    south_ref,
    matrix_ref,
    twiddle_ref,
    outer_ref,
    out_ref,
    first_ref,
    image_ref,
    sums_ref,
    left,
    right,
    low,
    high,
    tail,
):
    lane_row = lanes((groups, WIDE))
    stride = 3 * ROWS
    tail[...] = spec_ref[:, 128:]

    def halo_row(s):
        blank = jnp.zeros((groups, 128), jnp.float32)
        parts = [
            jnp.concatenate([tail[pl.ds(s + n, groups, stride=ROWS), :], blank], axis=1)
            for n in range(2)
        ]
        row = jnp.where(
            lane_row < FOLD, shifted(parts[0], 128 - HALO), shifted(parts[1], FOLD + 128 - HALO)
        )
        return row_back(row, matrix_ref, twiddle_ref, outer_ref)

    for start, s in ((ROWS - 1, 0), (2 * ROWS, 2)):
        row = halo_row(s)
        low[pl.ds(start, groups, stride=stride), :] = row[:, :128]
        high[pl.ds(start, groups, stride=stride), :] = row[:, 128:]

    def neighbour(start):
        at = slice(start, start + ROWS)
        return jnp.concatenate([low[at, :], high[at, :]], axis=1)

    cells = transform_back(spec_ref[...], groups, matrix_ref, twiddle_ref)
    for p in range(groups):
        v = jnp.where(own_ref[rows_of(p), :] > 0.0, cells[p], 0.0)
        first_ref[rows_of(p), :] = v
        low[stride * p + ROWS : stride * p + 2 * ROWS, :] = v[:, :128]
        high[stride * p + ROWS : stride * p + 2 * ROWS, :] = v[:, 128:]
    lane = lanes((ROWS, WIDE))
    count = lane_plan(length)[-1]
    rz = jnp.zeros((ROWS, WIDE), jnp.float32)
    curvature = jnp.zeros((ROWS, WIDE), jnp.float32)
    images, fluxes = [], []
    for p in range(groups):
        at = rows_of(p)
        v = first_ref[at, :]
        after = first_ref[rows_of((p + 1) % groups), 0:1]
        east = jnp.where(lane < count, east_ref[at, :], shifted(spec_ref[at, :], count - LATE))
        flux = v - shifted(jnp.where(lane == length, after, v), -1)
        fluxes.append(jnp.where(lane < length, east * next_ref[at, :] * flux, 0.0))
    for p in range(groups):
        at = rows_of(p)
        v = first_ref[at, :]
        before = fluxes[(p - 1) % groups][:, length - 1 : length]
        flux = fluxes[p]
        own = own_ref[at, :]
        base = stride * p + ROWS
        image = jnp.where(own > 0.0, own, 1.0) * v
        image = image + (flux - shifted(jnp.where(lane == WIDE - 1, before, flux), 1))
        image = image + north_ref[at, :] * (v - neighbour(base + 1))
        image = image + south_ref[at, :] * (v - neighbour(base - 1))
        image = jnp.where(lane < length, image, 0.0)
        image_ref[at, :] = image
        images.append(image)
        rz = rz + rhs_ref[at, :] * v
        curvature = curvature + v * image
    small = lanes((8, 128))
    at = SCALARS - 128
    sums_ref[...] = jnp.where(
        small == at, jnp.sum(rz), jnp.where(small == at + 1, jnp.sum(curvature), 0.0)
    )
    spectrum = transform(images, matrix_ref, twiddle_ref, left, right)
    out_ref[...] = jnp.where(
        lanes(out_ref.shape) < length, spectrum, shifted(first_ref[...], length)
    )


def last_kernel(
    groups,
    length,
    spec_ref,
    own_ref,
    first_ref,
    image_ref,
    three_ref,
    others_ref,
    pair_ref,
    matrix_ref,
    twiddle_ref,
    out_ref,
):
    cells = transform_back(spec_ref[...], groups, matrix_ref, twiddle_ref)
    lane = lanes((ROWS, WIDE))
    cut = WIDE - length
    image_cut = SCALARS - length
    image_at = 2 * length - cut
    totals = three_ref[...] + others_ref[...] + pair_ref[...]
    riders = jnp.concatenate([totals, totals], axis=1)
    for p in range(groups):
        at = rows_of(p)
        cell = jnp.where(own_ref[at, :] > 0.0, cells[p], 0.0)
        out = jnp.where(lane < length, cell, shifted(first_ref[at, :], length - cut))
        out = jnp.where(lane < image_at, out, shifted(image_ref[at, :], image_at - image_cut))
        out_ref[at, :] = jnp.where(lane < SCALARS, out, riders)


def unpack_kernel(length, count, slab_ref, out_ref):
    turned = slab_ref[:, 128:].T
    out_ref[:count, :] = turned[length - 128 : length - 128 + count]


def unpack_first_kernel(length, count, slab_ref, image_ref, out_ref, aside_ref):
    unpack_kernel(length, count, slab_ref, out_ref)
    lane = lanes(image_ref.shape)
    aside_ref[...] = jnp.where(lane < length, 0.0, shifted(image_ref[...], length))


def finish_kernel(
    length,
    back_ref,
    first_ref,
    image_ref,
    forcing_ref,
    mask_ref,
    solution_ref,
    residual_ref,
    direction_ref,
):
    at = SCALARS - 128
    totals = jnp.sum(back_ref[:, 128:], axis=0, keepdims=True) * (1.0 / ROWS)
    rz, curvature, own = [totals[:, at + n : at + n + 1] for n in range(3)]
    alpha = rz / curvature
    rz_next = rz - 2.0 * alpha * curvature + alpha * alpha * own
    beta = rz_next / rz
    back = back_ref[...].T
    cut = WIDE - length
    image_cut = SCALARS - length
    image_at = 2 * length - cut
    rhs = mask_ref[...].astype(jnp.float32) * forcing_ref[...]

    def store(where, rows_back, first):
        solution_ref[where, :] = alpha * first
        direction_ref[where, :] = (first - alpha * rows_back) + beta * first

    store(slice(0, cut), back[:cut], first_ref[:cut, :])
    store(slice(cut, length), back[cut:length], back[length:image_at])
    residual_ref[:image_cut, :] = rhs[:image_cut] - alpha * image_ref[:image_cut, :]
    residual_ref[image_cut:, :] = (
        rhs[image_cut:] - alpha * back[image_at : image_at + length - image_cut]
    )


def call(kernel, out_shapes, scratch=(), name=None):
    single = not isinstance(out_shapes, (list, tuple)) or isinstance(out_shapes[0], int)
    shapes = [out_shapes] if single else out_shapes
    outs = [jax.ShapeDtypeStruct(s, jnp.float32) for s in shapes]
    return pl.pallas_call(
        kernel,
        out_shape=outs[0] if single else outs,
        scratch_shapes=[pltpu.VMEM(s, jnp.float32) for s in scratch],
        compiler_params=pltpu.CompilerParams(vmem_limit_bytes=16 * 2**20),
        name=name,
    )


def exchanged(value):
    groups = lax.axis_size(LON)
    parts = value.reshape(groups, ROWS, value.shape[-1])
    return lax.all_to_all(parts, LON, split_axis=0, concat_axis=0, tiled=True).reshape(value.shape)


def from_lat(value, steps):
    count = lax.axis_size("lat")
    return lax.ppermute(value, "lat", [((d + steps) % count, d) for d in range(count)])


def after(value, *others):
    return lax.optimization_barrier((value, *others))[0]


def local(
    surface_forcing,
    ocean_mask,
    self_coupling,
    east_coupling,
    north_coupling,
    zonal_weight,
    aligned_inverse,
    staggered_inverse,
):
    groups = lax.axis_size(LON)
    length, rows = surface_forcing.shape
    norm = 1.0 / (groups * length)
    matrices, twiddle, outer, wave = tables(groups, length)
    channel = lax.axis_index(LON)
    count, block = aligned_inverse.shape[0], aligned_inverse.shape[1]
    half = block // 2
    wide = (rows, WIDE)
    transforms = [wide, wide]

    cells = (length, rows)
    wet_cells = ocean_mask.astype(jnp.float32)
    packed = call(pack_kernel, wide, [wide], name="pack")(
        wet_cells * surface_forcing, wet_cells * self_coupling
    )
    slab = exchanged(packed)

    mask, north_cells = lax.optimization_barrier((ocean_mask, north_coupling, packed))[:2]
    lat = lax.axis_index("lat")
    flag_row = lax.broadcasted_iota(jnp.int32, (8, WIDE), 0)
    north_of, south_of, weight = (
        jnp.where(condition, yes, no).astype(jnp.float32)
        for condition, yes, no in (
            (lat < lax.axis_size("lat") - 1, 1.0, 0.0),
            (lat > 0, 1.0, 0.0),
            (channel < 2, 1.0, 2.0),
        )
    )
    flags = jnp.where(flag_row == 0, north_of, jnp.where(flag_row == 1, south_of, weight))
    wet_first, top_last = call(
        edges_kernel, [(ROWS, WIDE)] * 2, [(WIDE, 128)], name="edges"
    )(mask, north_cells)
    rest, late = call(
        pack_rest_kernel,
        [(rows, 2 * WIDE), (rows, 128)],
        [(2 * WIDE, rows), (128, rows)],
        name="pack_rest",
    )(
        mask,
        self_coupling,
        east_coupling,
        north_cells,
        flags,
        from_lat(wet_first, 1),
        from_lat(top_last, -1),
    )
    spectrum = call(
        lambda *r: forward_kernel(groups, *r), (rows, 2 * WIDE), transforms, name="forward"
    )(slab, rest, matrices, twiddle)
    spec_rhs = exchanged(spectrum)

    stag_below = from_lat(after(staggered_inverse[count - 1], spectrum), -1)
    weights = after(zonal_weight, spectrum)
    scale = lax.rsqrt(1.0 + weights[:, None] * lax.dynamic_slice_in_dim(wave, channel, 1, 0))
    spec_rhs = after(spec_rhs, stag_below, scale)

    edge = (half + 16, WIDE)

    def blocks(spectrum):
        scaled, part, down, up = call(blocks_kernel, [wide, wide, edge, edge], name="blocks")(
            spectrum, scale, aligned_inverse
        )
        above, below = from_lat(down, 1), from_lat(up, -1)
        return scaled, part, scale, above, below, staggered_inverse, stag_below, flags

    pieces = blocks(spec_rhs)
    flat = call(
        lambda *r: coefficients_kernel(groups, length, *r), [wide] * 5, name="coefficients"
    )(slab, after(spec_rhs, pieces[0]))
    late = after(late, *flat)
    filtered = exchanged(
        call(lambda *r: halo_kernel(norm, *r), wide, [(rows, 128)] * 2, name="halo")(*pieces, late)
    )
    spec, first, image, sums = call(
        lambda *r: step_kernel(groups, length, *r),
        [wide, wide, wide, (8, 128)],
        transforms + [(3 * rows, 128)] * 2 + [(rows, 128)],
        name="step",
    )(filtered, slab, *flat, matrices, twiddle, outer)
    spec_image = exchanged(spec)
    pieces = blocks(spec_image)
    cut, image_cut = WIDE - length, SCALARS - length
    first_cells, aside = call(
        lambda *r: unpack_first_kernel(length, cut, *r), [cells, wide], name="unpack_first"
    )(after(spec_image, pieces[0]), image)
    summed, sums = call(
        lambda *r: sums_kernel(norm, length, *r), [wide, (8, 128)], name="sums"
    )(*pieces, spec_image, aside, sums)

    pair = sums + from_lat(sums, -1)
    three = pair + from_lat(sums, 1)
    others, last_pair = from_lat(three, 3), from_lat(pair, -2)
    filtered = exchanged(summed)
    image_cells = call(
        lambda *r: unpack_kernel(length, image_cut, *r), cells, name="unpack_image"
    )(filtered)
    packed = call(lambda *r: last_kernel(groups, length, *r), wide, name="last")(
        filtered, flat[0], first, image, three, others, last_pair, matrices, twiddle
    )
    return tuple(
        call(lambda *r: finish_kernel(length, *r), [cells] * 3, name="finish")(
            exchanged(packed), first_cells, image_cells, surface_forcing, ocean_mask
        )
    )


def solution(mesh):
    torus = Mesh(
        mesh.devices.reshape(mesh.shape["lat"], 4, 4, 2), ("lat", "lon_0", "lon_1", "lon_2")
    )
    return jax.shard_map(
        local,
        mesh=torus,
        in_specs=(
            P(LON, "lat"),
            P(LON, "lat"),
            P(LON, "lat"),
            P(LON, "lat"),
            P(LON, "lat"),
            P("lat"),
            P("lat", None, None),
            P("lat", None, None),
        ),
        out_specs=(P(LON, "lat"), P(LON, "lat"), P(LON, "lat")),
        check_vma=False,
    )
```

```python
import jax
import jax.numpy as jnp
import numpy as np
from jax import lax
from jax.experimental import pallas as pl
from jax.experimental.pallas import tpu as pltpu
from jax.sharding import Mesh
from jax.sharding import PartitionSpec as P

LON = ("lon_0", "lon_1", "lon_2")
TURN = 2.0 * np.pi
ROWS = 8
WIDE = 256
HALO = 136
FOLD = 68
LATE = HALO + FOLD
SCALARS = WIDE - 4


def tables(groups, length):
    period = groups * length
    index = np.arange(length)
    inner = TURN * (np.outer(index, index) % length) / length
    wave_of = np.zeros(groups, np.int64)
    wave_of[1] = groups // 2
    for m in range(1, groups // 2):
        wave_of[2 * m] = wave_of[2 * m + 1] = m
    turn = TURN * (np.outer(wave_of, index) % period) / period
    matrices = np.zeros((2, WIDE, WIDE), np.float32)
    matrices[0, :length, :length] = np.cos(inner)
    matrices[1, :length, :length] = np.sin(inner)
    coarse = matrices.astype(jnp.bfloat16)
    rest = (matrices - coarse.astype(np.float32)).astype(jnp.bfloat16)
    twiddle = np.zeros((2, groups, WIDE))
    twiddle[0, :, :length] = np.cos(turn)
    twiddle[1, :, :length] = np.sin(turn)
    chunk = np.arange(groups)
    outer = np.zeros((2, groups, groups))
    for c in range(groups):
        phase = TURN * (chunk * wave_of[c] % groups) / groups
        if c < 2:
            outer[0, :, c] = outer[1, :, c] = np.cos(phase)
        elif c % 2 == 0:
            outer[0, :, c], outer[1, :, c] = 2 * np.cos(phase), -2 * np.sin(phase)
        else:
            outer[0, :, c], outer[1, :, c] = -2 * np.sin(phase), -2 * np.cos(phase)
    modes = wave_of[:, None] + groups * index[None, :]
    wave = np.zeros((groups, WIDE))
    wave[:, :length] = 4.0 * np.sin(np.pi * modes / period) ** 2
    return (
        np.stack([coarse, rest]),
        twiddle.astype(np.float32),
        outer.astype(np.float32),
        wave.astype(np.float32),
    )


def real_fft(values):
    count = len(values)
    if count == 2:
        return [(values[0] + values[1], None), (values[0] - values[1], None)]
    even, odd = real_fft(values[0::2]), real_fft(values[1::2])
    out = [None] * (count // 2 + 1)
    for k in range(count // 4 + 1):
        (er, ei), (re, im) = even[k], odd[k]
        if k == 0:
            out[0], out[count // 2] = (er + re, None), (er - re, None)
        elif k == count // 4:
            out[k] = (er, -re)
        else:
            c, s = float(np.cos(TURN * k / count)), float(-np.sin(TURN * k / count))
            tr, ti = re * c - im * s, im * c + re * s
            out[k], out[count // 2 - k] = (er + tr, ei + ti), (er - tr, ti - ei)
    return out


def real_ifft(spectrum):
    count = 2 * (len(spectrum) - 1)
    if count == 2:
        return [spectrum[0][0] + spectrum[1][0], spectrum[0][0] - spectrum[1][0]]
    even, odd = [], []
    for k in range(count // 4 + 1):
        (ar, ai), (br, bi) = spectrum[k], spectrum[count // 2 - k]
        if k == 0:
            even.append((ar + br, None))
            odd.append((ar - br, None))
        elif k == count // 4:
            even.append((2.0 * ar, None))
            odd.append((-2.0 * ai, None))
        else:
            c, s = float(np.cos(TURN * k / count)), float(np.sin(TURN * k / count))
            dr, di = ar - br, ai + bi
            even.append((ar + br, ai - bi))
            odd.append((dr * c - di * s, dr * s + di * c))
    first, second = real_ifft(even), real_ifft(odd)
    out = []
    for a, b in zip(first, second, strict=True):
        out += [a, b]
    return out


def split(a):
    coarse = a.astype(jnp.bfloat16)
    return coarse, (a - coarse.astype(jnp.float32)).astype(jnp.bfloat16)


def product(a, b):
    (ac, ar), (bc, br) = a, b

    def one(x, y):
        return jnp.dot(x, y, preferred_element_type=jnp.float32)

    return one(ac, bc) + (one(ac, br) + one(ar, bc))


def dot(a, b):
    return product(split(a), split(b))


def table(matrix_ref, n):
    return matrix_ref[0, n], matrix_ref[1, n]


def rows_of(p):
    return slice(ROWS * p, ROWS * (p + 1))


def lanes(shape):
    return lax.broadcasted_iota(jnp.int32, shape, len(shape) - 1)


def sublanes(shape):
    return lax.broadcasted_iota(jnp.int32, shape, len(shape) - 2)


def shifted(value, lanes_right):
    return pltpu.roll(value, lanes_right % value.shape[1], 1)


def pack_kernel(rhs_ref, own_ref, out_ref, tall):
    length = rhs_ref.shape[0]
    tall[:length, :] = rhs_ref[...]
    tall[length:, :] = own_ref[: WIDE - length, :]
    out_ref[...] = tall[...].T


def edges_kernel(mask_ref, north_ref, wet_ref, top_ref, tall):
    length, rows = mask_ref.shape
    tall[length:, :] = jnp.zeros((WIDE - length, 128), jnp.float32)
    tall[:length, :] = mask_ref[:, :128].astype(jnp.float32)
    wet_ref[...] = tall[...].T[:ROWS]
    tall[:length, :] = mask_ref[:, rows - 128 :].astype(jnp.float32) * north_ref[:, rows - 128 :]
    top_ref[...] = tall[...].T[128 - ROWS :]


def lane_plan(length):
    cut = WIDE - length
    north = LATE
    south = north + length
    east = south + length
    return cut, 2 * cut - length, north, south, east


def pack_more_kernel(own_ref, mask_ref, east_ref, out_ref, tall):
    length, rows = mask_ref.shape
    cut, count = lane_plan(length)[:2]
    tall[:length, :] = jnp.zeros((length, rows), jnp.float32)
    tall[length : WIDE - count, :] = own_ref[cut:, :]
    tall[WIDE - count :, :] = (mask_ref[...].astype(jnp.float32) * east_ref[...])[:count]
    out_ref[...] = tall[...].T


def pack_rest_kernel(
    mask_ref, east_ref, north_ref, flags_ref, wet_above_ref, top_below_ref, out_ref, tall
):
    length, rows = mask_ref.shape
    _, count, n_at, s_at, e_at = lane_plan(length)
    lane = lanes((length, rows))
    wet = mask_ref[...].astype(jnp.float32)
    north = wet * north_ref[...]
    wet_above = wet_above_ref[...].T[:length, :1] * flags_ref[:1, :1]
    top_below = top_below_ref[...].T[:length, ROWS - 1 :] * flags_ref[1:2, :1]
    tall[128:n_at, :] = jnp.zeros((n_at - 128, rows), jnp.float32)
    tall[n_at:s_at, :] = north * jnp.where(lane == rows - 1, wet_above, shifted(wet, -1))
    tall[s_at:e_at, :] = wet * jnp.where(lane == 0, top_below, shifted(north, 1))
    tall[e_at : e_at + length - count, :] = (wet * east_ref[...])[count:]
    unused = 2 * WIDE - (e_at + length - count)
    tall[2 * WIDE - unused :, :] = jnp.zeros((unused, rows), jnp.float32)
    out_ref[...] = tall[128:, :].T


def coefficients_kernel(groups, length, slab_ref, second_ref, own_ref, next_ref, east_ref):
    cut, count = lane_plan(length)[:2]
    lane = lanes((ROWS, WIDE))
    for p in range(groups):
        at = rows_of(p)
        more = second_ref[at, :]
        own_ref[at, :] = jnp.where(
            lane < cut,
            shifted(slab_ref[at, :], -length),
            jnp.where(lane < length, shifted(more, cut - length), 0.0),
        )
        east_ref[at, :] = jnp.where(lane < count, shifted(more, count), 0.0)
    for p in range(groups):
        own = own_ref[rows_of(p), :]
        after = own_ref[rows_of((p + 1) % groups), 0:1]
        ocean = jnp.where(lane == length, after, own) > 0.0
        next_ref[rows_of(p), :] = shifted(ocean.astype(jnp.float32), -1)


def transform(chunks, matrix_ref, twiddle_ref, left, right):
    groups = len(chunks)
    mixed = real_fft(chunks)
    for m in range(groups // 2 + 1):
        re, im = mixed[m]
        if m == 0:
            left[rows_of(0), :] = re
            right[rows_of(0), :] = re
            continue
        c = 1 if m == groups // 2 else 2 * m
        cos, sin = twiddle_ref[0, c : c + 1, :], twiddle_ref[1, c : c + 1, :]
        if m == groups // 2:
            left[rows_of(1), :] = re * (cos + sin)
            right[rows_of(1), :] = re * (cos - sin)
        else:
            tr, ti = re * cos + im * sin, im * cos - re * sin
            left[rows_of(c), :] = tr
            right[rows_of(c), :] = ti
            left[rows_of(c + 1), :] = ti
            right[rows_of(c + 1), :] = -tr
    return product(split(left[...]), table(matrix_ref, 0)) + product(
        split(right[...]), table(matrix_ref, 1)
    )


def transform_back(spectrum, groups, matrix_ref, twiddle_ref):
    parts = split(spectrum)
    pc, ps = product(parts, table(matrix_ref, 0)), product(parts, table(matrix_ref, 1))
    mixed = []
    for m in range(groups // 2 + 1):
        if m == 0:
            mixed.append((pc[rows_of(0)] + ps[rows_of(0)], None))
            continue
        c = 1 if m == groups // 2 else 2 * m
        cos, sin = twiddle_ref[0, c : c + 1, :], twiddle_ref[1, c : c + 1, :]
        if m == groups // 2:
            mixed.append((pc[rows_of(1)] * (cos + sin) + ps[rows_of(1)] * (cos - sin), None))
        else:
            hr = pc[rows_of(c)] - ps[rows_of(c + 1)]
            hi = ps[rows_of(c)] + pc[rows_of(c + 1)]
            mixed.append((hr * cos - hi * sin, hi * cos + hr * sin))
    return real_ifft(mixed)


def row_back(spectrum, matrix_ref, twiddle_ref, outer_ref):
    parts = split(spectrum)
    pc, ps = product(parts, table(matrix_ref, 0)), product(parts, table(matrix_ref, 1))
    cos, sin = twiddle_ref[0], twiddle_ref[1]
    return dot(outer_ref[0], pc * cos - ps * sin) + dot(outer_ref[1], ps * cos + pc * sin)


def forward_kernel(groups, field_ref, rest_ref, matrix_ref, twiddle_ref, out_ref, left, right):
    chunks = [field_ref[rows_of(p), :] for p in range(groups)]
    spectrum = transform(chunks, matrix_ref, twiddle_ref, left, right)
    out_ref[...] = spectrum + rest_ref[...]


def blocks_kernel(spec_ref, scale_ref, aligned_ref, scaled_ref, part_ref, down_ref, up_ref):
    count, block = aligned_ref.shape[0], aligned_ref.shape[1]
    half, rows = block // 2, count * block
    scaled = spec_ref[...] * scale_ref[...]
    scaled_ref[...] = scaled
    for b in range(count):
        part_ref[b * block : (b + 1) * block, :] = dot(
            aligned_ref[b], scaled[b * block : (b + 1) * block]
        )
    down_ref[:half, :] = scaled[:half]
    down_ref[half : half + 8, :] = part_ref[:8, :]
    down_ref[half + 8 :, :] = scale_ref[:8, :]
    up_ref[:half, :] = scaled[rows - half :]
    up_ref[half : half + 8, :] = part_ref[rows - 8 :, :]
    up_ref[half + 8 :, :] = scale_ref[rows - 8 :, :]


def combine(
    norm, scaled_ref, part_ref, scale_ref, above_ref, below_ref, stag_ref, stag_below_ref, flags_ref
):
    count, block = stag_ref.shape[0], stag_ref.shape[1]
    half, rows = block // 2, count * block
    before = flags_ref[1:2, :] * dot(
        stag_below_ref[...],
        jnp.concatenate([below_ref[:half, :], scaled_ref[:half, :]], axis=0),
    )
    upper = above_ref[:half, :] * flags_ref[:1, :]
    pieces = [before[half:]]
    for b in range(count - 1):
        pieces.append(dot(stag_ref[b], scaled_ref[half + b * block : half + (b + 1) * block, :]))
    after = dot(
        stag_ref[count - 1],
        jnp.concatenate([scaled_ref[rows - half :, :], upper], axis=0),
    )
    pieces.append(after[:half])
    full = (part_ref[...] + jnp.concatenate(pieces, axis=0)) * (scale_ref[...] * norm)
    return full, before, after


def halo_kernel(
    norm,
    scaled_ref,
    part_ref,
    scale_ref,
    above_ref,
    below_ref,
    stag_ref,
    stag_below_ref,
    flags_ref,
    late_ref,
    out_ref,
    low,
    high,
):
    half = stag_ref.shape[1] // 2
    full, before, after = combine(
        norm,
        scaled_ref,
        part_ref,
        scale_ref,
        above_ref,
        below_ref,
        stag_ref,
        stag_below_ref,
        flags_ref,
    )
    row_below = (before[half - 1 : half] + below_ref[half + 7 : half + 8, :]) * (
        below_ref[half + 15 : half + 16, :] * norm
    )
    row_above = (after[half : half + 1] + above_ref[half : half + 1, :]) * (
        above_ref[half + 8 : half + 9, :] * norm
    )
    out_ref[:, :128] = full[:, :128]
    low[...] = full[:, :128]
    high[...] = full[:, 128:]
    groups = full.shape[0] // ROWS

    def strided(start):
        at = pl.ds(start, groups, stride=ROWS)
        return jnp.concatenate([low[at, :], high[at, :]], axis=1)

    row = lax.broadcasted_iota(jnp.int32, (groups, WIDE), 0)
    up = jnp.where(row == 0, row_below, pltpu.roll(strided(ROWS - 1), 1, 0))
    down = jnp.where(row == groups - 1, row_above, pltpu.roll(strided(0), groups - 1, 0))
    lane = lanes((groups, 128)) + 128
    for s, part in enumerate(
        (
            pltpu.roll(up, HALO, 1),
            pltpu.roll(up, HALO - FOLD, 1),
            pltpu.roll(down, HALO, 1),
            pltpu.roll(down, HALO - FOLD, 1),
        )
    ):
        at = pl.ds(s, groups, stride=ROWS)
        high[at, :] = jnp.where(lane >= HALO, part[:, 128:], high[at, :])
    out_ref[:, 128:WIDE] = jnp.where(
        lanes(high.shape) < LATE - 128, high[...], late_ref[:, :128]
    )
    out_ref[:, WIDE:] = late_ref[:, 128:]


def sums_kernel(
    norm,
    length,
    scaled_ref,
    part_ref,
    scale_ref,
    above_ref,
    below_ref,
    stag_ref,
    stag_below_ref,
    flags_ref,
    spec_ref,
    aside_ref,
    sums_ref,
    out_ref,
):
    full, _, _ = combine(
        norm,
        scaled_ref,
        part_ref,
        scale_ref,
        above_ref,
        below_ref,
        stag_ref,
        stag_below_ref,
        flags_ref,
    )
    lane = lanes(full.shape)
    held = jnp.where(lane < length, full, 0.0)
    own = jnp.sum(held * spec_ref[...], axis=0, keepdims=True)
    own = jnp.sum(own[:, :128] + own[:, 128:], axis=1, keepdims=True) * flags_ref[2:3, :1]
    full = held + aside_ref[...]
    full = jnp.where(lane == SCALARS + 2, own, full)
    out_ref[:, :128] = full[:, :128]
    out_ref[:, 128:] = jnp.where(
        (lane[:, 128:] == SCALARS) | (lane[:, 128:] == SCALARS + 1), sums_ref[:1, :], full[:, 128:]
    )


def gather_kernel(spec_ref, sums_ref):
    riders = jnp.sum(spec_ref[:, 128:], axis=0, keepdims=True) * (1.0 / ROWS)
    sums_ref[...] = jnp.broadcast_to(riders, (8, 128))


def step_kernel(
    groups,
    length,
    spec_ref,
    rhs_ref,
    own_ref,
    next_ref,
    east_ref,
    matrix_ref,
    twiddle_ref,
    outer_ref,
    out_ref,
    first_ref,
    image_ref,
    sums_ref,
    left,
    right,
    low,
    high,
    tail,
):
    lane_row = lanes((groups, WIDE))
    stride = 3 * ROWS
    tail[...] = spec_ref[:, 128:WIDE]

    def halo_row(s):
        blank = jnp.zeros((groups, 128), jnp.float32)
        parts = [
            jnp.concatenate([tail[pl.ds(s + n, groups, stride=ROWS), :], blank], axis=1)
            for n in range(2)
        ]
        row = jnp.where(
            lane_row < FOLD, shifted(parts[0], 128 - HALO), shifted(parts[1], FOLD + 128 - HALO)
        )
        return row_back(row, matrix_ref, twiddle_ref, outer_ref)

    for start, s in ((ROWS - 1, 0), (2 * ROWS, 2)):
        row = halo_row(s)
        low[pl.ds(start, groups, stride=stride), :] = row[:, :128]
        high[pl.ds(start, groups, stride=stride), :] = row[:, 128:]

    def neighbour(start):
        at = slice(start, start + ROWS)
        return jnp.concatenate([low[at, :], high[at, :]], axis=1)

    cells = transform_back(spec_ref[:, :WIDE], groups, matrix_ref, twiddle_ref)
    for p in range(groups):
        v = jnp.where(own_ref[rows_of(p), :] > 0.0, cells[p], 0.0)
        first_ref[rows_of(p), :] = v
        low[stride * p + ROWS : stride * p + 2 * ROWS, :] = v[:, :128]
        high[stride * p + ROWS : stride * p + 2 * ROWS, :] = v[:, 128:]
    lane = lanes((ROWS, WIDE))
    _, count, n_at, s_at, e_at = lane_plan(length)
    rz = jnp.zeros((ROWS, WIDE), jnp.float32)
    curvature = jnp.zeros((ROWS, WIDE), jnp.float32)
    images, fluxes = [], []
    for p in range(groups):
        at = rows_of(p)
        v = first_ref[at, :]
        after = first_ref[rows_of((p + 1) % groups), 0:1]
        east = jnp.where(
            lane < count, east_ref[at, :], shifted(spec_ref[at, WIDE:], count - (e_at - WIDE))
        )
        flux = v - shifted(jnp.where(lane == length, after, v), -1)
        fluxes.append(jnp.where(lane < length, east * next_ref[at, :] * flux, 0.0))
    for p in range(groups):
        at = rows_of(p)
        v = first_ref[at, :]
        before = fluxes[(p - 1) % groups][:, length - 1 : length]
        flux = fluxes[p]
        own = own_ref[at, :]
        base = stride * p + ROWS
        north = shifted(spec_ref[at, 128 : 128 + WIDE], 128 - n_at)
        south = shifted(spec_ref[at, WIDE:], WIDE - s_at)
        image = jnp.where(own > 0.0, own, 1.0) * v
        image = image + (flux - shifted(jnp.where(lane == WIDE - 1, before, flux), 1))
        image = image + north * (v - neighbour(base + 1))
        image = image + south * (v - neighbour(base - 1))
        image = jnp.where(lane < length, image, 0.0)
        image_ref[at, :] = image
        images.append(image)
        rz = rz + rhs_ref[at, :] * v
        curvature = curvature + v * image
    small = lanes((8, 128))
    at = SCALARS - 128
    sums_ref[...] = jnp.where(
        small == at, jnp.sum(rz), jnp.where(small == at + 1, jnp.sum(curvature), 0.0)
    )
    spectrum = transform(images, matrix_ref, twiddle_ref, left, right)
    out_ref[...] = jnp.where(
        lanes(out_ref.shape) < length, spectrum, shifted(first_ref[...], length)
    )


def last_kernel(
    groups,
    length,
    spec_ref,
    own_ref,
    first_ref,
    image_ref,
    matrix_ref,
    twiddle_ref,
    out_ref,
):
    cells = transform_back(spec_ref[...], groups, matrix_ref, twiddle_ref)
    lane = lanes((ROWS, WIDE))
    cut = WIDE - length
    image_cut = SCALARS - length
    image_at = 2 * length - cut
    for p in range(groups):
        at = rows_of(p)
        cell = jnp.where(own_ref[at, :] > 0.0, cells[p], 0.0)
        out = jnp.where(lane < length, cell, shifted(first_ref[at, :], length - cut))
        out_ref[at, :] = jnp.where(
            lane < image_at, out, shifted(image_ref[at, :], image_at - image_cut)
        )


def unpack_kernel(length, count, slab_ref, out_ref):
    turned = slab_ref[:, 128:].T
    out_ref[:count, :] = turned[length - 128 : length - 128 + count]


def unpack_first_kernel(length, count, slab_ref, image_ref, out_ref, aside_ref):
    unpack_kernel(length, count, slab_ref, out_ref)
    lane = lanes(image_ref.shape)
    aside_ref[...] = jnp.where(lane < length, 0.0, shifted(image_ref[...], length))


def finish_kernel(
    length,
    back_ref,
    first_ref,
    image_ref,
    forcing_ref,
    mask_ref,
    three_ref,
    others_ref,
    pair_ref,
    solution_ref,
    residual_ref,
    direction_ref,
):
    at = SCALARS - 128
    totals = three_ref[:1, :] + others_ref[:1, :] + pair_ref[:1, :]
    rz, curvature, own = [totals[:, at + n : at + n + 1] for n in range(3)]
    alpha = rz / curvature
    rz_next = rz - 2.0 * alpha * curvature + alpha * alpha * own
    beta = rz_next / rz
    back = back_ref[...].T
    cut = WIDE - length
    image_cut = SCALARS - length
    image_at = 2 * length - cut
    rhs = mask_ref[...].astype(jnp.float32) * forcing_ref[...]

    def store(where, rows_back, first):
        solution_ref[where, :] = alpha * first
        direction_ref[where, :] = (first - alpha * rows_back) + beta * first

    store(slice(0, cut), back[:cut], first_ref[:cut, :])
    store(slice(cut, length), back[cut:length], back[length:image_at])
    residual_ref[:image_cut, :] = rhs[:image_cut] - alpha * image_ref[:image_cut, :]
    residual_ref[image_cut:, :] = (
        rhs[image_cut:] - alpha * back[image_at : image_at + length - image_cut]
    )


def call(kernel, out_shapes, scratch=(), name=None):
    single = not isinstance(out_shapes, (list, tuple)) or isinstance(out_shapes[0], int)
    shapes = [out_shapes] if single else out_shapes
    outs = [jax.ShapeDtypeStruct(s, jnp.float32) for s in shapes]
    return pl.pallas_call(
        kernel,
        out_shape=outs[0] if single else outs,
        scratch_shapes=[pltpu.VMEM(s, jnp.float32) for s in scratch],
        compiler_params=pltpu.CompilerParams(vmem_limit_bytes=16 * 2**20),
        name=name,
    )


def exchanged(value):
    groups = lax.axis_size(LON)
    parts = value.reshape(groups, ROWS, value.shape[-1])
    return lax.all_to_all(parts, LON, split_axis=0, concat_axis=0, tiled=True).reshape(value.shape)


def from_lat(value, steps):
    count = lax.axis_size("lat")
    return lax.ppermute(value, "lat", [((d + steps) % count, d) for d in range(count)])


def after(value, *others):
    return lax.optimization_barrier((value, *others))[0]


def local(
    surface_forcing,
    ocean_mask,
    self_coupling,
    east_coupling,
    north_coupling,
    zonal_weight,
    aligned_inverse,
    staggered_inverse,
):
    groups = lax.axis_size(LON)
    length, rows = surface_forcing.shape
    norm = 1.0 / (groups * length)
    matrices, twiddle, outer, wave = tables(groups, length)
    channel = lax.axis_index(LON)
    count, block = aligned_inverse.shape[0], aligned_inverse.shape[1]
    half = block // 2
    wide = (rows, WIDE)
    transforms = [wide, wide]

    cells = (length, rows)
    wet_cells = ocean_mask.astype(jnp.float32)
    own_cells = wet_cells * self_coupling
    packed = call(pack_kernel, wide, [wide], name="pack")(wet_cells * surface_forcing, own_cells)
    slab = exchanged(packed)

    mask, east_cells, north_cells, weights, stag = lax.optimization_barrier(
        (ocean_mask, east_coupling, north_coupling, zonal_weight, staggered_inverse, packed)
    )[:-1]
    stag_below = from_lat(stag[count - 1], -1)
    more = call(pack_more_kernel, wide, [wide], name="pack_more")(own_cells, mask, east_cells)
    wet_first, top_last = call(
        edges_kernel, [(ROWS, WIDE)] * 2, [(WIDE, 128)], name="edges"
    )(mask, north_cells)
    scale = lax.rsqrt(1.0 + weights[:, None] * lax.dynamic_slice_in_dim(wave, channel, 1, 0))
    lat = lax.axis_index("lat")
    flag_row = lax.broadcasted_iota(jnp.int32, (8, WIDE), 0)
    north_of, south_of, weight = (
        jnp.where(condition, yes, no).astype(jnp.float32)
        for condition, yes, no in (
            (lat < lax.axis_size("lat") - 1, 1.0, 0.0),
            (lat > 0, 1.0, 0.0),
            (channel < 2, 1.0, 2.0),
        )
    )
    flags = jnp.where(flag_row == 0, north_of, jnp.where(flag_row == 1, south_of, weight))
    slab = after(slab, stag_below, scale, flags, wet_first)
    spectrum = call(lambda *r: forward_kernel(groups, *r), wide, transforms, name="forward")(
        slab, more, matrices, twiddle
    )
    spec_rhs = exchanged(spectrum)

    wet_first, top_last = lax.optimization_barrier((wet_first, top_last, spectrum))[:2]
    late = call(pack_rest_kernel, (rows, WIDE + 128), [(2 * WIDE, rows)], name="pack_rest")(
        mask, east_cells, north_cells, flags, from_lat(wet_first, 1), from_lat(top_last, -1)
    )
    spec_rhs = after(spec_rhs, late)

    edge = (half + 16, WIDE)

    def blocks(spectrum):
        scaled, part, down, up = call(blocks_kernel, [wide, wide, edge, edge], name="blocks")(
            spectrum, scale, aligned_inverse
        )
        above, below = from_lat(down, 1), from_lat(up, -1)
        return scaled, part, scale, above, below, stag, stag_below, flags

    pieces = blocks(spec_rhs)
    flat = call(
        lambda *r: coefficients_kernel(groups, length, *r), [wide] * 3, name="coefficients"
    )(slab, after(spec_rhs, pieces[0]))
    late = after(late, *flat)
    filtered = exchanged(
        call(
            lambda *r: halo_kernel(norm, *r), (rows, 2 * WIDE), [(rows, 128)] * 2, name="halo"
        )(*pieces, late)
    )
    spec, first, image, sums = call(
        lambda *r: step_kernel(groups, length, *r),
        [wide, wide, wide, (8, 128)],
        transforms + [(3 * rows, 128)] * 2 + [(rows, 128)],
        name="step",
    )(filtered, slab, *flat, matrices, twiddle, outer)
    spec_image = exchanged(spec)
    pieces = blocks(spec_image)
    cut, image_cut = WIDE - length, SCALARS - length
    first_cells, aside = call(
        lambda *r: unpack_first_kernel(length, cut, *r), [cells, wide], name="unpack_first"
    )(after(spec_image, pieces[0]), image)
    filtered = exchanged(
        call(lambda *r: sums_kernel(norm, length, *r), wide, name="sums")(
            *pieces, spec_image, aside, sums
        )
    )

    sums = call(gather_kernel, (8, 128), name="gather")(filtered)
    pair = sums + from_lat(sums, -1)
    three = pair + from_lat(sums, 1)
    image_cells = call(
        lambda *r: unpack_kernel(length, image_cut, *r), cells, name="unpack_image"
    )(filtered)
    packed = call(lambda *r: last_kernel(groups, length, *r), wide, name="last")(
        filtered, flat[0], first, image, matrices, twiddle
    )
    packed, three, pair = lax.optimization_barrier((packed, three, pair, image_cells))[:3]
    return tuple(
        call(lambda *r: finish_kernel(length, *r), [cells] * 3, name="finish")(
            exchanged(packed),
            first_cells,
            image_cells,
            surface_forcing,
            ocean_mask,
            three,
            from_lat(three, 3),
            from_lat(pair, -2),
        )
    )


def solution(mesh):
    torus = Mesh(
        mesh.devices.reshape(mesh.shape["lat"], 4, 4, 2), ("lat", "lon_0", "lon_1", "lon_2")
    )
    return jax.shard_map(
        local,
        mesh=torus,
        in_specs=(
            P(LON, "lat"),
            P(LON, "lat"),
            P(LON, "lat"),
            P(LON, "lat"),
            P(LON, "lat"),
            P("lat"),
            P("lat", None, None),
            P("lat", None, None),
        ),
        out_specs=(P(LON, "lat"), P(LON, "lat"), P(LON, "lat")),
        check_vma=False,
    )
```

```python
import jax
import jax.numpy as jnp
import numpy as np
from jax import lax
from jax.experimental import pallas as pl
from jax.experimental.pallas import tpu as pltpu
from jax.sharding import Mesh
from jax.sharding import PartitionSpec as P

LON = ("lon_0", "lon_1", "lon_2")
TURN = 2.0 * np.pi
ROWS = 8
WIDE = 256
HALO = 136
FOLD = 68
LATE = HALO + FOLD
SCALARS = WIDE - 4


def tables(groups, length):
    period = groups * length
    index = np.arange(length)
    inner = TURN * (np.outer(index, index) % length) / length
    wave_of = np.zeros(groups, np.int64)
    wave_of[1] = groups // 2
    for m in range(1, groups // 2):
        wave_of[2 * m] = wave_of[2 * m + 1] = m
    turn = TURN * (np.outer(wave_of, index) % period) / period
    matrices = np.zeros((2, WIDE, WIDE), np.float32)
    matrices[0, :length, :length] = np.cos(inner)
    matrices[1, :length, :length] = np.sin(inner)
    coarse = matrices.astype(jnp.bfloat16)
    rest = (matrices - coarse.astype(np.float32)).astype(jnp.bfloat16)
    twiddle = np.zeros((2, groups, WIDE))
    twiddle[0, :, :length] = np.cos(turn)
    twiddle[1, :, :length] = np.sin(turn)
    chunk = np.arange(groups)
    outer = np.zeros((2, groups, groups))
    for c in range(groups):
        phase = TURN * (chunk * wave_of[c] % groups) / groups
        if c < 2:
            outer[0, :, c] = outer[1, :, c] = np.cos(phase)
        elif c % 2 == 0:
            outer[0, :, c], outer[1, :, c] = 2 * np.cos(phase), -2 * np.sin(phase)
        else:
            outer[0, :, c], outer[1, :, c] = -2 * np.sin(phase), -2 * np.cos(phase)
    modes = wave_of[:, None] + groups * index[None, :]
    wave = np.zeros((groups, WIDE))
    wave[:, :length] = 4.0 * np.sin(np.pi * modes / period) ** 2
    return (
        np.stack([coarse, rest]),
        twiddle.astype(np.float32),
        outer.astype(np.float32),
        wave.astype(np.float32),
    )


def real_fft(values):
    count = len(values)
    if count == 2:
        return [(values[0] + values[1], None), (values[0] - values[1], None)]
    even, odd = real_fft(values[0::2]), real_fft(values[1::2])
    out = [None] * (count // 2 + 1)
    for k in range(count // 4 + 1):
        (er, ei), (re, im) = even[k], odd[k]
        if k == 0:
            out[0], out[count // 2] = (er + re, None), (er - re, None)
        elif k == count // 4:
            out[k] = (er, -re)
        else:
            c, s = float(np.cos(TURN * k / count)), float(-np.sin(TURN * k / count))
            tr, ti = re * c - im * s, im * c + re * s
            out[k], out[count // 2 - k] = (er + tr, ei + ti), (er - tr, ti - ei)
    return out


def real_ifft(spectrum):
    count = 2 * (len(spectrum) - 1)
    if count == 2:
        return [spectrum[0][0] + spectrum[1][0], spectrum[0][0] - spectrum[1][0]]
    even, odd = [], []
    for k in range(count // 4 + 1):
        (ar, ai), (br, bi) = spectrum[k], spectrum[count // 2 - k]
        if k == 0:
            even.append((ar + br, None))
            odd.append((ar - br, None))
        elif k == count // 4:
            even.append((2.0 * ar, None))
            odd.append((-2.0 * ai, None))
        else:
            c, s = float(np.cos(TURN * k / count)), float(np.sin(TURN * k / count))
            dr, di = ar - br, ai + bi
            even.append((ar + br, ai - bi))
            odd.append((dr * c - di * s, dr * s + di * c))
    first, second = real_ifft(even), real_ifft(odd)
    out = []
    for a, b in zip(first, second, strict=True):
        out += [a, b]
    return out


def split(a):
    coarse = a.astype(jnp.bfloat16)
    return coarse, (a - coarse.astype(jnp.float32)).astype(jnp.bfloat16)


def product(a, b):
    (ac, ar), (bc, br) = a, b

    def one(x, y):
        return jnp.dot(x, y, preferred_element_type=jnp.float32)

    return one(ac, bc) + (one(ac, br) + one(ar, bc))


def dot(a, b):
    return product(split(a), split(b))


def table(matrix_ref, n):
    return matrix_ref[0, n], matrix_ref[1, n]


def rows_of(p):
    return slice(ROWS * p, ROWS * (p + 1))


def lanes(shape):
    return lax.broadcasted_iota(jnp.int32, shape, len(shape) - 1)


def sublanes(shape):
    return lax.broadcasted_iota(jnp.int32, shape, len(shape) - 2)


def shifted(value, lanes_right):
    return pltpu.roll(value, lanes_right % value.shape[1], 1)


def pack_kernel(rhs_ref, own_ref, out_ref, tall):
    length = rhs_ref.shape[0]
    tall[:length, :] = rhs_ref[...]
    tall[length:, :] = own_ref[: WIDE - length, :]
    out_ref[...] = tall[...].T


def edges_kernel(mask_ref, north_ref, stag_ref, wet_ref, low_ref, tall):
    length, rows = mask_ref.shape
    count, block = stag_ref.shape[0], stag_ref.shape[1]
    tall[length:, :] = jnp.zeros((WIDE - length, 128), jnp.float32)
    tall[:length, :] = mask_ref[:, :128].astype(jnp.float32)
    wet_ref[...] = tall[...].T[:ROWS]
    tall[:length, :] = mask_ref[:, rows - 128 :].astype(jnp.float32) * north_ref[:, rows - 128 :]
    top = tall[...].T[127:]
    low_ref[:block, :] = stag_ref[count - 1]
    row = sublanes((ROWS, 128))
    low_ref[block:, :] = jnp.where(row == 0, top[:, :128], top[:, 128:])


def lane_plan(length):
    cut = WIDE - length
    count = 2 * cut - length
    north = LATE
    east = north + length
    return cut, count, north, east, east + length - count


def pack_more_kernel(own_ref, mask_ref, east_ref, out_ref, tall):
    length, rows = mask_ref.shape
    cut, count = lane_plan(length)[:2]
    tall[:length, :] = jnp.zeros((length, rows), jnp.float32)
    tall[length : WIDE - count, :] = own_ref[cut:, :]
    tall[WIDE - count :, :] = (mask_ref[...].astype(jnp.float32) * east_ref[...])[:count]
    out_ref[...] = tall[...].T


def pack_rest_kernel(
    mask_ref,
    east_ref,
    north_ref,
    flags_ref,
    wet_above_ref,
    from_below_ref,
    out_ref,
    tall,
    aside,
    low,
    high,
    last,
):
    length, rows = mask_ref.shape
    _, count, n_at, e_at, f_at = lane_plan(length)
    block = from_below_ref.shape[0] - ROWS
    lane = lanes((length, rows))
    wet = mask_ref[...].astype(jnp.float32)
    north = wet * north_ref[...]
    wet_above = wet_above_ref[...].T[:length, :1] * flags_ref[:1, :1]
    top = from_below_ref[block:, :].T
    top_below = jnp.concatenate([top[:, :1], top[: length - 128, 1:2]], axis=0) * flags_ref[1:2, :1]
    tall[128:n_at, :] = jnp.zeros((n_at - 128, rows), jnp.float32)
    tall[n_at:e_at, :] = north * jnp.where(lane == rows - 1, wet_above, shifted(wet, -1))
    tall[e_at:f_at, :] = (wet * east_ref[...])[count:]
    tall[f_at:, :] = jnp.zeros((WIDE + 128 - f_at, rows), jnp.float32)
    out_ref[:, :128] = tall[128:WIDE, :].T
    last[...] = tall[WIDE:, :].T
    aside[length:, :] = jnp.zeros((WIDE - length, rows), jnp.float32)
    aside[:length, :] = wet * jnp.where(lane == 0, top_below, shifted(north, 1))
    low[...] = aside[:128, :].T
    high[...] = aside[128:, :].T
    groups = rows // ROWS
    at = pl.ds(0, groups, stride=ROWS)
    before = jnp.concatenate([low[at, :], high[at, :]], axis=1)
    fold = f_at - WIDE
    lane = lanes((groups, 128))
    for n in range(ROWS):
        at = pl.ds(n, groups, stride=ROWS)
        piece = shifted(before, fold - n * (128 - fold))[:, :128]
        last[at, :] = jnp.where(lane >= fold, piece, last[at, :])
    out_ref[:, 128:] = last[...]


def coefficients_kernel(groups, length, slab_ref, second_ref, own_ref, next_ref, east_ref):
    cut, count = lane_plan(length)[:2]
    lane = lanes((ROWS, WIDE))
    for p in range(groups):
        at = rows_of(p)
        more = second_ref[at, :]
        own_ref[at, :] = jnp.where(
            lane < cut,
            shifted(slab_ref[at, :], -length),
            jnp.where(lane < length, shifted(more, cut - length), 0.0),
        )
        east_ref[at, :] = jnp.where(lane < count, shifted(more, count), 0.0)
    for p in range(groups):
        own = own_ref[rows_of(p), :]
        after = own_ref[rows_of((p + 1) % groups), 0:1]
        ocean = jnp.where(lane == length, after, own) > 0.0
        next_ref[rows_of(p), :] = shifted(ocean.astype(jnp.float32), -1)


def transform(chunks, matrix_ref, twiddle_ref, left, right):
    groups = len(chunks)
    mixed = real_fft(chunks)
    for m in range(groups // 2 + 1):
        re, im = mixed[m]
        if m == 0:
            left[rows_of(0), :] = re
            right[rows_of(0), :] = re
            continue
        c = 1 if m == groups // 2 else 2 * m
        cos, sin = twiddle_ref[0, c : c + 1, :], twiddle_ref[1, c : c + 1, :]
        if m == groups // 2:
            left[rows_of(1), :] = re * (cos + sin)
            right[rows_of(1), :] = re * (cos - sin)
        else:
            tr, ti = re * cos + im * sin, im * cos - re * sin
            left[rows_of(c), :] = tr
            right[rows_of(c), :] = ti
            left[rows_of(c + 1), :] = ti
            right[rows_of(c + 1), :] = -tr
    return product(split(left[...]), table(matrix_ref, 0)) + product(
        split(right[...]), table(matrix_ref, 1)
    )


def transform_back(spectrum, groups, matrix_ref, twiddle_ref):
    parts = split(spectrum)
    pc, ps = product(parts, table(matrix_ref, 0)), product(parts, table(matrix_ref, 1))
    mixed = []
    for m in range(groups // 2 + 1):
        if m == 0:
            mixed.append((pc[rows_of(0)] + ps[rows_of(0)], None))
            continue
        c = 1 if m == groups // 2 else 2 * m
        cos, sin = twiddle_ref[0, c : c + 1, :], twiddle_ref[1, c : c + 1, :]
        if m == groups // 2:
            mixed.append((pc[rows_of(1)] * (cos + sin) + ps[rows_of(1)] * (cos - sin), None))
        else:
            hr = pc[rows_of(c)] - ps[rows_of(c + 1)]
            hi = ps[rows_of(c)] + pc[rows_of(c + 1)]
            mixed.append((hr * cos - hi * sin, hi * cos + hr * sin))
    return real_ifft(mixed)


def row_back(spectrum, matrix_ref, twiddle_ref, outer_ref):
    parts = split(spectrum)
    pc, ps = product(parts, table(matrix_ref, 0)), product(parts, table(matrix_ref, 1))
    cos, sin = twiddle_ref[0], twiddle_ref[1]
    return dot(outer_ref[0], pc * cos - ps * sin) + dot(outer_ref[1], ps * cos + pc * sin)


def forward_kernel(groups, field_ref, rest_ref, matrix_ref, twiddle_ref, out_ref, left, right):
    chunks = [field_ref[rows_of(p), :] for p in range(groups)]
    spectrum = transform(chunks, matrix_ref, twiddle_ref, left, right)
    out_ref[...] = spectrum + rest_ref[...]


def blocks_kernel(spec_ref, scale_ref, aligned_ref, scaled_ref, part_ref, down_ref, up_ref):
    count, block = aligned_ref.shape[0], aligned_ref.shape[1]
    half, rows = block // 2, count * block
    scaled = spec_ref[...] * scale_ref[...]
    scaled_ref[...] = scaled
    for b in range(count):
        part_ref[b * block : (b + 1) * block, :] = dot(
            aligned_ref[b], scaled[b * block : (b + 1) * block]
        )
    down_ref[:half, :] = scaled[:half]
    down_ref[half : half + 8, :] = part_ref[:8, :]
    down_ref[half + 8 :, :] = scale_ref[:8, :]
    up_ref[:half, :] = scaled[rows - half :]
    up_ref[half : half + 8, :] = part_ref[rows - 8 :, :]
    up_ref[half + 8 :, :] = scale_ref[rows - 8 :, :]


def combine(
    norm, scaled_ref, part_ref, scale_ref, above_ref, below_ref, stag_ref, stag_below_ref, flags_ref
):
    count, block = stag_ref.shape[0], stag_ref.shape[1]
    half, rows = block // 2, count * block
    before = flags_ref[1:2, :] * dot(
        stag_below_ref[:block, :],
        jnp.concatenate([below_ref[:half, :], scaled_ref[:half, :]], axis=0),
    )
    upper = above_ref[:half, :] * flags_ref[:1, :]
    pieces = [before[half:]]
    for b in range(count - 1):
        pieces.append(dot(stag_ref[b], scaled_ref[half + b * block : half + (b + 1) * block, :]))
    after = dot(
        stag_ref[count - 1],
        jnp.concatenate([scaled_ref[rows - half :, :], upper], axis=0),
    )
    pieces.append(after[:half])
    full = (part_ref[...] + jnp.concatenate(pieces, axis=0)) * (scale_ref[...] * norm)
    return full, before, after


def halo_kernel(
    norm,
    scaled_ref,
    part_ref,
    scale_ref,
    above_ref,
    below_ref,
    stag_ref,
    stag_below_ref,
    flags_ref,
    late_ref,
    out_ref,
    low,
    high,
):
    half = stag_ref.shape[1] // 2
    full, before, after = combine(
        norm,
        scaled_ref,
        part_ref,
        scale_ref,
        above_ref,
        below_ref,
        stag_ref,
        stag_below_ref,
        flags_ref,
    )
    row_below = (before[half - 1 : half] + below_ref[half + 7 : half + 8, :]) * (
        below_ref[half + 15 : half + 16, :] * norm
    )
    row_above = (after[half : half + 1] + above_ref[half : half + 1, :]) * (
        above_ref[half + 8 : half + 9, :] * norm
    )
    out_ref[:, :128] = full[:, :128]
    low[...] = full[:, :128]
    high[...] = full[:, 128:]
    groups = full.shape[0] // ROWS

    def strided(start):
        at = pl.ds(start, groups, stride=ROWS)
        return jnp.concatenate([low[at, :], high[at, :]], axis=1)

    row = lax.broadcasted_iota(jnp.int32, (groups, WIDE), 0)
    up = jnp.where(row == 0, row_below, pltpu.roll(strided(ROWS - 1), 1, 0))
    down = jnp.where(row == groups - 1, row_above, pltpu.roll(strided(0), groups - 1, 0))
    lane = lanes((groups, 128)) + 128
    for s, part in enumerate(
        (
            pltpu.roll(up, HALO, 1),
            pltpu.roll(up, HALO - FOLD, 1),
            pltpu.roll(down, HALO, 1),
            pltpu.roll(down, HALO - FOLD, 1),
        )
    ):
        at = pl.ds(s, groups, stride=ROWS)
        high[at, :] = jnp.where(lane >= HALO, part[:, 128:], high[at, :])
    out_ref[:, 128:WIDE] = jnp.where(
        lanes(high.shape) < LATE - 128, high[...], late_ref[:, :128]
    )
    out_ref[:, WIDE:] = late_ref[:, 128:]


def sums_kernel(
    norm,
    length,
    scaled_ref,
    part_ref,
    scale_ref,
    above_ref,
    below_ref,
    stag_ref,
    stag_below_ref,
    flags_ref,
    spec_ref,
    aside_ref,
    sums_ref,
    out_ref,
):
    full, _, _ = combine(
        norm,
        scaled_ref,
        part_ref,
        scale_ref,
        above_ref,
        below_ref,
        stag_ref,
        stag_below_ref,
        flags_ref,
    )
    lane = lanes(full.shape)
    held = jnp.where(lane < length, full, 0.0)
    own = jnp.sum(held * spec_ref[...], axis=0, keepdims=True)
    own = jnp.sum(own[:, :128] + own[:, 128:], axis=1, keepdims=True) * flags_ref[2:3, :1]
    full = held + aside_ref[...]
    full = jnp.where(lane == SCALARS + 2, own, full)
    out_ref[:, :128] = full[:, :128]
    out_ref[:, 128:] = jnp.where(
        (lane[:, 128:] == SCALARS) | (lane[:, 128:] == SCALARS + 1), sums_ref[:1, :], full[:, 128:]
    )


def gather_kernel(spec_ref, sums_ref):
    riders = jnp.sum(spec_ref[:, 128:], axis=0, keepdims=True) * (1.0 / ROWS)
    sums_ref[...] = jnp.broadcast_to(riders, (8, 128))


def step_kernel(
    groups,
    length,
    spec_ref,
    rhs_ref,
    own_ref,
    next_ref,
    east_ref,
    matrix_ref,
    twiddle_ref,
    outer_ref,
    out_ref,
    first_ref,
    image_ref,
    sums_ref,
    left,
    right,
    low,
    high,
    tail,
    folded,
):
    lane_row = lanes((groups, WIDE))
    stride = 3 * ROWS
    tail[...] = spec_ref[:, 128:WIDE]

    def halo_row(s):
        blank = jnp.zeros((groups, 128), jnp.float32)
        parts = [
            jnp.concatenate([tail[pl.ds(s + n, groups, stride=ROWS), :], blank], axis=1)
            for n in range(2)
        ]
        row = jnp.where(
            lane_row < FOLD, shifted(parts[0], 128 - HALO), shifted(parts[1], FOLD + 128 - HALO)
        )
        return row_back(row, matrix_ref, twiddle_ref, outer_ref)

    for start, s in ((ROWS - 1, 0), (2 * ROWS, 2)):
        row = halo_row(s)
        low[pl.ds(start, groups, stride=stride), :] = row[:, :128]
        high[pl.ds(start, groups, stride=stride), :] = row[:, 128:]

    def neighbour(start):
        at = slice(start, start + ROWS)
        return jnp.concatenate([low[at, :], high[at, :]], axis=1)

    cells = transform_back(spec_ref[:, :WIDE], groups, matrix_ref, twiddle_ref)
    for p in range(groups):
        v = jnp.where(own_ref[rows_of(p), :] > 0.0, cells[p], 0.0)
        first_ref[rows_of(p), :] = v
        low[stride * p + ROWS : stride * p + 2 * ROWS, :] = v[:, :128]
        high[stride * p + ROWS : stride * p + 2 * ROWS, :] = v[:, 128:]
    lane, row = lanes((ROWS, WIDE)), sublanes((ROWS, WIDE))
    _, count, n_at, e_at, f_at = lane_plan(length)
    tail[...] = spec_ref[:, WIDE:]
    fold, blank = f_at - WIDE, jnp.zeros((groups, 128), jnp.float32)
    width = 128 - fold
    before = jnp.zeros((groups, WIDE), jnp.float32)
    for n in range(ROWS):
        piece = jnp.concatenate([tail[pl.ds(n, groups, stride=ROWS), :], blank], axis=1)
        inside = (lane_row >= n * width) & (lane_row < (n + 1) * width)
        before = jnp.where(inside, shifted(piece, n * width - fold), before)
    folded[...] = before
    rz = jnp.zeros((ROWS, WIDE), jnp.float32)
    curvature = jnp.zeros((ROWS, WIDE), jnp.float32)
    images, fluxes = [], []
    for p in range(groups):
        at = rows_of(p)
        v = first_ref[at, :]
        after = first_ref[rows_of((p + 1) % groups), 0:1]
        east = jnp.where(
            lane < count, east_ref[at, :], shifted(spec_ref[at, 128:], count - (e_at - 128))
        )
        flux = v - shifted(jnp.where(lane == length, after, v), -1)
        fluxes.append(jnp.where(lane < length, east * next_ref[at, :] * flux, 0.0))
    for p in range(groups):
        at = rows_of(p)
        v = first_ref[at, :]
        before = fluxes[(p - 1) % groups][:, length - 1 : length]
        flux = fluxes[p]
        own = own_ref[at, :]
        base = stride * p + ROWS
        north = shifted(spec_ref[at, 128:], 128 - n_at)
        south = jnp.where(row == 0, folded[p : p + 1, :], pltpu.roll(north, 1, 0))
        image = jnp.where(own > 0.0, own, 1.0) * v
        image = image + (flux - shifted(jnp.where(lane == WIDE - 1, before, flux), 1))
        image = image + north * (v - neighbour(base + 1))
        image = image + south * (v - neighbour(base - 1))
        image = jnp.where(lane < length, image, 0.0)
        image_ref[at, :] = image
        images.append(image)
        rz = rz + rhs_ref[at, :] * v
        curvature = curvature + v * image
    small = lanes((8, 128))
    at = SCALARS - 128
    sums_ref[...] = jnp.where(
        small == at, jnp.sum(rz), jnp.where(small == at + 1, jnp.sum(curvature), 0.0)
    )
    spectrum = transform(images, matrix_ref, twiddle_ref, left, right)
    out_ref[...] = jnp.where(
        lanes(out_ref.shape) < length, spectrum, shifted(first_ref[...], length)
    )


def last_kernel(
    groups,
    length,
    spec_ref,
    own_ref,
    first_ref,
    image_ref,
    matrix_ref,
    twiddle_ref,
    out_ref,
):
    cells = transform_back(spec_ref[...], groups, matrix_ref, twiddle_ref)
    lane = lanes((ROWS, WIDE))
    cut = WIDE - length
    image_cut = SCALARS - length
    image_at = 2 * length - cut
    for p in range(groups):
        at = rows_of(p)
        cell = jnp.where(own_ref[at, :] > 0.0, cells[p], 0.0)
        out = jnp.where(lane < length, cell, shifted(first_ref[at, :], length - cut))
        out_ref[at, :] = jnp.where(
            lane < image_at, out, shifted(image_ref[at, :], image_at - image_cut)
        )


def unpack_kernel(length, count, slab_ref, out_ref):
    turned = slab_ref[:, 128:].T
    out_ref[:count, :] = turned[length - 128 : length - 128 + count]


def unpack_first_kernel(length, count, slab_ref, image_ref, out_ref, aside_ref):
    unpack_kernel(length, count, slab_ref, out_ref)
    lane = lanes(image_ref.shape)
    aside_ref[...] = jnp.where(lane < length, 0.0, shifted(image_ref[...], length))


def finish_kernel(
    length,
    back_ref,
    first_ref,
    image_ref,
    forcing_ref,
    mask_ref,
    three_ref,
    others_ref,
    pair_ref,
    solution_ref,
    residual_ref,
    direction_ref,
):
    at = SCALARS - 128
    totals = three_ref[:1, :] + others_ref[:1, :] + pair_ref[:1, :]
    rz, curvature, own = [totals[:, at + n : at + n + 1] for n in range(3)]
    alpha = rz / curvature
    rz_next = rz - 2.0 * alpha * curvature + alpha * alpha * own
    beta = rz_next / rz
    back = back_ref[...].T
    cut = WIDE - length
    image_cut = SCALARS - length
    image_at = 2 * length - cut
    rhs = mask_ref[...].astype(jnp.float32) * forcing_ref[...]

    def store(where, rows_back, first):
        solution_ref[where, :] = alpha * first
        direction_ref[where, :] = (first - alpha * rows_back) + beta * first

    store(slice(0, cut), back[:cut], first_ref[:cut, :])
    store(slice(cut, length), back[cut:length], back[length:image_at])
    residual_ref[:image_cut, :] = rhs[:image_cut] - alpha * image_ref[:image_cut, :]
    residual_ref[image_cut:, :] = (
        rhs[image_cut:] - alpha * back[image_at : image_at + length - image_cut]
    )


def call(kernel, out_shapes, scratch=(), name=None):
    single = not isinstance(out_shapes, (list, tuple)) or isinstance(out_shapes[0], int)
    shapes = [out_shapes] if single else out_shapes
    outs = [jax.ShapeDtypeStruct(s, jnp.float32) for s in shapes]
    return pl.pallas_call(
        kernel,
        out_shape=outs[0] if single else outs,
        scratch_shapes=[pltpu.VMEM(s, jnp.float32) for s in scratch],
        compiler_params=pltpu.CompilerParams(vmem_limit_bytes=16 * 2**20),
        name=name,
    )


def exchanged(value):
    groups = lax.axis_size(LON)
    parts = value.reshape(groups, ROWS, value.shape[-1])
    return lax.all_to_all(parts, LON, split_axis=0, concat_axis=0, tiled=True).reshape(value.shape)


def from_lat(value, steps):
    count = lax.axis_size("lat")
    return lax.ppermute(value, "lat", [((d + steps) % count, d) for d in range(count)])


def after(value, *others):
    return lax.optimization_barrier((value, *others))[0]


def local(
    surface_forcing,
    ocean_mask,
    self_coupling,
    east_coupling,
    north_coupling,
    zonal_weight,
    aligned_inverse,
    staggered_inverse,
):
    groups = lax.axis_size(LON)
    length, rows = surface_forcing.shape
    norm = 1.0 / (groups * length)
    matrices, twiddle, outer, wave = tables(groups, length)
    channel = lax.axis_index(LON)
    count, block = aligned_inverse.shape[0], aligned_inverse.shape[1]
    half = block // 2
    wide = (rows, WIDE)
    transforms = [wide, wide]

    cells = (length, rows)
    wet_cells = ocean_mask.astype(jnp.float32)
    own_cells = wet_cells * self_coupling
    packed = call(pack_kernel, wide, [wide], name="pack")(wet_cells * surface_forcing, own_cells)
    slab = exchanged(packed)

    mask, east_cells, north_cells, weights, stag = lax.optimization_barrier(
        (ocean_mask, east_coupling, north_coupling, zonal_weight, staggered_inverse, packed)
    )[:-1]
    more = call(pack_more_kernel, wide, [wide], name="pack_more")(own_cells, mask, east_cells)
    wet_first, low_last = call(
        edges_kernel, [(ROWS, WIDE), (block + ROWS, 128)], [(WIDE, 128)], name="edges"
    )(mask, north_cells, stag)
    scale = lax.rsqrt(1.0 + weights[:, None] * lax.dynamic_slice_in_dim(wave, channel, 1, 0))
    lat = lax.axis_index("lat")
    flag_row = lax.broadcasted_iota(jnp.int32, (8, WIDE), 0)
    north_of, south_of, weight = (
        jnp.where(condition, yes, no).astype(jnp.float32)
        for condition, yes, no in (
            (lat < lax.axis_size("lat") - 1, 1.0, 0.0),
            (lat > 0, 1.0, 0.0),
            (channel < 2, 1.0, 2.0),
        )
    )
    flags = jnp.where(flag_row == 0, north_of, jnp.where(flag_row == 1, south_of, weight))
    slab = after(slab, scale, flags, wet_first)
    spectrum = call(lambda *r: forward_kernel(groups, *r), wide, transforms, name="forward")(
        slab, more, matrices, twiddle
    )
    spec_rhs = exchanged(spectrum)

    wet_first, low_last = lax.optimization_barrier((wet_first, low_last, spectrum))[:2]
    stag_below = from_lat(low_last, -1)
    late = call(
        pack_rest_kernel,
        wide,
        [(WIDE + 128, rows), wide, (rows, 128), (rows, 128), (rows, 128)],
        name="pack_rest",
    )(mask, east_cells, north_cells, flags, from_lat(wet_first, 1), stag_below)
    spec_rhs = after(spec_rhs, late)

    edge = (half + 16, WIDE)

    def blocks(spectrum):
        scaled, part, down, up = call(blocks_kernel, [wide, wide, edge, edge], name="blocks")(
            spectrum, scale, aligned_inverse
        )
        above, below = from_lat(down, 1), from_lat(up, -1)
        return scaled, part, scale, above, below, stag, stag_below, flags

    pieces = blocks(spec_rhs)
    flat = call(
        lambda *r: coefficients_kernel(groups, length, *r), [wide] * 3, name="coefficients"
    )(slab, after(spec_rhs, pieces[0]))
    late = after(late, *flat)
    filtered = exchanged(
        call(
            lambda *r: halo_kernel(norm, *r), (rows, WIDE + 128), [(rows, 128)] * 2, name="halo"
        )(*pieces, late)
    )
    spec, first, image, sums = call(
        lambda *r: step_kernel(groups, length, *r),
        [wide, wide, wide, (8, 128)],
        transforms + [(3 * rows, 128)] * 2 + [(rows, 128), (groups, WIDE)],
        name="step",
    )(filtered, slab, *flat, matrices, twiddle, outer)
    spec_image = exchanged(spec)
    pieces = blocks(spec_image)
    cut, image_cut = WIDE - length, SCALARS - length
    first_cells, aside = call(
        lambda *r: unpack_first_kernel(length, cut, *r), [cells, wide], name="unpack_first"
    )(after(spec_image, pieces[0]), image)
    filtered = exchanged(
        call(lambda *r: sums_kernel(norm, length, *r), wide, name="sums")(
            *pieces, spec_image, aside, sums
        )
    )

    sums = call(gather_kernel, (8, 128), name="gather")(filtered)
    pair = sums + from_lat(sums, -1)
    three = pair + from_lat(sums, 1)
    image_cells = call(
        lambda *r: unpack_kernel(length, image_cut, *r), cells, name="unpack_image"
    )(filtered)
    packed = call(lambda *r: last_kernel(groups, length, *r), wide, name="last")(
        filtered, flat[0], first, image, matrices, twiddle
    )
    packed, three, pair = lax.optimization_barrier((packed, three, pair, image_cells))[:3]
    return tuple(
        call(lambda *r: finish_kernel(length, *r), [cells] * 3, name="finish")(
            exchanged(packed),
            first_cells,
            image_cells,
            surface_forcing,
            ocean_mask,
            three,
            from_lat(three, 3),
            from_lat(pair, -2),
        )
    )


def solution(mesh):
    torus = Mesh(
        mesh.devices.reshape(mesh.shape["lat"], 4, 4, 2), ("lat", "lon_0", "lon_1", "lon_2")
    )
    return jax.shard_map(
        local,
        mesh=torus,
        in_specs=(
            P(LON, "lat"),
            P(LON, "lat"),
            P(LON, "lat"),
            P(LON, "lat"),
            P(LON, "lat"),
            P("lat"),
            P("lat", None, None),
            P("lat", None, None),
        ),
        out_specs=(P(LON, "lat"), P(LON, "lat"), P(LON, "lat")),
        check_vma=False,
    )
```

```python
import jax
import jax.numpy as jnp
import numpy as np
from jax import lax
from jax.experimental import pallas as pl
from jax.experimental.pallas import tpu as pltpu
from jax.sharding import Mesh
from jax.sharding import PartitionSpec as P

LON = ("lon_0", "lon_1", "lon_2")
TURN = 2.0 * np.pi
ROWS = 8
WIDE = 256
HALO = 136
FOLD = 68
LATE = HALO + FOLD
SCALARS = WIDE - 4


def tables(groups, length):
    period = groups * length
    index = np.arange(length)
    inner = TURN * (np.outer(index, index) % length) / length
    wave_of = np.zeros(groups, np.int64)
    wave_of[1] = groups // 2
    for m in range(1, groups // 2):
        wave_of[2 * m] = wave_of[2 * m + 1] = m
    turn = TURN * (np.outer(wave_of, index) % period) / period
    matrices = np.zeros((2, WIDE, WIDE), np.float32)
    matrices[0, :length, :length] = np.cos(inner)
    matrices[1, :length, :length] = np.sin(inner)
    coarse = matrices.astype(jnp.bfloat16)
    rest = (matrices - coarse.astype(np.float32)).astype(jnp.bfloat16)
    twiddle = np.zeros((2, groups, WIDE))
    twiddle[0, :, :length] = np.cos(turn)
    twiddle[1, :, :length] = np.sin(turn)
    chunk = np.arange(groups)
    outer = np.zeros((2, groups, groups))
    for c in range(groups):
        phase = TURN * (chunk * wave_of[c] % groups) / groups
        if c < 2:
            outer[0, :, c] = outer[1, :, c] = np.cos(phase)
        elif c % 2 == 0:
            outer[0, :, c], outer[1, :, c] = 2 * np.cos(phase), -2 * np.sin(phase)
        else:
            outer[0, :, c], outer[1, :, c] = -2 * np.sin(phase), -2 * np.cos(phase)
    modes = wave_of[:, None] + groups * index[None, :]
    wave = np.zeros((groups, WIDE))
    wave[:, :length] = 4.0 * np.sin(np.pi * modes / period) ** 2
    return (
        np.stack([coarse, rest]),
        twiddle.astype(np.float32),
        outer.astype(np.float32),
        wave.astype(np.float32),
    )


def real_fft(values):
    count = len(values)
    if count == 2:
        return [(values[0] + values[1], None), (values[0] - values[1], None)]
    even, odd = real_fft(values[0::2]), real_fft(values[1::2])
    out = [None] * (count // 2 + 1)
    for k in range(count // 4 + 1):
        (er, ei), (re, im) = even[k], odd[k]
        if k == 0:
            out[0], out[count // 2] = (er + re, None), (er - re, None)
        elif k == count // 4:
            out[k] = (er, -re)
        else:
            c, s = float(np.cos(TURN * k / count)), float(-np.sin(TURN * k / count))
            tr, ti = re * c - im * s, im * c + re * s
            out[k], out[count // 2 - k] = (er + tr, ei + ti), (er - tr, ti - ei)
    return out


def real_ifft(spectrum):
    count = 2 * (len(spectrum) - 1)
    if count == 2:
        return [spectrum[0][0] + spectrum[1][0], spectrum[0][0] - spectrum[1][0]]
    even, odd = [], []
    for k in range(count // 4 + 1):
        (ar, ai), (br, bi) = spectrum[k], spectrum[count // 2 - k]
        if k == 0:
            even.append((ar + br, None))
            odd.append((ar - br, None))
        elif k == count // 4:
            even.append((2.0 * ar, None))
            odd.append((-2.0 * ai, None))
        else:
            c, s = float(np.cos(TURN * k / count)), float(np.sin(TURN * k / count))
            dr, di = ar - br, ai + bi
            even.append((ar + br, ai - bi))
            odd.append((dr * c - di * s, dr * s + di * c))
    first, second = real_ifft(even), real_ifft(odd)
    out = []
    for a, b in zip(first, second, strict=True):
        out += [a, b]
    return out


def split(a):
    coarse = a.astype(jnp.bfloat16)
    return coarse, (a - coarse.astype(jnp.float32)).astype(jnp.bfloat16)


def product(a, b):
    (ac, ar), (bc, br) = a, b

    def one(x, y):
        return jnp.dot(x, y, preferred_element_type=jnp.float32)

    return one(ac, bc) + (one(ac, br) + one(ar, bc))


def dot(a, b):
    return product(split(a), split(b))


def table(matrix_ref, n):
    return matrix_ref[0, n], matrix_ref[1, n]


def rows_of(p):
    return slice(ROWS * p, ROWS * (p + 1))


def lanes(shape):
    return lax.broadcasted_iota(jnp.int32, shape, len(shape) - 1)


def sublanes(shape):
    return lax.broadcasted_iota(jnp.int32, shape, len(shape) - 2)


def shifted(value, lanes_right):
    return pltpu.roll(value, lanes_right % value.shape[1], 1)


def pack_kernel(rhs_ref, own_ref, out_ref, tall):
    length = rhs_ref.shape[0]
    tall[:length, :] = rhs_ref[...]
    tall[length:, :] = own_ref[: WIDE - length, :]
    out_ref[...] = tall[...].T


def edges_kernel(mask_ref, north_ref, stag_ref, wet_ref, low_ref, tall):
    length, rows = mask_ref.shape
    count, block = stag_ref.shape[0], stag_ref.shape[1]
    tall[length:, :] = jnp.zeros((WIDE - length, 128), jnp.float32)
    tall[:length, :] = mask_ref[:, :128].astype(jnp.float32)
    wet_ref[...] = tall[...].T[:ROWS]
    tall[:length, :] = mask_ref[:, rows - 128 :].astype(jnp.float32) * north_ref[:, rows - 128 :]
    top = tall[...].T[127:]
    low_ref[:block, :] = stag_ref[count - 1]
    row = sublanes((ROWS, 128))
    low_ref[block:, :] = jnp.where(row == 0, top[:, :128], top[:, 128:])


def lane_plan(length):
    cut = WIDE - length
    count = 2 * cut - length
    north = LATE
    east = north + length
    return cut, count, north, east, east + length - count


def pack_more_kernel(own_ref, mask_ref, east_ref, out_ref, tall):
    length, rows = mask_ref.shape
    cut, count = lane_plan(length)[:2]
    tall[:length, :] = jnp.zeros((length, rows), jnp.float32)
    tall[length : WIDE - count, :] = own_ref[cut:, :]
    tall[WIDE - count :, :] = (mask_ref[...].astype(jnp.float32) * east_ref[...])[:count]
    out_ref[...] = tall[...].T


def pack_rest_kernel(
    mask_ref,
    east_ref,
    north_ref,
    flags_ref,
    wet_above_ref,
    from_below_ref,
    out_ref,
    tall,
    aside,
    low,
    high,
    last,
):
    length, rows = mask_ref.shape
    _, count, n_at, e_at, f_at = lane_plan(length)
    block = from_below_ref.shape[0] - ROWS
    lane = lanes((length, rows))
    wet = mask_ref[...].astype(jnp.float32)
    north = wet * north_ref[...]
    wet_above = wet_above_ref[...].T[:length, :1] * flags_ref[:1, :1]
    top = from_below_ref[block:, :].T
    top_below = jnp.concatenate([top[:, :1], top[: length - 128, 1:2]], axis=0) * flags_ref[1:2, :1]
    tall[128:n_at, :] = jnp.zeros((n_at - 128, rows), jnp.float32)
    tall[n_at:e_at, :] = north * jnp.where(lane == rows - 1, wet_above, shifted(wet, -1))
    tall[e_at:f_at, :] = (wet * east_ref[...])[count:]
    tall[f_at:, :] = jnp.zeros((WIDE + 128 - f_at, rows), jnp.float32)
    out_ref[:, :128] = tall[128:WIDE, :].T
    last[...] = tall[WIDE:, :].T
    aside[length:, :] = jnp.zeros((WIDE - length, rows), jnp.float32)
    aside[:length, :] = wet * jnp.where(lane == 0, top_below, shifted(north, 1))
    low[...] = aside[:128, :].T
    high[...] = aside[128:, :].T
    groups = rows // ROWS
    at = pl.ds(0, groups, stride=ROWS)
    before = jnp.concatenate([low[at, :], high[at, :]], axis=1)
    fold = f_at - WIDE
    lane = lanes((groups, 128))
    for n in range(ROWS):
        at = pl.ds(n, groups, stride=ROWS)
        piece = shifted(before, fold - n * (128 - fold))[:, :128]
        last[at, :] = jnp.where(lane >= fold, piece, last[at, :])
    out_ref[:, 128:] = last[...]


def coefficients_kernel(groups, length, slab_ref, second_ref, own_ref, next_ref, east_ref):
    cut, count = lane_plan(length)[:2]
    lane = lanes((ROWS, WIDE))
    for p in range(groups):
        at = rows_of(p)
        more = second_ref[at, :]
        own_ref[at, :] = jnp.where(
            lane < cut,
            shifted(slab_ref[at, :], -length),
            jnp.where(lane < length, shifted(more, cut - length), 0.0),
        )
        east_ref[at, :] = jnp.where(lane < count, shifted(more, count), 0.0)
    for p in range(groups):
        own = own_ref[rows_of(p), :]
        after = own_ref[rows_of((p + 1) % groups), 0:1]
        ocean = jnp.where(lane == length, after, own) > 0.0
        next_ref[rows_of(p), :] = shifted(ocean.astype(jnp.float32), -1)


def transform(chunks, matrix_ref, twiddle_ref, left, right):
    groups = len(chunks)
    mixed = real_fft(chunks)
    for m in range(groups // 2 + 1):
        re, im = mixed[m]
        if m == 0:
            left[rows_of(0), :] = re
            right[rows_of(0), :] = re
            continue
        c = 1 if m == groups // 2 else 2 * m
        cos, sin = twiddle_ref[0, c : c + 1, :], twiddle_ref[1, c : c + 1, :]
        if m == groups // 2:
            left[rows_of(1), :] = re * (cos + sin)
            right[rows_of(1), :] = re * (cos - sin)
        else:
            tr, ti = re * cos + im * sin, im * cos - re * sin
            left[rows_of(c), :] = tr
            right[rows_of(c), :] = ti
            left[rows_of(c + 1), :] = ti
            right[rows_of(c + 1), :] = -tr
    return product(split(left[...]), table(matrix_ref, 0)) + product(
        split(right[...]), table(matrix_ref, 1)
    )


def transform_back(spectrum, groups, matrix_ref, twiddle_ref):
    parts = split(spectrum)
    pc, ps = product(parts, table(matrix_ref, 0)), product(parts, table(matrix_ref, 1))
    mixed = []
    for m in range(groups // 2 + 1):
        if m == 0:
            mixed.append((pc[rows_of(0)] + ps[rows_of(0)], None))
            continue
        c = 1 if m == groups // 2 else 2 * m
        cos, sin = twiddle_ref[0, c : c + 1, :], twiddle_ref[1, c : c + 1, :]
        if m == groups // 2:
            mixed.append((pc[rows_of(1)] * (cos + sin) + ps[rows_of(1)] * (cos - sin), None))
        else:
            hr = pc[rows_of(c)] - ps[rows_of(c + 1)]
            hi = ps[rows_of(c)] + pc[rows_of(c + 1)]
            mixed.append((hr * cos - hi * sin, hi * cos + hr * sin))
    return real_ifft(mixed)


def row_back(spectrum, matrix_ref, twiddle_ref, outer_ref):
    parts = split(spectrum)
    pc, ps = product(parts, table(matrix_ref, 0)), product(parts, table(matrix_ref, 1))
    cos, sin = twiddle_ref[0], twiddle_ref[1]
    return dot(outer_ref[0], pc * cos - ps * sin) + dot(outer_ref[1], ps * cos + pc * sin)


def forward_kernel(groups, field_ref, rest_ref, matrix_ref, twiddle_ref, out_ref, left, right):
    chunks = [field_ref[rows_of(p), :] for p in range(groups)]
    spectrum = transform(chunks, matrix_ref, twiddle_ref, left, right)
    out_ref[...] = spectrum + rest_ref[...]


def blocks_kernel(spec_ref, scale_ref, aligned_ref, scaled_ref, part_ref, down_ref, up_ref):
    count, block = aligned_ref.shape[0], aligned_ref.shape[1]
    half, rows = block // 2, count * block
    scaled = spec_ref[...] * scale_ref[...]
    scaled_ref[...] = scaled
    for b in range(count):
        part_ref[b * block : (b + 1) * block, :] = dot(
            aligned_ref[b], scaled[b * block : (b + 1) * block]
        )
    down_ref[:half, :] = scaled[:half]
    down_ref[half : half + 8, :] = part_ref[:8, :]
    down_ref[half + 8 :, :] = scale_ref[:8, :]
    up_ref[:half, :] = scaled[rows - half :]
    up_ref[half : half + 8, :] = part_ref[rows - 8 :, :]
    up_ref[half + 8 :, :] = scale_ref[rows - 8 :, :]


def combine(
    norm, scaled_ref, part_ref, scale_ref, above_ref, below_ref, stag_ref, stag_below_ref, flags_ref
):
    count, block = stag_ref.shape[0], stag_ref.shape[1]
    half, rows = block // 2, count * block
    before = flags_ref[1:2, :] * dot(
        stag_below_ref[:block, :],
        jnp.concatenate([below_ref[:half, :], scaled_ref[:half, :]], axis=0),
    )
    upper = above_ref[:half, :] * flags_ref[:1, :]
    pieces = [before[half:]]
    for b in range(count - 1):
        pieces.append(dot(stag_ref[b], scaled_ref[half + b * block : half + (b + 1) * block, :]))
    after = dot(
        stag_ref[count - 1],
        jnp.concatenate([scaled_ref[rows - half :, :], upper], axis=0),
    )
    pieces.append(after[:half])
    full = (part_ref[...] + jnp.concatenate(pieces, axis=0)) * (scale_ref[...] * norm)
    return full, before, after


def halo_kernel(
    norm,
    scaled_ref,
    part_ref,
    scale_ref,
    above_ref,
    below_ref,
    stag_ref,
    stag_below_ref,
    flags_ref,
    late_ref,
    out_ref,
    low,
    high,
):
    half = stag_ref.shape[1] // 2
    full, before, after = combine(
        norm,
        scaled_ref,
        part_ref,
        scale_ref,
        above_ref,
        below_ref,
        stag_ref,
        stag_below_ref,
        flags_ref,
    )
    row_below = (before[half - 1 : half] + below_ref[half + 7 : half + 8, :]) * (
        below_ref[half + 15 : half + 16, :] * norm
    )
    row_above = (after[half : half + 1] + above_ref[half : half + 1, :]) * (
        above_ref[half + 8 : half + 9, :] * norm
    )
    out_ref[:, :128] = full[:, :128]
    low[...] = full[:, :128]
    high[...] = full[:, 128:]
    groups = full.shape[0] // ROWS

    def strided(start):
        at = pl.ds(start, groups, stride=ROWS)
        return jnp.concatenate([low[at, :], high[at, :]], axis=1)

    row = lax.broadcasted_iota(jnp.int32, (groups, WIDE), 0)
    up = jnp.where(row == 0, row_below, pltpu.roll(strided(ROWS - 1), 1, 0))
    down = jnp.where(row == groups - 1, row_above, pltpu.roll(strided(0), groups - 1, 0))
    lane = lanes((groups, 128)) + 128
    for s, part in enumerate(
        (
            pltpu.roll(up, HALO, 1),
            pltpu.roll(up, HALO - FOLD, 1),
            pltpu.roll(down, HALO, 1),
            pltpu.roll(down, HALO - FOLD, 1),
        )
    ):
        at = pl.ds(s, groups, stride=ROWS)
        high[at, :] = jnp.where(lane >= HALO, part[:, 128:], high[at, :])
    out_ref[:, 128:WIDE] = jnp.where(
        lanes(high.shape) < LATE - 128, high[...], late_ref[:, :128]
    )
    out_ref[:, WIDE:] = late_ref[:, 128:]


def sums_kernel(
    norm,
    length,
    spec_ref,
    scale_ref,
    aligned_ref,
    stag_ref,
    stag_below_ref,
    flags_ref,
    sums_ref,
    scaled_ref,
    part_ref,
    down_ref,
    up_ref,
    own_ref,
):
    count, block = aligned_ref.shape[0], aligned_ref.shape[1]
    half, rows = block // 2, count * block
    scaled = spec_ref[...] * scale_ref[...]
    scaled_ref[...] = scaled
    for b in range(count):
        at = slice(b * block, (b + 1) * block)
        part_ref[at, :] = dot(aligned_ref[b], scaled[at])
    for b in range(count - 1):
        at = slice(half + b * block, half + (b + 1) * block)
        part_ref[at, :] = part_ref[at, :] + dot(stag_ref[b], scaled[at])
    first, last = slice(0, half), slice(rows - half, rows)
    part_ref[first, :] = part_ref[first, :] + flags_ref[1:2, :] * dot(
        stag_below_ref[half:block, half:], scaled[first]
    )
    part_ref[last, :] = part_ref[last, :] + dot(stag_ref[count - 1, :half, :half], scaled[last])
    total = total_of(scaled * part_ref[...], length) * (flags_ref[2:3, :1] * norm)
    small = lanes((8, 128))
    own = jnp.where(small == SCALARS - 128 + 2, total, sums_ref[...])
    own_ref[...] = own
    down_ref[:half, :] = scaled[first]
    up_ref[:half, :] = scaled[last]
    for ref in (down_ref, up_ref):
        ref[half:, :128] = own
        ref[half:, 128:] = own


def total_of(value, length):
    columns = jnp.sum(value, axis=0, keepdims=True)
    columns = jnp.where(lanes(columns.shape) < length, columns, 0.0)
    return jnp.sum(columns[:, :128] + columns[:, 128:], axis=1, keepdims=True)


def ends_kernel(
    norm,
    length,
    scaled_ref,
    part_ref,
    scale_ref,
    above_ref,
    below_ref,
    stag_ref,
    stag_below_ref,
    flags_ref,
    aside_ref,
    own_ref,
    out_ref,
):
    count, block = stag_ref.shape[0], stag_ref.shape[1]
    half, rows = block // 2, count * block
    first, last = slice(0, half), slice(rows - half, rows)
    low = dot(stag_below_ref[half:block, :half], below_ref[:half, :]) * flags_ref[1:2, :]
    high = dot(stag_ref[count - 1, :half, half:], above_ref[:half, :]) * flags_ref[:1, :]
    both = total_of(low * scaled_ref[first, :] + high * scaled_ref[last, :], length)
    both = both * (flags_ref[2:3, :1] * (2.0 * norm))
    pair = own_ref[:1, :] + below_ref[half : half + 1, 128:]
    pair = jnp.where(lanes(pair.shape) == SCALARS - 128 + 2, pair + both, pair)
    middle = slice(half, rows - half)
    for at, more in ((first, low), (middle, None), (last, high)):
        full = part_ref[at, :] if more is None else part_ref[at, :] + more
        full = full * (scale_ref[at, :] * norm)
        full = jnp.where(lanes(full.shape) < length, full, aside_ref[at, :])
        out_ref[at, :128] = full[:, :128]
        inside = lanes((full.shape[0], 128)) < SCALARS - 128
        out_ref[at, 128:] = jnp.where(inside, full[:, 128:], pair)


def gather_kernel(spec_ref, sums_ref):
    riders = jnp.sum(spec_ref[:, 128:], axis=0, keepdims=True) * (1.0 / ROWS)
    sums_ref[...] = jnp.broadcast_to(riders, (8, 128))


def step_kernel(
    groups,
    length,
    spec_ref,
    rhs_ref,
    own_ref,
    next_ref,
    east_ref,
    matrix_ref,
    twiddle_ref,
    outer_ref,
    out_ref,
    first_ref,
    image_ref,
    sums_ref,
    left,
    right,
    low,
    high,
    tail,
    folded,
):
    lane_row = lanes((groups, WIDE))
    stride = 3 * ROWS
    tail[...] = spec_ref[:, 128:WIDE]

    def halo_row(s):
        blank = jnp.zeros((groups, 128), jnp.float32)
        parts = [
            jnp.concatenate([tail[pl.ds(s + n, groups, stride=ROWS), :], blank], axis=1)
            for n in range(2)
        ]
        row = jnp.where(
            lane_row < FOLD, shifted(parts[0], 128 - HALO), shifted(parts[1], FOLD + 128 - HALO)
        )
        return row_back(row, matrix_ref, twiddle_ref, outer_ref)

    for start, s in ((ROWS - 1, 0), (2 * ROWS, 2)):
        row = halo_row(s)
        low[pl.ds(start, groups, stride=stride), :] = row[:, :128]
        high[pl.ds(start, groups, stride=stride), :] = row[:, 128:]

    def neighbour(start):
        at = slice(start, start + ROWS)
        return jnp.concatenate([low[at, :], high[at, :]], axis=1)

    cells = transform_back(spec_ref[:, :WIDE], groups, matrix_ref, twiddle_ref)
    for p in range(groups):
        v = jnp.where(own_ref[rows_of(p), :] > 0.0, cells[p], 0.0)
        first_ref[rows_of(p), :] = v
        low[stride * p + ROWS : stride * p + 2 * ROWS, :] = v[:, :128]
        high[stride * p + ROWS : stride * p + 2 * ROWS, :] = v[:, 128:]
    lane, row = lanes((ROWS, WIDE)), sublanes((ROWS, WIDE))
    _, count, n_at, e_at, f_at = lane_plan(length)
    tail[...] = spec_ref[:, WIDE:]
    fold, blank = f_at - WIDE, jnp.zeros((groups, 128), jnp.float32)
    width = 128 - fold
    before = jnp.zeros((groups, WIDE), jnp.float32)
    for n in range(ROWS):
        piece = jnp.concatenate([tail[pl.ds(n, groups, stride=ROWS), :], blank], axis=1)
        inside = (lane_row >= n * width) & (lane_row < (n + 1) * width)
        before = jnp.where(inside, shifted(piece, n * width - fold), before)
    folded[...] = before
    rz = jnp.zeros((ROWS, WIDE), jnp.float32)
    curvature = jnp.zeros((ROWS, WIDE), jnp.float32)
    images, fluxes = [], []
    for p in range(groups):
        at = rows_of(p)
        v = first_ref[at, :]
        after = first_ref[rows_of((p + 1) % groups), 0:1]
        east = jnp.where(
            lane < count, east_ref[at, :], shifted(spec_ref[at, 128:], count - (e_at - 128))
        )
        flux = v - shifted(jnp.where(lane == length, after, v), -1)
        fluxes.append(jnp.where(lane < length, east * next_ref[at, :] * flux, 0.0))
    for p in range(groups):
        at = rows_of(p)
        v = first_ref[at, :]
        before = fluxes[(p - 1) % groups][:, length - 1 : length]
        flux = fluxes[p]
        own = own_ref[at, :]
        base = stride * p + ROWS
        north = shifted(spec_ref[at, 128:], 128 - n_at)
        south = jnp.where(row == 0, folded[p : p + 1, :], pltpu.roll(north, 1, 0))
        image = jnp.where(own > 0.0, own, 1.0) * v
        image = image + (flux - shifted(jnp.where(lane == WIDE - 1, before, flux), 1))
        image = image + north * (v - neighbour(base + 1))
        image = image + south * (v - neighbour(base - 1))
        image = jnp.where(lane < length, image, 0.0)
        image_ref[at, :] = image
        images.append(image)
        rz = rz + rhs_ref[at, :] * v
        curvature = curvature + v * image
    small = lanes((8, 128))
    at = SCALARS - 128
    sums_ref[...] = jnp.where(
        small == at, jnp.sum(rz), jnp.where(small == at + 1, jnp.sum(curvature), 0.0)
    )
    spectrum = transform(images, matrix_ref, twiddle_ref, left, right)
    out_ref[...] = jnp.where(
        lanes(out_ref.shape) < length, spectrum, shifted(first_ref[...], length)
    )


def last_kernel(
    groups,
    length,
    spec_ref,
    own_ref,
    first_ref,
    image_ref,
    matrix_ref,
    twiddle_ref,
    out_ref,
):
    cells = transform_back(spec_ref[...], groups, matrix_ref, twiddle_ref)
    lane = lanes((ROWS, WIDE))
    cut = WIDE - length
    image_cut = SCALARS - length
    image_at = 2 * length - cut
    for p in range(groups):
        at = rows_of(p)
        cell = jnp.where(own_ref[at, :] > 0.0, cells[p], 0.0)
        out = jnp.where(lane < length, cell, shifted(first_ref[at, :], length - cut))
        out_ref[at, :] = jnp.where(
            lane < image_at, out, shifted(image_ref[at, :], image_at - image_cut)
        )


def unpack_kernel(length, count, slab_ref, out_ref):
    turned = slab_ref[:, 128:].T
    out_ref[:count, :] = turned[length - 128 : length - 128 + count]


def unpack_first_kernel(length, count, slab_ref, image_ref, out_ref, aside_ref):
    unpack_kernel(length, count, slab_ref, out_ref)
    lane = lanes(image_ref.shape)
    aside_ref[...] = jnp.where(lane < length, 0.0, shifted(image_ref[...], length))


def finish_kernel(
    length,
    back_ref,
    first_ref,
    image_ref,
    forcing_ref,
    mask_ref,
    pair_ref,
    ahead_ref,
    behind_ref,
    across_ref,
    solution_ref,
    residual_ref,
    direction_ref,
):
    at = SCALARS - 128
    totals = (pair_ref[:1, :] + across_ref[:1, :]) + (ahead_ref[:1, :] + behind_ref[:1, :])
    rz, curvature, own = [totals[:, at + n : at + n + 1] for n in range(3)]
    alpha = rz / curvature
    rz_next = rz - 2.0 * alpha * curvature + alpha * alpha * own
    beta = rz_next / rz
    back = back_ref[...].T
    cut = WIDE - length
    image_cut = SCALARS - length
    image_at = 2 * length - cut
    rhs = mask_ref[...].astype(jnp.float32) * forcing_ref[...]

    def store(where, rows_back, first):
        solution_ref[where, :] = alpha * first
        direction_ref[where, :] = (first - alpha * rows_back) + beta * first

    store(slice(0, cut), back[:cut], first_ref[:cut, :])
    store(slice(cut, length), back[cut:length], back[length:image_at])
    residual_ref[:image_cut, :] = rhs[:image_cut] - alpha * image_ref[:image_cut, :]
    residual_ref[image_cut:, :] = (
        rhs[image_cut:] - alpha * back[image_at : image_at + length - image_cut]
    )


def call(kernel, out_shapes, scratch=(), name=None):
    single = not isinstance(out_shapes, (list, tuple)) or isinstance(out_shapes[0], int)
    shapes = [out_shapes] if single else out_shapes
    outs = [jax.ShapeDtypeStruct(s, jnp.float32) for s in shapes]
    return pl.pallas_call(
        kernel,
        out_shape=outs[0] if single else outs,
        scratch_shapes=[pltpu.VMEM(s, jnp.float32) for s in scratch],
        compiler_params=pltpu.CompilerParams(vmem_limit_bytes=16 * 2**20),
        name=name,
    )


def exchanged(value):
    groups = lax.axis_size(LON)
    parts = value.reshape(groups, ROWS, value.shape[-1])
    return lax.all_to_all(parts, LON, split_axis=0, concat_axis=0, tiled=True).reshape(value.shape)


def from_lat(value, steps):
    count = lax.axis_size("lat")
    return lax.ppermute(value, "lat", [((d + steps) % count, d) for d in range(count)])


def after(value, *others):
    return lax.optimization_barrier((value, *others))[0]


def local(
    surface_forcing,
    ocean_mask,
    self_coupling,
    east_coupling,
    north_coupling,
    zonal_weight,
    aligned_inverse,
    staggered_inverse,
):
    groups = lax.axis_size(LON)
    length, rows = surface_forcing.shape
    norm = 1.0 / (groups * length)
    matrices, twiddle, outer, wave = tables(groups, length)
    channel = lax.axis_index(LON)
    count, block = aligned_inverse.shape[0], aligned_inverse.shape[1]
    half = block // 2
    wide = (rows, WIDE)
    transforms = [wide, wide]

    cells = (length, rows)
    wet_cells = ocean_mask.astype(jnp.float32)
    own_cells = wet_cells * self_coupling
    packed = call(pack_kernel, wide, [wide], name="pack")(wet_cells * surface_forcing, own_cells)
    slab = exchanged(packed)

    mask, east_cells, north_cells, weights, stag = lax.optimization_barrier(
        (ocean_mask, east_coupling, north_coupling, zonal_weight, staggered_inverse, packed)
    )[:-1]
    more = call(pack_more_kernel, wide, [wide], name="pack_more")(own_cells, mask, east_cells)
    wet_first, low_last = call(
        edges_kernel, [(ROWS, WIDE), (block + ROWS, 128)], [(WIDE, 128)], name="edges"
    )(mask, north_cells, stag)
    scale = lax.rsqrt(1.0 + weights[:, None] * lax.dynamic_slice_in_dim(wave, channel, 1, 0))
    lat = lax.axis_index("lat")
    flag_row = lax.broadcasted_iota(jnp.int32, (8, WIDE), 0)
    north_of, south_of, weight = (
        jnp.where(condition, yes, no).astype(jnp.float32)
        for condition, yes, no in (
            (lat < lax.axis_size("lat") - 1, 1.0, 0.0),
            (lat > 0, 1.0, 0.0),
            (channel < 2, 1.0, 2.0),
        )
    )
    flags = jnp.where(flag_row == 0, north_of, jnp.where(flag_row == 1, south_of, weight))
    slab = after(slab, scale, flags, wet_first)
    spectrum = call(lambda *r: forward_kernel(groups, *r), wide, transforms, name="forward")(
        slab, more, matrices, twiddle
    )
    spec_rhs = exchanged(spectrum)

    wet_first, low_last = lax.optimization_barrier((wet_first, low_last, spectrum))[:2]
    stag_below = from_lat(low_last, -1)
    late = call(
        pack_rest_kernel,
        wide,
        [(WIDE + 128, rows), wide, (rows, 128), (rows, 128), (rows, 128)],
        name="pack_rest",
    )(mask, east_cells, north_cells, flags, from_lat(wet_first, 1), stag_below)
    spec_rhs = after(spec_rhs, late)

    edge = (half + 16, WIDE)

    def blocks(spectrum):
        scaled, part, down, up = call(blocks_kernel, [wide, wide, edge, edge], name="blocks")(
            spectrum, scale, aligned_inverse
        )
        above, below = from_lat(down, 1), from_lat(up, -1)
        return scaled, part, scale, above, below, stag, stag_below, flags

    pieces = blocks(spec_rhs)
    flat = call(
        lambda *r: coefficients_kernel(groups, length, *r), [wide] * 3, name="coefficients"
    )(slab, after(spec_rhs, pieces[0]))
    late = after(late, *flat)
    filtered = exchanged(
        call(
            lambda *r: halo_kernel(norm, *r), (rows, WIDE + 128), [(rows, 128)] * 2, name="halo"
        )(*pieces, late)
    )
    spec, first, image, sums = call(
        lambda *r: step_kernel(groups, length, *r),
        [wide, wide, wide, (8, 128)],
        transforms + [(3 * rows, 128)] * 2 + [(rows, 128), (groups, WIDE)],
        name="step",
    )(filtered, slab, *flat, matrices, twiddle, outer)
    spec_image = exchanged(spec)
    edge = (half + ROWS, WIDE)
    scaled, part, down, up, own = call(
        lambda *r: sums_kernel(norm, length, *r), [wide, wide, edge, edge, (8, 128)], name="sums"
    )(spec_image, scale, aligned_inverse, stag, stag_below, flags, sums)
    above, below = from_lat(down, 1), from_lat(up, -1)
    cut, image_cut = WIDE - length, SCALARS - length
    first_cells, aside = call(
        lambda *r: unpack_first_kernel(length, cut, *r), [cells, wide], name="unpack_first"
    )(after(spec_image, scaled), image)
    filtered = exchanged(
        call(lambda *r: ends_kernel(norm, length, *r), wide, name="ends")(
            scaled, part, scale, above, below, stag, stag_below, flags, aside, own
        )
    )

    pair = call(gather_kernel, (8, 128), name="gather")(filtered)
    image_cells = call(
        lambda *r: unpack_kernel(length, image_cut, *r), cells, name="unpack_image"
    )(filtered)
    packed = call(lambda *r: last_kernel(groups, length, *r), wide, name="last")(
        filtered, flat[0], first, image, matrices, twiddle
    )
    return tuple(
        call(lambda *r: finish_kernel(length, *r), [cells] * 3, name="finish")(
            exchanged(packed),
            first_cells,
            image_cells,
            surface_forcing,
            ocean_mask,
            pair,
            from_lat(pair, 2),
            from_lat(pair, -2),
            from_lat(pair, 4),
        )
    )


def solution(mesh):
    torus = Mesh(
        mesh.devices.reshape(mesh.shape["lat"], 4, 4, 2), ("lat", "lon_0", "lon_1", "lon_2")
    )
    return jax.shard_map(
        local,
        mesh=torus,
        in_specs=(
            P(LON, "lat"),
            P(LON, "lat"),
            P(LON, "lat"),
            P(LON, "lat"),
            P(LON, "lat"),
            P("lat"),
            P("lat", None, None),
            P("lat", None, None),
        ),
        out_specs=(P(LON, "lat"), P(LON, "lat"), P(LON, "lat")),
        check_vma=False,
    )
```

```python
import jax
import jax.numpy as jnp
import numpy as np
from jax import lax
from jax.experimental import pallas as pl
from jax.experimental.pallas import tpu as pltpu
from jax.sharding import Mesh
from jax.sharding import PartitionSpec as P

LON = ("lon_0", "lon_1", "lon_2")
TURN = 2.0 * np.pi
ROWS = 8
WIDE = 256
HALO = 136
FOLD = 68
LATE = HALO + FOLD
SCALARS = WIDE - 4


def tables(groups, length):
    period = groups * length
    index = np.arange(length)
    inner = TURN * (np.outer(index, index) % length) / length
    wave_of = np.zeros(groups, np.int64)
    wave_of[1] = groups // 2
    for m in range(1, groups // 2):
        wave_of[2 * m] = wave_of[2 * m + 1] = m
    turn = TURN * (np.outer(wave_of, index) % period) / period
    matrices = np.zeros((2, WIDE, WIDE), np.float32)
    matrices[0, :length, :length] = np.cos(inner)
    matrices[1, :length, :length] = np.sin(inner)
    coarse = matrices.astype(jnp.bfloat16)
    rest = (matrices - coarse.astype(np.float32)).astype(jnp.bfloat16)
    twiddle = np.zeros((2, groups, WIDE))
    twiddle[0, :, :length] = np.cos(turn)
    twiddle[1, :, :length] = np.sin(turn)
    chunk = np.arange(groups)
    outer = np.zeros((2, groups, groups))
    for c in range(groups):
        phase = TURN * (chunk * wave_of[c] % groups) / groups
        if c < 2:
            outer[0, :, c] = outer[1, :, c] = np.cos(phase)
        elif c % 2 == 0:
            outer[0, :, c], outer[1, :, c] = 2 * np.cos(phase), -2 * np.sin(phase)
        else:
            outer[0, :, c], outer[1, :, c] = -2 * np.sin(phase), -2 * np.cos(phase)
    modes = wave_of[:, None] + groups * index[None, :]
    wave = np.zeros((groups, WIDE))
    wave[:, :length] = 4.0 * np.sin(np.pi * modes / period) ** 2
    return (
        np.stack([coarse, rest]),
        twiddle.astype(np.float32),
        np.concatenate([outer[0], outer[1]], axis=1).astype(np.float32),
        wave.astype(np.float32),
    )


def real_fft(values):
    count = len(values)
    if count == 2:
        return [(values[0] + values[1], None), (values[0] - values[1], None)]
    even, odd = real_fft(values[0::2]), real_fft(values[1::2])
    out = [None] * (count // 2 + 1)
    for k in range(count // 4 + 1):
        (er, ei), (re, im) = even[k], odd[k]
        if k == 0:
            out[0], out[count // 2] = (er + re, None), (er - re, None)
        elif k == count // 4:
            out[k] = (er, -re)
        else:
            c, s = float(np.cos(TURN * k / count)), float(-np.sin(TURN * k / count))
            tr, ti = re * c - im * s, im * c + re * s
            out[k], out[count // 2 - k] = (er + tr, ei + ti), (er - tr, ti - ei)
    return out


def real_ifft(spectrum):
    count = 2 * (len(spectrum) - 1)
    if count == 2:
        return [spectrum[0][0] + spectrum[1][0], spectrum[0][0] - spectrum[1][0]]
    even, odd = [], []
    for k in range(count // 4 + 1):
        (ar, ai), (br, bi) = spectrum[k], spectrum[count // 2 - k]
        if k == 0:
            even.append((ar + br, None))
            odd.append((ar - br, None))
        elif k == count // 4:
            even.append((2.0 * ar, None))
            odd.append((-2.0 * ai, None))
        else:
            c, s = float(np.cos(TURN * k / count)), float(np.sin(TURN * k / count))
            dr, di = ar - br, ai + bi
            even.append((ar + br, ai - bi))
            odd.append((dr * c - di * s, dr * s + di * c))
    first, second = real_ifft(even), real_ifft(odd)
    out = []
    for a, b in zip(first, second, strict=True):
        out += [a, b]
    return out


def split(a):
    coarse = a.astype(jnp.bfloat16)
    return coarse, (a - coarse.astype(jnp.float32)).astype(jnp.bfloat16)


def product(a, b):
    (ac, ar), (bc, br) = a, b

    def one(x, y):
        return jnp.dot(x, y, preferred_element_type=jnp.float32)

    return one(ac, bc) + (one(ac, br) + one(ar, bc))


def dot(a, b):
    return product(split(a), split(b))


def table(matrix_ref, n):
    return matrix_ref[0, n], matrix_ref[1, n]


def rows_of(p):
    return slice(ROWS * p, ROWS * (p + 1))


def lanes(shape):
    return lax.broadcasted_iota(jnp.int32, shape, len(shape) - 1)


def sublanes(shape):
    return lax.broadcasted_iota(jnp.int32, shape, len(shape) - 2)


def shifted(value, lanes_right):
    return pltpu.roll(value, lanes_right % value.shape[1], 1)


def pack_kernel(rhs_ref, own_ref, out_ref, tall):
    length = rhs_ref.shape[0]
    tall[:length, :] = rhs_ref[...]
    tall[length:, :] = own_ref[: WIDE - length, :]
    out_ref[...] = tall[...].T


def edges_kernel(mask_ref, north_ref, stag_ref, wet_ref, low_ref, tall):
    length, rows = mask_ref.shape
    count, block = stag_ref.shape[0], stag_ref.shape[1]
    tall[length:, :] = jnp.zeros((WIDE - length, 128), jnp.float32)
    tall[:length, :] = mask_ref[:, :128].astype(jnp.float32)
    wet_ref[...] = tall[...].T[:ROWS]
    tall[:length, :] = mask_ref[:, rows - 128 :].astype(jnp.float32) * north_ref[:, rows - 128 :]
    top = tall[...].T[127:]
    low_ref[:block, :] = stag_ref[count - 1]
    row = sublanes((ROWS, 128))
    low_ref[block:, :] = jnp.where(row == 0, top[:, :128], top[:, 128:])


def lane_plan(length):
    cut = WIDE - length
    count = 2 * cut - length
    north = LATE
    east = north + length
    return cut, count, north, east, east + length - count


def pack_more_kernel(own_ref, mask_ref, east_ref, out_ref, tall):
    length, rows = mask_ref.shape
    cut, count = lane_plan(length)[:2]
    tall[:length, :] = jnp.zeros((length, rows), jnp.float32)
    tall[length : WIDE - count, :] = own_ref[cut:, :]
    tall[WIDE - count :, :] = (mask_ref[...].astype(jnp.float32) * east_ref[...])[:count]
    out_ref[...] = tall[...].T


def pack_rest_kernel(
    mask_ref,
    east_ref,
    north_ref,
    flags_ref,
    wet_above_ref,
    from_below_ref,
    out_ref,
    tall,
    aside,
    low,
    high,
    last,
):
    length, rows = mask_ref.shape
    _, count, n_at, e_at, f_at = lane_plan(length)
    block = from_below_ref.shape[0] - ROWS
    lane = lanes((length, rows))
    wet = mask_ref[...].astype(jnp.float32)
    north = wet * north_ref[...]
    wet_above = wet_above_ref[...].T[:length, :1] * flags_ref[:1, :1]
    top = from_below_ref[block:, :].T
    top_below = jnp.concatenate([top[:, :1], top[: length - 128, 1:2]], axis=0) * flags_ref[1:2, :1]
    tall[128:n_at, :] = jnp.zeros((n_at - 128, rows), jnp.float32)
    tall[n_at:e_at, :] = north * jnp.where(lane == rows - 1, wet_above, shifted(wet, -1))
    tall[e_at:f_at, :] = (wet * east_ref[...])[count:]
    tall[f_at:, :] = jnp.zeros((WIDE + 128 - f_at, rows), jnp.float32)
    out_ref[:, :128] = tall[128:WIDE, :].T
    last[...] = tall[WIDE:, :].T
    aside[length:, :] = jnp.zeros((WIDE - length, rows), jnp.float32)
    aside[:length, :] = wet * jnp.where(lane == 0, top_below, shifted(north, 1))
    low[...] = aside[:128, :].T
    high[...] = aside[128:, :].T
    groups = rows // ROWS
    at = pl.ds(0, groups, stride=ROWS)
    before = jnp.concatenate([low[at, :], high[at, :]], axis=1)
    fold = f_at - WIDE
    lane = lanes((groups, 128))
    for n in range(ROWS):
        at = pl.ds(n, groups, stride=ROWS)
        piece = shifted(before, fold - n * (128 - fold))[:, :128]
        last[at, :] = jnp.where(lane >= fold, piece, last[at, :])
    out_ref[:, 128:] = last[...]


def coefficients_kernel(groups, length, slab_ref, second_ref, own_ref, next_ref, east_ref):
    cut, count = lane_plan(length)[:2]
    lane = lanes((ROWS, WIDE))
    for p in range(groups):
        at = rows_of(p)
        more = second_ref[at, :]
        own_ref[at, :] = jnp.where(
            lane < cut,
            shifted(slab_ref[at, :], -length),
            jnp.where(lane < length, shifted(more, cut - length), 0.0),
        )
        east_ref[at, :] = jnp.where(lane < count, shifted(more, count), 0.0)
    for p in range(groups):
        own = own_ref[rows_of(p), :]
        after = own_ref[rows_of((p + 1) % groups), 0:1]
        ocean = jnp.where(lane == length, after, own) > 0.0
        next_ref[rows_of(p), :] = shifted(ocean.astype(jnp.float32), -1)


def transform(chunks, matrix_ref, twiddle_ref, left, right):
    groups = len(chunks)
    mixed = real_fft(chunks)
    for m in range(groups // 2 + 1):
        re, im = mixed[m]
        if m == 0:
            left[rows_of(0), :] = re
            right[rows_of(0), :] = re
            continue
        c = 1 if m == groups // 2 else 2 * m
        cos, sin = twiddle_ref[0, c : c + 1, :], twiddle_ref[1, c : c + 1, :]
        if m == groups // 2:
            left[rows_of(1), :] = re * (cos + sin)
            right[rows_of(1), :] = re * (cos - sin)
        else:
            tr, ti = re * cos + im * sin, im * cos - re * sin
            left[rows_of(c), :] = tr
            right[rows_of(c), :] = ti
            left[rows_of(c + 1), :] = ti
            right[rows_of(c + 1), :] = -tr
    return product(split(left[...]), table(matrix_ref, 0)) + product(
        split(right[...]), table(matrix_ref, 1)
    )


def both_products(spectrum, matrix_ref):
    parts = split(spectrum)
    return product(parts, table(matrix_ref, 0)), product(parts, table(matrix_ref, 1))


def transform_back(products, groups, twiddle_ref):
    pc, ps = products
    mixed = []
    for m in range(groups // 2 + 1):
        if m == 0:
            mixed.append((pc[rows_of(0)] + ps[rows_of(0)], None))
            continue
        c = 1 if m == groups // 2 else 2 * m
        cos, sin = twiddle_ref[0, c : c + 1, :], twiddle_ref[1, c : c + 1, :]
        if m == groups // 2:
            mixed.append((pc[rows_of(1)] * (cos + sin) + ps[rows_of(1)] * (cos - sin), None))
        else:
            hr = pc[rows_of(c)] - ps[rows_of(c + 1)]
            hi = ps[rows_of(c)] + pc[rows_of(c + 1)]
            mixed.append((hr * cos - hi * sin, hi * cos + hr * sin))
    return real_ifft(mixed)


def rows_back(products, start, twiddle_ref, outer_ref):
    groups = outer_ref.shape[0]
    cos, sin = twiddle_ref[0], twiddle_ref[1]
    turned = [[], []]
    for n in range(2):
        pc, ps = (v[start + n * groups : start + (n + 1) * groups] for v in products)
        turned[0].append(pc * cos - ps * sin)
        turned[1].append(ps * cos + pc * sin)
    both = jnp.concatenate([jnp.concatenate(v, axis=1) for v in turned], axis=0)
    both = dot(outer_ref[...], both)
    return both[:, :WIDE], both[:, WIDE:]


def forward_kernel(groups, field_ref, rest_ref, matrix_ref, twiddle_ref, out_ref, left, right):
    chunks = [field_ref[rows_of(p), :] for p in range(groups)]
    spectrum = transform(chunks, matrix_ref, twiddle_ref, left, right)
    out_ref[...] = spectrum + rest_ref[...]


def store_edge(ref, value, extra):
    half = value.shape[0]
    ref[:half, :] = value[:, :128]
    ref[half : half + ROWS, :] = jnp.concatenate(
        [value[:, 128:].T[:ROWS], jnp.zeros((ROWS, 128 - half), jnp.float32)], axis=1
    )
    ref[half + ROWS :, :] = extra


def load_edge(ref):
    half = ref.shape[0] - 2 * ROWS
    turned = ref[half : half + ROWS, :].T[:half]
    blank = jnp.zeros((half, 128 - ROWS), jnp.float32)
    return jnp.concatenate([ref[:half, :], turned, blank], axis=1)


def store_rows(ref, value, part, scale):
    row = sublanes((ROWS, 128))
    extra = jnp.where(row == 0, part[:, :128], part[:, 128:])
    store_edge(
        ref,
        value,
        jnp.where(row < 2, extra, jnp.where(row == 2, scale[:, :128], scale[:, 128:])),
    )


def load_rows(ref):
    at = ref.shape[0] - ROWS
    lines = [ref[at + n : at + n + 1, :] for n in range(4)]
    return jnp.concatenate(lines[:2], axis=1), jnp.concatenate(lines[2:], axis=1)


def blocks_kernel(spec_ref, scale_ref, aligned_ref, scaled_ref, part_ref, down_ref, up_ref):
    count, block = aligned_ref.shape[0], aligned_ref.shape[1]
    half, rows = block // 2, count * block
    scaled = spec_ref[...] * scale_ref[...]
    scaled_ref[...] = scaled
    for b in range(count):
        part_ref[b * block : (b + 1) * block, :] = dot(
            aligned_ref[b], scaled[b * block : (b + 1) * block]
        )
    store_rows(down_ref, scaled[:half], part_ref[:1, :], scale_ref[:1, :])
    store_rows(up_ref, scaled[rows - half :], part_ref[rows - 1 :, :], scale_ref[rows - 1 :, :])


def combine(
    norm, scaled_ref, part_ref, scale_ref, above_ref, below_ref, stag_ref, stag_below_ref, flags_ref
):
    count, block = stag_ref.shape[0], stag_ref.shape[1]
    half, rows = block // 2, count * block
    before = flags_ref[1:2, :] * dot(
        stag_below_ref[:block, :],
        jnp.concatenate([load_edge(below_ref), scaled_ref[:half, :]], axis=0),
    )
    upper = load_edge(above_ref) * flags_ref[:1, :]
    pieces = [before[half:]]
    for b in range(count - 1):
        pieces.append(dot(stag_ref[b], scaled_ref[half + b * block : half + (b + 1) * block, :]))
    after = dot(
        stag_ref[count - 1],
        jnp.concatenate([scaled_ref[rows - half :, :], upper], axis=0),
    )
    pieces.append(after[:half])
    full = (part_ref[...] + jnp.concatenate(pieces, axis=0)) * (scale_ref[...] * norm)
    return full, before, after


def halo_kernel(
    norm,
    scaled_ref,
    part_ref,
    scale_ref,
    above_ref,
    below_ref,
    stag_ref,
    stag_below_ref,
    flags_ref,
    late_ref,
    out_ref,
    low,
    high,
):
    half = stag_ref.shape[1] // 2
    full, before, after = combine(
        norm,
        scaled_ref,
        part_ref,
        scale_ref,
        above_ref,
        below_ref,
        stag_ref,
        stag_below_ref,
        flags_ref,
    )
    part, scale = load_rows(below_ref)
    row_below = (before[half - 1 : half] + part) * (scale * norm)
    part, scale = load_rows(above_ref)
    row_above = (after[half : half + 1] + part) * (scale * norm)
    out_ref[:, :128] = full[:, :128]
    low[...] = full[:, :128]
    high[...] = full[:, 128:]
    groups = full.shape[0] // ROWS

    def strided(start):
        at = pl.ds(start, groups, stride=ROWS)
        return jnp.concatenate([low[at, :], high[at, :]], axis=1)

    row = lax.broadcasted_iota(jnp.int32, (groups, WIDE), 0)
    up = jnp.where(row == 0, row_below, pltpu.roll(strided(ROWS - 1), 1, 0))
    down = jnp.where(row == groups - 1, row_above, pltpu.roll(strided(0), groups - 1, 0))
    lane = lanes((groups, 128)) + 128
    for s, part in enumerate(
        (
            pltpu.roll(up, HALO, 1),
            pltpu.roll(up, HALO - FOLD, 1),
            pltpu.roll(down, HALO, 1),
            pltpu.roll(down, HALO - FOLD, 1),
        )
    ):
        at = pl.ds(s, groups, stride=ROWS)
        high[at, :] = jnp.where(lane >= HALO, part[:, 128:], high[at, :])
    out_ref[:, 128:WIDE] = jnp.where(
        lanes(high.shape) < LATE - 128, high[...], late_ref[:, :128]
    )
    out_ref[:, WIDE:] = late_ref[:, 128:]


def sums_kernel(
    norm,
    length,
    spec_ref,
    scale_ref,
    aligned_ref,
    stag_ref,
    stag_below_ref,
    flags_ref,
    sums_ref,
    scaled_ref,
    part_ref,
    down_ref,
    up_ref,
    own_ref,
):
    count, block = aligned_ref.shape[0], aligned_ref.shape[1]
    half, rows = block // 2, count * block
    scaled = spec_ref[...] * scale_ref[...]
    scaled_ref[...] = scaled
    for b in range(count):
        at = slice(b * block, (b + 1) * block)
        part_ref[at, :] = dot(aligned_ref[b], scaled[at])
    for b in range(count - 1):
        at = slice(half + b * block, half + (b + 1) * block)
        part_ref[at, :] = part_ref[at, :] + dot(stag_ref[b], scaled[at])
    first, last = slice(0, half), slice(rows - half, rows)
    part_ref[first, :] = part_ref[first, :] + flags_ref[1:2, :] * dot(
        stag_below_ref[half:block, half:], scaled[first]
    )
    part_ref[last, :] = part_ref[last, :] + dot(stag_ref[count - 1, :half, :half], scaled[last])
    total = total_of(scaled * part_ref[...], length) * (flags_ref[2:3, :1] * norm)
    small = lanes((8, 128))
    own = jnp.where(small == SCALARS - 128 + 2, total, sums_ref[...])
    own_ref[...] = own
    store_edge(down_ref, scaled[first], own)
    store_edge(up_ref, scaled[last], own)


def total_of(value, length):
    columns = jnp.sum(value, axis=0, keepdims=True)
    columns = jnp.where(lanes(columns.shape) < length, columns, 0.0)
    return jnp.sum(columns[:, :128] + columns[:, 128:], axis=1, keepdims=True)


def ends_kernel(
    norm,
    length,
    scaled_ref,
    part_ref,
    scale_ref,
    above_ref,
    below_ref,
    stag_ref,
    stag_below_ref,
    flags_ref,
    aside_ref,
    own_ref,
    out_ref,
):
    count, block = stag_ref.shape[0], stag_ref.shape[1]
    half, rows = block // 2, count * block
    first, last = slice(0, half), slice(rows - half, rows)
    low = dot(stag_below_ref[half:block, :half], load_edge(below_ref)) * flags_ref[1:2, :]
    high = dot(stag_ref[count - 1, :half, half:], load_edge(above_ref)) * flags_ref[:1, :]
    both = total_of(low * scaled_ref[first, :] + high * scaled_ref[last, :], length)
    both = both * (flags_ref[2:3, :1] * (2.0 * norm))
    pair = own_ref[:1, :] + below_ref[half + ROWS : half + ROWS + 1, :]
    pair = jnp.where(lanes(pair.shape) == SCALARS - 128 + 2, pair + both, pair)
    middle = slice(half, rows - half)
    for at, more in ((first, low), (middle, None), (last, high)):
        full = part_ref[at, :] if more is None else part_ref[at, :] + more
        full = full * (scale_ref[at, :] * norm)
        full = jnp.where(lanes(full.shape) < length, full, aside_ref[at, :])
        out_ref[at, :128] = full[:, :128]
        inside = lanes((full.shape[0], 128)) < SCALARS - 128
        out_ref[at, 128:] = jnp.where(inside, full[:, 128:], pair)


def gather_kernel(spec_ref, sums_ref):
    riders = jnp.sum(spec_ref[:, 128:], axis=0, keepdims=True) * (1.0 / ROWS)
    sums_ref[...] = jnp.broadcast_to(riders, (8, 128))


def step_kernel(
    groups,
    length,
    spec_ref,
    rhs_ref,
    own_ref,
    next_ref,
    east_ref,
    matrix_ref,
    twiddle_ref,
    outer_ref,
    out_ref,
    first_ref,
    image_ref,
    sums_ref,
    left,
    right,
    low,
    high,
    tail,
    folded,
):
    lane_row = lanes((groups, WIDE))
    stride = 3 * ROWS
    tail[...] = spec_ref[:, 128:WIDE]

    def halo_row(s):
        blank = jnp.zeros((groups, 128), jnp.float32)
        parts = [
            jnp.concatenate([tail[pl.ds(s + n, groups, stride=ROWS), :], blank], axis=1)
            for n in range(2)
        ]
        return jnp.where(
            lane_row < FOLD, shifted(parts[0], 128 - HALO), shifted(parts[1], FOLD + 128 - HALO)
        )

    stacked = jnp.concatenate([spec_ref[:, :WIDE], halo_row(0), halo_row(2)], axis=0)
    products = both_products(stacked, matrix_ref)
    halos = rows_back(products, groups * ROWS, twiddle_ref, outer_ref)
    for start, row in zip((ROWS - 1, 2 * ROWS), halos, strict=True):
        low[pl.ds(start, groups, stride=stride), :] = row[:, :128]
        high[pl.ds(start, groups, stride=stride), :] = row[:, 128:]

    def neighbour(start):
        at = slice(start, start + ROWS)
        return jnp.concatenate([low[at, :], high[at, :]], axis=1)

    cells = transform_back(products, groups, twiddle_ref)
    for p in range(groups):
        v = jnp.where(own_ref[rows_of(p), :] > 0.0, cells[p], 0.0)
        first_ref[rows_of(p), :] = v
        low[stride * p + ROWS : stride * p + 2 * ROWS, :] = v[:, :128]
        high[stride * p + ROWS : stride * p + 2 * ROWS, :] = v[:, 128:]
    lane, row = lanes((ROWS, WIDE)), sublanes((ROWS, WIDE))
    _, count, n_at, e_at, f_at = lane_plan(length)
    tail[...] = spec_ref[:, WIDE:]
    fold, blank = f_at - WIDE, jnp.zeros((groups, 128), jnp.float32)
    width = 128 - fold
    before = jnp.zeros((groups, WIDE), jnp.float32)
    for n in range(ROWS):
        piece = jnp.concatenate([tail[pl.ds(n, groups, stride=ROWS), :], blank], axis=1)
        inside = (lane_row >= n * width) & (lane_row < (n + 1) * width)
        before = jnp.where(inside, shifted(piece, n * width - fold), before)
    folded[...] = before
    rz = jnp.zeros((ROWS, WIDE), jnp.float32)
    curvature = jnp.zeros((ROWS, WIDE), jnp.float32)
    images, fluxes = [], []
    for p in range(groups):
        at = rows_of(p)
        v = first_ref[at, :]
        after = first_ref[rows_of((p + 1) % groups), 0:1]
        east = jnp.where(
            lane < count, east_ref[at, :], shifted(spec_ref[at, 128:], count - (e_at - 128))
        )
        flux = v - shifted(jnp.where(lane == length, after, v), -1)
        fluxes.append(jnp.where(lane < length, east * next_ref[at, :] * flux, 0.0))
    for p in range(groups):
        at = rows_of(p)
        v = first_ref[at, :]
        before = fluxes[(p - 1) % groups][:, length - 1 : length]
        flux = fluxes[p]
        own = own_ref[at, :]
        base = stride * p + ROWS
        north = shifted(spec_ref[at, 128:], 128 - n_at)
        south = jnp.where(row == 0, folded[p : p + 1, :], pltpu.roll(north, 1, 0))
        image = jnp.where(own > 0.0, own, 1.0) * v
        image = image + (flux - shifted(jnp.where(lane == WIDE - 1, before, flux), 1))
        image = image + north * (v - neighbour(base + 1))
        image = image + south * (v - neighbour(base - 1))
        image = jnp.where(lane < length, image, 0.0)
        image_ref[at, :] = image
        images.append(image)
        rz = rz + rhs_ref[at, :] * v
        curvature = curvature + v * image
    small = lanes((8, 128))
    at = SCALARS - 128
    sums_ref[...] = jnp.where(
        small == at, jnp.sum(rz), jnp.where(small == at + 1, jnp.sum(curvature), 0.0)
    )
    spectrum = transform(images, matrix_ref, twiddle_ref, left, right)
    out_ref[...] = jnp.where(
        lanes(out_ref.shape) < length, spectrum, shifted(first_ref[...], length)
    )


def last_kernel(
    groups,
    length,
    spec_ref,
    own_ref,
    first_ref,
    image_ref,
    matrix_ref,
    twiddle_ref,
    out_ref,
):
    cells = transform_back(both_products(spec_ref[...], matrix_ref), groups, twiddle_ref)
    lane = lanes((ROWS, WIDE))
    cut = WIDE - length
    image_cut = SCALARS - length
    image_at = 2 * length - cut
    for p in range(groups):
        at = rows_of(p)
        cell = jnp.where(own_ref[at, :] > 0.0, cells[p], 0.0)
        out = jnp.where(lane < length, cell, shifted(first_ref[at, :], length - cut))
        out_ref[at, :] = jnp.where(
            lane < image_at, out, shifted(image_ref[at, :], image_at - image_cut)
        )


def unpack_kernel(length, count, slab_ref, out_ref):
    turned = slab_ref[:, 128:].T
    out_ref[:count, :] = turned[length - 128 : length - 128 + count]


def unpack_first_kernel(length, count, slab_ref, image_ref, out_ref, aside_ref):
    unpack_kernel(length, count, slab_ref, out_ref)
    lane = lanes(image_ref.shape)
    aside_ref[...] = jnp.where(lane < length, 0.0, shifted(image_ref[...], length))


def finish_kernel(
    length,
    back_ref,
    first_ref,
    image_ref,
    forcing_ref,
    mask_ref,
    pair_ref,
    ahead_ref,
    behind_ref,
    across_ref,
    solution_ref,
    residual_ref,
    direction_ref,
):
    at = SCALARS - 128
    totals = (pair_ref[:1, :] + across_ref[:1, :]) + (ahead_ref[:1, :] + behind_ref[:1, :])
    rz, curvature, own = [totals[:, at + n : at + n + 1] for n in range(3)]
    alpha = rz / curvature
    rz_next = rz - 2.0 * alpha * curvature + alpha * alpha * own
    beta = rz_next / rz
    back = back_ref[...].T
    cut = WIDE - length
    image_cut = SCALARS - length
    image_at = 2 * length - cut
    rhs = mask_ref[...].astype(jnp.float32) * forcing_ref[...]

    def store(where, rows_back, first):
        solution_ref[where, :] = alpha * first
        direction_ref[where, :] = (first - alpha * rows_back) + beta * first

    store(slice(0, cut), back[:cut], first_ref[:cut, :])
    store(slice(cut, length), back[cut:length], back[length:image_at])
    residual_ref[:image_cut, :] = rhs[:image_cut] - alpha * image_ref[:image_cut, :]
    residual_ref[image_cut:, :] = (
        rhs[image_cut:] - alpha * back[image_at : image_at + length - image_cut]
    )


def call(kernel, out_shapes, scratch=(), name=None):
    single = not isinstance(out_shapes, (list, tuple)) or isinstance(out_shapes[0], int)
    shapes = [out_shapes] if single else out_shapes
    outs = [jax.ShapeDtypeStruct(s, jnp.float32) for s in shapes]
    return pl.pallas_call(
        kernel,
        out_shape=outs[0] if single else outs,
        scratch_shapes=[pltpu.VMEM(s, jnp.float32) for s in scratch],
        compiler_params=pltpu.CompilerParams(vmem_limit_bytes=16 * 2**20),
        name=name,
    )


def exchanged(value):
    groups = lax.axis_size(LON)
    parts = value.reshape(groups, ROWS, value.shape[-1])
    return lax.all_to_all(parts, LON, split_axis=0, concat_axis=0, tiled=True).reshape(value.shape)


def from_lat(value, steps):
    count = lax.axis_size("lat")
    return lax.ppermute(value, "lat", [((d + steps) % count, d) for d in range(count)])


def after(value, *others):
    return lax.optimization_barrier((value, *others))[0]


def local(
    surface_forcing,
    ocean_mask,
    self_coupling,
    east_coupling,
    north_coupling,
    zonal_weight,
    aligned_inverse,
    staggered_inverse,
):
    groups = lax.axis_size(LON)
    length, rows = surface_forcing.shape
    norm = 1.0 / (groups * length)
    matrices, twiddle, outer, wave = tables(groups, length)
    channel = lax.axis_index(LON)
    count, block = aligned_inverse.shape[0], aligned_inverse.shape[1]
    half = block // 2
    wide = (rows, WIDE)
    transforms = [wide, wide]

    cells = (length, rows)
    wet_cells = ocean_mask.astype(jnp.float32)
    own_cells = wet_cells * self_coupling
    packed = call(pack_kernel, wide, [wide], name="pack")(wet_cells * surface_forcing, own_cells)
    slab = exchanged(packed)

    mask, east_cells, north_cells, weights, stag = lax.optimization_barrier(
        (ocean_mask, east_coupling, north_coupling, zonal_weight, staggered_inverse, packed)
    )[:-1]
    more = call(pack_more_kernel, wide, [wide], name="pack_more")(own_cells, mask, east_cells)
    wet_first, low_last = call(
        edges_kernel, [(ROWS, WIDE), (block + ROWS, 128)], [(WIDE, 128)], name="edges"
    )(mask, north_cells, stag)
    scale = lax.rsqrt(1.0 + weights[:, None] * lax.dynamic_slice_in_dim(wave, channel, 1, 0))
    lat = lax.axis_index("lat")
    flag_row = lax.broadcasted_iota(jnp.int32, (8, WIDE), 0)
    north_of, south_of, weight = (
        jnp.where(condition, yes, no).astype(jnp.float32)
        for condition, yes, no in (
            (lat < lax.axis_size("lat") - 1, 1.0, 0.0),
            (lat > 0, 1.0, 0.0),
            (channel < 2, 1.0, 2.0),
        )
    )
    flags = jnp.where(flag_row == 0, north_of, jnp.where(flag_row == 1, south_of, weight))
    slab = after(slab, scale, flags, wet_first)
    spectrum = call(lambda *r: forward_kernel(groups, *r), wide, transforms, name="forward")(
        slab, more, matrices, twiddle
    )
    spec_rhs = exchanged(spectrum)

    wet_first, low_last = lax.optimization_barrier((wet_first, low_last, spectrum))[:2]
    stag_below = from_lat(low_last, -1)
    late = call(
        pack_rest_kernel,
        wide,
        [(WIDE + 128, rows), wide, (rows, 128), (rows, 128), (rows, 128)],
        name="pack_rest",
    )(mask, east_cells, north_cells, flags, from_lat(wet_first, 1), stag_below)
    spec_rhs = after(spec_rhs, late)

    edge = (half + 2 * ROWS, 128)

    def blocks(spectrum):
        scaled, part, down, up = call(blocks_kernel, [wide, wide, edge, edge], name="blocks")(
            spectrum, scale, aligned_inverse
        )
        above, below = from_lat(down, 1), from_lat(up, -1)
        return scaled, part, scale, above, below, stag, stag_below, flags

    pieces = blocks(spec_rhs)
    flat = call(
        lambda *r: coefficients_kernel(groups, length, *r), [wide] * 3, name="coefficients"
    )(slab, after(spec_rhs, pieces[0]))
    late = after(late, *flat)
    filtered = exchanged(
        call(
            lambda *r: halo_kernel(norm, *r), (rows, WIDE + 128), [(rows, 128)] * 2, name="halo"
        )(*pieces, late)
    )
    spec, first, image, sums = call(
        lambda *r: step_kernel(groups, length, *r),
        [wide, wide, wide, (8, 128)],
        transforms + [(3 * rows, 128)] * 2 + [(rows, 128), (groups, WIDE)],
        name="step",
    )(filtered, slab, *flat, matrices, twiddle, outer)
    spec_image = exchanged(spec)
    scaled, part, down, up, own = call(
        lambda *r: sums_kernel(norm, length, *r), [wide, wide, edge, edge, (8, 128)], name="sums"
    )(spec_image, scale, aligned_inverse, stag, stag_below, flags, sums)
    above, below = from_lat(down, 1), from_lat(up, -1)
    cut, image_cut = WIDE - length, SCALARS - length
    first_cells, aside = call(
        lambda *r: unpack_first_kernel(length, cut, *r), [cells, wide], name="unpack_first"
    )(after(spec_image, scaled), image)
    filtered = exchanged(
        call(lambda *r: ends_kernel(norm, length, *r), wide, name="ends")(
            scaled, part, scale, above, below, stag, stag_below, flags, aside, own
        )
    )

    pair = call(gather_kernel, (8, 128), name="gather")(filtered)
    image_cells = call(
        lambda *r: unpack_kernel(length, image_cut, *r), cells, name="unpack_image"
    )(filtered)
    packed = call(lambda *r: last_kernel(groups, length, *r), wide, name="last")(
        filtered, flat[0], first, image, matrices, twiddle
    )
    return tuple(
        call(lambda *r: finish_kernel(length, *r), [cells] * 3, name="finish")(
            exchanged(packed),
            first_cells,
            image_cells,
            surface_forcing,
            ocean_mask,
            pair,
            from_lat(pair, 2),
            from_lat(pair, -2),
            from_lat(pair, 4),
        )
    )


def solution(mesh):
    torus = Mesh(
        mesh.devices.reshape(mesh.shape["lat"], 4, 4, 2), ("lat", "lon_0", "lon_1", "lon_2")
    )
    return jax.shard_map(
        local,
        mesh=torus,
        in_specs=(
            P(LON, "lat"),
            P(LON, "lat"),
            P(LON, "lat"),
            P(LON, "lat"),
            P(LON, "lat"),
            P("lat"),
            P("lat", None, None),
            P("lat", None, None),
        ),
        out_specs=(P(LON, "lat"), P(LON, "lat"), P(LON, "lat")),
        check_vma=False,
    )
```

```python
import jax
import jax.numpy as jnp
import numpy as np
from jax import lax
from jax.experimental import pallas as pl
from jax.experimental.pallas import tpu as pltpu
from jax.sharding import Mesh
from jax.sharding import PartitionSpec as P

LON = ("lon_0", "lon_1", "lon_2")
TURN = 2.0 * np.pi
ROWS = 8
WIDE = 256
HALO = 136
FOLD = 68
LATE = HALO + FOLD
SCALARS = WIDE - 4


def tables(groups, length):
    period = groups * length
    index = np.arange(length)
    inner = TURN * (np.outer(index, index) % length) / length
    wave_of = np.zeros(groups, np.int64)
    wave_of[1] = groups // 2
    for m in range(1, groups // 2):
        wave_of[2 * m] = wave_of[2 * m + 1] = m
    turn = TURN * (np.outer(wave_of, index) % period) / period
    matrices = np.zeros((2, WIDE, WIDE), np.float32)
    matrices[0, :length, :length] = np.cos(inner)
    matrices[1, :length, :length] = np.sin(inner)
    coarse = matrices.astype(jnp.bfloat16)
    rest = (matrices - coarse.astype(np.float32)).astype(jnp.bfloat16)
    twiddle = np.zeros((2, groups, WIDE))
    twiddle[0, :, :length] = np.cos(turn)
    twiddle[1, :, :length] = np.sin(turn)
    chunk = np.arange(groups)
    outer = np.zeros((2, groups, groups))
    for c in range(groups):
        phase = TURN * (chunk * wave_of[c] % groups) / groups
        if c < 2:
            outer[0, :, c] = outer[1, :, c] = np.cos(phase)
        elif c % 2 == 0:
            outer[0, :, c], outer[1, :, c] = 2 * np.cos(phase), -2 * np.sin(phase)
        else:
            outer[0, :, c], outer[1, :, c] = -2 * np.sin(phase), -2 * np.cos(phase)
    modes = wave_of[:, None] + groups * index[None, :]
    wave = np.zeros((groups, WIDE))
    wave[:, :length] = 4.0 * np.sin(np.pi * modes / period) ** 2
    return (
        np.stack([coarse, rest]),
        twiddle.astype(np.float32),
        np.concatenate([outer[0], outer[1]], axis=1).astype(np.float32),
        wave.astype(np.float32),
    )


def real_fft(values):
    count = len(values)
    if count == 2:
        return [(values[0] + values[1], None), (values[0] - values[1], None)]
    even, odd = real_fft(values[0::2]), real_fft(values[1::2])
    out = [None] * (count // 2 + 1)
    for k in range(count // 4 + 1):
        (er, ei), (re, im) = even[k], odd[k]
        if k == 0:
            out[0], out[count // 2] = (er + re, None), (er - re, None)
        elif k == count // 4:
            out[k] = (er, -re)
        else:
            c, s = float(np.cos(TURN * k / count)), float(-np.sin(TURN * k / count))
            tr, ti = re * c - im * s, im * c + re * s
            out[k], out[count // 2 - k] = (er + tr, ei + ti), (er - tr, ti - ei)
    return out


def real_ifft(spectrum):
    count = 2 * (len(spectrum) - 1)
    if count == 2:
        return [spectrum[0][0] + spectrum[1][0], spectrum[0][0] - spectrum[1][0]]
    even, odd = [], []
    for k in range(count // 4 + 1):
        (ar, ai), (br, bi) = spectrum[k], spectrum[count // 2 - k]
        if k == 0:
            even.append((ar + br, None))
            odd.append((ar - br, None))
        elif k == count // 4:
            even.append((2.0 * ar, None))
            odd.append((-2.0 * ai, None))
        else:
            c, s = float(np.cos(TURN * k / count)), float(np.sin(TURN * k / count))
            dr, di = ar - br, ai + bi
            even.append((ar + br, ai - bi))
            odd.append((dr * c - di * s, dr * s + di * c))
    first, second = real_ifft(even), real_ifft(odd)
    out = []
    for a, b in zip(first, second, strict=True):
        out += [a, b]
    return out


def split(a):
    coarse = a.astype(jnp.bfloat16)
    return coarse, (a - coarse.astype(jnp.float32)).astype(jnp.bfloat16)


def product(a, b):
    (ac, ar), (bc, br) = a, b

    def one(x, y):
        return jnp.dot(x, y, preferred_element_type=jnp.float32)

    return one(ac, bc) + (one(ac, br) + one(ar, bc))


def dot(a, b):
    return product(split(a), split(b))


def table(matrix_ref, n):
    return matrix_ref[0, n], matrix_ref[1, n]


def rows_of(p):
    return slice(ROWS * p, ROWS * (p + 1))


def lanes(shape):
    return lax.broadcasted_iota(jnp.int32, shape, len(shape) - 1)


def sublanes(shape):
    return lax.broadcasted_iota(jnp.int32, shape, len(shape) - 2)


def shifted(value, lanes_right):
    return pltpu.roll(value, lanes_right % value.shape[1], 1)


def pack_kernel(rhs_ref, own_ref, out_ref, tall):
    length = rhs_ref.shape[0]
    tall[:length, :] = rhs_ref[...]
    tall[length:, :] = own_ref[: WIDE - length, :]
    out_ref[...] = tall[...].T


def edges_kernel(mask_ref, north_ref, stag_ref, wet_ref, low_ref, tall):
    length, rows = mask_ref.shape
    count, block = stag_ref.shape[0], stag_ref.shape[1]
    tall[length:, :] = jnp.zeros((WIDE - length, 128), jnp.float32)
    tall[:length, :] = mask_ref[:, :128].astype(jnp.float32)
    wet_ref[...] = tall[...].T[:ROWS]
    tall[:length, :] = mask_ref[:, rows - 128 :].astype(jnp.float32) * north_ref[:, rows - 128 :]
    top = tall[...].T[127:]
    low_ref[:block, :] = stag_ref[count - 1]
    row = sublanes((ROWS, 128))
    low_ref[block:, :] = jnp.where(row == 0, top[:, :128], top[:, 128:])


def lane_plan(length):
    cut = WIDE - length
    count = 2 * cut - length
    north = LATE
    east = north + length
    return cut, count, north, east, east + length - count


def pack_more_kernel(own_ref, mask_ref, east_ref, out_ref, tall):
    length, rows = mask_ref.shape
    cut, count = lane_plan(length)[:2]
    tall[:length, :] = jnp.zeros((length, rows), jnp.float32)
    tall[length : WIDE - count, :] = own_ref[cut:, :]
    tall[WIDE - count :, :] = (mask_ref[...].astype(jnp.float32) * east_ref[...])[:count]
    out_ref[...] = tall[...].T


def pack_rest_kernel(
    mask_ref,
    east_ref,
    north_ref,
    flags_ref,
    wet_above_ref,
    from_below_ref,
    out_ref,
    tall,
    aside,
    low,
    high,
    last,
):
    length, rows = mask_ref.shape
    _, count, n_at, e_at, f_at = lane_plan(length)
    block = from_below_ref.shape[0] - ROWS
    lane = lanes((length, rows))
    wet = mask_ref[...].astype(jnp.float32)
    north = wet * north_ref[...]
    wet_above = wet_above_ref[...].T[:length, :1] * flags_ref[:1, :1]
    top = from_below_ref[block:, :].T
    top_below = jnp.concatenate([top[:, :1], top[: length - 128, 1:2]], axis=0) * flags_ref[1:2, :1]
    tall[128:n_at, :] = jnp.zeros((n_at - 128, rows), jnp.float32)
    tall[n_at:e_at, :] = north * jnp.where(lane == rows - 1, wet_above, shifted(wet, -1))
    tall[e_at:f_at, :] = (wet * east_ref[...])[count:]
    tall[f_at:, :] = jnp.zeros((WIDE + 128 - f_at, rows), jnp.float32)
    out_ref[:, :128] = tall[128:WIDE, :].T
    last[...] = tall[WIDE:, :].T
    aside[length:, :] = jnp.zeros((WIDE - length, rows), jnp.float32)
    aside[:length, :] = wet * jnp.where(lane == 0, top_below, shifted(north, 1))
    low[...] = aside[:128, :].T
    high[...] = aside[128:, :].T
    groups = rows // ROWS
    at = pl.ds(0, groups, stride=ROWS)
    before = jnp.concatenate([low[at, :], high[at, :]], axis=1)
    fold = f_at - WIDE
    lane = lanes((groups, 128))
    for n in range(ROWS):
        at = pl.ds(n, groups, stride=ROWS)
        piece = shifted(before, fold - n * (128 - fold))[:, :128]
        last[at, :] = jnp.where(lane >= fold, piece, last[at, :])
    out_ref[:, 128:] = last[...]


def coefficients_kernel(groups, length, slab_ref, second_ref, own_ref, next_ref, east_ref):
    cut, count = lane_plan(length)[:2]
    lane = lanes((ROWS, WIDE))
    for p in range(groups):
        at = rows_of(p)
        more = second_ref[at, :]
        own_ref[at, :] = jnp.where(
            lane < cut,
            shifted(slab_ref[at, :], -length),
            jnp.where(lane < length, shifted(more, cut - length), 0.0),
        )
        east_ref[at, :] = jnp.where(lane < count, shifted(more, count), 0.0)
    for p in range(groups):
        own = own_ref[rows_of(p), :]
        after = own_ref[rows_of((p + 1) % groups), 0:1]
        ocean = jnp.where(lane == length, after, own) > 0.0
        next_ref[rows_of(p), :] = shifted(ocean.astype(jnp.float32), -1)


def transform(chunks, matrix_ref, twiddle_ref, left, right):
    groups = len(chunks)
    mixed = real_fft(chunks)
    for m in range(groups // 2 + 1):
        re, im = mixed[m]
        if m == 0:
            left[rows_of(0), :] = re
            right[rows_of(0), :] = re
            continue
        c = 1 if m == groups // 2 else 2 * m
        cos, sin = twiddle_ref[0, c : c + 1, :], twiddle_ref[1, c : c + 1, :]
        if m == groups // 2:
            left[rows_of(1), :] = re * (cos + sin)
            right[rows_of(1), :] = re * (cos - sin)
        else:
            tr, ti = re * cos + im * sin, im * cos - re * sin
            left[rows_of(c), :] = tr
            right[rows_of(c), :] = ti
            left[rows_of(c + 1), :] = ti
            right[rows_of(c + 1), :] = -tr
    return product(split(left[...]), table(matrix_ref, 0)) + product(
        split(right[...]), table(matrix_ref, 1)
    )


def both_products(spectrum, matrix_ref):
    parts = split(spectrum)
    return product(parts, table(matrix_ref, 0)), product(parts, table(matrix_ref, 1))


def transform_back(products, groups, twiddle_ref):
    pc, ps = products
    mixed = []
    for m in range(groups // 2 + 1):
        if m == 0:
            mixed.append((pc[rows_of(0)] + ps[rows_of(0)], None))
            continue
        c = 1 if m == groups // 2 else 2 * m
        cos, sin = twiddle_ref[0, c : c + 1, :], twiddle_ref[1, c : c + 1, :]
        if m == groups // 2:
            mixed.append((pc[rows_of(1)] * (cos + sin) + ps[rows_of(1)] * (cos - sin), None))
        else:
            hr = pc[rows_of(c)] - ps[rows_of(c + 1)]
            hi = ps[rows_of(c)] + pc[rows_of(c + 1)]
            mixed.append((hr * cos - hi * sin, hi * cos + hr * sin))
    return real_ifft(mixed)


def rows_back(products, start, twiddle_ref, outer_ref):
    groups = outer_ref.shape[0]
    cos, sin = twiddle_ref[0], twiddle_ref[1]
    turned = [[], []]
    for n in range(2):
        pc, ps = (v[start + n * groups : start + (n + 1) * groups] for v in products)
        turned[0].append(pc * cos - ps * sin)
        turned[1].append(ps * cos + pc * sin)
    both = jnp.concatenate([jnp.concatenate(v, axis=1) for v in turned], axis=0)
    both = dot(outer_ref[...], both)
    return both[:, :WIDE], both[:, WIDE:]


def forward_kernel(groups, field_ref, rest_ref, matrix_ref, twiddle_ref, out_ref, left, right):
    chunks = [field_ref[rows_of(p), :] for p in range(groups)]
    spectrum = transform(chunks, matrix_ref, twiddle_ref, left, right)
    out_ref[...] = spectrum + rest_ref[...]


def store_edge(ref, value, extra):
    half = value.shape[0]
    ref[:half, :] = value[:, :128]
    ref[half : half + ROWS, :] = jnp.concatenate(
        [value[:, 128:].T[:ROWS], jnp.zeros((ROWS, 128 - half), jnp.float32)], axis=1
    )
    ref[half + ROWS :, :] = extra


def load_edge(ref):
    half = ref.shape[0] - 2 * ROWS
    turned = ref[half : half + ROWS, :].T[:half]
    blank = jnp.zeros((half, 128 - ROWS), jnp.float32)
    return jnp.concatenate([ref[:half, :], turned, blank], axis=1)


def store_rows(ref, value, part, scale):
    row = sublanes((ROWS, 128))
    extra = jnp.where(row == 0, part[:, :128], part[:, 128:])
    store_edge(
        ref,
        value,
        jnp.where(row < 2, extra, jnp.where(row == 2, scale[:, :128], scale[:, 128:])),
    )


def load_rows(ref):
    at = ref.shape[0] - ROWS
    lines = [ref[at + n : at + n + 1, :] for n in range(4)]
    return jnp.concatenate(lines[:2], axis=1), jnp.concatenate(lines[2:], axis=1)


def blocks_kernel(spec_ref, scale_ref, aligned_ref, scaled_ref, part_ref, down_ref, up_ref):
    count, block = aligned_ref.shape[0], aligned_ref.shape[1]
    half, rows = block // 2, count * block
    scaled = spec_ref[...] * scale_ref[...]
    scaled_ref[...] = scaled
    for b in range(count):
        part_ref[b * block : (b + 1) * block, :] = dot(
            aligned_ref[b], scaled[b * block : (b + 1) * block]
        )
    store_rows(down_ref, scaled[:half], part_ref[:1, :], scale_ref[:1, :])
    store_rows(up_ref, scaled[rows - half :], part_ref[rows - 1 :, :], scale_ref[rows - 1 :, :])


def combine(
    norm, scaled_ref, part_ref, scale_ref, above_ref, below_ref, stag_ref, stag_below_ref, flags_ref
):
    count, block = stag_ref.shape[0], stag_ref.shape[1]
    half, rows = block // 2, count * block
    before = flags_ref[1:2, :] * dot(
        stag_below_ref[:block, :],
        jnp.concatenate([load_edge(below_ref), scaled_ref[:half, :]], axis=0),
    )
    upper = load_edge(above_ref) * flags_ref[:1, :]
    pieces = [before[half:]]
    for b in range(count - 1):
        pieces.append(dot(stag_ref[b], scaled_ref[half + b * block : half + (b + 1) * block, :]))
    after = dot(
        stag_ref[count - 1],
        jnp.concatenate([scaled_ref[rows - half :, :], upper], axis=0),
    )
    pieces.append(after[:half])
    full = (part_ref[...] + jnp.concatenate(pieces, axis=0)) * (scale_ref[...] * norm)
    return full, before, after


def halo_kernel(
    norm,
    scaled_ref,
    part_ref,
    scale_ref,
    above_ref,
    below_ref,
    stag_ref,
    stag_below_ref,
    flags_ref,
    late_ref,
    out_ref,
    low,
    high,
):
    half = stag_ref.shape[1] // 2
    full, before, after = combine(
        norm,
        scaled_ref,
        part_ref,
        scale_ref,
        above_ref,
        below_ref,
        stag_ref,
        stag_below_ref,
        flags_ref,
    )
    part, scale = load_rows(below_ref)
    row_below = (before[half - 1 : half] + part) * (scale * norm)
    part, scale = load_rows(above_ref)
    row_above = (after[half : half + 1] + part) * (scale * norm)
    out_ref[:, :128] = full[:, :128]
    low[...] = full[:, :128]
    high[...] = full[:, 128:]
    groups = full.shape[0] // ROWS

    def strided(start):
        at = pl.ds(start, groups, stride=ROWS)
        return jnp.concatenate([low[at, :], high[at, :]], axis=1)

    row = lax.broadcasted_iota(jnp.int32, (groups, WIDE), 0)
    up = jnp.where(row == 0, row_below, pltpu.roll(strided(ROWS - 1), 1, 0))
    down = jnp.where(row == groups - 1, row_above, pltpu.roll(strided(0), groups - 1, 0))
    lane = lanes((groups, 128)) + 128
    for s, part in enumerate(
        (
            pltpu.roll(up, HALO, 1),
            pltpu.roll(up, HALO - FOLD, 1),
            pltpu.roll(down, HALO, 1),
            pltpu.roll(down, HALO - FOLD, 1),
        )
    ):
        at = pl.ds(s, groups, stride=ROWS)
        high[at, :] = jnp.where(lane >= HALO, part[:, 128:], high[at, :])
    out_ref[:, 128:WIDE] = jnp.where(
        lanes(high.shape) < LATE - 128, high[...], late_ref[:, :128]
    )
    out_ref[:, WIDE:] = late_ref[:, 128:]


def sums_kernel(
    norm,
    length,
    spec_ref,
    scale_ref,
    aligned_ref,
    stag_ref,
    stag_below_ref,
    flags_ref,
    sums_ref,
    scaled_ref,
    part_ref,
    down_ref,
    up_ref,
    own_ref,
):
    count, block = aligned_ref.shape[0], aligned_ref.shape[1]
    half, rows = block // 2, count * block
    scaled = spec_ref[...] * scale_ref[...]
    scaled_ref[...] = scaled
    for b in range(count):
        at = slice(b * block, (b + 1) * block)
        part_ref[at, :] = dot(aligned_ref[b], scaled[at])
    for b in range(count - 1):
        at = slice(half + b * block, half + (b + 1) * block)
        part_ref[at, :] = part_ref[at, :] + dot(stag_ref[b], scaled[at])
    first, last = slice(0, half), slice(rows - half, rows)
    part_ref[first, :] = part_ref[first, :] + flags_ref[1:2, :] * dot(
        stag_below_ref[half:block, half:], scaled[first]
    )
    part_ref[last, :] = part_ref[last, :] + dot(stag_ref[count - 1, :half, :half], scaled[last])
    total = total_of(scaled * part_ref[...], length) * (flags_ref[2:3, :1] * norm)
    small = lanes((8, 128))
    own = jnp.where(small == SCALARS - 128 + 2, total, sums_ref[...])
    own_ref[...] = own
    store_edge(down_ref, scaled[first], own)
    store_edge(up_ref, scaled[last], own)


def total_of(value, length):
    columns = jnp.sum(value, axis=0, keepdims=True)
    columns = jnp.where(lanes(columns.shape) < length, columns, 0.0)
    return jnp.sum(columns[:, :128] + columns[:, 128:], axis=1, keepdims=True)


def ends_kernel(
    norm,
    length,
    scaled_ref,
    part_ref,
    scale_ref,
    above_ref,
    below_ref,
    stag_ref,
    stag_below_ref,
    flags_ref,
    aside_ref,
    own_ref,
    out_ref,
):
    count, block = stag_ref.shape[0], stag_ref.shape[1]
    half, rows = block // 2, count * block
    first, last = slice(0, half), slice(rows - half, rows)
    low = dot(stag_below_ref[half:block, :half], load_edge(below_ref)) * flags_ref[1:2, :]
    high = dot(stag_ref[count - 1, :half, half:], load_edge(above_ref)) * flags_ref[:1, :]
    both = total_of(low * scaled_ref[first, :] + high * scaled_ref[last, :], length)
    both = both * (flags_ref[2:3, :1] * (2.0 * norm))
    pair = own_ref[:1, :] + below_ref[half + ROWS : half + ROWS + 1, :]
    pair = jnp.where(lanes(pair.shape) == SCALARS - 128 + 2, pair + both, pair)
    middle = slice(half, rows - half)
    for at, more in ((first, low), (middle, None), (last, high)):
        full = part_ref[at, :] if more is None else part_ref[at, :] + more
        full = full * (scale_ref[at, :] * norm)
        full = jnp.where(lanes(full.shape) < length, full, aside_ref[at, :])
        out_ref[at, :128] = full[:, :128]
        inside = lanes((full.shape[0], 128)) < SCALARS - 128
        out_ref[at, 128:] = jnp.where(inside, full[:, 128:], pair)


def gather_kernel(spec_ref, sums_ref):
    riders = jnp.sum(spec_ref[:, 128:], axis=0, keepdims=True) * (1.0 / ROWS)
    sums_ref[...] = jnp.broadcast_to(riders, (8, 128))


def step_kernel(
    groups,
    length,
    spec_ref,
    rhs_ref,
    own_ref,
    next_ref,
    east_ref,
    matrix_ref,
    twiddle_ref,
    outer_ref,
    out_ref,
    first_ref,
    image_ref,
    sums_ref,
    left,
    right,
    low,
    high,
    tail,
    folded,
):
    lane_row = lanes((groups, WIDE))
    stride = 3 * ROWS
    tail[...] = spec_ref[:, 128:WIDE]

    def halo_row(s):
        blank = jnp.zeros((groups, 128), jnp.float32)
        parts = [
            jnp.concatenate([tail[pl.ds(s + n, groups, stride=ROWS), :], blank], axis=1)
            for n in range(2)
        ]
        return jnp.where(
            lane_row < FOLD, shifted(parts[0], 128 - HALO), shifted(parts[1], FOLD + 128 - HALO)
        )

    stacked = jnp.concatenate([spec_ref[:, :WIDE], halo_row(0), halo_row(2)], axis=0)
    products = both_products(stacked, matrix_ref)
    halos = rows_back(products, groups * ROWS, twiddle_ref, outer_ref)
    for start, row in zip((ROWS - 1, 2 * ROWS), halos, strict=True):
        low[pl.ds(start, groups, stride=stride), :] = row[:, :128]
        high[pl.ds(start, groups, stride=stride), :] = row[:, 128:]

    def neighbour(start):
        at = slice(start, start + ROWS)
        return jnp.concatenate([low[at, :], high[at, :]], axis=1)

    cells = transform_back(products, groups, twiddle_ref)
    for p in range(groups):
        v = jnp.where(own_ref[rows_of(p), :] > 0.0, cells[p], 0.0)
        first_ref[rows_of(p), :] = v
        low[stride * p + ROWS : stride * p + 2 * ROWS, :] = v[:, :128]
        high[stride * p + ROWS : stride * p + 2 * ROWS, :] = v[:, 128:]
    lane, row = lanes((ROWS, WIDE)), sublanes((ROWS, WIDE))
    _, count, n_at, e_at, f_at = lane_plan(length)
    tail[...] = spec_ref[:, WIDE:]
    fold, blank = f_at - WIDE, jnp.zeros((groups, 128), jnp.float32)
    width = 128 - fold
    before = jnp.zeros((groups, WIDE), jnp.float32)
    for n in range(ROWS):
        piece = jnp.concatenate([tail[pl.ds(n, groups, stride=ROWS), :], blank], axis=1)
        inside = (lane_row >= n * width) & (lane_row < (n + 1) * width)
        before = jnp.where(inside, shifted(piece, n * width - fold), before)
    folded[...] = before
    rz = jnp.zeros((ROWS, WIDE), jnp.float32)
    curvature = jnp.zeros((ROWS, WIDE), jnp.float32)
    images, fluxes = [], []
    for p in range(groups):
        at = rows_of(p)
        v = first_ref[at, :]
        after = first_ref[rows_of((p + 1) % groups), 0:1]
        east = jnp.where(
            lane < count, east_ref[at, :], shifted(spec_ref[at, 128:], count - (e_at - 128))
        )
        flux = v - shifted(jnp.where(lane == length, after, v), -1)
        fluxes.append(jnp.where(lane < length, east * next_ref[at, :] * flux, 0.0))
    for p in range(groups):
        at = rows_of(p)
        v = first_ref[at, :]
        before = fluxes[(p - 1) % groups][:, length - 1 : length]
        flux = fluxes[p]
        own = own_ref[at, :]
        base = stride * p + ROWS
        north = shifted(spec_ref[at, 128:], 128 - n_at)
        south = jnp.where(row == 0, folded[p : p + 1, :], pltpu.roll(north, 1, 0))
        image = jnp.where(own > 0.0, own, 1.0) * v
        image = image + (flux - shifted(jnp.where(lane == WIDE - 1, before, flux), 1))
        image = image + north * (v - neighbour(base + 1))
        image = image + south * (v - neighbour(base - 1))
        image = jnp.where(lane < length, image, 0.0)
        image_ref[at, :] = image
        images.append(image)
        rz = rz + rhs_ref[at, :] * v
        curvature = curvature + v * image
    small = lanes((8, 128))
    at = SCALARS - 128
    sums_ref[...] = jnp.where(
        small == at, jnp.sum(rz), jnp.where(small == at + 1, jnp.sum(curvature), 0.0)
    )
    spectrum = transform(images, matrix_ref, twiddle_ref, left, right)
    out_ref[...] = jnp.where(
        lanes(out_ref.shape) < length, spectrum, shifted(first_ref[...], length)
    )


def last_kernel(
    groups,
    length,
    spec_ref,
    own_ref,
    first_ref,
    image_ref,
    matrix_ref,
    twiddle_ref,
    out_ref,
):
    cells = transform_back(both_products(spec_ref[...], matrix_ref), groups, twiddle_ref)
    lane = lanes((ROWS, WIDE))
    cut = WIDE - length
    image_cut = SCALARS - length
    image_at = 2 * length - cut
    for p in range(groups):
        at = rows_of(p)
        cell = jnp.where(own_ref[at, :] > 0.0, cells[p], 0.0)
        out = jnp.where(lane < length, cell, shifted(first_ref[at, :], length - cut))
        out_ref[at, :] = jnp.where(
            lane < image_at, out, shifted(image_ref[at, :], image_at - image_cut)
        )


def unpack_kernel(length, count, slab_ref, out_ref):
    turned = slab_ref[:, 128:].T
    out_ref[:count, :] = turned[length - 128 : length - 128 + count]


def unpack_first_kernel(length, count, slab_ref, image_ref, out_ref, aside_ref):
    unpack_kernel(length, count, slab_ref, out_ref)
    lane = lanes(image_ref.shape)
    aside_ref[...] = jnp.where(lane < length, 0.0, shifted(image_ref[...], length))


def finish_kernel(
    length,
    back_ref,
    first_ref,
    image_ref,
    forcing_ref,
    mask_ref,
    pair_ref,
    ahead_ref,
    behind_ref,
    across_ref,
    solution_ref,
    residual_ref,
    direction_ref,
):
    at = SCALARS - 128
    totals = (pair_ref[:1, :] + across_ref[:1, :]) + (ahead_ref[:1, :] + behind_ref[:1, :])
    rz, curvature, own = [totals[:, at + n : at + n + 1] for n in range(3)]
    alpha = rz / curvature
    rz_next = rz - 2.0 * alpha * curvature + alpha * alpha * own
    beta = rz_next / rz
    back = back_ref[...].T
    cut = WIDE - length
    image_cut = SCALARS - length
    image_at = 2 * length - cut
    rhs = mask_ref[...].astype(jnp.float32) * forcing_ref[...]

    def store(where, rows_back, first):
        solution_ref[where, :] = alpha * first
        direction_ref[where, :] = (first - alpha * rows_back) + beta * first

    store(slice(0, cut), back[:cut], first_ref[:cut, :])
    store(slice(cut, length), back[cut:length], back[length:image_at])
    residual_ref[:image_cut, :] = rhs[:image_cut] - alpha * image_ref[:image_cut, :]
    residual_ref[image_cut:, :] = (
        rhs[image_cut:] - alpha * back[image_at : image_at + length - image_cut]
    )


def call(kernel, out_shapes, scratch=(), name=None):
    single = not isinstance(out_shapes, (list, tuple)) or isinstance(out_shapes[0], int)
    shapes = [out_shapes] if single else out_shapes
    outs = [jax.ShapeDtypeStruct(s, jnp.float32) for s in shapes]
    return pl.pallas_call(
        kernel,
        out_shape=outs[0] if single else outs,
        scratch_shapes=[pltpu.VMEM(s, jnp.float32) for s in scratch],
        compiler_params=pltpu.CompilerParams(vmem_limit_bytes=16 * 2**20),
        name=name,
    )


def exchanged(value):
    groups = lax.axis_size(LON)
    parts = value.reshape(groups, ROWS, value.shape[-1])
    return lax.all_to_all(parts, LON, split_axis=0, concat_axis=0, tiled=True).reshape(value.shape)


def from_lat(value, steps):
    count = lax.axis_size("lat")
    return lax.ppermute(value, "lat", [((d + steps) % count, d) for d in range(count)])


def after(value, *others):
    return lax.optimization_barrier((value, *others))[0]


def local(
    surface_forcing,
    ocean_mask,
    self_coupling,
    east_coupling,
    north_coupling,
    zonal_weight,
    aligned_inverse,
    staggered_inverse,
):
    groups = lax.axis_size(LON)
    length, rows = surface_forcing.shape
    norm = 1.0 / (groups * length)
    matrices, twiddle, outer, wave = tables(groups, length)
    count, block = aligned_inverse.shape[0], aligned_inverse.shape[1]
    half = block // 2
    wide = (rows, WIDE)
    transforms = [wide, wide]

    cells = (length, rows)
    places = (lax.axis_index(LON), lax.axis_index("lat"))
    flag_row = lax.broadcasted_iota(jnp.int32, (8, WIDE), 0)
    surface_forcing, channel, lat = lax.optimization_barrier((surface_forcing, *places))
    wet_cells = ocean_mask.astype(jnp.float32)
    own_cells = wet_cells * self_coupling
    packed = call(pack_kernel, wide, [wide], name="pack")(wet_cells * surface_forcing, own_cells)
    slab = exchanged(packed)

    mask, east_cells = lax.optimization_barrier((ocean_mask, east_coupling, slab))[:2]
    more = call(pack_more_kernel, wide, [wide], name="pack_more")(own_cells, mask, east_cells)
    spectrum = call(lambda *r: forward_kernel(groups, *r), wide, transforms, name="forward")(
        slab, more, matrices, twiddle
    )
    spec_rhs = exchanged(spectrum)

    north_cells, stag = lax.optimization_barrier((north_coupling, staggered_inverse, spectrum))[:-1]
    wet_first, low_last = call(
        edges_kernel, [(ROWS, WIDE), (block + ROWS, 128)], [(WIDE, 128)], name="edges"
    )(mask, north_cells, stag)
    weights, channel, lat, flag_row = lax.optimization_barrier(
        (
            zonal_weight,
            channel,
            lat,
            flag_row,
            wet_first,
        )
    )[:-1]
    scale = lax.rsqrt(1.0 + weights[:, None] * lax.dynamic_slice_in_dim(wave, channel, 1, 0))
    north_of, south_of, weight = (
        jnp.where(condition, yes, no).astype(jnp.float32)
        for condition, yes, no in (
            (lat < lax.axis_size("lat") - 1, 1.0, 0.0),
            (lat > 0, 1.0, 0.0),
            (channel < 2, 1.0, 2.0),
        )
    )
    flags = jnp.where(flag_row == 0, north_of, jnp.where(flag_row == 1, south_of, weight))
    stag_below = from_lat(low_last, -1)
    late = call(
        pack_rest_kernel,
        wide,
        [(WIDE + 128, rows), wide, (rows, 128), (rows, 128), (rows, 128)],
        name="pack_rest",
    )(mask, east_cells, north_cells, flags, from_lat(wet_first, 1), stag_below)
    spec_rhs = after(spec_rhs, late, scale, flags)

    edge = (half + 2 * ROWS, 128)

    def blocks(spectrum):
        scaled, part, down, up = call(blocks_kernel, [wide, wide, edge, edge], name="blocks")(
            spectrum, scale, aligned_inverse
        )
        above, below = from_lat(down, 1), from_lat(up, -1)
        return scaled, part, scale, above, below, stag, stag_below, flags

    pieces = blocks(spec_rhs)
    flat = call(
        lambda *r: coefficients_kernel(groups, length, *r), [wide] * 3, name="coefficients"
    )(slab, after(spec_rhs, pieces[0]))
    late = after(late, *flat)
    filtered = exchanged(
        call(
            lambda *r: halo_kernel(norm, *r), (rows, WIDE + 128), [(rows, 128)] * 2, name="halo"
        )(*pieces, late)
    )
    spec, first, image, sums = call(
        lambda *r: step_kernel(groups, length, *r),
        [wide, wide, wide, (8, 128)],
        transforms + [(3 * rows, 128)] * 2 + [(rows, 128), (groups, WIDE)],
        name="step",
    )(filtered, slab, *flat, matrices, twiddle, outer)
    spec_image = exchanged(spec)
    scaled, part, down, up, own = call(
        lambda *r: sums_kernel(norm, length, *r), [wide, wide, edge, edge, (8, 128)], name="sums"
    )(spec_image, scale, aligned_inverse, stag, stag_below, flags, sums)
    above, below = from_lat(down, 1), from_lat(up, -1)
    cut, image_cut = WIDE - length, SCALARS - length
    first_cells, aside = call(
        lambda *r: unpack_first_kernel(length, cut, *r), [cells, wide], name="unpack_first"
    )(after(spec_image, scaled), image)
    filtered = exchanged(
        call(lambda *r: ends_kernel(norm, length, *r), wide, name="ends")(
            scaled, part, scale, above, below, stag, stag_below, flags, aside, own
        )
    )

    pair = call(gather_kernel, (8, 128), name="gather")(filtered)
    image_cells = call(
        lambda *r: unpack_kernel(length, image_cut, *r), cells, name="unpack_image"
    )(filtered)
    packed = call(lambda *r: last_kernel(groups, length, *r), wide, name="last")(
        filtered, flat[0], first, image, matrices, twiddle
    )
    return tuple(
        call(lambda *r: finish_kernel(length, *r), [cells] * 3, name="finish")(
            exchanged(packed),
            first_cells,
            image_cells,
            surface_forcing,
            ocean_mask,
            pair,
            from_lat(pair, 2),
            from_lat(pair, -2),
            from_lat(pair, 4),
        )
    )


def solution(mesh):
    torus = Mesh(
        mesh.devices.reshape(mesh.shape["lat"], 4, 4, 2), ("lat", "lon_0", "lon_1", "lon_2")
    )
    return jax.shard_map(
        local,
        mesh=torus,
        in_specs=(
            P(LON, "lat"),
            P(LON, "lat"),
            P(LON, "lat"),
            P(LON, "lat"),
            P(LON, "lat"),
            P("lat"),
            P("lat", None, None),
            P("lat", None, None),
        ),
        out_specs=(P(LON, "lat"), P(LON, "lat"), P(LON, "lat")),
        check_vma=False,
    )
```

```python
import jax
import jax.numpy as jnp
import numpy as np
from jax import lax
from jax.experimental import pallas as pl
from jax.experimental.pallas import tpu as pltpu
from jax.sharding import Mesh
from jax.sharding import PartitionSpec as P

LON = ("lon_0", "lon_1", "lon_2")
TURN = 2.0 * np.pi
ROWS = 8
WIDE = 256
HALO = 136
FOLD = 68
LATE = HALO + FOLD
SCALARS = WIDE - 4


def tables(groups, length):
    period = groups * length
    index = np.arange(length)
    inner = TURN * (np.outer(index, index) % length) / length
    wave_of = np.zeros(groups, np.int64)
    wave_of[1] = groups // 2
    for m in range(1, groups // 2):
        wave_of[2 * m] = wave_of[2 * m + 1] = m
    turn = TURN * (np.outer(wave_of, index) % period) / period
    rows = np.zeros((2 * WIDE + 2 * groups, WIDE), np.float32)
    rows[:length, :length] = np.cos(inner)
    rows[WIDE : WIDE + length, :length] = np.sin(inner)
    rows[2 * WIDE : 2 * WIDE + groups, :length] = np.cos(turn)
    rows[2 * WIDE + groups :, :length] = np.sin(turn)
    coarse = rows.astype(jnp.bfloat16)
    rest = (rows - coarse.astype(np.float32)).astype(jnp.bfloat16)
    chunk = np.arange(groups)
    outer = np.zeros((2, groups, groups))
    for c in range(groups):
        phase = TURN * (chunk * wave_of[c] % groups) / groups
        if c < 2:
            outer[0, :, c] = outer[1, :, c] = np.cos(phase)
        elif c % 2 == 0:
            outer[0, :, c], outer[1, :, c] = 2 * np.cos(phase), -2 * np.sin(phase)
        else:
            outer[0, :, c], outer[1, :, c] = -2 * np.sin(phase), -2 * np.cos(phase)
    modes = wave_of[:, None] + groups * index[None, :]
    wave = np.zeros((groups, WIDE))
    wave[:, :length] = 4.0 * np.sin(np.pi * modes / period) ** 2
    return (
        np.stack([coarse, rest]),
        np.concatenate([outer[0], outer[1]], axis=1).astype(np.float32),
        wave.astype(np.float32),
    )


def real_fft(values):
    count = len(values)
    if count == 2:
        return [(values[0] + values[1], None), (values[0] - values[1], None)]
    even, odd = real_fft(values[0::2]), real_fft(values[1::2])
    out = [None] * (count // 2 + 1)
    for k in range(count // 4 + 1):
        (er, ei), (re, im) = even[k], odd[k]
        if k == 0:
            out[0], out[count // 2] = (er + re, None), (er - re, None)
        elif k == count // 4:
            out[k] = (er, -re)
        else:
            c, s = float(np.cos(TURN * k / count)), float(-np.sin(TURN * k / count))
            tr, ti = re * c - im * s, im * c + re * s
            out[k], out[count // 2 - k] = (er + tr, ei + ti), (er - tr, ti - ei)
    return out


def real_ifft(spectrum):
    count = 2 * (len(spectrum) - 1)
    if count == 2:
        return [spectrum[0][0] + spectrum[1][0], spectrum[0][0] - spectrum[1][0]]
    even, odd = [], []
    for k in range(count // 4 + 1):
        (ar, ai), (br, bi) = spectrum[k], spectrum[count // 2 - k]
        if k == 0:
            even.append((ar + br, None))
            odd.append((ar - br, None))
        elif k == count // 4:
            even.append((2.0 * ar, None))
            odd.append((-2.0 * ai, None))
        else:
            c, s = float(np.cos(TURN * k / count)), float(np.sin(TURN * k / count))
            dr, di = ar - br, ai + bi
            even.append((ar + br, ai - bi))
            odd.append((dr * c - di * s, dr * s + di * c))
    first, second = real_ifft(even), real_ifft(odd)
    out = []
    for a, b in zip(first, second, strict=True):
        out += [a, b]
    return out


def split(a):
    coarse = a.astype(jnp.bfloat16)
    return coarse, (a - coarse.astype(jnp.float32)).astype(jnp.bfloat16)


def product(a, b):
    (ac, ar), (bc, br) = a, b

    def one(x, y):
        return jnp.dot(x, y, preferred_element_type=jnp.float32)

    return one(ac, bc) + (one(ac, br) + one(ar, bc))


def dot(a, b):
    return product(split(a), split(b))


def table(matrix_ref, n):
    at = slice(n * WIDE, (n + 1) * WIDE)
    return matrix_ref[0, at, :], matrix_ref[1, at, :]


def load_twiddle(matrix_ref, twiddle):
    groups = twiddle.shape[1]
    for n in range(2):
        at = slice(2 * WIDE + n * groups, 2 * WIDE + (n + 1) * groups)
        twiddle[n] = matrix_ref[0, at, :].astype(jnp.float32) + matrix_ref[1, at, :].astype(
            jnp.float32
        )


def rows_of(p):
    return slice(ROWS * p, ROWS * (p + 1))


def lanes(shape):
    return lax.broadcasted_iota(jnp.int32, shape, len(shape) - 1)


def sublanes(shape):
    return lax.broadcasted_iota(jnp.int32, shape, len(shape) - 2)


def shifted(value, lanes_right):
    return pltpu.roll(value, lanes_right % value.shape[1], 1)


def pack_kernel(rhs_ref, own_ref, out_ref, tall):
    length = rhs_ref.shape[0]
    tall[:length, :] = rhs_ref[...]
    tall[length:, :] = own_ref[: WIDE - length, :]
    out_ref[...] = tall[...].T


def edges_kernel(mask_ref, north_ref, stag_ref, wet_ref, low_ref, tall):
    length, rows = mask_ref.shape
    count, block = stag_ref.shape[0], stag_ref.shape[1]
    tall[length:, :] = jnp.zeros((WIDE - length, 128), jnp.float32)
    tall[:length, :] = mask_ref[:, :128].astype(jnp.float32)
    wet_ref[...] = tall[...].T[:ROWS]
    tall[:length, :] = mask_ref[:, rows - 128 :].astype(jnp.float32) * north_ref[:, rows - 128 :]
    top = tall[...].T[127:]
    low_ref[:block, :] = stag_ref[count - 1]
    row = sublanes((ROWS, 128))
    low_ref[block:, :] = jnp.where(row == 0, top[:, :128], top[:, 128:])


def lane_plan(length):
    cut = WIDE - length
    count = 2 * cut - length
    north = LATE
    east = north + length
    return cut, count, north, east, east + length - count


def pack_more_kernel(own_ref, mask_ref, east_ref, out_ref, tall):
    length, rows = mask_ref.shape
    cut, count = lane_plan(length)[:2]
    tall[:length, :] = jnp.zeros((length, rows), jnp.float32)
    tall[length : WIDE - count, :] = own_ref[cut:, :]
    tall[WIDE - count :, :] = (mask_ref[...].astype(jnp.float32) * east_ref[...])[:count]
    out_ref[...] = tall[...].T


def pack_rest_kernel(
    mask_ref,
    east_ref,
    north_ref,
    flags_ref,
    wet_above_ref,
    from_below_ref,
    out_ref,
    tall,
    aside,
    low,
    high,
    last,
):
    length, rows = mask_ref.shape
    _, count, n_at, e_at, f_at = lane_plan(length)
    block = from_below_ref.shape[0] - ROWS
    lane = lanes((length, rows))
    wet = mask_ref[...].astype(jnp.float32)
    north = wet * north_ref[...]
    wet_above = wet_above_ref[...].T[:length, :1] * flags_ref[:1, :1]
    top = from_below_ref[block:, :].T
    top_below = jnp.concatenate([top[:, :1], top[: length - 128, 1:2]], axis=0) * flags_ref[1:2, :1]
    tall[128:n_at, :] = jnp.zeros((n_at - 128, rows), jnp.float32)
    tall[n_at:e_at, :] = north * jnp.where(lane == rows - 1, wet_above, shifted(wet, -1))
    tall[e_at:f_at, :] = (wet * east_ref[...])[count:]
    tall[f_at:, :] = jnp.zeros((WIDE + 128 - f_at, rows), jnp.float32)
    out_ref[:, :128] = tall[128:WIDE, :].T
    last[...] = tall[WIDE:, :].T
    aside[length:, :] = jnp.zeros((WIDE - length, rows), jnp.float32)
    aside[:length, :] = wet * jnp.where(lane == 0, top_below, shifted(north, 1))
    low[...] = aside[:128, :].T
    high[...] = aside[128:, :].T
    groups = rows // ROWS
    at = pl.ds(0, groups, stride=ROWS)
    before = jnp.concatenate([low[at, :], high[at, :]], axis=1)
    fold = f_at - WIDE
    lane = lanes((groups, 128))
    for n in range(ROWS):
        at = pl.ds(n, groups, stride=ROWS)
        piece = shifted(before, fold - n * (128 - fold))[:, :128]
        last[at, :] = jnp.where(lane >= fold, piece, last[at, :])
    out_ref[:, 128:] = last[...]


def coefficients_kernel(groups, length, slab_ref, second_ref, own_ref, next_ref, east_ref):
    cut, count = lane_plan(length)[:2]
    lane = lanes((ROWS, WIDE))
    for p in range(groups):
        at = rows_of(p)
        more = second_ref[at, :]
        own_ref[at, :] = jnp.where(
            lane < cut,
            shifted(slab_ref[at, :], -length),
            jnp.where(lane < length, shifted(more, cut - length), 0.0),
        )
        east_ref[at, :] = jnp.where(lane < count, shifted(more, count), 0.0)
    for p in range(groups):
        own = own_ref[rows_of(p), :]
        after = own_ref[rows_of((p + 1) % groups), 0:1]
        ocean = jnp.where(lane == length, after, own) > 0.0
        next_ref[rows_of(p), :] = shifted(ocean.astype(jnp.float32), -1)


def transform(chunks, matrix_ref, twiddle_ref, left, right):
    groups = len(chunks)
    mixed = real_fft(chunks)
    for m in range(groups // 2 + 1):
        re, im = mixed[m]
        if m == 0:
            left[rows_of(0), :] = re
            right[rows_of(0), :] = re
            continue
        c = 1 if m == groups // 2 else 2 * m
        cos, sin = twiddle_ref[0, c : c + 1, :], twiddle_ref[1, c : c + 1, :]
        if m == groups // 2:
            left[rows_of(1), :] = re * (cos + sin)
            right[rows_of(1), :] = re * (cos - sin)
        else:
            tr, ti = re * cos + im * sin, im * cos - re * sin
            left[rows_of(c), :] = tr
            right[rows_of(c), :] = ti
            left[rows_of(c + 1), :] = ti
            right[rows_of(c + 1), :] = -tr
    return product(split(left[...]), table(matrix_ref, 0)) + product(
        split(right[...]), table(matrix_ref, 1)
    )


def both_products(spectrum, matrix_ref):
    parts = split(spectrum)
    return product(parts, table(matrix_ref, 0)), product(parts, table(matrix_ref, 1))


def transform_back(products, groups, twiddle_ref):
    pc, ps = products
    mixed = []
    for m in range(groups // 2 + 1):
        if m == 0:
            mixed.append((pc[rows_of(0)] + ps[rows_of(0)], None))
            continue
        c = 1 if m == groups // 2 else 2 * m
        cos, sin = twiddle_ref[0, c : c + 1, :], twiddle_ref[1, c : c + 1, :]
        if m == groups // 2:
            mixed.append((pc[rows_of(1)] * (cos + sin) + ps[rows_of(1)] * (cos - sin), None))
        else:
            hr = pc[rows_of(c)] - ps[rows_of(c + 1)]
            hi = ps[rows_of(c)] + pc[rows_of(c + 1)]
            mixed.append((hr * cos - hi * sin, hi * cos + hr * sin))
    return real_ifft(mixed)


def rows_back(products, start, twiddle_ref, outer_ref):
    groups = outer_ref.shape[0]
    cos, sin = twiddle_ref[0], twiddle_ref[1]
    turned = [[], []]
    for n in range(2):
        pc, ps = (v[start + n * groups : start + (n + 1) * groups] for v in products)
        turned[0].append(pc * cos - ps * sin)
        turned[1].append(ps * cos + pc * sin)
    both = jnp.concatenate([jnp.concatenate(v, axis=1) for v in turned], axis=0)
    both = dot(outer_ref[...], both)
    return both[:, :WIDE], both[:, WIDE:]


def forward_kernel(groups, field_ref, rest_ref, matrix_ref, out_ref, left, right, twiddle_ref):
    load_twiddle(matrix_ref, twiddle_ref)
    chunks = [field_ref[rows_of(p), :] for p in range(groups)]
    spectrum = transform(chunks, matrix_ref, twiddle_ref, left, right)
    out_ref[...] = spectrum + rest_ref[...]


def store_edge(ref, value, extra):
    half = value.shape[0]
    ref[:half, :] = value[:, :128]
    ref[half : half + ROWS, :] = jnp.concatenate(
        [value[:, 128:].T[:ROWS], jnp.zeros((ROWS, 128 - half), jnp.float32)], axis=1
    )
    ref[half + ROWS :, :] = extra


def load_edge(ref):
    half = ref.shape[0] - 2 * ROWS
    turned = ref[half : half + ROWS, :].T[:half]
    blank = jnp.zeros((half, 128 - ROWS), jnp.float32)
    return jnp.concatenate([ref[:half, :], turned, blank], axis=1)


def store_rows(ref, value, part, scale):
    row = sublanes((ROWS, 128))
    extra = jnp.where(row == 0, part[:, :128], part[:, 128:])
    store_edge(
        ref,
        value,
        jnp.where(row < 2, extra, jnp.where(row == 2, scale[:, :128], scale[:, 128:])),
    )


def load_rows(ref):
    at = ref.shape[0] - ROWS
    lines = [ref[at + n : at + n + 1, :] for n in range(4)]
    return jnp.concatenate(lines[:2], axis=1), jnp.concatenate(lines[2:], axis=1)


def blocks_kernel(spec_ref, scale_ref, aligned_ref, scaled_ref, part_ref, down_ref, up_ref):
    count, block = aligned_ref.shape[0], aligned_ref.shape[1]
    half, rows = block // 2, count * block
    scaled = spec_ref[...] * scale_ref[...]
    scaled_ref[...] = scaled
    for b in range(count):
        part_ref[b * block : (b + 1) * block, :] = dot(
            aligned_ref[b], scaled[b * block : (b + 1) * block]
        )
    store_rows(down_ref, scaled[:half], part_ref[:1, :], scale_ref[:1, :])
    store_rows(up_ref, scaled[rows - half :], part_ref[rows - 1 :, :], scale_ref[rows - 1 :, :])


def combine(
    norm, scaled_ref, part_ref, scale_ref, above_ref, below_ref, stag_ref, stag_below_ref, flags_ref
):
    count, block = stag_ref.shape[0], stag_ref.shape[1]
    half, rows = block // 2, count * block
    before = flags_ref[1:2, :] * dot(
        stag_below_ref[:block, :],
        jnp.concatenate([load_edge(below_ref), scaled_ref[:half, :]], axis=0),
    )
    upper = load_edge(above_ref) * flags_ref[:1, :]
    pieces = [before[half:]]
    for b in range(count - 1):
        pieces.append(dot(stag_ref[b], scaled_ref[half + b * block : half + (b + 1) * block, :]))
    after = dot(
        stag_ref[count - 1],
        jnp.concatenate([scaled_ref[rows - half :, :], upper], axis=0),
    )
    pieces.append(after[:half])
    full = (part_ref[...] + jnp.concatenate(pieces, axis=0)) * (scale_ref[...] * norm)
    return full, before, after


def halo_kernel(
    norm,
    scaled_ref,
    part_ref,
    scale_ref,
    above_ref,
    below_ref,
    stag_ref,
    stag_below_ref,
    flags_ref,
    late_ref,
    out_ref,
    low,
    high,
):
    half = stag_ref.shape[1] // 2
    full, before, after = combine(
        norm,
        scaled_ref,
        part_ref,
        scale_ref,
        above_ref,
        below_ref,
        stag_ref,
        stag_below_ref,
        flags_ref,
    )
    part, scale = load_rows(below_ref)
    row_below = (before[half - 1 : half] + part) * (scale * norm)
    part, scale = load_rows(above_ref)
    row_above = (after[half : half + 1] + part) * (scale * norm)
    out_ref[:, :128] = full[:, :128]
    low[...] = full[:, :128]
    high[...] = full[:, 128:]
    groups = full.shape[0] // ROWS

    def strided(start):
        at = pl.ds(start, groups, stride=ROWS)
        return jnp.concatenate([low[at, :], high[at, :]], axis=1)

    row = lax.broadcasted_iota(jnp.int32, (groups, WIDE), 0)
    up = jnp.where(row == 0, row_below, pltpu.roll(strided(ROWS - 1), 1, 0))
    down = jnp.where(row == groups - 1, row_above, pltpu.roll(strided(0), groups - 1, 0))
    lane = lanes((groups, 128)) + 128
    for s, part in enumerate(
        (
            pltpu.roll(up, HALO, 1),
            pltpu.roll(up, HALO - FOLD, 1),
            pltpu.roll(down, HALO, 1),
            pltpu.roll(down, HALO - FOLD, 1),
        )
    ):
        at = pl.ds(s, groups, stride=ROWS)
        high[at, :] = jnp.where(lane >= HALO, part[:, 128:], high[at, :])
    out_ref[:, 128:WIDE] = jnp.where(
        lanes(high.shape) < LATE - 128, high[...], late_ref[:, :128]
    )
    out_ref[:, WIDE:] = late_ref[:, 128:]


def sums_kernel(
    norm,
    length,
    spec_ref,
    scale_ref,
    aligned_ref,
    stag_ref,
    stag_below_ref,
    flags_ref,
    sums_ref,
    scaled_ref,
    part_ref,
    down_ref,
    up_ref,
    own_ref,
):
    count, block = aligned_ref.shape[0], aligned_ref.shape[1]
    half, rows = block // 2, count * block
    scaled = spec_ref[...] * scale_ref[...]
    scaled_ref[...] = scaled
    for b in range(count):
        at = slice(b * block, (b + 1) * block)
        part_ref[at, :] = dot(aligned_ref[b], scaled[at])
    for b in range(count - 1):
        at = slice(half + b * block, half + (b + 1) * block)
        part_ref[at, :] = part_ref[at, :] + dot(stag_ref[b], scaled[at])
    first, last = slice(0, half), slice(rows - half, rows)
    part_ref[first, :] = part_ref[first, :] + flags_ref[1:2, :] * dot(
        stag_below_ref[half:block, half:], scaled[first]
    )
    part_ref[last, :] = part_ref[last, :] + dot(stag_ref[count - 1, :half, :half], scaled[last])
    total = total_of(scaled * part_ref[...], length) * (flags_ref[2:3, :1] * norm)
    small = lanes((8, 128))
    own = jnp.where(small == SCALARS - 128 + 2, total, sums_ref[...])
    own_ref[...] = own
    store_edge(down_ref, scaled[first], own)
    store_edge(up_ref, scaled[last], own)


def total_of(value, length):
    columns = jnp.sum(value, axis=0, keepdims=True)
    columns = jnp.where(lanes(columns.shape) < length, columns, 0.0)
    return jnp.sum(columns[:, :128] + columns[:, 128:], axis=1, keepdims=True)


def ends_kernel(
    norm,
    length,
    scaled_ref,
    part_ref,
    scale_ref,
    above_ref,
    below_ref,
    stag_ref,
    stag_below_ref,
    flags_ref,
    aside_ref,
    own_ref,
    out_ref,
):
    count, block = stag_ref.shape[0], stag_ref.shape[1]
    half, rows = block // 2, count * block
    first, last = slice(0, half), slice(rows - half, rows)
    low = dot(stag_below_ref[half:block, :half], load_edge(below_ref)) * flags_ref[1:2, :]
    high = dot(stag_ref[count - 1, :half, half:], load_edge(above_ref)) * flags_ref[:1, :]
    both = total_of(low * scaled_ref[first, :] + high * scaled_ref[last, :], length)
    both = both * (flags_ref[2:3, :1] * (2.0 * norm))
    pair = own_ref[:1, :] + below_ref[half + ROWS : half + ROWS + 1, :]
    pair = jnp.where(lanes(pair.shape) == SCALARS - 128 + 2, pair + both, pair)
    middle = slice(half, rows - half)
    for at, more in ((first, low), (middle, None), (last, high)):
        full = part_ref[at, :] if more is None else part_ref[at, :] + more
        full = full * (scale_ref[at, :] * norm)
        full = jnp.where(lanes(full.shape) < length, full, aside_ref[at, :])
        out_ref[at, :128] = full[:, :128]
        inside = lanes((full.shape[0], 128)) < SCALARS - 128
        out_ref[at, 128:] = jnp.where(inside, full[:, 128:], pair)


def gather_kernel(spec_ref, sums_ref):
    riders = jnp.sum(spec_ref[:, 128:], axis=0, keepdims=True) * (1.0 / ROWS)
    sums_ref[...] = jnp.broadcast_to(riders, (8, 128))


def step_kernel(
    groups,
    length,
    spec_ref,
    rhs_ref,
    own_ref,
    next_ref,
    east_ref,
    matrix_ref,
    outer_ref,
    out_ref,
    first_ref,
    image_ref,
    sums_ref,
    left,
    right,
    low,
    high,
    tail,
    folded,
    twiddle_ref,
):
    load_twiddle(matrix_ref, twiddle_ref)
    lane_row = lanes((groups, WIDE))
    stride = 3 * ROWS
    tail[...] = spec_ref[:, 128:WIDE]

    def halo_row(s):
        blank = jnp.zeros((groups, 128), jnp.float32)
        parts = [
            jnp.concatenate([tail[pl.ds(s + n, groups, stride=ROWS), :], blank], axis=1)
            for n in range(2)
        ]
        return jnp.where(
            lane_row < FOLD, shifted(parts[0], 128 - HALO), shifted(parts[1], FOLD + 128 - HALO)
        )

    stacked = jnp.concatenate([spec_ref[:, :WIDE], halo_row(0), halo_row(2)], axis=0)
    products = both_products(stacked, matrix_ref)
    halos = rows_back(products, groups * ROWS, twiddle_ref, outer_ref)
    for start, row in zip((ROWS - 1, 2 * ROWS), halos, strict=True):
        low[pl.ds(start, groups, stride=stride), :] = row[:, :128]
        high[pl.ds(start, groups, stride=stride), :] = row[:, 128:]

    def neighbour(start):
        at = slice(start, start + ROWS)
        return jnp.concatenate([low[at, :], high[at, :]], axis=1)

    cells = transform_back(products, groups, twiddle_ref)
    for p in range(groups):
        v = jnp.where(own_ref[rows_of(p), :] > 0.0, cells[p], 0.0)
        first_ref[rows_of(p), :] = v
        low[stride * p + ROWS : stride * p + 2 * ROWS, :] = v[:, :128]
        high[stride * p + ROWS : stride * p + 2 * ROWS, :] = v[:, 128:]
    lane, row = lanes((ROWS, WIDE)), sublanes((ROWS, WIDE))
    _, count, n_at, e_at, f_at = lane_plan(length)
    tail[...] = spec_ref[:, WIDE:]
    fold, blank = f_at - WIDE, jnp.zeros((groups, 128), jnp.float32)
    width = 128 - fold
    before = jnp.zeros((groups, WIDE), jnp.float32)
    for n in range(ROWS):
        piece = jnp.concatenate([tail[pl.ds(n, groups, stride=ROWS), :], blank], axis=1)
        inside = (lane_row >= n * width) & (lane_row < (n + 1) * width)
        before = jnp.where(inside, shifted(piece, n * width - fold), before)
    folded[...] = before
    rz = jnp.zeros((ROWS, WIDE), jnp.float32)
    curvature = jnp.zeros((ROWS, WIDE), jnp.float32)
    images, fluxes = [], []
    for p in range(groups):
        at = rows_of(p)
        v = first_ref[at, :]
        after = first_ref[rows_of((p + 1) % groups), 0:1]
        east = jnp.where(
            lane < count, east_ref[at, :], shifted(spec_ref[at, 128:], count - (e_at - 128))
        )
        flux = v - shifted(jnp.where(lane == length, after, v), -1)
        fluxes.append(jnp.where(lane < length, east * next_ref[at, :] * flux, 0.0))
    for p in range(groups):
        at = rows_of(p)
        v = first_ref[at, :]
        before = fluxes[(p - 1) % groups][:, length - 1 : length]
        flux = fluxes[p]
        own = own_ref[at, :]
        base = stride * p + ROWS
        north = shifted(spec_ref[at, 128:], 128 - n_at)
        south = jnp.where(row == 0, folded[p : p + 1, :], pltpu.roll(north, 1, 0))
        image = jnp.where(own > 0.0, own, 1.0) * v
        image = image + (flux - shifted(jnp.where(lane == WIDE - 1, before, flux), 1))
        image = image + north * (v - neighbour(base + 1))
        image = image + south * (v - neighbour(base - 1))
        image = jnp.where(lane < length, image, 0.0)
        image_ref[at, :] = image
        images.append(image)
        rz = rz + rhs_ref[at, :] * v
        curvature = curvature + v * image
    small = lanes((8, 128))
    at = SCALARS - 128
    sums_ref[...] = jnp.where(
        small == at, jnp.sum(rz), jnp.where(small == at + 1, jnp.sum(curvature), 0.0)
    )
    spectrum = transform(images, matrix_ref, twiddle_ref, left, right)
    out_ref[...] = jnp.where(
        lanes(out_ref.shape) < length, spectrum, shifted(first_ref[...], length)
    )


def last_kernel(
    groups,
    length,
    spec_ref,
    own_ref,
    first_ref,
    image_ref,
    matrix_ref,
    out_ref,
    twiddle_ref,
):
    load_twiddle(matrix_ref, twiddle_ref)
    cells = transform_back(both_products(spec_ref[...], matrix_ref), groups, twiddle_ref)
    lane = lanes((ROWS, WIDE))
    cut = WIDE - length
    image_cut = SCALARS - length
    image_at = 2 * length - cut
    for p in range(groups):
        at = rows_of(p)
        cell = jnp.where(own_ref[at, :] > 0.0, cells[p], 0.0)
        out = jnp.where(lane < length, cell, shifted(first_ref[at, :], length - cut))
        out_ref[at, :] = jnp.where(
            lane < image_at, out, shifted(image_ref[at, :], image_at - image_cut)
        )


def unpack_kernel(length, count, slab_ref, out_ref):
    turned = slab_ref[:, 128:].T
    out_ref[:count, :] = turned[length - 128 : length - 128 + count]


def unpack_first_kernel(length, count, slab_ref, image_ref, out_ref, aside_ref):
    unpack_kernel(length, count, slab_ref, out_ref)
    lane = lanes(image_ref.shape)
    aside_ref[...] = jnp.where(lane < length, 0.0, shifted(image_ref[...], length))


def finish_kernel(
    length,
    back_ref,
    first_ref,
    image_ref,
    forcing_ref,
    mask_ref,
    pair_ref,
    ahead_ref,
    behind_ref,
    across_ref,
    solution_ref,
    residual_ref,
    direction_ref,
):
    at = SCALARS - 128
    totals = (pair_ref[:1, :] + across_ref[:1, :]) + (ahead_ref[:1, :] + behind_ref[:1, :])
    rz, curvature, own = [totals[:, at + n : at + n + 1] for n in range(3)]
    alpha = rz / curvature
    rz_next = rz - 2.0 * alpha * curvature + alpha * alpha * own
    beta = rz_next / rz
    back = back_ref[...].T
    cut = WIDE - length
    image_cut = SCALARS - length
    image_at = 2 * length - cut
    rhs = mask_ref[...].astype(jnp.float32) * forcing_ref[...]

    def store(where, rows_back, first):
        solution_ref[where, :] = alpha * first
        direction_ref[where, :] = (first - alpha * rows_back) + beta * first

    store(slice(0, cut), back[:cut], first_ref[:cut, :])
    store(slice(cut, length), back[cut:length], back[length:image_at])
    residual_ref[:image_cut, :] = rhs[:image_cut] - alpha * image_ref[:image_cut, :]
    residual_ref[image_cut:, :] = (
        rhs[image_cut:] - alpha * back[image_at : image_at + length - image_cut]
    )


def call(kernel, out_shapes, scratch=(), name=None):
    single = not isinstance(out_shapes, (list, tuple)) or isinstance(out_shapes[0], int)
    shapes = [out_shapes] if single else out_shapes
    outs = [jax.ShapeDtypeStruct(s, jnp.float32) for s in shapes]
    return pl.pallas_call(
        kernel,
        out_shape=outs[0] if single else outs,
        scratch_shapes=[pltpu.VMEM(s, jnp.float32) for s in scratch],
        compiler_params=pltpu.CompilerParams(vmem_limit_bytes=16 * 2**20),
        name=name,
    )


def exchanged(value):
    groups = lax.axis_size(LON)
    parts = value.reshape(groups, ROWS, value.shape[-1])
    return lax.all_to_all(parts, LON, split_axis=0, concat_axis=0, tiled=True).reshape(value.shape)


def from_lat(value, steps):
    count = lax.axis_size("lat")
    return lax.ppermute(value, "lat", [((d + steps) % count, d) for d in range(count)])


def after(value, *others):
    return lax.optimization_barrier((value, *others))[0]


def local(
    surface_forcing,
    ocean_mask,
    self_coupling,
    east_coupling,
    north_coupling,
    zonal_weight,
    aligned_inverse,
    staggered_inverse,
):
    groups = lax.axis_size(LON)
    length, rows = surface_forcing.shape
    norm = 1.0 / (groups * length)
    matrices, outer, wave = tables(groups, length)
    count, block = aligned_inverse.shape[0], aligned_inverse.shape[1]
    half = block // 2
    wide = (rows, WIDE)
    turns = [(2, groups, WIDE)]
    transforms = [wide, wide]

    cells = (length, rows)
    places = (lax.axis_index(LON), lax.axis_index("lat"))
    flag_row = lax.broadcasted_iota(jnp.int32, (8, WIDE), 0)
    surface_forcing, channel, lat = lax.optimization_barrier((surface_forcing, *places))
    wet_cells = ocean_mask.astype(jnp.float32)
    own_cells = wet_cells * self_coupling
    packed = call(pack_kernel, wide, [wide], name="pack")(wet_cells * surface_forcing, own_cells)
    slab = exchanged(packed)

    mask, east_cells = lax.optimization_barrier((ocean_mask, east_coupling, slab))[:2]
    more = call(pack_more_kernel, wide, [wide], name="pack_more")(own_cells, mask, east_cells)
    spectrum = call(lambda *r: forward_kernel(groups, *r), wide, transforms + turns, name="forward")(
        slab, more, matrices
    )
    spec_rhs = exchanged(spectrum)

    north_cells, stag = lax.optimization_barrier((north_coupling, staggered_inverse, spectrum))[:-1]
    wet_first, low_last = call(
        edges_kernel, [(ROWS, WIDE), (block + ROWS, 128)], [(WIDE, 128)], name="edges"
    )(mask, north_cells, stag)
    weights, channel, lat, flag_row = lax.optimization_barrier(
        (
            zonal_weight,
            channel,
            lat,
            flag_row,
            wet_first,
        )
    )[:-1]
    scale = lax.rsqrt(1.0 + weights[:, None] * lax.dynamic_slice_in_dim(wave, channel, 1, 0))
    north_of, south_of, weight = (
        jnp.where(condition, yes, no).astype(jnp.float32)
        for condition, yes, no in (
            (lat < lax.axis_size("lat") - 1, 1.0, 0.0),
            (lat > 0, 1.0, 0.0),
            (channel < 2, 1.0, 2.0),
        )
    )
    flags = jnp.where(flag_row == 0, north_of, jnp.where(flag_row == 1, south_of, weight))
    stag_below = from_lat(low_last, -1)
    late = call(
        pack_rest_kernel,
        wide,
        [(WIDE + 128, rows), wide, (rows, 128), (rows, 128), (rows, 128)],
        name="pack_rest",
    )(mask, east_cells, north_cells, flags, from_lat(wet_first, 1), stag_below)
    spec_rhs = after(spec_rhs, late, scale, flags)

    edge = (half + 2 * ROWS, 128)

    def blocks(spectrum):
        scaled, part, down, up = call(blocks_kernel, [wide, wide, edge, edge], name="blocks")(
            spectrum, scale, aligned_inverse
        )
        above, below = from_lat(down, 1), from_lat(up, -1)
        return scaled, part, scale, above, below, stag, stag_below, flags

    pieces = blocks(spec_rhs)
    flat = call(
        lambda *r: coefficients_kernel(groups, length, *r), [wide] * 3, name="coefficients"
    )(slab, after(spec_rhs, pieces[0]))
    late = after(late, *flat)
    filtered = exchanged(
        call(
            lambda *r: halo_kernel(norm, *r), (rows, WIDE + 128), [(rows, 128)] * 2, name="halo"
        )(*pieces, late)
    )
    spec, first, image, sums = call(
        lambda *r: step_kernel(groups, length, *r),
        [wide, wide, wide, (8, 128)],
        transforms + [(3 * rows, 128)] * 2 + [(rows, 128), (groups, WIDE)] + turns,
        name="step",
    )(filtered, slab, *flat, matrices, outer)
    spec_image = exchanged(spec)
    scaled, part, down, up, own = call(
        lambda *r: sums_kernel(norm, length, *r), [wide, wide, edge, edge, (8, 128)], name="sums"
    )(spec_image, scale, aligned_inverse, stag, stag_below, flags, sums)
    above, below = from_lat(down, 1), from_lat(up, -1)
    cut, image_cut = WIDE - length, SCALARS - length
    first_cells, aside = call(
        lambda *r: unpack_first_kernel(length, cut, *r), [cells, wide], name="unpack_first"
    )(after(spec_image, scaled), image)
    filtered = exchanged(
        call(lambda *r: ends_kernel(norm, length, *r), wide, name="ends")(
            scaled, part, scale, above, below, stag, stag_below, flags, aside, own
        )
    )

    pair = call(gather_kernel, (8, 128), name="gather")(filtered)
    image_cells = call(
        lambda *r: unpack_kernel(length, image_cut, *r), cells, name="unpack_image"
    )(filtered)
    packed = call(lambda *r: last_kernel(groups, length, *r), wide, turns, name="last")(
        filtered, flat[0], first, image, matrices
    )
    return tuple(
        call(lambda *r: finish_kernel(length, *r), [cells] * 3, name="finish")(
            exchanged(packed),
            first_cells,
            image_cells,
            surface_forcing,
            ocean_mask,
            pair,
            from_lat(pair, 2),
            from_lat(pair, -2),
            from_lat(pair, 4),
        )
    )


def solution(mesh):
    torus = Mesh(
        mesh.devices.reshape(mesh.shape["lat"], 4, 4, 2), ("lat", "lon_0", "lon_1", "lon_2")
    )
    return jax.shard_map(
        local,
        mesh=torus,
        in_specs=(
            P(LON, "lat"),
            P(LON, "lat"),
            P(LON, "lat"),
            P(LON, "lat"),
            P(LON, "lat"),
            P("lat"),
            P("lat", None, None),
            P("lat", None, None),
        ),
        out_specs=(P(LON, "lat"), P(LON, "lat"), P(LON, "lat")),
        check_vma=False,
    )
```

```python
import jax
import jax.numpy as jnp
import numpy as np
from jax import lax
from jax.experimental import pallas as pl
from jax.experimental.pallas import tpu as pltpu
from jax.sharding import Mesh
from jax.sharding import PartitionSpec as P

LON = ("lon_0", "lon_1", "lon_2")
TURN = 2.0 * np.pi
ROWS = 8
WIDE = 256
HALO = 136
FOLD = 68
LATE = HALO + FOLD
SCALARS = WIDE - 4


def tables(groups, length):
    period = groups * length
    index = np.arange(length)
    inner = TURN * (np.outer(index, index) % length) / length
    wave_of = np.zeros(groups, np.int64)
    wave_of[1] = groups // 2
    for m in range(1, groups // 2):
        wave_of[2 * m] = wave_of[2 * m + 1] = m
    turn = TURN * (np.outer(wave_of, index) % period) / period
    rows = np.zeros((2 * WIDE + 2 * groups, WIDE), np.float32)
    rows[:length, :length] = np.cos(inner)
    rows[WIDE : WIDE + length, :length] = np.sin(inner)
    rows[2 * WIDE : 2 * WIDE + groups, :length] = np.cos(turn)
    rows[2 * WIDE + groups :, :length] = np.sin(turn)
    coarse = rows.astype(jnp.bfloat16)
    rest = (rows - coarse.astype(np.float32)).astype(jnp.bfloat16)
    chunk = np.arange(groups)
    outer = np.zeros((2, groups, groups))
    for c in range(groups):
        phase = TURN * (chunk * wave_of[c] % groups) / groups
        if c < 2:
            outer[0, :, c] = outer[1, :, c] = np.cos(phase)
        elif c % 2 == 0:
            outer[0, :, c], outer[1, :, c] = 2 * np.cos(phase), -2 * np.sin(phase)
        else:
            outer[0, :, c], outer[1, :, c] = -2 * np.sin(phase), -2 * np.cos(phase)
    modes = wave_of[:, None] + groups * index[None, :]
    wave = np.zeros((groups, WIDE))
    wave[:, :length] = 4.0 * np.sin(np.pi * modes / period) ** 2
    return (
        np.stack([coarse, rest]),
        np.concatenate([outer[0], outer[1]], axis=1).astype(np.float32),
        wave.astype(np.float32),
    )


def real_fft(values):
    count = len(values)
    if count == 2:
        return [(values[0] + values[1], None), (values[0] - values[1], None)]
    even, odd = real_fft(values[0::2]), real_fft(values[1::2])
    out = [None] * (count // 2 + 1)
    for k in range(count // 4 + 1):
        (er, ei), (re, im) = even[k], odd[k]
        if k == 0:
            out[0], out[count // 2] = (er + re, None), (er - re, None)
        elif k == count // 4:
            out[k] = (er, -re)
        else:
            c, s = float(np.cos(TURN * k / count)), float(-np.sin(TURN * k / count))
            tr, ti = re * c - im * s, im * c + re * s
            out[k], out[count // 2 - k] = (er + tr, ei + ti), (er - tr, ti - ei)
    return out


def real_ifft(spectrum):
    count = 2 * (len(spectrum) - 1)
    if count == 2:
        return [spectrum[0][0] + spectrum[1][0], spectrum[0][0] - spectrum[1][0]]
    even, odd = [], []
    for k in range(count // 4 + 1):
        (ar, ai), (br, bi) = spectrum[k], spectrum[count // 2 - k]
        if k == 0:
            even.append((ar + br, None))
            odd.append((ar - br, None))
        elif k == count // 4:
            even.append((2.0 * ar, None))
            odd.append((-2.0 * ai, None))
        else:
            c, s = float(np.cos(TURN * k / count)), float(np.sin(TURN * k / count))
            dr, di = ar - br, ai + bi
            even.append((ar + br, ai - bi))
            odd.append((dr * c - di * s, dr * s + di * c))
    first, second = real_ifft(even), real_ifft(odd)
    out = []
    for a, b in zip(first, second, strict=True):
        out += [a, b]
    return out


def split(a):
    coarse = a.astype(jnp.bfloat16)
    return coarse, (a - coarse.astype(jnp.float32)).astype(jnp.bfloat16)


def product(a, b):
    (ac, ar), (bc, br) = a, b

    def one(x, y):
        return jnp.dot(x, y, preferred_element_type=jnp.float32)

    return one(ac, bc) + (one(ac, br) + one(ar, bc))


def dot(a, b):
    return product(split(a), split(b))


def table(matrix_ref, n):
    at = slice(n * WIDE, (n + 1) * WIDE)
    return matrix_ref[0, at, :], matrix_ref[1, at, :]


def load_twiddle(matrix_ref, twiddle):
    groups = twiddle.shape[1]
    for n in range(2):
        at = slice(2 * WIDE + n * groups, 2 * WIDE + (n + 1) * groups)
        twiddle[n] = matrix_ref[0, at, :].astype(jnp.float32) + matrix_ref[1, at, :].astype(
            jnp.float32
        )


def rows_of(p):
    return slice(ROWS * p, ROWS * (p + 1))


def lanes(shape):
    return lax.broadcasted_iota(jnp.int32, shape, len(shape) - 1)


def sublanes(shape):
    return lax.broadcasted_iota(jnp.int32, shape, len(shape) - 2)


def shifted(value, lanes_right):
    return pltpu.roll(value, lanes_right % value.shape[1], 1)


def pack_kernel(rhs_ref, own_ref, out_ref, tall):
    length = rhs_ref.shape[0]
    tall[:length, :] = rhs_ref[...]
    tall[length:, :] = own_ref[: WIDE - length, :]
    out_ref[...] = tall[...].T


def edges_kernel(mask_ref, north_ref, stag_ref, wet_ref, low_ref, tall):
    length, rows = mask_ref.shape
    count, block = stag_ref.shape[0], stag_ref.shape[1]
    tall[length:, :] = jnp.zeros((WIDE - length, 128), jnp.float32)
    tall[:length, :] = mask_ref[:, :128].astype(jnp.float32)
    wet_ref[...] = tall[...].T[:ROWS]
    tall[:length, :] = mask_ref[:, rows - 128 :].astype(jnp.float32) * north_ref[:, rows - 128 :]
    top = tall[...].T[127:]
    keep = block // 2 + ROWS
    low_ref[:keep, :] = stag_ref[count - 1, block - keep :, :]
    row = sublanes((ROWS, 128))
    low_ref[keep:, :] = jnp.where(row == 0, top[:, :128], top[:, 128:])


def lane_plan(length):
    cut = WIDE - length
    count = 2 * cut - length
    north = LATE
    east = north + length
    return cut, count, north, east, east + length - count


def pack_more_kernel(own_ref, mask_ref, east_ref, out_ref, tall):
    length, rows = mask_ref.shape
    cut, count = lane_plan(length)[:2]
    tall[:length, :] = jnp.zeros((length, rows), jnp.float32)
    tall[length : WIDE - count, :] = own_ref[cut:, :]
    tall[WIDE - count :, :] = (mask_ref[...].astype(jnp.float32) * east_ref[...])[:count]
    out_ref[...] = tall[...].T


def pack_rest_kernel(
    mask_ref,
    east_ref,
    north_ref,
    flags_ref,
    wet_above_ref,
    from_below_ref,
    out_ref,
    tall,
    aside,
    low,
    high,
    last,
):
    length, rows = mask_ref.shape
    _, count, n_at, e_at, f_at = lane_plan(length)
    block = from_below_ref.shape[0] - ROWS
    lane = lanes((length, rows))
    wet = mask_ref[...].astype(jnp.float32)
    north = wet * north_ref[...]
    wet_above = wet_above_ref[...].T[:length, :1] * flags_ref[:1, :1]
    top = from_below_ref[block:, :].T
    top_below = jnp.concatenate([top[:, :1], top[: length - 128, 1:2]], axis=0) * flags_ref[1:2, :1]
    tall[128:n_at, :] = jnp.zeros((n_at - 128, rows), jnp.float32)
    tall[n_at:e_at, :] = north * jnp.where(lane == rows - 1, wet_above, shifted(wet, -1))
    tall[e_at:f_at, :] = (wet * east_ref[...])[count:]
    tall[f_at:, :] = jnp.zeros((WIDE + 128 - f_at, rows), jnp.float32)
    out_ref[:, :128] = tall[128:WIDE, :].T
    last[...] = tall[WIDE:, :].T
    aside[length:, :] = jnp.zeros((WIDE - length, rows), jnp.float32)
    aside[:length, :] = wet * jnp.where(lane == 0, top_below, shifted(north, 1))
    low[...] = aside[:128, :].T
    high[...] = aside[128:, :].T
    groups = rows // ROWS
    at = pl.ds(0, groups, stride=ROWS)
    before = jnp.concatenate([low[at, :], high[at, :]], axis=1)
    fold = f_at - WIDE
    lane = lanes((groups, 128))
    for n in range(ROWS):
        at = pl.ds(n, groups, stride=ROWS)
        piece = shifted(before, fold - n * (128 - fold))[:, :128]
        last[at, :] = jnp.where(lane >= fold, piece, last[at, :])
    out_ref[:, 128:] = last[...]


def coefficients_kernel(groups, length, slab_ref, second_ref, own_ref, next_ref, east_ref):
    cut, count = lane_plan(length)[:2]
    lane = lanes((ROWS, WIDE))
    for p in range(groups):
        at = rows_of(p)
        more = second_ref[at, :]
        own_ref[at, :] = jnp.where(
            lane < cut,
            shifted(slab_ref[at, :], -length),
            jnp.where(lane < length, shifted(more, cut - length), 0.0),
        )
        east_ref[at, :] = jnp.where(lane < count, shifted(more, count), 0.0)
    for p in range(groups):
        own = own_ref[rows_of(p), :]
        after = own_ref[rows_of((p + 1) % groups), 0:1]
        ocean = jnp.where(lane == length, after, own) > 0.0
        next_ref[rows_of(p), :] = shifted(ocean.astype(jnp.float32), -1)


def transform(chunks, matrix_ref, twiddle_ref, left, right):
    groups = len(chunks)
    mixed = real_fft(chunks)
    for m in range(groups // 2 + 1):
        re, im = mixed[m]
        if m == 0:
            left[rows_of(0), :] = re
            right[rows_of(0), :] = re
            continue
        c = 1 if m == groups // 2 else 2 * m
        cos, sin = twiddle_ref[0, c : c + 1, :], twiddle_ref[1, c : c + 1, :]
        if m == groups // 2:
            left[rows_of(1), :] = re * (cos + sin)
            right[rows_of(1), :] = re * (cos - sin)
        else:
            tr, ti = re * cos + im * sin, im * cos - re * sin
            left[rows_of(c), :] = tr
            right[rows_of(c), :] = ti
            left[rows_of(c + 1), :] = ti
            right[rows_of(c + 1), :] = -tr
    return product(split(left[...]), table(matrix_ref, 0)) + product(
        split(right[...]), table(matrix_ref, 1)
    )


def both_products(spectrum, matrix_ref):
    parts = split(spectrum)
    return product(parts, table(matrix_ref, 0)), product(parts, table(matrix_ref, 1))


def transform_back(products, groups, twiddle_ref):
    pc, ps = products
    mixed = []
    for m in range(groups // 2 + 1):
        if m == 0:
            mixed.append((pc[rows_of(0)] + ps[rows_of(0)], None))
            continue
        c = 1 if m == groups // 2 else 2 * m
        cos, sin = twiddle_ref[0, c : c + 1, :], twiddle_ref[1, c : c + 1, :]
        if m == groups // 2:
            mixed.append((pc[rows_of(1)] * (cos + sin) + ps[rows_of(1)] * (cos - sin), None))
        else:
            hr = pc[rows_of(c)] - ps[rows_of(c + 1)]
            hi = ps[rows_of(c)] + pc[rows_of(c + 1)]
            mixed.append((hr * cos - hi * sin, hi * cos + hr * sin))
    return real_ifft(mixed)


def rows_back(products, start, twiddle_ref, outer_ref):
    groups = outer_ref.shape[0]
    cos, sin = twiddle_ref[0], twiddle_ref[1]
    turned = [[], []]
    for n in range(2):
        pc, ps = (v[start + n * groups : start + (n + 1) * groups] for v in products)
        turned[0].append(pc * cos - ps * sin)
        turned[1].append(ps * cos + pc * sin)
    both = jnp.concatenate([jnp.concatenate(v, axis=1) for v in turned], axis=0)
    both = dot(outer_ref[...], both)
    return both[:, :WIDE], both[:, WIDE:]


def forward_kernel(groups, field_ref, rest_ref, matrix_ref, out_ref, left, right, twiddle_ref):
    load_twiddle(matrix_ref, twiddle_ref)
    chunks = [field_ref[rows_of(p), :] for p in range(groups)]
    spectrum = transform(chunks, matrix_ref, twiddle_ref, left, right)
    out_ref[...] = spectrum + rest_ref[...]


def store_edge(ref, value, extra):
    half = value.shape[0]
    ref[:half, :] = value[:, :128]
    ref[half : half + ROWS, :] = jnp.concatenate(
        [value[:, 128:].T[:ROWS], jnp.zeros((ROWS, 128 - half), jnp.float32)], axis=1
    )
    ref[half + ROWS :, :] = extra


def load_edge(ref):
    half = ref.shape[0] - 2 * ROWS
    turned = ref[half : half + ROWS, :].T[:half]
    blank = jnp.zeros((half, 128 - ROWS), jnp.float32)
    return jnp.concatenate([ref[:half, :], turned, blank], axis=1)


def store_rows(ref, value, part, scale):
    row = sublanes((ROWS, 128))
    extra = jnp.where(row == 0, part[:, :128], part[:, 128:])
    store_edge(
        ref,
        value,
        jnp.where(row < 2, extra, jnp.where(row == 2, scale[:, :128], scale[:, 128:])),
    )


def load_rows(ref):
    at = ref.shape[0] - ROWS
    lines = [ref[at + n : at + n + 1, :] for n in range(4)]
    return jnp.concatenate(lines[:2], axis=1), jnp.concatenate(lines[2:], axis=1)


def blocks_kernel(spec_ref, scale_ref, aligned_ref, scaled_ref, part_ref, down_ref, up_ref):
    count, block = aligned_ref.shape[0], aligned_ref.shape[1]
    half, rows = block // 2, count * block
    scaled = spec_ref[...] * scale_ref[...]
    scaled_ref[...] = scaled
    for b in range(count):
        part_ref[b * block : (b + 1) * block, :] = dot(
            aligned_ref[b], scaled[b * block : (b + 1) * block]
        )
    store_rows(down_ref, scaled[:half], part_ref[:1, :], scale_ref[:1, :])
    store_rows(up_ref, scaled[rows - half :], part_ref[rows - 1 :, :], scale_ref[rows - 1 :, :])


def combine(
    norm, scaled_ref, part_ref, scale_ref, above_ref, below_ref, stag_ref, stag_below_ref, flags_ref
):
    count, block = stag_ref.shape[0], stag_ref.shape[1]
    half, rows = block // 2, count * block
    before = flags_ref[1:2, :] * dot(
        stag_below_ref[: ROWS + half, :],
        jnp.concatenate([load_edge(below_ref), scaled_ref[:half, :]], axis=0),
    )
    upper = load_edge(above_ref) * flags_ref[:1, :]
    pieces = [before[ROWS:]]
    for b in range(count - 1):
        pieces.append(dot(stag_ref[b], scaled_ref[half + b * block : half + (b + 1) * block, :]))
    after = dot(
        stag_ref[count - 1, : half + ROWS, :],
        jnp.concatenate([scaled_ref[rows - half :, :], upper], axis=0),
    )
    pieces.append(after[:half])
    full = (part_ref[...] + jnp.concatenate(pieces, axis=0)) * (scale_ref[...] * norm)
    return full, before, after


def halo_kernel(
    norm,
    scaled_ref,
    part_ref,
    scale_ref,
    above_ref,
    below_ref,
    stag_ref,
    stag_below_ref,
    flags_ref,
    late_ref,
    out_ref,
    low,
    high,
):
    half = stag_ref.shape[1] // 2
    full, before, after = combine(
        norm,
        scaled_ref,
        part_ref,
        scale_ref,
        above_ref,
        below_ref,
        stag_ref,
        stag_below_ref,
        flags_ref,
    )
    part, scale = load_rows(below_ref)
    row_below = (before[ROWS - 1 : ROWS] + part) * (scale * norm)
    part, scale = load_rows(above_ref)
    row_above = (after[half : half + 1] + part) * (scale * norm)
    out_ref[:, :128] = full[:, :128]
    low[...] = full[:, :128]
    high[...] = full[:, 128:]
    groups = full.shape[0] // ROWS

    def strided(start):
        at = pl.ds(start, groups, stride=ROWS)
        return jnp.concatenate([low[at, :], high[at, :]], axis=1)

    row = lax.broadcasted_iota(jnp.int32, (groups, WIDE), 0)
    up = jnp.where(row == 0, row_below, pltpu.roll(strided(ROWS - 1), 1, 0))
    down = jnp.where(row == groups - 1, row_above, pltpu.roll(strided(0), groups - 1, 0))
    lane = lanes((groups, 128)) + 128
    for s, part in enumerate(
        (
            pltpu.roll(up, HALO, 1),
            pltpu.roll(up, HALO - FOLD, 1),
            pltpu.roll(down, HALO, 1),
            pltpu.roll(down, HALO - FOLD, 1),
        )
    ):
        at = pl.ds(s, groups, stride=ROWS)
        high[at, :] = jnp.where(lane >= HALO, part[:, 128:], high[at, :])
    out_ref[:, 128:WIDE] = jnp.where(
        lanes(high.shape) < LATE - 128, high[...], late_ref[:, :128]
    )
    out_ref[:, WIDE:] = late_ref[:, 128:]


def sums_kernel(
    norm,
    length,
    spec_ref,
    scale_ref,
    aligned_ref,
    stag_ref,
    stag_below_ref,
    flags_ref,
    sums_ref,
    scaled_ref,
    part_ref,
    down_ref,
    up_ref,
    own_ref,
):
    count, block = aligned_ref.shape[0], aligned_ref.shape[1]
    half, rows = block // 2, count * block
    scaled = spec_ref[...] * scale_ref[...]
    scaled_ref[...] = scaled
    for b in range(count):
        at = slice(b * block, (b + 1) * block)
        part_ref[at, :] = dot(aligned_ref[b], scaled[at])
    for b in range(count - 1):
        at = slice(half + b * block, half + (b + 1) * block)
        part_ref[at, :] = part_ref[at, :] + dot(stag_ref[b], scaled[at])
    first, last = slice(0, half), slice(rows - half, rows)
    part_ref[first, :] = part_ref[first, :] + flags_ref[1:2, :] * dot(
        stag_below_ref[ROWS : ROWS + half, half:], scaled[first]
    )
    part_ref[last, :] = part_ref[last, :] + dot(stag_ref[count - 1, :half, :half], scaled[last])
    total = total_of(scaled * part_ref[...], length) * (flags_ref[2:3, :1] * norm)
    small = lanes((8, 128))
    own = jnp.where(small == SCALARS - 128 + 2, total, sums_ref[...])
    own_ref[...] = own
    store_edge(down_ref, scaled[first], own)
    store_edge(up_ref, scaled[last], own)


def total_of(value, length):
    columns = jnp.sum(value, axis=0, keepdims=True)
    columns = jnp.where(lanes(columns.shape) < length, columns, 0.0)
    return jnp.sum(columns[:, :128] + columns[:, 128:], axis=1, keepdims=True)


def ends_kernel(
    norm,
    length,
    scaled_ref,
    part_ref,
    scale_ref,
    above_ref,
    below_ref,
    stag_ref,
    stag_below_ref,
    flags_ref,
    aside_ref,
    own_ref,
    out_ref,
):
    count, block = stag_ref.shape[0], stag_ref.shape[1]
    half, rows = block // 2, count * block
    first, last = slice(0, half), slice(rows - half, rows)
    low = dot(stag_below_ref[ROWS : ROWS + half, :half], load_edge(below_ref)) * flags_ref[1:2, :]
    high = dot(stag_ref[count - 1, :half, half:], load_edge(above_ref)) * flags_ref[:1, :]
    both = total_of(low * scaled_ref[first, :] + high * scaled_ref[last, :], length)
    both = both * (flags_ref[2:3, :1] * (2.0 * norm))
    pair = own_ref[:1, :] + below_ref[half + ROWS : half + ROWS + 1, :]
    pair = jnp.where(lanes(pair.shape) == SCALARS - 128 + 2, pair + both, pair)
    middle = slice(half, rows - half)
    for at, more in ((first, low), (middle, None), (last, high)):
        full = part_ref[at, :] if more is None else part_ref[at, :] + more
        full = full * (scale_ref[at, :] * norm)
        full = jnp.where(lanes(full.shape) < length, full, aside_ref[at, :])
        out_ref[at, :128] = full[:, :128]
        inside = lanes((full.shape[0], 128)) < SCALARS - 128
        out_ref[at, 128:] = jnp.where(inside, full[:, 128:], pair)


def gather_kernel(spec_ref, sums_ref):
    riders = jnp.sum(spec_ref[:, 128:], axis=0, keepdims=True) * (1.0 / ROWS)
    sums_ref[...] = jnp.broadcast_to(riders, (8, 128))


def step_kernel(
    groups,
    length,
    spec_ref,
    rhs_ref,
    own_ref,
    next_ref,
    east_ref,
    matrix_ref,
    outer_ref,
    out_ref,
    first_ref,
    image_ref,
    sums_ref,
    left,
    right,
    low,
    high,
    tail,
    folded,
    twiddle_ref,
):
    load_twiddle(matrix_ref, twiddle_ref)
    lane_row = lanes((groups, WIDE))
    stride = 3 * ROWS
    tail[...] = spec_ref[:, 128:WIDE]

    def halo_row(s):
        blank = jnp.zeros((groups, 128), jnp.float32)
        parts = [
            jnp.concatenate([tail[pl.ds(s + n, groups, stride=ROWS), :], blank], axis=1)
            for n in range(2)
        ]
        return jnp.where(
            lane_row < FOLD, shifted(parts[0], 128 - HALO), shifted(parts[1], FOLD + 128 - HALO)
        )

    stacked = jnp.concatenate([spec_ref[:, :WIDE], halo_row(0), halo_row(2)], axis=0)
    products = both_products(stacked, matrix_ref)
    halos = rows_back(products, groups * ROWS, twiddle_ref, outer_ref)
    for start, row in zip((ROWS - 1, 2 * ROWS), halos, strict=True):
        low[pl.ds(start, groups, stride=stride), :] = row[:, :128]
        high[pl.ds(start, groups, stride=stride), :] = row[:, 128:]

    def neighbour(start):
        at = slice(start, start + ROWS)
        return jnp.concatenate([low[at, :], high[at, :]], axis=1)

    cells = transform_back(products, groups, twiddle_ref)
    for p in range(groups):
        v = jnp.where(own_ref[rows_of(p), :] > 0.0, cells[p], 0.0)
        first_ref[rows_of(p), :] = v
        low[stride * p + ROWS : stride * p + 2 * ROWS, :] = v[:, :128]
        high[stride * p + ROWS : stride * p + 2 * ROWS, :] = v[:, 128:]
    lane, row = lanes((ROWS, WIDE)), sublanes((ROWS, WIDE))
    _, count, n_at, e_at, f_at = lane_plan(length)
    tail[...] = spec_ref[:, WIDE:]
    fold, blank = f_at - WIDE, jnp.zeros((groups, 128), jnp.float32)
    width = 128 - fold
    before = jnp.zeros((groups, WIDE), jnp.float32)
    for n in range(ROWS):
        piece = jnp.concatenate([tail[pl.ds(n, groups, stride=ROWS), :], blank], axis=1)
        inside = (lane_row >= n * width) & (lane_row < (n + 1) * width)
        before = jnp.where(inside, shifted(piece, n * width - fold), before)
    folded[...] = before
    rz = jnp.zeros((ROWS, WIDE), jnp.float32)
    curvature = jnp.zeros((ROWS, WIDE), jnp.float32)
    images, fluxes = [], []
    for p in range(groups):
        at = rows_of(p)
        v = first_ref[at, :]
        after = first_ref[rows_of((p + 1) % groups), 0:1]
        east = jnp.where(
            lane < count, east_ref[at, :], shifted(spec_ref[at, 128:], count - (e_at - 128))
        )
        flux = v - shifted(jnp.where(lane == length, after, v), -1)
        fluxes.append(jnp.where(lane < length, east * next_ref[at, :] * flux, 0.0))
    for p in range(groups):
        at = rows_of(p)
        v = first_ref[at, :]
        before = fluxes[(p - 1) % groups][:, length - 1 : length]
        flux = fluxes[p]
        own = own_ref[at, :]
        base = stride * p + ROWS
        north = shifted(spec_ref[at, 128:], 128 - n_at)
        south = jnp.where(row == 0, folded[p : p + 1, :], pltpu.roll(north, 1, 0))
        image = jnp.where(own > 0.0, own, 1.0) * v
        image = image + (flux - shifted(jnp.where(lane == WIDE - 1, before, flux), 1))
        image = image + north * (v - neighbour(base + 1))
        image = image + south * (v - neighbour(base - 1))
        image = jnp.where(lane < length, image, 0.0)
        image_ref[at, :] = image
        images.append(image)
        rz = rz + rhs_ref[at, :] * v
        curvature = curvature + v * image
    small = lanes((8, 128))
    at = SCALARS - 128
    sums_ref[...] = jnp.where(
        small == at, jnp.sum(rz), jnp.where(small == at + 1, jnp.sum(curvature), 0.0)
    )
    spectrum = transform(images, matrix_ref, twiddle_ref, left, right)
    out_ref[...] = jnp.where(
        lanes(out_ref.shape) < length, spectrum, shifted(first_ref[...], length)
    )


def last_kernel(
    groups,
    length,
    spec_ref,
    own_ref,
    first_ref,
    image_ref,
    matrix_ref,
    out_ref,
    twiddle_ref,
):
    load_twiddle(matrix_ref, twiddle_ref)
    cells = transform_back(both_products(spec_ref[...], matrix_ref), groups, twiddle_ref)
    lane = lanes((ROWS, WIDE))
    cut = WIDE - length
    image_cut = SCALARS - length
    image_at = 2 * length - cut
    for p in range(groups):
        at = rows_of(p)
        cell = jnp.where(own_ref[at, :] > 0.0, cells[p], 0.0)
        out = jnp.where(lane < length, cell, shifted(first_ref[at, :], length - cut))
        out_ref[at, :] = jnp.where(
            lane < image_at, out, shifted(image_ref[at, :], image_at - image_cut)
        )


def unpack_kernel(length, count, slab_ref, out_ref):
    turned = slab_ref[:, 128:].T
    out_ref[:count, :] = turned[length - 128 : length - 128 + count]


def unpack_first_kernel(length, count, slab_ref, image_ref, out_ref, aside_ref):
    unpack_kernel(length, count, slab_ref, out_ref)
    lane = lanes(image_ref.shape)
    aside_ref[...] = jnp.where(lane < length, 0.0, shifted(image_ref[...], length))


def finish_kernel(
    length,
    back_ref,
    first_ref,
    image_ref,
    forcing_ref,
    mask_ref,
    pair_ref,
    ahead_ref,
    behind_ref,
    across_ref,
    solution_ref,
    residual_ref,
    direction_ref,
):
    at = SCALARS - 128
    totals = (pair_ref[:1, :] + across_ref[:1, :]) + (ahead_ref[:1, :] + behind_ref[:1, :])
    rz, curvature, own = [totals[:, at + n : at + n + 1] for n in range(3)]
    alpha = rz / curvature
    rz_next = rz - 2.0 * alpha * curvature + alpha * alpha * own
    beta = rz_next / rz
    back = back_ref[...].T
    cut = WIDE - length
    image_cut = SCALARS - length
    image_at = 2 * length - cut
    rhs = mask_ref[...].astype(jnp.float32) * forcing_ref[...]

    def store(where, rows_back, first):
        solution_ref[where, :] = alpha * first
        direction_ref[where, :] = (first - alpha * rows_back) + beta * first

    store(slice(0, cut), back[:cut], first_ref[:cut, :])
    store(slice(cut, length), back[cut:length], back[length:image_at])
    residual_ref[:image_cut, :] = rhs[:image_cut] - alpha * image_ref[:image_cut, :]
    residual_ref[image_cut:, :] = (
        rhs[image_cut:] - alpha * back[image_at : image_at + length - image_cut]
    )


def call(kernel, out_shapes, scratch=(), name=None):
    single = not isinstance(out_shapes, (list, tuple)) or isinstance(out_shapes[0], int)
    shapes = [out_shapes] if single else out_shapes
    outs = [jax.ShapeDtypeStruct(s, jnp.float32) for s in shapes]
    return pl.pallas_call(
        kernel,
        out_shape=outs[0] if single else outs,
        scratch_shapes=[pltpu.VMEM(s, jnp.float32) for s in scratch],
        compiler_params=pltpu.CompilerParams(vmem_limit_bytes=16 * 2**20),
        name=name,
    )


def exchanged(value):
    groups = lax.axis_size(LON)
    parts = value.reshape(groups, ROWS, value.shape[-1])
    return lax.all_to_all(parts, LON, split_axis=0, concat_axis=0, tiled=True).reshape(value.shape)


def from_lat(value, steps):
    count = lax.axis_size("lat")
    return lax.ppermute(value, "lat", [((d + steps) % count, d) for d in range(count)])


def after(value, *others):
    return lax.optimization_barrier((value, *others))[0]


def local(
    surface_forcing,
    ocean_mask,
    self_coupling,
    east_coupling,
    north_coupling,
    zonal_weight,
    aligned_inverse,
    staggered_inverse,
):
    groups = lax.axis_size(LON)
    length, rows = surface_forcing.shape
    norm = 1.0 / (groups * length)
    matrices, outer, wave = tables(groups, length)
    count, block = aligned_inverse.shape[0], aligned_inverse.shape[1]
    half = block // 2
    wide = (rows, WIDE)
    turns = [(2, groups, WIDE)]
    transforms = [wide, wide]

    cells = (length, rows)
    places = (lax.axis_index(LON), lax.axis_index("lat"))
    flag_row = lax.broadcasted_iota(jnp.int32, (8, WIDE), 0)
    surface_forcing, channel, lat = lax.optimization_barrier((surface_forcing, *places))
    wet_cells = ocean_mask.astype(jnp.float32)
    own_cells = wet_cells * self_coupling
    packed = call(pack_kernel, wide, [wide], name="pack")(wet_cells * surface_forcing, own_cells)
    slab = exchanged(packed)

    mask, east_cells = lax.optimization_barrier((ocean_mask, east_coupling, slab))[:2]
    more = call(pack_more_kernel, wide, [wide], name="pack_more")(own_cells, mask, east_cells)
    spectrum = call(lambda *r: forward_kernel(groups, *r), wide, transforms + turns, name="forward")(
        slab, more, matrices
    )
    spec_rhs = exchanged(spectrum)

    north_cells, stag = lax.optimization_barrier((north_coupling, staggered_inverse, spectrum))[:-1]
    wet_first, low_last = call(
        edges_kernel, [(ROWS, WIDE), (half + 2 * ROWS, 128)], [(WIDE, 128)], name="edges"
    )(mask, north_cells, stag)
    weights, channel, lat, flag_row = lax.optimization_barrier(
        (
            zonal_weight,
            channel,
            lat,
            flag_row,
            wet_first,
        )
    )[:-1]
    scale = lax.rsqrt(1.0 + weights[:, None] * lax.dynamic_slice_in_dim(wave, channel, 1, 0))
    north_of, south_of, weight = (
        jnp.where(condition, yes, no).astype(jnp.float32)
        for condition, yes, no in (
            (lat < lax.axis_size("lat") - 1, 1.0, 0.0),
            (lat > 0, 1.0, 0.0),
            (channel < 2, 1.0, 2.0),
        )
    )
    flags = jnp.where(flag_row == 0, north_of, jnp.where(flag_row == 1, south_of, weight))
    stag_below = from_lat(low_last, -1)
    late = call(
        pack_rest_kernel,
        wide,
        [(WIDE + 128, rows), wide, (rows, 128), (rows, 128), (rows, 128)],
        name="pack_rest",
    )(mask, east_cells, north_cells, flags, from_lat(wet_first, 1), stag_below)
    spec_rhs = after(spec_rhs, late, scale, flags)

    edge = (half + 2 * ROWS, 128)

    def blocks(spectrum):
        scaled, part, down, up = call(blocks_kernel, [wide, wide, edge, edge], name="blocks")(
            spectrum, scale, aligned_inverse
        )
        above, below = from_lat(down, 1), from_lat(up, -1)
        return scaled, part, scale, above, below, stag, stag_below, flags

    pieces = blocks(spec_rhs)
    flat = call(
        lambda *r: coefficients_kernel(groups, length, *r), [wide] * 3, name="coefficients"
    )(slab, after(spec_rhs, pieces[0]))
    late = after(late, *flat)
    filtered = exchanged(
        call(
            lambda *r: halo_kernel(norm, *r), (rows, WIDE + 128), [(rows, 128)] * 2, name="halo"
        )(*pieces, late)
    )
    spec, first, image, sums = call(
        lambda *r: step_kernel(groups, length, *r),
        [wide, wide, wide, (8, 128)],
        transforms + [(3 * rows, 128)] * 2 + [(rows, 128), (groups, WIDE)] + turns,
        name="step",
    )(filtered, slab, *flat, matrices, outer)
    spec_image = exchanged(spec)
    scaled, part, down, up, own = call(
        lambda *r: sums_kernel(norm, length, *r), [wide, wide, edge, edge, (8, 128)], name="sums"
    )(spec_image, scale, aligned_inverse, stag, stag_below, flags, sums)
    above, below = from_lat(down, 1), from_lat(up, -1)
    cut, image_cut = WIDE - length, SCALARS - length
    first_cells, aside = call(
        lambda *r: unpack_first_kernel(length, cut, *r), [cells, wide], name="unpack_first"
    )(after(spec_image, scaled), image)
    filtered = exchanged(
        call(lambda *r: ends_kernel(norm, length, *r), wide, name="ends")(
            scaled, part, scale, above, below, stag, stag_below, flags, aside, own
        )
    )

    pair = call(gather_kernel, (8, 128), name="gather")(filtered)
    image_cells = call(
        lambda *r: unpack_kernel(length, image_cut, *r), cells, name="unpack_image"
    )(filtered)
    packed = call(lambda *r: last_kernel(groups, length, *r), wide, turns, name="last")(
        filtered, flat[0], first, image, matrices
    )
    return tuple(
        call(lambda *r: finish_kernel(length, *r), [cells] * 3, name="finish")(
            exchanged(packed),
            first_cells,
            image_cells,
            surface_forcing,
            ocean_mask,
            pair,
            from_lat(pair, 2),
            from_lat(pair, -2),
            from_lat(pair, 4),
        )
    )


def solution(mesh):
    torus = Mesh(
        mesh.devices.reshape(mesh.shape["lat"], 4, 4, 2), ("lat", "lon_0", "lon_1", "lon_2")
    )
    return jax.shard_map(
        local,
        mesh=torus,
        in_specs=(
            P(LON, "lat"),
            P(LON, "lat"),
            P(LON, "lat"),
            P(LON, "lat"),
            P(LON, "lat"),
            P("lat"),
            P("lat", None, None),
            P("lat", None, None),
        ),
        out_specs=(P(LON, "lat"), P(LON, "lat"), P(LON, "lat")),
        check_vma=False,
    )
```

```python
import jax
import jax.numpy as jnp
import numpy as np
from jax import lax
from jax.experimental import pallas as pl
from jax.experimental.pallas import tpu as pltpu
from jax.sharding import Mesh
from jax.sharding import PartitionSpec as P

LON = ("lon_0", "lon_1", "lon_2")
TURN = 2.0 * np.pi
ROWS = 8
WIDE = 256
HALO = 136
FOLD = 68
LATE = HALO + FOLD
SCALARS = WIDE - 4


def tables(groups, length):
    period = groups * length
    index = np.arange(length)
    inner = TURN * (np.outer(index, index) % length) / length
    wave_of = np.zeros(groups, np.int64)
    wave_of[1] = groups // 2
    for m in range(1, groups // 2):
        wave_of[2 * m] = wave_of[2 * m + 1] = m
    turn = TURN * (np.outer(wave_of, index) % period) / period
    rows = np.zeros((2 * WIDE + 2 * groups, WIDE), np.float32)
    rows[:length, :length] = np.cos(inner)
    rows[WIDE : WIDE + length, :length] = np.sin(inner)
    rows[2 * WIDE : 2 * WIDE + groups, :length] = np.cos(turn)
    rows[2 * WIDE + groups :, :length] = np.sin(turn)
    coarse = rows.astype(jnp.bfloat16)
    rest = (rows - coarse.astype(np.float32)).astype(jnp.bfloat16)
    chunk = np.arange(groups)
    outer = np.zeros((2, groups, groups))
    for c in range(groups):
        phase = TURN * (chunk * wave_of[c] % groups) / groups
        if c < 2:
            outer[0, :, c] = outer[1, :, c] = np.cos(phase)
        elif c % 2 == 0:
            outer[0, :, c], outer[1, :, c] = 2 * np.cos(phase), -2 * np.sin(phase)
        else:
            outer[0, :, c], outer[1, :, c] = -2 * np.sin(phase), -2 * np.cos(phase)
    modes = wave_of[:, None] + groups * index[None, :]
    wave = np.zeros((groups, WIDE))
    wave[:, :length] = 4.0 * np.sin(np.pi * modes / period) ** 2
    return (
        np.stack([coarse, rest]),
        np.concatenate([outer[0], outer[1]], axis=1).astype(np.float32),
        wave.astype(np.float32),
    )


def real_fft(values):
    count = len(values)
    if count == 2:
        return [(values[0] + values[1], None), (values[0] - values[1], None)]
    even, odd = real_fft(values[0::2]), real_fft(values[1::2])
    out = [None] * (count // 2 + 1)
    for k in range(count // 4 + 1):
        (er, ei), (re, im) = even[k], odd[k]
        if k == 0:
            out[0], out[count // 2] = (er + re, None), (er - re, None)
        elif k == count // 4:
            out[k] = (er, -re)
        else:
            c, s = float(np.cos(TURN * k / count)), float(-np.sin(TURN * k / count))
            tr, ti = re * c - im * s, im * c + re * s
            out[k], out[count // 2 - k] = (er + tr, ei + ti), (er - tr, ti - ei)
    return out


def real_ifft(spectrum):
    count = 2 * (len(spectrum) - 1)
    if count == 2:
        return [spectrum[0][0] + spectrum[1][0], spectrum[0][0] - spectrum[1][0]]
    even, odd = [], []
    for k in range(count // 4 + 1):
        (ar, ai), (br, bi) = spectrum[k], spectrum[count // 2 - k]
        if k == 0:
            even.append((ar + br, None))
            odd.append((ar - br, None))
        elif k == count // 4:
            even.append((2.0 * ar, None))
            odd.append((-2.0 * ai, None))
        else:
            c, s = float(np.cos(TURN * k / count)), float(np.sin(TURN * k / count))
            dr, di = ar - br, ai + bi
            even.append((ar + br, ai - bi))
            odd.append((dr * c - di * s, dr * s + di * c))
    first, second = real_ifft(even), real_ifft(odd)
    out = []
    for a, b in zip(first, second, strict=True):
        out += [a, b]
    return out


def split(a):
    coarse = a.astype(jnp.bfloat16)
    return coarse, (a - coarse.astype(jnp.float32)).astype(jnp.bfloat16)


def product(a, b):
    (ac, ar), (bc, br) = a, b

    def one(x, y):
        return jnp.dot(x, y, preferred_element_type=jnp.float32)

    return one(ac, bc) + (one(ac, br) + one(ar, bc))


def dot(a, b):
    return product(split(a), split(b))


def table(matrix_ref, n):
    at = slice(n * WIDE, (n + 1) * WIDE)
    return matrix_ref[0, at, :], matrix_ref[1, at, :]


def load_twiddle(matrix_ref, twiddle):
    groups = twiddle.shape[1]
    for n in range(2):
        at = slice(2 * WIDE + n * groups, 2 * WIDE + (n + 1) * groups)
        twiddle[n] = matrix_ref[0, at, :].astype(jnp.float32) + matrix_ref[1, at, :].astype(
            jnp.float32
        )


def rows_of(p):
    return slice(ROWS * p, ROWS * (p + 1))


def lanes(shape):
    return lax.broadcasted_iota(jnp.int32, shape, len(shape) - 1)


def sublanes(shape):
    return lax.broadcasted_iota(jnp.int32, shape, len(shape) - 2)


def shifted(value, lanes_right):
    return pltpu.roll(value, lanes_right % value.shape[1], 1)


def pack_kernel(rhs_ref, own_ref, out_ref, tall):
    length = rhs_ref.shape[0]
    tall[:length, :] = rhs_ref[...]
    tall[length:, :] = own_ref[: WIDE - length, :]
    out_ref[...] = tall[...].T


def edges_kernel(mask_ref, north_ref, stag_ref, wet_ref, low_ref, tall):
    length, rows = mask_ref.shape
    count, block = stag_ref.shape[0], stag_ref.shape[1]
    tall[length:, :] = jnp.zeros((WIDE - length, 128), jnp.float32)
    tall[:length, :] = mask_ref[:, :128].astype(jnp.float32)
    wet_ref[...] = tall[...].T[:ROWS]
    tall[:length, :] = mask_ref[:, rows - 128 :].astype(jnp.float32) * north_ref[:, rows - 128 :]
    top = tall[...].T[127:]
    keep = block // 2 + ROWS
    low_ref[:keep, :] = stag_ref[count - 1, block - keep :, :]
    row = sublanes((ROWS, 128))
    low_ref[keep:, :] = jnp.where(row == 0, top[:, :128], top[:, 128:])


def lane_plan(length):
    cut = WIDE - length
    count = 2 * cut - length
    north = LATE
    east = north + length
    return cut, count, north, east, east + length - count


def pack_more_kernel(own_ref, mask_ref, east_ref, out_ref, tall):
    length, rows = mask_ref.shape
    cut, count = lane_plan(length)[:2]
    tall[:length, :] = jnp.zeros((length, rows), jnp.float32)
    tall[length : WIDE - count, :] = own_ref[cut:, :]
    tall[WIDE - count :, :] = (mask_ref[...].astype(jnp.float32) * east_ref[...])[:count]
    out_ref[...] = tall[...].T


def pack_rest_kernel(
    mask_ref,
    east_ref,
    north_ref,
    flags_ref,
    wet_above_ref,
    from_below_ref,
    out_ref,
    tall,
    aside,
    low,
    high,
    last,
):
    length, rows = mask_ref.shape
    _, count, n_at, e_at, f_at = lane_plan(length)
    block = from_below_ref.shape[0] - ROWS
    lane = lanes((length, rows))
    wet = mask_ref[...].astype(jnp.float32)
    north = wet * north_ref[...]
    wet_above = wet_above_ref[...].T[:length, :1] * flags_ref[:1, :1]
    top = from_below_ref[block:, :].T
    top_below = jnp.concatenate([top[:, :1], top[: length - 128, 1:2]], axis=0) * flags_ref[1:2, :1]
    tall[128:n_at, :] = jnp.zeros((n_at - 128, rows), jnp.float32)
    tall[n_at:e_at, :] = north * jnp.where(lane == rows - 1, wet_above, shifted(wet, -1))
    tall[e_at:f_at, :] = (wet * east_ref[...])[count:]
    tall[f_at:, :] = jnp.zeros((WIDE + 128 - f_at, rows), jnp.float32)
    out_ref[:, :128] = tall[128:WIDE, :].T
    last[...] = tall[WIDE:, :].T
    aside[length:, :] = jnp.zeros((WIDE - length, rows), jnp.float32)
    aside[:length, :] = wet * jnp.where(lane == 0, top_below, shifted(north, 1))
    low[...] = aside[:128, :].T
    high[...] = aside[128:, :].T
    groups = rows // ROWS
    at = pl.ds(0, groups, stride=ROWS)
    before = jnp.concatenate([low[at, :], high[at, :]], axis=1)
    fold = f_at - WIDE
    lane = lanes((groups, 128))
    for n in range(ROWS):
        at = pl.ds(n, groups, stride=ROWS)
        piece = shifted(before, fold - n * (128 - fold))[:, :128]
        last[at, :] = jnp.where(lane >= fold, piece, last[at, :])
    out_ref[:, 128:] = last[...]


def coefficients_kernel(groups, length, slab_ref, second_ref, own_ref, next_ref, east_ref):
    cut, count = lane_plan(length)[:2]
    lane = lanes((ROWS, WIDE))
    for p in range(groups):
        at = rows_of(p)
        more = second_ref[at, :]
        own_ref[at, :] = jnp.where(
            lane < cut,
            shifted(slab_ref[at, :], -length),
            jnp.where(lane < length, shifted(more, cut - length), 0.0),
        )
        east_ref[at, :] = jnp.where(lane < count, shifted(more, count), 0.0)
    for p in range(groups):
        own = own_ref[rows_of(p), :]
        after = own_ref[rows_of((p + 1) % groups), 0:1]
        ocean = jnp.where(lane == length, after, own) > 0.0
        next_ref[rows_of(p), :] = shifted(ocean.astype(jnp.float32), -1)


def transform(chunks, matrix_ref, twiddle_ref, left, right):
    groups = len(chunks)
    mixed = real_fft(chunks)
    for m in range(groups // 2 + 1):
        re, im = mixed[m]
        if m == 0:
            left[rows_of(0), :] = re
            right[rows_of(0), :] = re
            continue
        c = 1 if m == groups // 2 else 2 * m
        cos, sin = twiddle_ref[0, c : c + 1, :], twiddle_ref[1, c : c + 1, :]
        if m == groups // 2:
            left[rows_of(1), :] = re * (cos + sin)
            right[rows_of(1), :] = re * (cos - sin)
        else:
            tr, ti = re * cos + im * sin, im * cos - re * sin
            left[rows_of(c), :] = tr
            right[rows_of(c), :] = ti
            left[rows_of(c + 1), :] = ti
            right[rows_of(c + 1), :] = -tr
    return product(split(left[...]), table(matrix_ref, 0)) + product(
        split(right[...]), table(matrix_ref, 1)
    )


def both_products(spectrum, matrix_ref):
    parts = split(spectrum)
    return product(parts, table(matrix_ref, 0)), product(parts, table(matrix_ref, 1))


def transform_back(products, groups, twiddle_ref):
    pc, ps = products
    mixed = []
    for m in range(groups // 2 + 1):
        if m == 0:
            mixed.append((pc[rows_of(0)] + ps[rows_of(0)], None))
            continue
        c = 1 if m == groups // 2 else 2 * m
        cos, sin = twiddle_ref[0, c : c + 1, :], twiddle_ref[1, c : c + 1, :]
        if m == groups // 2:
            mixed.append((pc[rows_of(1)] * (cos + sin) + ps[rows_of(1)] * (cos - sin), None))
        else:
            hr = pc[rows_of(c)] - ps[rows_of(c + 1)]
            hi = ps[rows_of(c)] + pc[rows_of(c + 1)]
            mixed.append((hr * cos - hi * sin, hi * cos + hr * sin))
    return real_ifft(mixed)


def rows_back(products, start, twiddle_ref, outer_ref):
    groups = outer_ref.shape[0]
    cos, sin = twiddle_ref[0], twiddle_ref[1]
    turned = [[], []]
    for n in range(2):
        pc, ps = (v[start + n * groups : start + (n + 1) * groups] for v in products)
        turned[0].append(pc * cos - ps * sin)
        turned[1].append(ps * cos + pc * sin)
    both = jnp.concatenate([jnp.concatenate(v, axis=1) for v in turned], axis=0)
    both = dot(outer_ref[...], both)
    return both[:, :WIDE], both[:, WIDE:]


def forward_kernel(groups, field_ref, rest_ref, matrix_ref, out_ref, left, right, twiddle_ref):
    load_twiddle(matrix_ref, twiddle_ref)
    chunks = [field_ref[rows_of(p), :] for p in range(groups)]
    spectrum = transform(chunks, matrix_ref, twiddle_ref, left, right)
    out_ref[...] = spectrum + rest_ref[...]


def store_edge(ref, value, extra):
    half = value.shape[0]
    ref[:half, :] = value[:, :128]
    ref[half : half + ROWS, :] = jnp.concatenate(
        [value[:, 128:].T[:ROWS], jnp.zeros((ROWS, 128 - half), jnp.float32)], axis=1
    )
    ref[half + ROWS :, :] = extra


def load_edge(ref):
    half = ref.shape[0] - 2 * ROWS
    turned = ref[half : half + ROWS, :].T[:half]
    blank = jnp.zeros((half, 128 - ROWS), jnp.float32)
    return jnp.concatenate([ref[:half, :], turned, blank], axis=1)


def store_rows(ref, value, part, scale):
    row = sublanes((ROWS, 128))
    extra = jnp.where(row == 0, part[:, :128], part[:, 128:])
    store_edge(
        ref,
        value,
        jnp.where(row < 2, extra, jnp.where(row == 2, scale[:, :128], scale[:, 128:])),
    )


def load_rows(ref):
    at = ref.shape[0] - ROWS
    lines = [ref[at + n : at + n + 1, :] for n in range(4)]
    return jnp.concatenate(lines[:2], axis=1), jnp.concatenate(lines[2:], axis=1)


def blocks_kernel(spec_ref, scale_ref, aligned_ref, scaled_ref, down_ref, up_ref):
    count, block = aligned_ref.shape[0], aligned_ref.shape[1]
    half, rows = block // 2, count * block
    scaled = spec_ref[...] * scale_ref[...]
    scaled_ref[...] = scaled
    first = dot(aligned_ref[0, :ROWS, :], scaled[:block])
    last = dot(aligned_ref[count - 1, block - ROWS :, :], scaled[rows - block :])
    store_rows(down_ref, scaled[:half], first[:1], scale_ref[:1, :])
    store_rows(up_ref, scaled[rows - half :], last[ROWS - 1 :], scale_ref[rows - 1 :, :])


def inner_kernel(scaled_ref, aligned_ref, stag_ref, part_ref):
    count, block = aligned_ref.shape[0], aligned_ref.shape[1]
    half = block // 2
    for b in range(count):
        at = slice(b * block, (b + 1) * block)
        part_ref[at, :] = dot(aligned_ref[b], scaled_ref[at, :])
    for b in range(count - 1):
        at = slice(half + b * block, half + (b + 1) * block)
        part_ref[at, :] = part_ref[at, :] + dot(stag_ref[b], scaled_ref[at, :])


def combine(
    norm, scaled_ref, part_ref, scale_ref, above_ref, below_ref, stag_ref, stag_below_ref, flags_ref
):
    count, block = stag_ref.shape[0], stag_ref.shape[1]
    half, rows = block // 2, count * block
    before = flags_ref[1:2, :] * dot(
        stag_below_ref[: ROWS + half, :],
        jnp.concatenate([load_edge(below_ref), scaled_ref[:half, :]], axis=0),
    )
    upper = load_edge(above_ref) * flags_ref[:1, :]
    after = dot(
        stag_ref[count - 1, : half + ROWS, :],
        jnp.concatenate([scaled_ref[rows - half :, :], upper], axis=0),
    )
    pieces = [
        part_ref[:half, :] + before[ROWS:],
        part_ref[half : rows - half, :],
        part_ref[rows - half :, :] + after[:half],
    ]
    full = jnp.concatenate(pieces, axis=0) * (scale_ref[...] * norm)
    return full, before, after


def halo_kernel(
    norm,
    scaled_ref,
    part_ref,
    scale_ref,
    above_ref,
    below_ref,
    stag_ref,
    stag_below_ref,
    flags_ref,
    late_ref,
    out_ref,
    low,
    high,
):
    half = stag_ref.shape[1] // 2
    full, before, after = combine(
        norm,
        scaled_ref,
        part_ref,
        scale_ref,
        above_ref,
        below_ref,
        stag_ref,
        stag_below_ref,
        flags_ref,
    )
    part, scale = load_rows(below_ref)
    row_below = (before[ROWS - 1 : ROWS] + part) * (scale * norm)
    part, scale = load_rows(above_ref)
    row_above = (after[half : half + 1] + part) * (scale * norm)
    out_ref[:, :128] = full[:, :128]
    low[...] = full[:, :128]
    high[...] = full[:, 128:]
    groups = full.shape[0] // ROWS

    def strided(start):
        at = pl.ds(start, groups, stride=ROWS)
        return jnp.concatenate([low[at, :], high[at, :]], axis=1)

    row = lax.broadcasted_iota(jnp.int32, (groups, WIDE), 0)
    up = jnp.where(row == 0, row_below, pltpu.roll(strided(ROWS - 1), 1, 0))
    down = jnp.where(row == groups - 1, row_above, pltpu.roll(strided(0), groups - 1, 0))
    lane = lanes((groups, 128)) + 128
    for s, part in enumerate(
        (
            pltpu.roll(up, HALO, 1),
            pltpu.roll(up, HALO - FOLD, 1),
            pltpu.roll(down, HALO, 1),
            pltpu.roll(down, HALO - FOLD, 1),
        )
    ):
        at = pl.ds(s, groups, stride=ROWS)
        high[at, :] = jnp.where(lane >= HALO, part[:, 128:], high[at, :])
    out_ref[:, 128:WIDE] = jnp.where(
        lanes(high.shape) < LATE - 128, high[...], late_ref[:, :128]
    )
    out_ref[:, WIDE:] = late_ref[:, 128:]


def sums_kernel(
    norm,
    length,
    spec_ref,
    scale_ref,
    aligned_ref,
    stag_ref,
    stag_below_ref,
    flags_ref,
    sums_ref,
    scaled_ref,
    part_ref,
    down_ref,
    up_ref,
    own_ref,
):
    count, block = aligned_ref.shape[0], aligned_ref.shape[1]
    half, rows = block // 2, count * block
    scaled = spec_ref[...] * scale_ref[...]
    scaled_ref[...] = scaled
    for b in range(count):
        at = slice(b * block, (b + 1) * block)
        part_ref[at, :] = dot(aligned_ref[b], scaled[at])
    for b in range(count - 1):
        at = slice(half + b * block, half + (b + 1) * block)
        part_ref[at, :] = part_ref[at, :] + dot(stag_ref[b], scaled[at])
    first, last = slice(0, half), slice(rows - half, rows)
    part_ref[first, :] = part_ref[first, :] + flags_ref[1:2, :] * dot(
        stag_below_ref[ROWS : ROWS + half, half:], scaled[first]
    )
    part_ref[last, :] = part_ref[last, :] + dot(stag_ref[count - 1, :half, :half], scaled[last])
    total = total_of(scaled * part_ref[...], length) * (flags_ref[2:3, :1] * norm)
    small = lanes((8, 128))
    own = jnp.where(small == SCALARS - 128 + 2, total, sums_ref[...])
    own_ref[...] = own
    store_edge(down_ref, scaled[first], own)
    store_edge(up_ref, scaled[last], own)


def total_of(value, length):
    columns = jnp.sum(value, axis=0, keepdims=True)
    columns = jnp.where(lanes(columns.shape) < length, columns, 0.0)
    return jnp.sum(columns[:, :128] + columns[:, 128:], axis=1, keepdims=True)


def ends_kernel(
    norm,
    length,
    scaled_ref,
    part_ref,
    scale_ref,
    above_ref,
    below_ref,
    stag_ref,
    stag_below_ref,
    flags_ref,
    aside_ref,
    own_ref,
    out_ref,
):
    count, block = stag_ref.shape[0], stag_ref.shape[1]
    half, rows = block // 2, count * block
    first, last = slice(0, half), slice(rows - half, rows)
    low = dot(stag_below_ref[ROWS : ROWS + half, :half], load_edge(below_ref)) * flags_ref[1:2, :]
    high = dot(stag_ref[count - 1, :half, half:], load_edge(above_ref)) * flags_ref[:1, :]
    both = total_of(low * scaled_ref[first, :] + high * scaled_ref[last, :], length)
    both = both * (flags_ref[2:3, :1] * (2.0 * norm))
    pair = own_ref[:1, :] + below_ref[half + ROWS : half + ROWS + 1, :]
    pair = jnp.where(lanes(pair.shape) == SCALARS - 128 + 2, pair + both, pair)
    middle = slice(half, rows - half)
    for at, more in ((first, low), (middle, None), (last, high)):
        full = part_ref[at, :] if more is None else part_ref[at, :] + more
        full = full * (scale_ref[at, :] * norm)
        full = jnp.where(lanes(full.shape) < length, full, aside_ref[at, :])
        out_ref[at, :128] = full[:, :128]
        inside = lanes((full.shape[0], 128)) < SCALARS - 128
        out_ref[at, 128:] = jnp.where(inside, full[:, 128:], pair)


def gather_kernel(spec_ref, sums_ref):
    riders = jnp.sum(spec_ref[:, 128:], axis=0, keepdims=True) * (1.0 / ROWS)
    sums_ref[...] = jnp.broadcast_to(riders, (8, 128))


def step_kernel(
    groups,
    length,
    spec_ref,
    rhs_ref,
    own_ref,
    next_ref,
    east_ref,
    matrix_ref,
    outer_ref,
    out_ref,
    first_ref,
    image_ref,
    sums_ref,
    left,
    right,
    low,
    high,
    tail,
    folded,
    twiddle_ref,
):
    load_twiddle(matrix_ref, twiddle_ref)
    lane_row = lanes((groups, WIDE))
    stride = 3 * ROWS
    tail[...] = spec_ref[:, 128:WIDE]

    def halo_row(s):
        blank = jnp.zeros((groups, 128), jnp.float32)
        parts = [
            jnp.concatenate([tail[pl.ds(s + n, groups, stride=ROWS), :], blank], axis=1)
            for n in range(2)
        ]
        return jnp.where(
            lane_row < FOLD, shifted(parts[0], 128 - HALO), shifted(parts[1], FOLD + 128 - HALO)
        )

    stacked = jnp.concatenate([spec_ref[:, :WIDE], halo_row(0), halo_row(2)], axis=0)
    products = both_products(stacked, matrix_ref)
    halos = rows_back(products, groups * ROWS, twiddle_ref, outer_ref)
    for start, row in zip((ROWS - 1, 2 * ROWS), halos, strict=True):
        low[pl.ds(start, groups, stride=stride), :] = row[:, :128]
        high[pl.ds(start, groups, stride=stride), :] = row[:, 128:]

    def neighbour(start):
        at = slice(start, start + ROWS)
        return jnp.concatenate([low[at, :], high[at, :]], axis=1)

    cells = transform_back(products, groups, twiddle_ref)
    for p in range(groups):
        v = jnp.where(own_ref[rows_of(p), :] > 0.0, cells[p], 0.0)
        first_ref[rows_of(p), :] = v
        low[stride * p + ROWS : stride * p + 2 * ROWS, :] = v[:, :128]
        high[stride * p + ROWS : stride * p + 2 * ROWS, :] = v[:, 128:]
    lane, row = lanes((ROWS, WIDE)), sublanes((ROWS, WIDE))
    _, count, n_at, e_at, f_at = lane_plan(length)
    tail[...] = spec_ref[:, WIDE:]
    fold, blank = f_at - WIDE, jnp.zeros((groups, 128), jnp.float32)
    width = 128 - fold
    before = jnp.zeros((groups, WIDE), jnp.float32)
    for n in range(ROWS):
        piece = jnp.concatenate([tail[pl.ds(n, groups, stride=ROWS), :], blank], axis=1)
        inside = (lane_row >= n * width) & (lane_row < (n + 1) * width)
        before = jnp.where(inside, shifted(piece, n * width - fold), before)
    folded[...] = before
    rz = jnp.zeros((ROWS, WIDE), jnp.float32)
    curvature = jnp.zeros((ROWS, WIDE), jnp.float32)
    images, fluxes = [], []
    for p in range(groups):
        at = rows_of(p)
        v = first_ref[at, :]
        after = first_ref[rows_of((p + 1) % groups), 0:1]
        east = jnp.where(
            lane < count, east_ref[at, :], shifted(spec_ref[at, 128:], count - (e_at - 128))
        )
        flux = v - shifted(jnp.where(lane == length, after, v), -1)
        fluxes.append(jnp.where(lane < length, east * next_ref[at, :] * flux, 0.0))
    for p in range(groups):
        at = rows_of(p)
        v = first_ref[at, :]
        before = fluxes[(p - 1) % groups][:, length - 1 : length]
        flux = fluxes[p]
        own = own_ref[at, :]
        base = stride * p + ROWS
        north = shifted(spec_ref[at, 128:], 128 - n_at)
        south = jnp.where(row == 0, folded[p : p + 1, :], pltpu.roll(north, 1, 0))
        image = jnp.where(own > 0.0, own, 1.0) * v
        image = image + (flux - shifted(jnp.where(lane == WIDE - 1, before, flux), 1))
        image = image + north * (v - neighbour(base + 1))
        image = image + south * (v - neighbour(base - 1))
        image = jnp.where(lane < length, image, 0.0)
        image_ref[at, :] = image
        images.append(image)
        rz = rz + rhs_ref[at, :] * v
        curvature = curvature + v * image
    small = lanes((8, 128))
    at = SCALARS - 128
    sums_ref[...] = jnp.where(
        small == at, jnp.sum(rz), jnp.where(small == at + 1, jnp.sum(curvature), 0.0)
    )
    spectrum = transform(images, matrix_ref, twiddle_ref, left, right)
    out_ref[...] = jnp.where(
        lanes(out_ref.shape) < length, spectrum, shifted(first_ref[...], length)
    )


def last_kernel(
    groups,
    length,
    spec_ref,
    own_ref,
    first_ref,
    image_ref,
    matrix_ref,
    out_ref,
    twiddle_ref,
):
    load_twiddle(matrix_ref, twiddle_ref)
    cells = transform_back(both_products(spec_ref[...], matrix_ref), groups, twiddle_ref)
    lane = lanes((ROWS, WIDE))
    cut = WIDE - length
    image_cut = SCALARS - length
    image_at = 2 * length - cut
    for p in range(groups):
        at = rows_of(p)
        cell = jnp.where(own_ref[at, :] > 0.0, cells[p], 0.0)
        out = jnp.where(lane < length, cell, shifted(first_ref[at, :], length - cut))
        out_ref[at, :] = jnp.where(
            lane < image_at, out, shifted(image_ref[at, :], image_at - image_cut)
        )


def unpack_kernel(length, count, slab_ref, out_ref):
    turned = slab_ref[:, 128:].T
    out_ref[:count, :] = turned[length - 128 : length - 128 + count]


def unpack_first_kernel(length, count, slab_ref, image_ref, out_ref, aside_ref):
    unpack_kernel(length, count, slab_ref, out_ref)
    lane = lanes(image_ref.shape)
    aside_ref[...] = jnp.where(lane < length, 0.0, shifted(image_ref[...], length))


def finish_kernel(
    length,
    back_ref,
    first_ref,
    image_ref,
    forcing_ref,
    mask_ref,
    pair_ref,
    ahead_ref,
    behind_ref,
    across_ref,
    solution_ref,
    residual_ref,
    direction_ref,
):
    at = SCALARS - 128
    totals = (pair_ref[:1, :] + across_ref[:1, :]) + (ahead_ref[:1, :] + behind_ref[:1, :])
    rz, curvature, own = [totals[:, at + n : at + n + 1] for n in range(3)]
    alpha = rz / curvature
    rz_next = rz - 2.0 * alpha * curvature + alpha * alpha * own
    beta = rz_next / rz
    back = back_ref[...].T
    cut = WIDE - length
    image_cut = SCALARS - length
    image_at = 2 * length - cut
    rhs = mask_ref[...].astype(jnp.float32) * forcing_ref[...]

    def store(where, rows_back, first):
        solution_ref[where, :] = alpha * first
        direction_ref[where, :] = (first - alpha * rows_back) + beta * first

    store(slice(0, cut), back[:cut], first_ref[:cut, :])
    store(slice(cut, length), back[cut:length], back[length:image_at])
    residual_ref[:image_cut, :] = rhs[:image_cut] - alpha * image_ref[:image_cut, :]
    residual_ref[image_cut:, :] = (
        rhs[image_cut:] - alpha * back[image_at : image_at + length - image_cut]
    )


def call(kernel, out_shapes, scratch=(), name=None):
    single = not isinstance(out_shapes, (list, tuple)) or isinstance(out_shapes[0], int)
    shapes = [out_shapes] if single else out_shapes
    outs = [jax.ShapeDtypeStruct(s, jnp.float32) for s in shapes]
    return pl.pallas_call(
        kernel,
        out_shape=outs[0] if single else outs,
        scratch_shapes=[pltpu.VMEM(s, jnp.float32) for s in scratch],
        compiler_params=pltpu.CompilerParams(vmem_limit_bytes=16 * 2**20),
        name=name,
    )


def exchanged(value):
    groups = lax.axis_size(LON)
    parts = value.reshape(groups, ROWS, value.shape[-1])
    return lax.all_to_all(parts, LON, split_axis=0, concat_axis=0, tiled=True).reshape(value.shape)


def from_lat(value, steps):
    count = lax.axis_size("lat")
    return lax.ppermute(value, "lat", [((d + steps) % count, d) for d in range(count)])


def after(value, *others):
    return lax.optimization_barrier((value, *others))[0]


def local(
    surface_forcing,
    ocean_mask,
    self_coupling,
    east_coupling,
    north_coupling,
    zonal_weight,
    aligned_inverse,
    staggered_inverse,
):
    groups = lax.axis_size(LON)
    length, rows = surface_forcing.shape
    norm = 1.0 / (groups * length)
    matrices, outer, wave = tables(groups, length)
    count, block = aligned_inverse.shape[0], aligned_inverse.shape[1]
    half = block // 2
    wide = (rows, WIDE)
    turns = [(2, groups, WIDE)]
    transforms = [wide, wide]

    cells = (length, rows)
    places = (lax.axis_index(LON), lax.axis_index("lat"))
    flag_row = lax.broadcasted_iota(jnp.int32, (8, WIDE), 0)
    surface_forcing, channel, lat = lax.optimization_barrier((surface_forcing, *places))
    wet_cells = ocean_mask.astype(jnp.float32)
    own_cells = wet_cells * self_coupling
    packed = call(pack_kernel, wide, [wide], name="pack")(wet_cells * surface_forcing, own_cells)
    slab = exchanged(packed)

    mask, east_cells = lax.optimization_barrier((ocean_mask, east_coupling, slab))[:2]
    more = call(pack_more_kernel, wide, [wide], name="pack_more")(own_cells, mask, east_cells)
    spectrum = call(lambda *r: forward_kernel(groups, *r), wide, transforms + turns, name="forward")(
        slab, more, matrices
    )
    spec_rhs = exchanged(spectrum)

    north_cells, stag = lax.optimization_barrier((north_coupling, staggered_inverse, spectrum))[:-1]
    wet_first, low_last = call(
        edges_kernel, [(ROWS, WIDE), (half + 2 * ROWS, 128)], [(WIDE, 128)], name="edges"
    )(mask, north_cells, stag)
    weights, channel, lat, flag_row = lax.optimization_barrier(
        (
            zonal_weight,
            channel,
            lat,
            flag_row,
            wet_first,
        )
    )[:-1]
    scale = lax.rsqrt(1.0 + weights[:, None] * lax.dynamic_slice_in_dim(wave, channel, 1, 0))
    north_of, south_of, weight = (
        jnp.where(condition, yes, no).astype(jnp.float32)
        for condition, yes, no in (
            (lat < lax.axis_size("lat") - 1, 1.0, 0.0),
            (lat > 0, 1.0, 0.0),
            (channel < 2, 1.0, 2.0),
        )
    )
    flags = jnp.where(flag_row == 0, north_of, jnp.where(flag_row == 1, south_of, weight))
    stag_below = from_lat(low_last, -1)
    late = call(
        pack_rest_kernel,
        wide,
        [(WIDE + 128, rows), wide, (rows, 128), (rows, 128), (rows, 128)],
        name="pack_rest",
    )(mask, east_cells, north_cells, flags, from_lat(wet_first, 1), stag_below)
    spec_rhs = after(spec_rhs, late, scale, flags)

    edge = (half + 2 * ROWS, 128)

    scaled, down, up = call(blocks_kernel, [wide, edge, edge], name="blocks")(
        spec_rhs, scale, aligned_inverse
    )
    above, below = from_lat(down, 1), from_lat(up, -1)
    part = call(inner_kernel, wide, name="inner")(scaled, aligned_inverse, stag)
    pieces = (scaled, part, scale, above, below, stag, stag_below, flags)
    flat = call(
        lambda *r: coefficients_kernel(groups, length, *r), [wide] * 3, name="coefficients"
    )(slab, after(spec_rhs, scaled))
    late = after(late, *flat)
    filtered = exchanged(
        call(
            lambda *r: halo_kernel(norm, *r), (rows, WIDE + 128), [(rows, 128)] * 2, name="halo"
        )(*pieces, late)
    )
    spec, first, image, sums = call(
        lambda *r: step_kernel(groups, length, *r),
        [wide, wide, wide, (8, 128)],
        transforms + [(3 * rows, 128)] * 2 + [(rows, 128), (groups, WIDE)] + turns,
        name="step",
    )(filtered, slab, *flat, matrices, outer)
    spec_image = exchanged(spec)
    scaled, part, down, up, own = call(
        lambda *r: sums_kernel(norm, length, *r), [wide, wide, edge, edge, (8, 128)], name="sums"
    )(spec_image, scale, aligned_inverse, stag, stag_below, flags, sums)
    above, below = from_lat(down, 1), from_lat(up, -1)
    cut, image_cut = WIDE - length, SCALARS - length
    first_cells, aside = call(
        lambda *r: unpack_first_kernel(length, cut, *r), [cells, wide], name="unpack_first"
    )(after(spec_image, scaled), image)
    filtered = exchanged(
        call(lambda *r: ends_kernel(norm, length, *r), wide, name="ends")(
            scaled, part, scale, above, below, stag, stag_below, flags, aside, own
        )
    )

    pair = call(gather_kernel, (8, 128), name="gather")(filtered)
    image_cells = call(
        lambda *r: unpack_kernel(length, image_cut, *r), cells, name="unpack_image"
    )(filtered)
    packed = call(lambda *r: last_kernel(groups, length, *r), wide, turns, name="last")(
        filtered, flat[0], first, image, matrices
    )
    return tuple(
        call(lambda *r: finish_kernel(length, *r), [cells] * 3, name="finish")(
            exchanged(packed),
            first_cells,
            image_cells,
            surface_forcing,
            ocean_mask,
            pair,
            from_lat(pair, 2),
            from_lat(pair, -2),
            from_lat(pair, 4),
        )
    )


def solution(mesh):
    torus = Mesh(
        mesh.devices.reshape(mesh.shape["lat"], 4, 4, 2), ("lat", "lon_0", "lon_1", "lon_2")
    )
    return jax.shard_map(
        local,
        mesh=torus,
        in_specs=(
            P(LON, "lat"),
            P(LON, "lat"),
            P(LON, "lat"),
            P(LON, "lat"),
            P(LON, "lat"),
            P("lat"),
            P("lat", None, None),
            P("lat", None, None),
        ),
        out_specs=(P(LON, "lat"), P(LON, "lat"), P(LON, "lat")),
        check_vma=False,
    )
```

```python
import jax
import jax.numpy as jnp
import numpy as np
from jax import lax
from jax.experimental import pallas as pl
from jax.experimental.pallas import tpu as pltpu
from jax.sharding import Mesh
from jax.sharding import PartitionSpec as P

LON = ("lon_0", "lon_1", "lon_2")
TURN = 2.0 * np.pi
ROWS = 8
WIDE = 256
HALO = 136
FOLD = 68
LATE = HALO + FOLD
SCALARS = WIDE - 4


def tables(groups, length):
    period = groups * length
    index = np.arange(length)
    inner = TURN * (np.outer(index, index) % length) / length
    wave_of = np.zeros(groups, np.int64)
    wave_of[1] = groups // 2
    for m in range(1, groups // 2):
        wave_of[2 * m] = wave_of[2 * m + 1] = m
    turn = TURN * (np.outer(wave_of, index) % period) / period
    rows = np.zeros((2 * WIDE + 2 * groups, WIDE), np.float32)
    rows[:length, :length] = np.cos(inner)
    rows[WIDE : WIDE + length, :length] = np.sin(inner)
    rows[2 * WIDE : 2 * WIDE + groups, :length] = np.cos(turn)
    rows[2 * WIDE + groups :, :length] = np.sin(turn)
    coarse = rows.astype(jnp.bfloat16)
    rest = (rows - coarse.astype(np.float32)).astype(jnp.bfloat16)
    chunk = np.arange(groups)
    outer = np.zeros((2, groups, groups))
    for c in range(groups):
        phase = TURN * (chunk * wave_of[c] % groups) / groups
        if c < 2:
            outer[0, :, c] = outer[1, :, c] = np.cos(phase)
        elif c % 2 == 0:
            outer[0, :, c], outer[1, :, c] = 2 * np.cos(phase), -2 * np.sin(phase)
        else:
            outer[0, :, c], outer[1, :, c] = -2 * np.sin(phase), -2 * np.cos(phase)
    modes = wave_of[:, None] + groups * index[None, :]
    wave = np.zeros((groups, WIDE))
    wave[:, :length] = 4.0 * np.sin(np.pi * modes / period) ** 2
    return (
        np.stack([coarse, rest]),
        np.concatenate([outer[0], outer[1]], axis=1).astype(np.float32),
        wave.astype(np.float32),
    )


def real_fft(values):
    count = len(values)
    if count == 2:
        return [(values[0] + values[1], None), (values[0] - values[1], None)]
    even, odd = real_fft(values[0::2]), real_fft(values[1::2])
    out = [None] * (count // 2 + 1)
    for k in range(count // 4 + 1):
        (er, ei), (re, im) = even[k], odd[k]
        if k == 0:
            out[0], out[count // 2] = (er + re, None), (er - re, None)
        elif k == count // 4:
            out[k] = (er, -re)
        else:
            c, s = float(np.cos(TURN * k / count)), float(-np.sin(TURN * k / count))
            tr, ti = re * c - im * s, im * c + re * s
            out[k], out[count // 2 - k] = (er + tr, ei + ti), (er - tr, ti - ei)
    return out


def real_ifft(spectrum):
    count = 2 * (len(spectrum) - 1)
    if count == 2:
        return [spectrum[0][0] + spectrum[1][0], spectrum[0][0] - spectrum[1][0]]
    even, odd = [], []
    for k in range(count // 4 + 1):
        (ar, ai), (br, bi) = spectrum[k], spectrum[count // 2 - k]
        if k == 0:
            even.append((ar + br, None))
            odd.append((ar - br, None))
        elif k == count // 4:
            even.append((2.0 * ar, None))
            odd.append((-2.0 * ai, None))
        else:
            c, s = float(np.cos(TURN * k / count)), float(np.sin(TURN * k / count))
            dr, di = ar - br, ai + bi
            even.append((ar + br, ai - bi))
            odd.append((dr * c - di * s, dr * s + di * c))
    first, second = real_ifft(even), real_ifft(odd)
    out = []
    for a, b in zip(first, second, strict=True):
        out += [a, b]
    return out


def split(a):
    coarse = a.astype(jnp.bfloat16)
    return coarse, (a - coarse.astype(jnp.float32)).astype(jnp.bfloat16)


def product(a, b):
    (ac, ar), (bc, br) = a, b

    def one(x, y):
        return jnp.dot(x, y, preferred_element_type=jnp.float32)

    return one(ac, bc) + (one(ac, br) + one(ar, bc))


def dot(a, b):
    return product(split(a), split(b))


def table(matrix_ref, n):
    at = slice(n * WIDE, (n + 1) * WIDE)
    return matrix_ref[0, at, :], matrix_ref[1, at, :]


def load_twiddle(matrix_ref, twiddle):
    groups = twiddle.shape[1]
    for n in range(2):
        at = slice(2 * WIDE + n * groups, 2 * WIDE + (n + 1) * groups)
        twiddle[n] = matrix_ref[0, at, :].astype(jnp.float32) + matrix_ref[1, at, :].astype(
            jnp.float32
        )


def rows_of(p):
    return slice(ROWS * p, ROWS * (p + 1))


def lanes(shape):
    return lax.broadcasted_iota(jnp.int32, shape, len(shape) - 1)


def sublanes(shape):
    return lax.broadcasted_iota(jnp.int32, shape, len(shape) - 2)


def shifted(value, lanes_right):
    return pltpu.roll(value, lanes_right % value.shape[1], 1)


def pack_kernel(rhs_ref, own_ref, out_ref, tall):
    length = rhs_ref.shape[0]
    tall[:length, :] = rhs_ref[...]
    tall[length:, :] = own_ref[: WIDE - length, :]
    out_ref[...] = tall[...].T


def edges_kernel(mask_ref, north_ref, stag_ref, wet_ref, low_ref, tall):
    length, rows = mask_ref.shape
    count, block = stag_ref.shape[0], stag_ref.shape[1]
    tall[length:, :] = jnp.zeros((WIDE - length, 128), jnp.float32)
    tall[:length, :] = mask_ref[:, :128].astype(jnp.float32)
    wet_ref[...] = tall[...].T[:ROWS]
    tall[:length, :] = mask_ref[:, rows - 128 :].astype(jnp.float32) * north_ref[:, rows - 128 :]
    top = tall[...].T[127:]
    keep = block // 2 + ROWS
    low_ref[:keep, :] = stag_ref[count - 1, block - keep :, :]
    row = sublanes((ROWS, 128))
    low_ref[keep:, :] = jnp.where(row == 0, top[:, :128], top[:, 128:])


def lane_plan(length):
    cut = WIDE - length
    count = 2 * cut - length
    north = LATE
    east = north + length
    return cut, count, north, east, east + length - count


def pack_more_kernel(own_ref, mask_ref, east_ref, out_ref, tall):
    length, rows = mask_ref.shape
    cut, count = lane_plan(length)[:2]
    tall[:length, :] = jnp.zeros((length, rows), jnp.float32)
    tall[length : WIDE - count, :] = own_ref[cut:, :]
    tall[WIDE - count :, :] = (mask_ref[...].astype(jnp.float32) * east_ref[...])[:count]
    out_ref[...] = tall[...].T


def pack_rest_kernel(
    mask_ref,
    east_ref,
    north_ref,
    flags_ref,
    wet_above_ref,
    from_below_ref,
    out_ref,
    tall,
    aside,
    low,
    high,
    last,
):
    length, rows = mask_ref.shape
    _, count, n_at, e_at, f_at = lane_plan(length)
    block = from_below_ref.shape[0] - ROWS
    lane = lanes((length, rows))
    wet = mask_ref[...].astype(jnp.float32)
    north = wet * north_ref[...]
    wet_above = wet_above_ref[...].T[:length, :1] * flags_ref[:1, :1]
    top = from_below_ref[block:, :].T
    top_below = jnp.concatenate([top[:, :1], top[: length - 128, 1:2]], axis=0) * flags_ref[1:2, :1]
    tall[128:n_at, :] = jnp.zeros((n_at - 128, rows), jnp.float32)
    tall[n_at:e_at, :] = north * jnp.where(lane == rows - 1, wet_above, shifted(wet, -1))
    tall[e_at:f_at, :] = (wet * east_ref[...])[count:]
    tall[f_at:, :] = jnp.zeros((WIDE + 128 - f_at, rows), jnp.float32)
    out_ref[:, :128] = tall[128:WIDE, :].T
    last[...] = tall[WIDE:, :].T
    aside[length:, :] = jnp.zeros((WIDE - length, rows), jnp.float32)
    aside[:length, :] = wet * jnp.where(lane == 0, top_below, shifted(north, 1))
    low[...] = aside[:128, :].T
    high[...] = aside[128:, :].T
    groups = rows // ROWS
    at = pl.ds(0, groups, stride=ROWS)
    before = jnp.concatenate([low[at, :], high[at, :]], axis=1)
    fold = f_at - WIDE
    lane = lanes((groups, 128))
    for n in range(ROWS):
        at = pl.ds(n, groups, stride=ROWS)
        piece = shifted(before, fold - n * (128 - fold))[:, :128]
        last[at, :] = jnp.where(lane >= fold, piece, last[at, :])
    out_ref[:, 128:] = last[...]


def coefficients_kernel(groups, length, slab_ref, second_ref, own_ref, next_ref, east_ref):
    cut, count = lane_plan(length)[:2]
    lane = lanes((ROWS, WIDE))
    for p in range(groups):
        at = rows_of(p)
        more = second_ref[at, :]
        own_ref[at, :] = jnp.where(
            lane < cut,
            shifted(slab_ref[at, :], -length),
            jnp.where(lane < length, shifted(more, cut - length), 0.0),
        )
        east_ref[at, :] = jnp.where(lane < count, shifted(more, count), 0.0)
    for p in range(groups):
        own = own_ref[rows_of(p), :]
        after = own_ref[rows_of((p + 1) % groups), 0:1]
        ocean = jnp.where(lane == length, after, own) > 0.0
        next_ref[rows_of(p), :] = shifted(ocean.astype(jnp.float32), -1)


def transform(chunks, matrix_ref, twiddle_ref, left, right):
    groups = len(chunks)
    mixed = real_fft(chunks)
    for m in range(groups // 2 + 1):
        re, im = mixed[m]
        if m == 0:
            left[rows_of(0), :] = re
            right[rows_of(0), :] = re
            continue
        c = 1 if m == groups // 2 else 2 * m
        cos, sin = twiddle_ref[0, c : c + 1, :], twiddle_ref[1, c : c + 1, :]
        if m == groups // 2:
            left[rows_of(1), :] = re * (cos + sin)
            right[rows_of(1), :] = re * (cos - sin)
        else:
            tr, ti = re * cos + im * sin, im * cos - re * sin
            left[rows_of(c), :] = tr
            right[rows_of(c), :] = ti
            left[rows_of(c + 1), :] = ti
            right[rows_of(c + 1), :] = -tr
    return product(split(left[...]), table(matrix_ref, 0)) + product(
        split(right[...]), table(matrix_ref, 1)
    )


def both_products(spectrum, matrix_ref):
    parts = split(spectrum)
    return product(parts, table(matrix_ref, 0)), product(parts, table(matrix_ref, 1))


def transform_back(products, groups, twiddle_ref):
    pc, ps = products
    mixed = []
    for m in range(groups // 2 + 1):
        if m == 0:
            mixed.append((pc[rows_of(0)] + ps[rows_of(0)], None))
            continue
        c = 1 if m == groups // 2 else 2 * m
        cos, sin = twiddle_ref[0, c : c + 1, :], twiddle_ref[1, c : c + 1, :]
        if m == groups // 2:
            mixed.append((pc[rows_of(1)] * (cos + sin) + ps[rows_of(1)] * (cos - sin), None))
        else:
            hr = pc[rows_of(c)] - ps[rows_of(c + 1)]
            hi = ps[rows_of(c)] + pc[rows_of(c + 1)]
            mixed.append((hr * cos - hi * sin, hi * cos + hr * sin))
    return real_ifft(mixed)


def rows_back(products, start, twiddle_ref, outer_ref):
    groups = outer_ref.shape[0]
    cos, sin = twiddle_ref[0], twiddle_ref[1]
    turned = [[], []]
    for n in range(2):
        pc, ps = (v[start + n * groups : start + (n + 1) * groups] for v in products)
        turned[0].append(pc * cos - ps * sin)
        turned[1].append(ps * cos + pc * sin)
    both = jnp.concatenate([jnp.concatenate(v, axis=1) for v in turned], axis=0)
    both = dot(outer_ref[...], both)
    return both[:, :WIDE], both[:, WIDE:]


def forward_kernel(groups, field_ref, rest_ref, matrix_ref, out_ref, left, right, twiddle_ref):
    load_twiddle(matrix_ref, twiddle_ref)
    chunks = [field_ref[rows_of(p), :] for p in range(groups)]
    spectrum = transform(chunks, matrix_ref, twiddle_ref, left, right)
    out_ref[...] = spectrum + rest_ref[...]


def store_edge(ref, value, extra):
    half = value.shape[0]
    ref[:half, :] = value[:, :128]
    ref[half : half + ROWS, :] = jnp.concatenate(
        [value[:, 128:].T[:ROWS], jnp.zeros((ROWS, 128 - half), jnp.float32)], axis=1
    )
    ref[half + ROWS :, :] = extra


def load_edge(ref):
    half = ref.shape[0] - 2 * ROWS
    turned = ref[half : half + ROWS, :].T[:half]
    blank = jnp.zeros((half, 128 - ROWS), jnp.float32)
    return jnp.concatenate([ref[:half, :], turned, blank], axis=1)


def store_rows(ref, value, part, scale):
    row = sublanes((ROWS, 128))
    extra = jnp.where(row == 0, part[:, :128], part[:, 128:])
    store_edge(
        ref,
        value,
        jnp.where(row < 2, extra, jnp.where(row == 2, scale[:, :128], scale[:, 128:])),
    )


def load_rows(ref):
    at = ref.shape[0] - ROWS
    lines = [ref[at + n : at + n + 1, :] for n in range(4)]
    return jnp.concatenate(lines[:2], axis=1), jnp.concatenate(lines[2:], axis=1)


def blocks_kernel(spec_ref, scale_ref, aligned_ref, scaled_ref, down_ref, up_ref):
    count, block = aligned_ref.shape[0], aligned_ref.shape[1]
    half, rows = block // 2, count * block
    scaled = spec_ref[...] * scale_ref[...]
    scaled_ref[...] = scaled
    first = dot(aligned_ref[0, :ROWS, :], scaled[:block])
    last = dot(aligned_ref[count - 1, block - ROWS :, :], scaled[rows - block :])
    store_rows(down_ref, scaled[:half], first[:1], scale_ref[:1, :])
    store_rows(up_ref, scaled[rows - half :], last[ROWS - 1 :], scale_ref[rows - 1 :, :])


def inner_kernel(scaled_ref, aligned_ref, stag_ref, part_ref):
    count, block = aligned_ref.shape[0], aligned_ref.shape[1]
    half = block // 2
    for b in range(count):
        at = slice(b * block, (b + 1) * block)
        part_ref[at, :] = dot(aligned_ref[b], scaled_ref[at, :])
    for b in range(count - 1):
        at = slice(half + b * block, half + (b + 1) * block)
        part_ref[at, :] = part_ref[at, :] + dot(stag_ref[b], scaled_ref[at, :])


def combine(
    norm, scaled_ref, part_ref, scale_ref, above_ref, below_ref, stag_ref, stag_below_ref, flags_ref
):
    count, block = stag_ref.shape[0], stag_ref.shape[1]
    half, rows = block // 2, count * block
    before = flags_ref[1:2, :] * dot(
        stag_below_ref[: ROWS + half, :],
        jnp.concatenate([load_edge(below_ref), scaled_ref[:half, :]], axis=0),
    )
    upper = load_edge(above_ref) * flags_ref[:1, :]
    after = dot(
        stag_ref[count - 1, : half + ROWS, :],
        jnp.concatenate([scaled_ref[rows - half :, :], upper], axis=0),
    )
    pieces = [
        part_ref[:half, :] + before[ROWS:],
        part_ref[half : rows - half, :],
        part_ref[rows - half :, :] + after[:half],
    ]
    full = jnp.concatenate(pieces, axis=0) * (scale_ref[...] * norm)
    return full, before, after


def halo_kernel(
    norm,
    scaled_ref,
    part_ref,
    scale_ref,
    above_ref,
    below_ref,
    stag_ref,
    stag_below_ref,
    flags_ref,
    late_ref,
    out_ref,
    low,
    high,
):
    half = stag_ref.shape[1] // 2
    full, before, after = combine(
        norm,
        scaled_ref,
        part_ref,
        scale_ref,
        above_ref,
        below_ref,
        stag_ref,
        stag_below_ref,
        flags_ref,
    )
    part, scale = load_rows(below_ref)
    row_below = (before[ROWS - 1 : ROWS] + part) * (scale * norm)
    part, scale = load_rows(above_ref)
    row_above = (after[half : half + 1] + part) * (scale * norm)
    out_ref[:, :128] = full[:, :128]
    low[...] = full[:, :128]
    high[...] = full[:, 128:]
    groups = full.shape[0] // ROWS

    def strided(start):
        at = pl.ds(start, groups, stride=ROWS)
        return jnp.concatenate([low[at, :], high[at, :]], axis=1)

    row = lax.broadcasted_iota(jnp.int32, (groups, WIDE), 0)
    up = jnp.where(row == 0, row_below, pltpu.roll(strided(ROWS - 1), 1, 0))
    down = jnp.where(row == groups - 1, row_above, pltpu.roll(strided(0), groups - 1, 0))
    lane = lanes((groups, 128)) + 128
    for s, part in enumerate(
        (
            pltpu.roll(up, HALO, 1),
            pltpu.roll(up, HALO - FOLD, 1),
            pltpu.roll(down, HALO, 1),
            pltpu.roll(down, HALO - FOLD, 1),
        )
    ):
        at = pl.ds(s, groups, stride=ROWS)
        high[at, :] = jnp.where(lane >= HALO, part[:, 128:], high[at, :])
    out_ref[:, 128:WIDE] = jnp.where(
        lanes(high.shape) < LATE - 128, high[...], late_ref[:, :128]
    )
    out_ref[:, WIDE:] = late_ref[:, 128:]


def sums_kernel(
    norm,
    length,
    spec_ref,
    scale_ref,
    aligned_ref,
    stag_ref,
    stag_below_ref,
    flags_ref,
    sums_ref,
    scaled_ref,
    part_ref,
    down_ref,
    up_ref,
    own_ref,
):
    count, block = aligned_ref.shape[0], aligned_ref.shape[1]
    half, rows = block // 2, count * block
    scaled = spec_ref[...] * scale_ref[...]
    scaled_ref[...] = scaled
    coarse, rest = split(scaled)

    def applied(matrix, at):
        return product(split(matrix), (coarse[at], rest[at]))

    for b in range(count):
        at = slice(b * block, (b + 1) * block)
        part_ref[at, :] = applied(aligned_ref[b], at)
    for b in range(count - 1):
        at = slice(half + b * block, half + (b + 1) * block)
        part_ref[at, :] = part_ref[at, :] + applied(stag_ref[b], at)
    first, last = slice(0, half), slice(rows - half, rows)
    part_ref[first, :] = part_ref[first, :] + flags_ref[1:2, :] * applied(
        stag_below_ref[ROWS : ROWS + half, half:], first
    )
    part_ref[last, :] = part_ref[last, :] + applied(stag_ref[count - 1, :half, :half], last)
    total = total_of(scaled * part_ref[...], length) * (flags_ref[2:3, :1] * norm)
    small = lanes((8, 128))
    own = jnp.where(small == SCALARS - 128 + 2, total, sums_ref[...])
    own_ref[...] = own
    store_edge(down_ref, scaled[first], own)
    store_edge(up_ref, scaled[last], own)


def total_of(value, length):
    columns = jnp.sum(value, axis=0, keepdims=True)
    columns = jnp.where(lanes(columns.shape) < length, columns, 0.0)
    return jnp.sum(columns[:, :128] + columns[:, 128:], axis=1, keepdims=True)


def ends_kernel(
    norm,
    length,
    scaled_ref,
    part_ref,
    scale_ref,
    above_ref,
    below_ref,
    stag_ref,
    stag_below_ref,
    flags_ref,
    aside_ref,
    own_ref,
    out_ref,
):
    count, block = stag_ref.shape[0], stag_ref.shape[1]
    half, rows = block // 2, count * block
    first, last = slice(0, half), slice(rows - half, rows)
    low = dot(stag_below_ref[ROWS : ROWS + half, :half], load_edge(below_ref)) * flags_ref[1:2, :]
    high = dot(stag_ref[count - 1, :half, half:], load_edge(above_ref)) * flags_ref[:1, :]
    both = total_of(low * scaled_ref[first, :] + high * scaled_ref[last, :], length)
    both = both * (flags_ref[2:3, :1] * (2.0 * norm))
    pair = own_ref[:1, :] + below_ref[half + ROWS : half + ROWS + 1, :]
    pair = jnp.where(lanes(pair.shape) == SCALARS - 128 + 2, pair + both, pair)
    middle = slice(half, rows - half)
    for at, more in ((first, low), (middle, None), (last, high)):
        full = part_ref[at, :] if more is None else part_ref[at, :] + more
        full = full * (scale_ref[at, :] * norm)
        full = jnp.where(lanes(full.shape) < length, full, aside_ref[at, :])
        out_ref[at, :128] = full[:, :128]
        inside = lanes((full.shape[0], 128)) < SCALARS - 128
        out_ref[at, 128:] = jnp.where(inside, full[:, 128:], pair)


def gather_kernel(spec_ref, sums_ref):
    riders = jnp.sum(spec_ref[:, 128:], axis=0, keepdims=True) * (1.0 / ROWS)
    sums_ref[...] = jnp.broadcast_to(riders, (8, 128))


def step_kernel(
    groups,
    length,
    spec_ref,
    rhs_ref,
    own_ref,
    next_ref,
    east_ref,
    matrix_ref,
    outer_ref,
    out_ref,
    first_ref,
    image_ref,
    sums_ref,
    left,
    right,
    low,
    high,
    tail,
    folded,
    twiddle_ref,
):
    load_twiddle(matrix_ref, twiddle_ref)
    lane_row = lanes((groups, WIDE))
    stride = 3 * ROWS
    tail[...] = spec_ref[:, 128:WIDE]

    def halo_row(s):
        blank = jnp.zeros((groups, 128), jnp.float32)
        parts = [
            jnp.concatenate([tail[pl.ds(s + n, groups, stride=ROWS), :], blank], axis=1)
            for n in range(2)
        ]
        return jnp.where(
            lane_row < FOLD, shifted(parts[0], 128 - HALO), shifted(parts[1], FOLD + 128 - HALO)
        )

    stacked = jnp.concatenate([spec_ref[:, :WIDE], halo_row(0), halo_row(2)], axis=0)
    products = both_products(stacked, matrix_ref)
    halos = rows_back(products, groups * ROWS, twiddle_ref, outer_ref)
    for start, row in zip((ROWS - 1, 2 * ROWS), halos, strict=True):
        low[pl.ds(start, groups, stride=stride), :] = row[:, :128]
        high[pl.ds(start, groups, stride=stride), :] = row[:, 128:]

    def neighbour(start):
        at = slice(start, start + ROWS)
        return jnp.concatenate([low[at, :], high[at, :]], axis=1)

    cells = transform_back(products, groups, twiddle_ref)
    for p in range(groups):
        v = jnp.where(own_ref[rows_of(p), :] > 0.0, cells[p], 0.0)
        first_ref[rows_of(p), :] = v
        low[stride * p + ROWS : stride * p + 2 * ROWS, :] = v[:, :128]
        high[stride * p + ROWS : stride * p + 2 * ROWS, :] = v[:, 128:]
    lane, row = lanes((ROWS, WIDE)), sublanes((ROWS, WIDE))
    _, count, n_at, e_at, f_at = lane_plan(length)
    tail[...] = spec_ref[:, WIDE:]
    fold, blank = f_at - WIDE, jnp.zeros((groups, 128), jnp.float32)
    width = 128 - fold
    before = jnp.zeros((groups, WIDE), jnp.float32)
    for n in range(ROWS):
        piece = jnp.concatenate([tail[pl.ds(n, groups, stride=ROWS), :], blank], axis=1)
        inside = (lane_row >= n * width) & (lane_row < (n + 1) * width)
        before = jnp.where(inside, shifted(piece, n * width - fold), before)
    folded[...] = before
    rz = jnp.zeros((ROWS, WIDE), jnp.float32)
    curvature = jnp.zeros((ROWS, WIDE), jnp.float32)
    images, fluxes = [], []
    for p in range(groups):
        at = rows_of(p)
        v = first_ref[at, :]
        after = first_ref[rows_of((p + 1) % groups), 0:1]
        east = jnp.where(
            lane < count, east_ref[at, :], shifted(spec_ref[at, 128:], count - (e_at - 128))
        )
        flux = v - shifted(jnp.where(lane == length, after, v), -1)
        fluxes.append(jnp.where(lane < length, east * next_ref[at, :] * flux, 0.0))
    for p in range(groups):
        at = rows_of(p)
        v = first_ref[at, :]
        before = fluxes[(p - 1) % groups][:, length - 1 : length]
        flux = fluxes[p]
        own = own_ref[at, :]
        base = stride * p + ROWS
        north = shifted(spec_ref[at, 128:], 128 - n_at)
        south = jnp.where(row == 0, folded[p : p + 1, :], pltpu.roll(north, 1, 0))
        image = jnp.where(own > 0.0, own, 1.0) * v
        image = image + (flux - shifted(jnp.where(lane == WIDE - 1, before, flux), 1))
        image = image + north * (v - neighbour(base + 1))
        image = image + south * (v - neighbour(base - 1))
        image = jnp.where(lane < length, image, 0.0)
        image_ref[at, :] = image
        images.append(image)
        rz = rz + rhs_ref[at, :] * v
        curvature = curvature + v * image
    small = lanes((8, 128))
    at = SCALARS - 128
    sums_ref[...] = jnp.where(
        small == at, jnp.sum(rz), jnp.where(small == at + 1, jnp.sum(curvature), 0.0)
    )
    spectrum = transform(images, matrix_ref, twiddle_ref, left, right)
    out_ref[...] = jnp.where(
        lanes(out_ref.shape) < length, spectrum, shifted(first_ref[...], length)
    )


def last_kernel(
    groups,
    length,
    spec_ref,
    own_ref,
    first_ref,
    image_ref,
    matrix_ref,
    out_ref,
    twiddle_ref,
):
    load_twiddle(matrix_ref, twiddle_ref)
    cells = transform_back(both_products(spec_ref[...], matrix_ref), groups, twiddle_ref)
    lane = lanes((ROWS, WIDE))
    cut = WIDE - length
    image_cut = SCALARS - length
    image_at = 2 * length - cut
    for p in range(groups):
        at = rows_of(p)
        cell = jnp.where(own_ref[at, :] > 0.0, cells[p], 0.0)
        out = jnp.where(lane < length, cell, shifted(first_ref[at, :], length - cut))
        out_ref[at, :] = jnp.where(
            lane < image_at, out, shifted(image_ref[at, :], image_at - image_cut)
        )


def unpack_kernel(length, count, slab_ref, out_ref):
    turned = slab_ref[:, 128:].T
    out_ref[:count, :] = turned[length - 128 : length - 128 + count]


def unpack_first_kernel(length, count, slab_ref, image_ref, out_ref, aside_ref):
    unpack_kernel(length, count, slab_ref, out_ref)
    lane = lanes(image_ref.shape)
    aside_ref[...] = jnp.where(lane < length, 0.0, shifted(image_ref[...], length))


def finish_kernel(
    length,
    back_ref,
    first_ref,
    image_ref,
    forcing_ref,
    mask_ref,
    pair_ref,
    ahead_ref,
    behind_ref,
    across_ref,
    solution_ref,
    residual_ref,
    direction_ref,
):
    at = SCALARS - 128
    totals = (pair_ref[:1, :] + across_ref[:1, :]) + (ahead_ref[:1, :] + behind_ref[:1, :])
    rz, curvature, own = [totals[:, at + n : at + n + 1] for n in range(3)]
    alpha = rz / curvature
    rz_next = rz - 2.0 * alpha * curvature + alpha * alpha * own
    beta = rz_next / rz
    back = back_ref[...].T
    cut = WIDE - length
    image_cut = SCALARS - length
    image_at = 2 * length - cut
    rhs = mask_ref[...].astype(jnp.float32) * forcing_ref[...]

    def store(where, rows_back, first):
        solution_ref[where, :] = alpha * first
        direction_ref[where, :] = (first - alpha * rows_back) + beta * first

    store(slice(0, cut), back[:cut], first_ref[:cut, :])
    store(slice(cut, length), back[cut:length], back[length:image_at])
    residual_ref[:image_cut, :] = rhs[:image_cut] - alpha * image_ref[:image_cut, :]
    residual_ref[image_cut:, :] = (
        rhs[image_cut:] - alpha * back[image_at : image_at + length - image_cut]
    )


def call(kernel, out_shapes, scratch=(), name=None):
    single = not isinstance(out_shapes, (list, tuple)) or isinstance(out_shapes[0], int)
    shapes = [out_shapes] if single else out_shapes
    outs = [jax.ShapeDtypeStruct(s, jnp.float32) for s in shapes]
    return pl.pallas_call(
        kernel,
        out_shape=outs[0] if single else outs,
        scratch_shapes=[pltpu.VMEM(s, jnp.float32) for s in scratch],
        compiler_params=pltpu.CompilerParams(vmem_limit_bytes=16 * 2**20),
        name=name,
    )


def exchanged(value):
    groups = lax.axis_size(LON)
    parts = value.reshape(groups, ROWS, value.shape[-1])
    return lax.all_to_all(parts, LON, split_axis=0, concat_axis=0, tiled=True).reshape(value.shape)


def from_lat(value, steps):
    count = lax.axis_size("lat")
    return lax.ppermute(value, "lat", [((d + steps) % count, d) for d in range(count)])


def after(value, *others):
    return lax.optimization_barrier((value, *others))[0]


def local(
    surface_forcing,
    ocean_mask,
    self_coupling,
    east_coupling,
    north_coupling,
    zonal_weight,
    aligned_inverse,
    staggered_inverse,
):
    groups = lax.axis_size(LON)
    length, rows = surface_forcing.shape
    norm = 1.0 / (groups * length)
    matrices, outer, wave = tables(groups, length)
    count, block = aligned_inverse.shape[0], aligned_inverse.shape[1]
    half = block // 2
    wide = (rows, WIDE)
    turns = [(2, groups, WIDE)]
    transforms = [wide, wide]

    cells = (length, rows)
    places = (lax.axis_index(LON), lax.axis_index("lat"))
    flag_row = lax.broadcasted_iota(jnp.int32, (8, WIDE), 0)
    surface_forcing, channel, lat = lax.optimization_barrier((surface_forcing, *places))
    wet_cells = ocean_mask.astype(jnp.float32)
    own_cells = wet_cells * self_coupling
    packed = call(pack_kernel, wide, [wide], name="pack")(wet_cells * surface_forcing, own_cells)
    slab = exchanged(packed)

    mask, east_cells = lax.optimization_barrier((ocean_mask, east_coupling, slab))[:2]
    more = call(pack_more_kernel, wide, [wide], name="pack_more")(own_cells, mask, east_cells)
    spectrum = call(lambda *r: forward_kernel(groups, *r), wide, transforms + turns, name="forward")(
        slab, more, matrices
    )
    spec_rhs = exchanged(spectrum)

    north_cells, stag = lax.optimization_barrier((north_coupling, staggered_inverse, spectrum))[:-1]
    wet_first, low_last = call(
        edges_kernel, [(ROWS, WIDE), (half + 2 * ROWS, 128)], [(WIDE, 128)], name="edges"
    )(mask, north_cells, stag)
    weights, channel, lat, flag_row = lax.optimization_barrier(
        (
            zonal_weight,
            channel,
            lat,
            flag_row,
            wet_first,
        )
    )[:-1]
    scale = lax.rsqrt(1.0 + weights[:, None] * lax.dynamic_slice_in_dim(wave, channel, 1, 0))
    north_of, south_of, weight = (
        jnp.where(condition, yes, no).astype(jnp.float32)
        for condition, yes, no in (
            (lat < lax.axis_size("lat") - 1, 1.0, 0.0),
            (lat > 0, 1.0, 0.0),
            (channel < 2, 1.0, 2.0),
        )
    )
    flags = jnp.where(flag_row == 0, north_of, jnp.where(flag_row == 1, south_of, weight))
    stag_below = from_lat(low_last, -1)
    late = call(
        pack_rest_kernel,
        wide,
        [(WIDE + 128, rows), wide, (rows, 128), (rows, 128), (rows, 128)],
        name="pack_rest",
    )(mask, east_cells, north_cells, flags, from_lat(wet_first, 1), stag_below)
    spec_rhs = after(spec_rhs, late, scale, flags)

    edge = (half + 2 * ROWS, 128)

    scaled, down, up = call(blocks_kernel, [wide, edge, edge], name="blocks")(
        spec_rhs, scale, aligned_inverse
    )
    above, below = from_lat(down, 1), from_lat(up, -1)
    part = call(inner_kernel, wide, name="inner")(scaled, aligned_inverse, stag)
    pieces = (scaled, part, scale, above, below, stag, stag_below, flags)
    flat = call(
        lambda *r: coefficients_kernel(groups, length, *r), [wide] * 3, name="coefficients"
    )(slab, after(spec_rhs, scaled))
    late = after(late, *flat)
    filtered = exchanged(
        call(
            lambda *r: halo_kernel(norm, *r), (rows, WIDE + 128), [(rows, 128)] * 2, name="halo"
        )(*pieces, late)
    )
    spec, first, image, sums = call(
        lambda *r: step_kernel(groups, length, *r),
        [wide, wide, wide, (8, 128)],
        transforms + [(3 * rows, 128)] * 2 + [(rows, 128), (groups, WIDE)] + turns,
        name="step",
    )(filtered, slab, *flat, matrices, outer)
    spec_image = exchanged(spec)
    scaled, part, down, up, own = call(
        lambda *r: sums_kernel(norm, length, *r), [wide, wide, edge, edge, (8, 128)], name="sums"
    )(spec_image, scale, aligned_inverse, stag, stag_below, flags, sums)
    above, below = from_lat(down, 1), from_lat(up, -1)
    cut, image_cut = WIDE - length, SCALARS - length
    first_cells, aside = call(
        lambda *r: unpack_first_kernel(length, cut, *r), [cells, wide], name="unpack_first"
    )(after(spec_image, scaled), image)
    filtered = exchanged(
        call(lambda *r: ends_kernel(norm, length, *r), wide, name="ends")(
            scaled, part, scale, above, below, stag, stag_below, flags, aside, own
        )
    )

    pair = call(gather_kernel, (8, 128), name="gather")(filtered)
    image_cells = call(
        lambda *r: unpack_kernel(length, image_cut, *r), cells, name="unpack_image"
    )(filtered)
    packed = call(lambda *r: last_kernel(groups, length, *r), wide, turns, name="last")(
        filtered, flat[0], first, image, matrices
    )
    return tuple(
        call(lambda *r: finish_kernel(length, *r), [cells] * 3, name="finish")(
            exchanged(packed),
            first_cells,
            image_cells,
            surface_forcing,
            ocean_mask,
            pair,
            from_lat(pair, 2),
            from_lat(pair, -2),
            from_lat(pair, 4),
        )
    )


def solution(mesh):
    torus = Mesh(
        mesh.devices.reshape(mesh.shape["lat"], 4, 4, 2), ("lat", "lon_0", "lon_1", "lon_2")
    )
    return jax.shard_map(
        local,
        mesh=torus,
        in_specs=(
            P(LON, "lat"),
            P(LON, "lat"),
            P(LON, "lat"),
            P(LON, "lat"),
            P(LON, "lat"),
            P("lat"),
            P("lat", None, None),
            P("lat", None, None),
        ),
        out_specs=(P(LON, "lat"), P(LON, "lat"), P(LON, "lat")),
        check_vma=False,
    )
```

```python
import jax
import jax.numpy as jnp
import numpy as np
from jax import lax
from jax.experimental import pallas as pl
from jax.experimental.pallas import tpu as pltpu
from jax.sharding import Mesh
from jax.sharding import PartitionSpec as P

LON = ("lon_0", "lon_1", "lon_2")
TURN = 2.0 * np.pi
ROWS = 8
WIDE = 256
HALO = 136
FOLD = 68
LATE = HALO + FOLD
SCALARS = WIDE - 4


def tables(groups, length):
    period = groups * length
    index = np.arange(length)
    inner = TURN * (np.outer(index, index) % length) / length
    wave_of = np.zeros(groups, np.int64)
    wave_of[1] = groups // 2
    for m in range(1, groups // 2):
        wave_of[2 * m] = wave_of[2 * m + 1] = m
    turn = TURN * (np.outer(wave_of, index) % period) / period
    rows = np.zeros((2 * WIDE + 2 * groups, WIDE), np.float32)
    rows[:length, :length] = np.cos(inner)
    rows[WIDE : WIDE + length, :length] = np.sin(inner)
    rows[2 * WIDE : 2 * WIDE + groups, :length] = np.cos(turn)
    rows[2 * WIDE + groups :, :length] = np.sin(turn)
    coarse = rows.astype(jnp.bfloat16)
    rest = (rows - coarse.astype(np.float32)).astype(jnp.bfloat16)
    chunk = np.arange(groups)
    outer = np.zeros((2, groups, groups))
    for c in range(groups):
        phase = TURN * (chunk * wave_of[c] % groups) / groups
        if c < 2:
            outer[0, :, c] = outer[1, :, c] = np.cos(phase)
        elif c % 2 == 0:
            outer[0, :, c], outer[1, :, c] = 2 * np.cos(phase), -2 * np.sin(phase)
        else:
            outer[0, :, c], outer[1, :, c] = -2 * np.sin(phase), -2 * np.cos(phase)
    modes = wave_of[:, None] + groups * index[None, :]
    wave = np.zeros((groups, WIDE))
    wave[:, :length] = 4.0 * np.sin(np.pi * modes / period) ** 2
    return (
        np.stack([coarse, rest]),
        np.concatenate([outer[0], outer[1]], axis=1).astype(np.float32),
        wave.astype(np.float32),
    )


def real_fft(values):
    count = len(values)
    if count == 2:
        return [(values[0] + values[1], None), (values[0] - values[1], None)]
    even, odd = real_fft(values[0::2]), real_fft(values[1::2])
    out = [None] * (count // 2 + 1)
    for k in range(count // 4 + 1):
        (er, ei), (re, im) = even[k], odd[k]
        if k == 0:
            out[0], out[count // 2] = (er + re, None), (er - re, None)
        elif k == count // 4:
            out[k] = (er, -re)
        else:
            c, s = float(np.cos(TURN * k / count)), float(-np.sin(TURN * k / count))
            tr, ti = re * c - im * s, im * c + re * s
            out[k], out[count // 2 - k] = (er + tr, ei + ti), (er - tr, ti - ei)
    return out


def real_ifft(spectrum):
    count = 2 * (len(spectrum) - 1)
    if count == 2:
        return [spectrum[0][0] + spectrum[1][0], spectrum[0][0] - spectrum[1][0]]
    even, odd = [], []
    for k in range(count // 4 + 1):
        (ar, ai), (br, bi) = spectrum[k], spectrum[count // 2 - k]
        if k == 0:
            even.append((ar + br, None))
            odd.append((ar - br, None))
        elif k == count // 4:
            even.append((2.0 * ar, None))
            odd.append((-2.0 * ai, None))
        else:
            c, s = float(np.cos(TURN * k / count)), float(np.sin(TURN * k / count))
            dr, di = ar - br, ai + bi
            even.append((ar + br, ai - bi))
            odd.append((dr * c - di * s, dr * s + di * c))
    first, second = real_ifft(even), real_ifft(odd)
    out = []
    for a, b in zip(first, second, strict=True):
        out += [a, b]
    return out


def split(a):
    coarse = a.astype(jnp.bfloat16)
    return coarse, (a - coarse.astype(jnp.float32)).astype(jnp.bfloat16)


def product(a, b):
    (ac, ar), (bc, br) = a, b

    def one(x, y):
        return jnp.dot(x, y, preferred_element_type=jnp.float32)

    return one(ac, bc) + (one(ac, br) + one(ar, bc))


def dot(a, b):
    return product(split(a), split(b))


def table(matrix_ref, n):
    at = slice(n * WIDE, (n + 1) * WIDE)
    return matrix_ref[0, at, :], matrix_ref[1, at, :]


def load_twiddle(matrix_ref, twiddle):
    groups = twiddle.shape[1]
    for n in range(2):
        at = slice(2 * WIDE + n * groups, 2 * WIDE + (n + 1) * groups)
        twiddle[n] = matrix_ref[0, at, :].astype(jnp.float32) + matrix_ref[1, at, :].astype(
            jnp.float32
        )


def rows_of(p):
    return slice(ROWS * p, ROWS * (p + 1))


def lanes(shape):
    return lax.broadcasted_iota(jnp.int32, shape, len(shape) - 1)


def sublanes(shape):
    return lax.broadcasted_iota(jnp.int32, shape, len(shape) - 2)


def shifted(value, lanes_right):
    return pltpu.roll(value, lanes_right % value.shape[1], 1)


def pack_kernel(rhs_ref, own_ref, out_ref, tall):
    length = rhs_ref.shape[0]
    tall[:length, :] = rhs_ref[...]
    tall[length:, :] = own_ref[: WIDE - length, :]
    out_ref[...] = tall[...].T


def edges_kernel(mask_ref, north_ref, stag_ref, wet_ref, low_ref, tall):
    length, rows = mask_ref.shape
    count, block = stag_ref.shape[0], stag_ref.shape[1]
    tall[length:, :] = jnp.zeros((WIDE - length, 128), jnp.float32)
    tall[:length, :] = mask_ref[:, :128].astype(jnp.float32)
    wet_ref[...] = tall[...].T[:ROWS]
    tall[:length, :] = mask_ref[:, rows - 128 :].astype(jnp.float32) * north_ref[:, rows - 128 :]
    top = tall[...].T[127:]
    keep = block // 2 + ROWS
    low_ref[:keep, :] = stag_ref[count - 1, block - keep :, :]
    row = sublanes((ROWS, 128))
    low_ref[keep:, :] = jnp.where(row == 0, top[:, :128], top[:, 128:])


def lane_plan(length):
    cut = WIDE - length
    count = 2 * cut - length
    north = LATE
    east = north + length
    return cut, count, north, east, east + length - count


def pack_more_kernel(own_ref, mask_ref, east_ref, out_ref, tall):
    length, rows = mask_ref.shape
    cut, count = lane_plan(length)[:2]
    tall[:length, :] = jnp.zeros((length, rows), jnp.float32)
    tall[length : WIDE - count, :] = own_ref[cut:, :]
    tall[WIDE - count :, :] = (mask_ref[...].astype(jnp.float32) * east_ref[...])[:count]
    out_ref[...] = tall[...].T


def pack_rest_kernel(
    mask_ref,
    east_ref,
    north_ref,
    flags_ref,
    wet_above_ref,
    from_below_ref,
    out_ref,
    tall,
    aside,
    low,
    high,
    last,
):
    length, rows = mask_ref.shape
    _, count, n_at, e_at, f_at = lane_plan(length)
    block = from_below_ref.shape[0] - ROWS
    lane = lanes((length, rows))
    wet = mask_ref[...].astype(jnp.float32)
    north = wet * north_ref[...]
    wet_above = wet_above_ref[...].T[:length, :1] * flags_ref[:1, :1]
    top = from_below_ref[block:, :].T
    top_below = jnp.concatenate([top[:, :1], top[: length - 128, 1:2]], axis=0) * flags_ref[1:2, :1]
    tall[128:n_at, :] = jnp.zeros((n_at - 128, rows), jnp.float32)
    tall[n_at:e_at, :] = north * jnp.where(lane == rows - 1, wet_above, shifted(wet, -1))
    tall[e_at:f_at, :] = (wet * east_ref[...])[count:]
    tall[f_at:, :] = jnp.zeros((WIDE + 128 - f_at, rows), jnp.float32)
    out_ref[:, :128] = tall[128:WIDE, :].T
    last[...] = tall[WIDE:, :].T
    aside[length:, :] = jnp.zeros((WIDE - length, rows), jnp.float32)
    aside[:length, :] = wet * jnp.where(lane == 0, top_below, shifted(north, 1))
    low[...] = aside[:128, :].T
    high[...] = aside[128:, :].T
    groups = rows // ROWS
    at = pl.ds(0, groups, stride=ROWS)
    before = jnp.concatenate([low[at, :], high[at, :]], axis=1)
    fold = f_at - WIDE
    lane = lanes((groups, 128))
    for n in range(ROWS):
        at = pl.ds(n, groups, stride=ROWS)
        piece = shifted(before, fold - n * (128 - fold))[:, :128]
        last[at, :] = jnp.where(lane >= fold, piece, last[at, :])
    out_ref[:, 128:] = last[...]


def coefficients_kernel(groups, length, slab_ref, second_ref, own_ref, next_ref, east_ref):
    cut, count = lane_plan(length)[:2]
    lane = lanes((ROWS, WIDE))
    for p in range(groups):
        at = rows_of(p)
        more = second_ref[at, :]
        own_ref[at, :] = jnp.where(
            lane < cut,
            shifted(slab_ref[at, :], -length),
            jnp.where(lane < length, shifted(more, cut - length), 0.0),
        )
        east_ref[at, :] = jnp.where(lane < count, shifted(more, count), 0.0)
    for p in range(groups):
        own = own_ref[rows_of(p), :]
        after = own_ref[rows_of((p + 1) % groups), 0:1]
        ocean = jnp.where(lane == length, after, own) > 0.0
        next_ref[rows_of(p), :] = shifted(ocean.astype(jnp.float32), -1)


def transform(chunks, matrix_ref, twiddle_ref, left, right):
    groups = len(chunks)
    mixed = real_fft(chunks)
    for m in range(groups // 2 + 1):
        re, im = mixed[m]
        if m == 0:
            left[rows_of(0), :] = re
            right[rows_of(0), :] = re
            continue
        c = 1 if m == groups // 2 else 2 * m
        cos, sin = twiddle_ref[0, c : c + 1, :], twiddle_ref[1, c : c + 1, :]
        if m == groups // 2:
            left[rows_of(1), :] = re * (cos + sin)
            right[rows_of(1), :] = re * (cos - sin)
        else:
            tr, ti = re * cos + im * sin, im * cos - re * sin
            left[rows_of(c), :] = tr
            right[rows_of(c), :] = ti
            left[rows_of(c + 1), :] = ti
            right[rows_of(c + 1), :] = -tr
    return product(split(left[...]), table(matrix_ref, 0)) + product(
        split(right[...]), table(matrix_ref, 1)
    )


def both_products(spectrum, matrix_ref):
    parts = split(spectrum)
    return product(parts, table(matrix_ref, 0)), product(parts, table(matrix_ref, 1))


def transform_back(products, groups, twiddle_ref):
    pc, ps = products
    mixed = []
    for m in range(groups // 2 + 1):
        if m == 0:
            mixed.append((pc[rows_of(0)] + ps[rows_of(0)], None))
            continue
        c = 1 if m == groups // 2 else 2 * m
        cos, sin = twiddle_ref[0, c : c + 1, :], twiddle_ref[1, c : c + 1, :]
        if m == groups // 2:
            mixed.append((pc[rows_of(1)] * (cos + sin) + ps[rows_of(1)] * (cos - sin), None))
        else:
            hr = pc[rows_of(c)] - ps[rows_of(c + 1)]
            hi = ps[rows_of(c)] + pc[rows_of(c + 1)]
            mixed.append((hr * cos - hi * sin, hi * cos + hr * sin))
    return real_ifft(mixed)


def rows_back(products, start, twiddle_ref, outer_ref):
    groups = outer_ref.shape[0]
    cos, sin = twiddle_ref[0], twiddle_ref[1]
    turned = [[], []]
    for n in range(2):
        pc, ps = (v[start + n * groups : start + (n + 1) * groups] for v in products)
        turned[0].append(pc * cos - ps * sin)
        turned[1].append(ps * cos + pc * sin)
    both = jnp.concatenate([jnp.concatenate(v, axis=1) for v in turned], axis=0)
    both = dot(outer_ref[...], both)
    return both[:, :WIDE], both[:, WIDE:]


def forward_kernel(
    groups,
    field_ref,
    own_ref,
    mask_ref,
    east_ref,
    matrix_ref,
    out_ref,
    left,
    right,
    twiddle_ref,
    rest_ref,
    tall,
):
    pack_more_kernel(own_ref, mask_ref, east_ref, rest_ref, tall)
    load_twiddle(matrix_ref, twiddle_ref)
    chunks = [field_ref[rows_of(p), :] for p in range(groups)]
    spectrum = transform(chunks, matrix_ref, twiddle_ref, left, right)
    out_ref[...] = spectrum + rest_ref[...]


def store_edge(ref, value, extra):
    half = value.shape[0]
    ref[:half, :] = value[:, :128]
    ref[half : half + ROWS, :] = jnp.concatenate(
        [value[:, 128:].T[:ROWS], jnp.zeros((ROWS, 128 - half), jnp.float32)], axis=1
    )
    ref[half + ROWS :, :] = extra


def load_edge(ref):
    half = ref.shape[0] - 2 * ROWS
    turned = ref[half : half + ROWS, :].T[:half]
    blank = jnp.zeros((half, 128 - ROWS), jnp.float32)
    return jnp.concatenate([ref[:half, :], turned, blank], axis=1)


def store_rows(ref, value, part, scale):
    row = sublanes((ROWS, 128))
    extra = jnp.where(row == 0, part[:, :128], part[:, 128:])
    store_edge(
        ref,
        value,
        jnp.where(row < 2, extra, jnp.where(row == 2, scale[:, :128], scale[:, 128:])),
    )


def load_rows(ref):
    at = ref.shape[0] - ROWS
    lines = [ref[at + n : at + n + 1, :] for n in range(4)]
    return jnp.concatenate(lines[:2], axis=1), jnp.concatenate(lines[2:], axis=1)


def blocks_kernel(spec_ref, scale_ref, aligned_ref, scaled_ref, down_ref, up_ref):
    count, block = aligned_ref.shape[0], aligned_ref.shape[1]
    half, rows = block // 2, count * block
    scaled = spec_ref[...] * scale_ref[...]
    scaled_ref[...] = scaled
    first = dot(aligned_ref[0, :ROWS, :], scaled[:block])
    last = dot(aligned_ref[count - 1, block - ROWS :, :], scaled[rows - block :])
    store_rows(down_ref, scaled[:half], first[:1], scale_ref[:1, :])
    store_rows(up_ref, scaled[rows - half :], last[ROWS - 1 :], scale_ref[rows - 1 :, :])


def inner_kernel(scaled_ref, aligned_ref, stag_ref, part_ref):
    count, block = aligned_ref.shape[0], aligned_ref.shape[1]
    half = block // 2
    for b in range(count):
        at = slice(b * block, (b + 1) * block)
        part_ref[at, :] = dot(aligned_ref[b], scaled_ref[at, :])
    for b in range(count - 1):
        at = slice(half + b * block, half + (b + 1) * block)
        part_ref[at, :] = part_ref[at, :] + dot(stag_ref[b], scaled_ref[at, :])


def combine(
    norm, scaled_ref, part_ref, scale_ref, above_ref, below_ref, stag_ref, stag_below_ref, flags_ref
):
    count, block = stag_ref.shape[0], stag_ref.shape[1]
    half, rows = block // 2, count * block
    before = flags_ref[1:2, :] * dot(
        stag_below_ref[: ROWS + half, :],
        jnp.concatenate([load_edge(below_ref), scaled_ref[:half, :]], axis=0),
    )
    upper = load_edge(above_ref) * flags_ref[:1, :]
    after = dot(
        stag_ref[count - 1, : half + ROWS, :],
        jnp.concatenate([scaled_ref[rows - half :, :], upper], axis=0),
    )
    pieces = [
        part_ref[:half, :] + before[ROWS:],
        part_ref[half : rows - half, :],
        part_ref[rows - half :, :] + after[:half],
    ]
    full = jnp.concatenate(pieces, axis=0) * (scale_ref[...] * norm)
    return full, before, after


def halo_kernel(
    norm,
    scaled_ref,
    part_ref,
    scale_ref,
    above_ref,
    below_ref,
    stag_ref,
    stag_below_ref,
    flags_ref,
    late_ref,
    out_ref,
    low,
    high,
):
    half = stag_ref.shape[1] // 2
    full, before, after = combine(
        norm,
        scaled_ref,
        part_ref,
        scale_ref,
        above_ref,
        below_ref,
        stag_ref,
        stag_below_ref,
        flags_ref,
    )
    part, scale = load_rows(below_ref)
    row_below = (before[ROWS - 1 : ROWS] + part) * (scale * norm)
    part, scale = load_rows(above_ref)
    row_above = (after[half : half + 1] + part) * (scale * norm)
    out_ref[:, :128] = full[:, :128]
    low[...] = full[:, :128]
    high[...] = full[:, 128:]
    groups = full.shape[0] // ROWS

    def strided(start):
        at = pl.ds(start, groups, stride=ROWS)
        return jnp.concatenate([low[at, :], high[at, :]], axis=1)

    row = lax.broadcasted_iota(jnp.int32, (groups, WIDE), 0)
    up = jnp.where(row == 0, row_below, pltpu.roll(strided(ROWS - 1), 1, 0))
    down = jnp.where(row == groups - 1, row_above, pltpu.roll(strided(0), groups - 1, 0))
    lane = lanes((groups, 128)) + 128
    for s, part in enumerate(
        (
            pltpu.roll(up, HALO, 1),
            pltpu.roll(up, HALO - FOLD, 1),
            pltpu.roll(down, HALO, 1),
            pltpu.roll(down, HALO - FOLD, 1),
        )
    ):
        at = pl.ds(s, groups, stride=ROWS)
        high[at, :] = jnp.where(lane >= HALO, part[:, 128:], high[at, :])
    out_ref[:, 128:WIDE] = jnp.where(
        lanes(high.shape) < LATE - 128, high[...], late_ref[:, :128]
    )
    out_ref[:, WIDE:] = late_ref[:, 128:]


def sums_kernel(
    norm,
    length,
    spec_ref,
    scale_ref,
    aligned_ref,
    stag_ref,
    stag_below_ref,
    flags_ref,
    sums_ref,
    scaled_ref,
    part_ref,
    down_ref,
    up_ref,
    own_ref,
):
    count, block = aligned_ref.shape[0], aligned_ref.shape[1]
    half, rows = block // 2, count * block
    scaled = spec_ref[...] * scale_ref[...]
    scaled_ref[...] = scaled
    for b in range(count):
        at = slice(b * block, (b + 1) * block)
        part_ref[at, :] = dot(aligned_ref[b], scaled[at])
    for b in range(count - 1):
        at = slice(half + b * block, half + (b + 1) * block)
        part_ref[at, :] = part_ref[at, :] + dot(stag_ref[b], scaled[at])
    first, last = slice(0, half), slice(rows - half, rows)
    part_ref[first, :] = part_ref[first, :] + flags_ref[1:2, :] * dot(
        stag_below_ref[ROWS : ROWS + half, half:], scaled[first]
    )
    part_ref[last, :] = part_ref[last, :] + dot(stag_ref[count - 1, :half, :half], scaled[last])
    total = total_of(scaled * part_ref[...], length) * (flags_ref[2:3, :1] * norm)
    small = lanes((8, 128))
    own = jnp.where(small == SCALARS - 128 + 2, total, sums_ref[...])
    own_ref[...] = own
    store_edge(down_ref, scaled[first], own)
    store_edge(up_ref, scaled[last], own)


def total_of(value, length):
    columns = jnp.sum(value, axis=0, keepdims=True)
    columns = jnp.where(lanes(columns.shape) < length, columns, 0.0)
    return jnp.sum(columns[:, :128] + columns[:, 128:], axis=1, keepdims=True)


def ends_kernel(
    norm,
    length,
    scaled_ref,
    part_ref,
    scale_ref,
    above_ref,
    below_ref,
    stag_ref,
    stag_below_ref,
    flags_ref,
    aside_ref,
    own_ref,
    out_ref,
):
    count, block = stag_ref.shape[0], stag_ref.shape[1]
    half, rows = block // 2, count * block
    first, last = slice(0, half), slice(rows - half, rows)
    low = dot(stag_below_ref[ROWS : ROWS + half, :half], load_edge(below_ref)) * flags_ref[1:2, :]
    high = dot(stag_ref[count - 1, :half, half:], load_edge(above_ref)) * flags_ref[:1, :]
    both = total_of(low * scaled_ref[first, :] + high * scaled_ref[last, :], length)
    both = both * (flags_ref[2:3, :1] * (2.0 * norm))
    pair = own_ref[:1, :] + below_ref[half + ROWS : half + ROWS + 1, :]
    pair = jnp.where(lanes(pair.shape) == SCALARS - 128 + 2, pair + both, pair)
    middle = slice(half, rows - half)
    for at, more in ((first, low), (middle, None), (last, high)):
        full = part_ref[at, :] if more is None else part_ref[at, :] + more
        full = full * (scale_ref[at, :] * norm)
        full = jnp.where(lanes(full.shape) < length, full, aside_ref[at, :])
        out_ref[at, :128] = full[:, :128]
        inside = lanes((full.shape[0], 128)) < SCALARS - 128
        out_ref[at, 128:] = jnp.where(inside, full[:, 128:], pair)


def gather_kernel(spec_ref, sums_ref):
    riders = jnp.sum(spec_ref[:, 128:], axis=0, keepdims=True) * (1.0 / ROWS)
    sums_ref[...] = jnp.broadcast_to(riders, (8, 128))


def step_kernel(
    groups,
    length,
    spec_ref,
    rhs_ref,
    own_ref,
    next_ref,
    east_ref,
    matrix_ref,
    outer_ref,
    out_ref,
    first_ref,
    image_ref,
    sums_ref,
    left,
    right,
    low,
    high,
    tail,
    folded,
    twiddle_ref,
):
    load_twiddle(matrix_ref, twiddle_ref)
    lane_row = lanes((groups, WIDE))
    stride = 3 * ROWS
    tail[...] = spec_ref[:, 128:WIDE]

    def halo_row(s):
        blank = jnp.zeros((groups, 128), jnp.float32)
        parts = [
            jnp.concatenate([tail[pl.ds(s + n, groups, stride=ROWS), :], blank], axis=1)
            for n in range(2)
        ]
        return jnp.where(
            lane_row < FOLD, shifted(parts[0], 128 - HALO), shifted(parts[1], FOLD + 128 - HALO)
        )

    stacked = jnp.concatenate([spec_ref[:, :WIDE], halo_row(0), halo_row(2)], axis=0)
    products = both_products(stacked, matrix_ref)
    halos = rows_back(products, groups * ROWS, twiddle_ref, outer_ref)
    for start, row in zip((ROWS - 1, 2 * ROWS), halos, strict=True):
        low[pl.ds(start, groups, stride=stride), :] = row[:, :128]
        high[pl.ds(start, groups, stride=stride), :] = row[:, 128:]

    def neighbour(start):
        at = slice(start, start + ROWS)
        return jnp.concatenate([low[at, :], high[at, :]], axis=1)

    cells = transform_back(products, groups, twiddle_ref)
    for p in range(groups):
        v = jnp.where(own_ref[rows_of(p), :] > 0.0, cells[p], 0.0)
        first_ref[rows_of(p), :] = v
        low[stride * p + ROWS : stride * p + 2 * ROWS, :] = v[:, :128]
        high[stride * p + ROWS : stride * p + 2 * ROWS, :] = v[:, 128:]
    lane, row = lanes((ROWS, WIDE)), sublanes((ROWS, WIDE))
    _, count, n_at, e_at, f_at = lane_plan(length)
    tail[...] = spec_ref[:, WIDE:]
    fold, blank = f_at - WIDE, jnp.zeros((groups, 128), jnp.float32)
    width = 128 - fold
    before = jnp.zeros((groups, WIDE), jnp.float32)
    for n in range(ROWS):
        piece = jnp.concatenate([tail[pl.ds(n, groups, stride=ROWS), :], blank], axis=1)
        inside = (lane_row >= n * width) & (lane_row < (n + 1) * width)
        before = jnp.where(inside, shifted(piece, n * width - fold), before)
    folded[...] = before
    rz = jnp.zeros((ROWS, WIDE), jnp.float32)
    curvature = jnp.zeros((ROWS, WIDE), jnp.float32)
    images, fluxes = [], []
    for p in range(groups):
        at = rows_of(p)
        v = first_ref[at, :]
        after = first_ref[rows_of((p + 1) % groups), 0:1]
        east = jnp.where(
            lane < count, east_ref[at, :], shifted(spec_ref[at, 128:], count - (e_at - 128))
        )
        flux = v - shifted(jnp.where(lane == length, after, v), -1)
        fluxes.append(jnp.where(lane < length, east * next_ref[at, :] * flux, 0.0))
    for p in range(groups):
        at = rows_of(p)
        v = first_ref[at, :]
        before = fluxes[(p - 1) % groups][:, length - 1 : length]
        flux = fluxes[p]
        own = own_ref[at, :]
        base = stride * p + ROWS
        north = shifted(spec_ref[at, 128:], 128 - n_at)
        south = jnp.where(row == 0, folded[p : p + 1, :], pltpu.roll(north, 1, 0))
        image = jnp.where(own > 0.0, own, 1.0) * v
        image = image + (flux - shifted(jnp.where(lane == WIDE - 1, before, flux), 1))
        image = image + north * (v - neighbour(base + 1))
        image = image + south * (v - neighbour(base - 1))
        image = jnp.where(lane < length, image, 0.0)
        image_ref[at, :] = image
        images.append(image)
        rz = rz + rhs_ref[at, :] * v
        curvature = curvature + v * image
    small = lanes((8, 128))
    at = SCALARS - 128
    sums_ref[...] = jnp.where(
        small == at, jnp.sum(rz), jnp.where(small == at + 1, jnp.sum(curvature), 0.0)
    )
    spectrum = transform(images, matrix_ref, twiddle_ref, left, right)
    out_ref[...] = jnp.where(
        lanes(out_ref.shape) < length, spectrum, shifted(first_ref[...], length)
    )


def last_kernel(
    groups,
    length,
    spec_ref,
    own_ref,
    first_ref,
    image_ref,
    matrix_ref,
    out_ref,
    twiddle_ref,
):
    load_twiddle(matrix_ref, twiddle_ref)
    cells = transform_back(both_products(spec_ref[...], matrix_ref), groups, twiddle_ref)
    lane = lanes((ROWS, WIDE))
    cut = WIDE - length
    image_cut = SCALARS - length
    image_at = 2 * length - cut
    for p in range(groups):
        at = rows_of(p)
        cell = jnp.where(own_ref[at, :] > 0.0, cells[p], 0.0)
        out = jnp.where(lane < length, cell, shifted(first_ref[at, :], length - cut))
        out_ref[at, :] = jnp.where(
            lane < image_at, out, shifted(image_ref[at, :], image_at - image_cut)
        )


def unpack_kernel(length, count, slab_ref, out_ref):
    turned = slab_ref[:, 128:].T
    out_ref[:count, :] = turned[length - 128 : length - 128 + count]


def unpack_first_kernel(length, count, slab_ref, image_ref, out_ref, aside_ref):
    unpack_kernel(length, count, slab_ref, out_ref)
    lane = lanes(image_ref.shape)
    aside_ref[...] = jnp.where(lane < length, 0.0, shifted(image_ref[...], length))


def finish_kernel(
    length,
    back_ref,
    first_ref,
    image_ref,
    forcing_ref,
    mask_ref,
    pair_ref,
    ahead_ref,
    behind_ref,
    across_ref,
    solution_ref,
    residual_ref,
    direction_ref,
):
    at = SCALARS - 128
    totals = (pair_ref[:1, :] + across_ref[:1, :]) + (ahead_ref[:1, :] + behind_ref[:1, :])
    rz, curvature, own = [totals[:, at + n : at + n + 1] for n in range(3)]
    alpha = rz / curvature
    rz_next = rz - 2.0 * alpha * curvature + alpha * alpha * own
    beta = rz_next / rz
    back = back_ref[...].T
    cut = WIDE - length
    image_cut = SCALARS - length
    image_at = 2 * length - cut
    rhs = mask_ref[...].astype(jnp.float32) * forcing_ref[...]

    def store(where, rows_back, first):
        solution_ref[where, :] = alpha * first
        direction_ref[where, :] = (first - alpha * rows_back) + beta * first

    store(slice(0, cut), back[:cut], first_ref[:cut, :])
    store(slice(cut, length), back[cut:length], back[length:image_at])
    residual_ref[:image_cut, :] = rhs[:image_cut] - alpha * image_ref[:image_cut, :]
    residual_ref[image_cut:, :] = (
        rhs[image_cut:] - alpha * back[image_at : image_at + length - image_cut]
    )


def call(kernel, out_shapes, scratch=(), name=None):
    single = not isinstance(out_shapes, (list, tuple)) or isinstance(out_shapes[0], int)
    shapes = [out_shapes] if single else out_shapes
    outs = [jax.ShapeDtypeStruct(s, jnp.float32) for s in shapes]
    return pl.pallas_call(
        kernel,
        out_shape=outs[0] if single else outs,
        scratch_shapes=[pltpu.VMEM(s, jnp.float32) for s in scratch],
        compiler_params=pltpu.CompilerParams(vmem_limit_bytes=16 * 2**20),
        name=name,
    )


def exchanged(value):
    groups = lax.axis_size(LON)
    parts = value.reshape(groups, ROWS, value.shape[-1])
    return lax.all_to_all(parts, LON, split_axis=0, concat_axis=0, tiled=True).reshape(value.shape)


def from_lat(value, steps):
    count = lax.axis_size("lat")
    return lax.ppermute(value, "lat", [((d + steps) % count, d) for d in range(count)])


def after(value, *others):
    return lax.optimization_barrier((value, *others))[0]


def local(
    surface_forcing,
    ocean_mask,
    self_coupling,
    east_coupling,
    north_coupling,
    zonal_weight,
    aligned_inverse,
    staggered_inverse,
):
    groups = lax.axis_size(LON)
    length, rows = surface_forcing.shape
    norm = 1.0 / (groups * length)
    matrices, outer, wave = tables(groups, length)
    count, block = aligned_inverse.shape[0], aligned_inverse.shape[1]
    half = block // 2
    wide = (rows, WIDE)
    turns = [(2, groups, WIDE)]
    transforms = [wide, wide]

    cells = (length, rows)
    places = (lax.axis_index(LON), lax.axis_index("lat"))
    flag_row = lax.broadcasted_iota(jnp.int32, (8, WIDE), 0)
    surface_forcing, channel, lat = lax.optimization_barrier((surface_forcing, *places))
    wet_cells = ocean_mask.astype(jnp.float32)
    own_cells = wet_cells * self_coupling
    packed = call(pack_kernel, wide, [wide], name="pack")(wet_cells * surface_forcing, own_cells)
    slab = exchanged(packed)

    mask, east_cells = lax.optimization_barrier((ocean_mask, east_coupling, slab))[:2]
    spectrum = call(lambda *r: forward_kernel(groups, *r), wide, transforms + turns + [wide] * 2, name="forward")(
        slab, own_cells, mask, east_cells, matrices
    )
    spec_rhs = exchanged(spectrum)

    north_cells, stag = lax.optimization_barrier((north_coupling, staggered_inverse, spectrum))[:-1]
    wet_first, low_last = call(
        edges_kernel, [(ROWS, WIDE), (half + 2 * ROWS, 128)], [(WIDE, 128)], name="edges"
    )(mask, north_cells, stag)
    weights, channel, lat, flag_row = lax.optimization_barrier(
        (
            zonal_weight,
            channel,
            lat,
            flag_row,
            wet_first,
        )
    )[:-1]
    scale = lax.rsqrt(1.0 + weights[:, None] * lax.dynamic_slice_in_dim(wave, channel, 1, 0))
    north_of, south_of, weight = (
        jnp.where(condition, yes, no).astype(jnp.float32)
        for condition, yes, no in (
            (lat < lax.axis_size("lat") - 1, 1.0, 0.0),
            (lat > 0, 1.0, 0.0),
            (channel < 2, 1.0, 2.0),
        )
    )
    flags = jnp.where(flag_row == 0, north_of, jnp.where(flag_row == 1, south_of, weight))
    stag_below = from_lat(low_last, -1)
    late = call(
        pack_rest_kernel,
        wide,
        [(WIDE + 128, rows), wide, (rows, 128), (rows, 128), (rows, 128)],
        name="pack_rest",
    )(mask, east_cells, north_cells, flags, from_lat(wet_first, 1), stag_below)
    spec_rhs = after(spec_rhs, late, scale, flags)

    edge = (half + 2 * ROWS, 128)

    scaled, down, up = call(blocks_kernel, [wide, edge, edge], name="blocks")(
        spec_rhs, scale, aligned_inverse
    )
    above, below = from_lat(down, 1), from_lat(up, -1)
    part = call(inner_kernel, wide, name="inner")(scaled, aligned_inverse, stag)
    pieces = (scaled, part, scale, above, below, stag, stag_below, flags)
    flat = call(
        lambda *r: coefficients_kernel(groups, length, *r), [wide] * 3, name="coefficients"
    )(slab, after(spec_rhs, scaled))
    late = after(late, *flat)
    filtered = exchanged(
        call(
            lambda *r: halo_kernel(norm, *r), (rows, WIDE + 128), [(rows, 128)] * 2, name="halo"
        )(*pieces, late)
    )
    spec, first, image, sums = call(
        lambda *r: step_kernel(groups, length, *r),
        [wide, wide, wide, (8, 128)],
        transforms + [(3 * rows, 128)] * 2 + [(rows, 128), (groups, WIDE)] + turns,
        name="step",
    )(filtered, slab, *flat, matrices, outer)
    spec_image = exchanged(spec)
    scaled, part, down, up, own = call(
        lambda *r: sums_kernel(norm, length, *r), [wide, wide, edge, edge, (8, 128)], name="sums"
    )(spec_image, scale, aligned_inverse, stag, stag_below, flags, sums)
    above, below = from_lat(down, 1), from_lat(up, -1)
    cut, image_cut = WIDE - length, SCALARS - length
    first_cells, aside = call(
        lambda *r: unpack_first_kernel(length, cut, *r), [cells, wide], name="unpack_first"
    )(after(spec_image, scaled), image)
    filtered = exchanged(
        call(lambda *r: ends_kernel(norm, length, *r), wide, name="ends")(
            scaled, part, scale, above, below, stag, stag_below, flags, aside, own
        )
    )

    pair = call(gather_kernel, (8, 128), name="gather")(filtered)
    image_cells = call(
        lambda *r: unpack_kernel(length, image_cut, *r), cells, name="unpack_image"
    )(filtered)
    packed = call(lambda *r: last_kernel(groups, length, *r), wide, turns, name="last")(
        filtered, flat[0], first, image, matrices
    )
    return tuple(
        call(lambda *r: finish_kernel(length, *r), [cells] * 3, name="finish")(
            exchanged(packed),
            first_cells,
            image_cells,
            surface_forcing,
            ocean_mask,
            pair,
            from_lat(pair, 2),
            from_lat(pair, -2),
            from_lat(pair, 4),
        )
    )


def solution(mesh):
    torus = Mesh(
        mesh.devices.reshape(mesh.shape["lat"], 4, 4, 2), ("lat", "lon_0", "lon_1", "lon_2")
    )
    return jax.shard_map(
        local,
        mesh=torus,
        in_specs=(
            P(LON, "lat"),
            P(LON, "lat"),
            P(LON, "lat"),
            P(LON, "lat"),
            P(LON, "lat"),
            P("lat"),
            P("lat", None, None),
            P("lat", None, None),
        ),
        out_specs=(P(LON, "lat"), P(LON, "lat"), P(LON, "lat")),
        check_vma=False,
    )
```
